128 devices in a mesh: blk: 32 (over z_hi, y, x), head: 4 (over z_lo, core).
Axes of the slice: x: 4, y: 4, z: 4 (z_hi: 2, z_lo: 2; z = z_hi * 2 + z_lo), core: 2. Of those that a mesh axis runs over, the one named last changes fastest.
Arguments:
- tokens: bfloat16 [12288, 1024], P(('blk', 'head')), may hold values from -18 to 18
- block_order: int32 [64], replicated, may hold values from 0 to 63, as said below
- request_lengths: int32 [9], replicated, may hold values from 1 to 9216, 12288 in all
- enc_lengths: int32 [9], replicated, may hold values from 1 to 512, 2048 in all
- w_qkv: bfloat16 [3, 1024, 1024], P(None, None, 'head'), may hold values from -0.1875 to 0.1875
- w_out: bfloat16 [1024, 1024], P('head'), may hold values from -0.1875 to 0.1875
- enc_kv: bfloat16 [2, 2048, 1024], P(None, 'blk', 'head'), may hold values from -18 to 18
- w_cq: bfloat16 [1024, 1024], replicated, may hold values from -0.1875 to 0.1875
- w_co: bfloat16 [1024, 1024], replicated, may hold values from -0.1875 to 0.1875
- w_up: bfloat16 [1024, 4096], replicated, may hold values from -0.1875 to 0.1875
- w_down: bfloat16 [4096, 1024], replicated, may hold values from -0.09375 to 0.09375
- w_next: bfloat16 [3, 1024, 1024], P(None, None, 'head'), may hold values from -0.1875 to 0.1875
Outputs:
- output: float32 [12288, 1024], P(('blk', 'head'))
- cache: bfloat16 [2, 12288, 1024], P(None, 'blk', 'head')
- next_qkv: float32 [3, 12288, 1024], P(None, 'blk', 'head')
The draws below stay inside these ranges and needn't reach their ends.
Inputs may be any that keep to these rules, and one draw needn't show every extreme that they name: `block_order`: each half-block index appears once, and stored half-blocks 2i and 2i + 1 hold position blocks that add up to 63. `request_lengths`: the lengths sum to 12288. `enc_lengths`: the lengths sum to 2048.
All inputs are finite; a program needn't handle non-finite values.
Results may differ from the reference program's by a relative error of at most 0.024.
Values may be sent and summed in bfloat16 or wider, within the bound.
A program may use at most 128 MiB of HBM per device.

```python
import math
import jax
import jax.numpy as jnp
import numpy as np
from jax import lax

D = 1024
HEADS = 16
FF = 4096
HD = 64
REQS = 9
TOK_DEV = 384
ENC = 2048
TOKENS = 12288


def scaled_rows(key, shape_rows, shape_cols):
    first = jax.random.fold_in(key, 0)
    values = jnp.clip(jax.random.normal(first, (shape_rows, shape_cols), jnp.float32), -6.0, 6.0)
    return values


def draw_tokens(key, part):
    return scaled_rows(key, TOKENS, D).astype(jnp.bfloat16)


def draw_enc_kv(key, part):
    key_part = scaled_rows(jax.random.fold_in(key, 11), ENC, D)
    value_part = scaled_rows(jax.random.fold_in(key, 12), ENC, D)
    return jnp.stack([key_part, value_part]).astype(jnp.bfloat16)


def draw_block_order(key, part):
    blocks = TOKENS // TOK_DEV
    chosen = jax.random.permutation(jax.random.fold_in(key, 21), blocks).astype(jnp.int32)
    mirror = (2 * blocks - 1 - chosen).astype(jnp.int32)
    flips = jax.random.randint(jax.random.fold_in(key, 22), (blocks,), 0, 2)
    first = jnp.where(flips == 1, mirror, chosen)
    later = jnp.where(flips == 1, chosen, mirror)
    return jnp.stack([first, later], axis=1).reshape(2 * blocks).astype(jnp.int32)


def block_scale(stream_key, shape, pieces, least, top_value):
    def one(dim, shards_of):
        draws = jax.random.uniform(jax.random.fold_in(jax.random.fold_in(stream_key, 6), dim), (shards_of,), jnp.float32, least / len(pieces), top_value / len(pieces))
        return jnp.repeat(jnp.exp(draws), shape[dim] // shards_of).reshape((-1,) + (1,) * (len(shape) - dim - 1))

    gain = one(*pieces[0])
    for cut in pieces[1:]:
        gain = gain * one(*cut)
    return gain


def length_profile(count, total, most, slope):
    loads = [(1 << 20) // math.isqrt(standing ** slope) + 1 for standing in range(2, count + 1)]
    surplus, given = total - most - (count - 1), [1] * (count - 1)
    while surplus > 0:
        free = [i for i in range(count - 1) if given[i] < most]
        whole, left = sum([loads[i] for i in free]), surplus
        for i in free:
            addition = min(most - given[i], max(1, left * loads[i] // whole), surplus)
            given[i] = given[i] + addition
            surplus = surplus - addition
    return np.array([most] + given)


def uneven(rng, amount, total, reach, lean):
    if amount == 2:
        one = jax.random.randint(rng, (), max(1, total - reach), min(reach, total - 1) + 1)
        return jnp.stack([one, total - one])
    sizes = jnp.asarray(length_profile(amount, total, reach, lean), jnp.int32)
    twos = (amount - 1) // 2
    source_of, sink = sizes[1:1 + 2 * twos:2], sizes[2:2 + 2 * twos:2]
    room = jnp.minimum(source_of - 1, reach - sink)
    shifted = jax.random.randint(jax.random.fold_in(rng, 1), (twos,), 0, 1 << 20) % (room + 1)
    sizes = sizes.at[1:1 + 2 * twos:2].set(source_of - shifted).at[2:2 + 2 * twos:2].set(sink + shifted)
    return sizes[jax.random.permutation(jax.random.fold_in(rng, 2), amount)]


def bell_draw(own_key, extent, scale, limit, cuts=(), kind=jnp.bfloat16):
    gain = block_scale(own_key, extent, cuts, -0.22, 0.18) if cuts else 1.0
    array = jax.random.normal(own_key, extent, jnp.float32) * scale * gain
    return jnp.minimum(jnp.maximum(array, -limit), limit).astype(kind)


def setup_inputs(seed: int = 0) -> dict:
    keys = jax.random.split(jax.random.key(seed), 13)
    return {
        "tokens": draw_tokens(jax.random.fold_in(keys[12], 71), 0),
        "block_order": draw_block_order(jax.random.fold_in(keys[12], 71), 0),
        "request_lengths": uneven(keys[2], REQS, TOKENS, TOKENS * 3 // 4, 0).astype(jnp.int32),
        "enc_lengths": uneven(keys[3], REQS, ENC, ENC // 4, 2).astype(jnp.int32),
        "w_qkv": bell_draw(keys[4], (3, D, D), D ** -0.5, 0.1875, ((2, 4),)),
        "w_out": bell_draw(keys[5], (D, D), D ** -0.5, 0.1875, ((0, 4),)),
        "enc_kv": draw_enc_kv(jax.random.fold_in(keys[12], 71), 0),
        "w_cq": bell_draw(keys[7], (D, D), D ** -0.5, 0.1875),
        "w_co": bell_draw(keys[8], (D, D), D ** -0.5, 0.1875),
        "w_up": bell_draw(keys[9], (D, FF), D ** -0.5, 0.1875),
        "w_down": bell_draw(keys[10], (FF, D), FF ** -0.5, 0.09375),
        "w_next": bell_draw(keys[11], (3, D, D), D ** -0.5, 0.1875, ((2, 4),)),
    }


NEGATIVE = -1e+30
EPSILON = 1e-05

def normalize(matrix):
    center = matrix - lax.optimization_barrier(jnp.mean(matrix, axis=-1, keepdims=True))
    return center * lax.rsqrt(lax.optimization_barrier(jnp.mean(center * center, axis=-1, keepdims=True)) + EPSILON)

def group_of(places, lengths):
    ends = jnp.cumsum(lengths).astype(jnp.int32)
    return lax.optimization_barrier(jnp.sum((places[:, None] >= ends[None, :]).astype(jnp.int32), axis=1)).astype(jnp.int32)

def attention(queries, key_rows, value_rows, query_places, key_places, query_groups, key_groups):
    count_q = queries.shape[0]
    count_k = key_rows.shape[0]
    query_heads = queries.reshape(count_q, HEADS, HD).transpose(1, 0, 2)
    key_heads = key_rows.reshape(count_k, HEADS, HD).transpose(1, 0, 2)
    value_heads = value_rows.reshape(count_k, HEADS, HD).transpose(1, 0, 2)
    place_blocks = query_places.reshape(-1, TOK_DEV)
    group_blocks = query_groups.reshape(-1, TOK_DEV)

    def per_head(element):
        query_one, key_one, value_one = element
        query_blocks = query_one.reshape(-1, TOK_DEV, HD)

        def per_block(paired):
            query_block, place_block, group_block = paired
            scores = jnp.dot(query_block, key_one.T, preferred_element_type=jnp.float32) * 0.125
            visible = key_groups[None, :] == group_block[:, None]
            if key_places is not None:
                visible = visible & (key_places[None, :] <= place_block[:, None])
            scores = jnp.where(visible, scores, NEGATIVE)
            maxima = lax.optimization_barrier(jnp.max(scores, axis=1, keepdims=True))
            weights = jnp.where(visible, jnp.exp(scores - maxima), 0.0)
            totals = lax.optimization_barrier(jnp.sum(weights, axis=1, keepdims=True))
            return jnp.dot(weights.astype(jnp.bfloat16), value_one, preferred_element_type=jnp.float32) / totals
        return lax.map(per_block, (query_blocks, place_blocks, group_blocks)).reshape(count_q, HD)
    merged = lax.map(per_head, (query_heads, key_heads, value_heads))
    return merged.transpose(1, 0, 2).reshape(count_q, D).astype(jnp.bfloat16)

def reference(tokens, block_order, request_lengths, enc_lengths, w_qkv, w_out, enc_kv, w_cq, w_co, w_up, w_down, w_next):
    halfway = TOK_DEV // 2
    indices = jnp.arange(TOKENS, dtype=jnp.int32)
    position = (block_order[indices // halfway] * halfway + indices % halfway).astype(jnp.int32)
    request = group_of(position, request_lengths)
    enc_request = group_of(jnp.arange(ENC, dtype=jnp.int32), enc_lengths)
    query = jnp.dot(tokens, w_qkv[0], preferred_element_type=jnp.float32).astype(jnp.bfloat16)
    key_all = jnp.dot(tokens, w_qkv[1], preferred_element_type=jnp.float32).astype(jnp.bfloat16)
    value_all = jnp.dot(tokens, w_qkv[2], preferred_element_type=jnp.float32).astype(jnp.bfloat16)
    stored_kv = jnp.stack([key_all, value_all])
    cache = jnp.zeros_like(stored_kv).at[:, position].set(stored_kv)
    attended = attention(query, key_all, value_all, position, position, request, request)
    hidden = normalize(jnp.dot(attended, w_out, preferred_element_type=jnp.float32) + tokens.astype(jnp.float32))
    hidden_b = hidden.astype(jnp.bfloat16)
    cross_query = jnp.dot(hidden_b, w_cq, preferred_element_type=jnp.float32).astype(jnp.bfloat16)
    crossed = attention(cross_query, enc_kv[0], enc_kv[1], position, None, request, enc_request)
    second = normalize(jnp.dot(crossed, w_co, preferred_element_type=jnp.float32) + hidden)
    second_b = second.astype(jnp.bfloat16)
    inner = jax.nn.gelu(jnp.dot(second_b, w_up, preferred_element_type=jnp.float32), approximate=False).astype(jnp.bfloat16)
    output = normalize(jnp.dot(inner, w_down, preferred_element_type=jnp.float32) + second)
    output_b = output.astype(jnp.bfloat16)
    next_qkv = jnp.stack([jnp.dot(output_b, w_next[0], preferred_element_type=jnp.float32), jnp.dot(output_b, w_next[1], preferred_element_type=jnp.float32), jnp.dot(output_b, w_next[2], preferred_element_type=jnp.float32)])
    return (output, cache, next_qkv)
```

```python
import math

import jax
import jax.numpy as jnp
from jax import lax
from jax.sharding import PartitionSpec as P

HEADS = 16


NEGATIVE = -1e30
SCALING = 0.125
EPSILON = 1e-05


def normalize(matrix):
    center = matrix - jnp.mean(matrix, axis=-1, keepdims=True)
    return center * lax.rsqrt(jnp.mean(center * center, axis=-1, keepdims=True) + EPSILON)


def position_of(order_table, indices, halfway):
    slots = jnp.arange(order_table.shape[0], dtype=jnp.int32)
    picked = jnp.sum(
        jnp.where((indices // halfway)[:, None] == slots[None, :], order_table[None, :], 0), axis=1
    )
    return picked * halfway + indices % halfway


def group_of(places, lengths):
    ends = jnp.cumsum(lengths)
    return jnp.sum((places[:, None] >= ends[None, :]).astype(jnp.int32), axis=1)


def online_update(carried, queries, key_rows, value_rows, visible):
    maxima, totals, running = carried
    heads_here = queries.shape[1]
    key_split = key_rows.reshape(key_rows.shape[0], heads_here, -1)
    value_split = value_rows.reshape(value_rows.shape[0], heads_here, -1)
    scores = (
        jnp.einsum("qhd,khd->qhk", queries, key_split, preferred_element_type=jnp.float32) * SCALING
    )
    scores = jnp.where(visible[:, None, :], scores, NEGATIVE)
    updated = jnp.maximum(maxima, jnp.max(scores, axis=2))
    factor = jnp.exp(maxima - updated)
    weights = jnp.exp(scores - updated[:, :, None])
    totals = totals * factor + jnp.sum(weights, axis=2)
    running = running * factor[:, :, None] + jnp.einsum(
        "qhk,khd->qhd",
        weights.astype(jnp.bfloat16),
        value_split,
        preferred_element_type=jnp.float32,
    )
    return (updated, totals, running)


def sweep(
    carried, queries, key_rows, value_rows, key_places, key_groups, query_places, query_groups
):
    length = key_rows.shape[0]
    block_size = math.gcd(length, 2048)
    blocks_count = length // block_size
    key_blocks = key_rows.reshape(blocks_count, block_size, key_rows.shape[1])
    value_blocks = value_rows.reshape(blocks_count, block_size, value_rows.shape[1])
    group_blocks = key_groups.reshape(blocks_count, block_size)
    if key_places is None:
        place_blocks = group_blocks
    else:
        place_blocks = key_places.reshape(blocks_count, block_size)

    def advance(status, element):
        key_block, value_block, place_block, group_block = element
        visible = group_block[None, :] == query_groups[:, None]
        if key_places is None:
            return (online_update(status, queries, key_block, value_block, visible), None)
        visible = visible & (place_block[None, :] <= query_places[:, None])
        updated = online_update(status, queries, key_block, value_block, visible)
        return (updated, None)

    carried, unused = lax.scan(
        advance, carried, (key_blocks, value_blocks, place_blocks, group_blocks)
    )
    return carried


def empty_state(count_q, heads_here, head_width):
    return (
        jnp.full((count_q, heads_here), NEGATIVE, jnp.float32),
        jnp.zeros((count_q, heads_here), jnp.float32),
        jnp.zeros((count_q, heads_here, head_width), jnp.float32),
    )


def finish(carried):
    maxima, totals, running = carried
    return (running / totals[:, :, None]).reshape(running.shape[0], -1).astype(jnp.bfloat16)


def on_device(
    tokens,
    block_order,
    request_lengths,
    enc_lengths,
    w_qkv,
    w_out,
    enc_kv,
    w_cq,
    w_co,
    w_up,
    w_down,
    w_next,
):
    rows_here = tokens.shape[0]
    model_width = tokens.shape[1]
    group_size = lax.axis_size("head")
    cycle_size = lax.axis_size("blk")
    block_rows = rows_here * group_size
    halfway = block_rows // 2
    group_width = w_qkv.shape[2]
    head_width = model_width // HEADS
    group_heads = group_width // head_width
    member = lax.axis_index("head")
    cycle_index = lax.axis_index("blk")
    encoder = lax.all_gather(enc_kv, "blk", axis=1, tiled=True)
    gathered = lax.all_gather(tokens, "head", axis=0, tiled=True)
    projected = jnp.einsum(
        "td,cde->cte", gathered, w_qkv, preferred_element_type=jnp.float32
    ).astype(jnp.bfloat16)
    block_start = cycle_index * block_rows
    query_places = position_of(
        block_order, block_start + jnp.arange(block_rows, dtype=jnp.int32), halfway
    )
    query_groups = group_of(query_places, request_lengths)
    queries = projected[0].reshape(block_rows, group_heads, head_width)
    slots = jnp.arange(2 * cycle_size, dtype=jnp.int32)
    holders = jnp.sum(jnp.where(block_order[:, None] == slots[None, :], slots[:, None], 0), axis=0)
    shards = lax.all_gather(projected[1:], "blk", axis=1, tiled=True)
    shard_length = shards.shape[1]
    key_places = position_of(block_order, jnp.arange(shard_length, dtype=jnp.int32), halfway)
    key_groups = group_of(key_places, request_lengths)
    final_state = sweep(
        empty_state(block_rows, group_heads, head_width),
        queries,
        shards[0],
        shards[1],
        key_places,
        key_groups,
        query_places,
        query_groups,
    )
    attended = finish(final_state)
    first_holder = lax.dynamic_index_in_dim(holders, 2 * cycle_index, 0, keepdims=False)
    second_holder = lax.dynamic_index_in_dim(holders, 2 * cycle_index + 1, 0, keepdims=False)
    cache = jnp.concatenate(
        [
            lax.dynamic_slice_in_dim(shards, first_holder * halfway, halfway, 1),
            lax.dynamic_slice_in_dim(shards, second_holder * halfway, halfway, 1),
        ],
        axis=1,
    )
    mixed = lax.psum_scatter(
        jnp.dot(attended, w_out, preferred_element_type=jnp.float32),
        "head",
        scatter_dimension=0,
        tiled=True,
    )
    hidden = normalize(mixed + tokens.astype(jnp.float32))
    hidden_b = hidden.astype(jnp.bfloat16)
    block_hidden = lax.all_gather(hidden_b, "head", axis=0, tiled=True)
    w_cq_group = lax.dynamic_slice_in_dim(w_cq, member * group_width, group_width, 1)
    cross_query = jnp.dot(
        block_hidden, w_cq_group, preferred_element_type=jnp.float32
    ).astype(jnp.bfloat16)
    cross_split = cross_query.reshape(block_rows, group_heads, head_width)
    encoder_groups = group_of(jnp.arange(encoder.shape[1], dtype=jnp.int32), enc_lengths)
    crossed_group = finish(
        sweep(
            empty_state(block_rows, group_heads, head_width),
            cross_split,
            encoder[0],
            encoder[1],
            None,
            encoder_groups,
            None,
            query_groups,
        )
    )
    exchanged = lax.all_to_all(
        crossed_group.reshape(group_size, rows_here, group_width), "head", 0, 0, tiled=True
    )
    crossed = exchanged.transpose(1, 0, 2).reshape(rows_here, model_width)
    summed = jnp.dot(crossed, w_co, preferred_element_type=jnp.float32)
    second = normalize(summed + hidden)
    second_b = second.astype(jnp.bfloat16)
    inner = jax.nn.gelu(
        jnp.dot(second_b, w_up, preferred_element_type=jnp.float32), approximate=False
    ).astype(jnp.bfloat16)
    output = normalize(jnp.dot(inner, w_down, preferred_element_type=jnp.float32) + second)
    output_b = output.astype(jnp.bfloat16)
    block_output = lax.all_gather(output_b, "head", axis=0, tiled=True)
    next_qkv = jnp.einsum("td,cde->cte", block_output, w_next, preferred_element_type=jnp.float32)
    return (output, cache, next_qkv)


def solution(mesh):
    in_specs = (
        P(("blk", "head"), None),
        P(),
        P(),
        P(),
        P(None, None, "head"),
        P("head", None),
        P(None, "blk", "head"),
        P(),
        P(),
        P(),
        P(),
        P(None, None, "head"),
    )
    out_specs = (P(("blk", "head"), None), P(None, "blk", "head"), P(None, "blk", "head"))
    return jax.shard_map(
        on_device, mesh=mesh, in_specs=in_specs, out_specs=out_specs, check_vma=False
    )
```

```python
import functools
import math

import jax
import jax.numpy as jnp
from jax import lax
from jax.experimental import pallas as pl
from jax.experimental.pallas import tpu as pltpu
from jax.sharding import PartitionSpec as P

HEADS = 16


NEGATIVE = -1e30
SCALING = 0.125
EPSILON = 1e-05


def normalize(matrix):
    center = matrix - jnp.mean(matrix, axis=-1, keepdims=True)
    return center * lax.rsqrt(jnp.mean(center * center, axis=-1, keepdims=True) + EPSILON)


def position_of(order_table, indices, halfway):
    slots = jnp.arange(order_table.shape[0], dtype=jnp.int32)
    picked = jnp.sum(
        jnp.where((indices // halfway)[:, None] == slots[None, :], order_table[None, :], 0), axis=1
    )
    return picked * halfway + indices % halfway


def group_of(places, lengths):
    ends = jnp.cumsum(lengths)
    return jnp.sum((places[:, None] >= ends[None, :]).astype(jnp.int32), axis=1)


def online_update(carried, queries, key_rows, value_rows, visible):
    maxima, totals, running = carried
    heads_here = queries.shape[1]
    key_split = key_rows.reshape(key_rows.shape[0], heads_here, -1)
    value_split = value_rows.reshape(value_rows.shape[0], heads_here, -1)
    scores = (
        jnp.einsum("qhd,khd->qhk", queries, key_split, preferred_element_type=jnp.float32) * SCALING
    )
    scores = jnp.where(visible[:, None, :], scores, NEGATIVE)
    updated = jnp.maximum(maxima, jnp.max(scores, axis=2))
    factor = jnp.exp(maxima - updated)
    weights = jnp.exp(scores - updated[:, :, None])
    totals = totals * factor + jnp.sum(weights, axis=2)
    running = running * factor[:, :, None] + jnp.einsum(
        "qhk,khd->qhd",
        weights.astype(jnp.bfloat16),
        value_split,
        preferred_element_type=jnp.float32,
    )
    return (updated, totals, running)


def sweep(
    carried, queries, key_rows, value_rows, key_places, key_groups, query_places, query_groups
):
    length = key_rows.shape[0]
    block_size = math.gcd(length, 2048)
    blocks_count = length // block_size
    key_blocks = key_rows.reshape(blocks_count, block_size, key_rows.shape[1])
    value_blocks = value_rows.reshape(blocks_count, block_size, value_rows.shape[1])
    group_blocks = key_groups.reshape(blocks_count, block_size)
    if key_places is None:
        place_blocks = group_blocks
    else:
        place_blocks = key_places.reshape(blocks_count, block_size)

    def advance(status, element):
        key_block, value_block, place_block, group_block = element
        visible = group_block[None, :] == query_groups[:, None]
        if key_places is None:
            return (online_update(status, queries, key_block, value_block, visible), None)
        visible = visible & (place_block[None, :] <= query_places[:, None])
        updated = online_update(status, queries, key_block, value_block, visible)
        return (updated, None)

    carried, unused = lax.scan(
        advance, carried, (key_blocks, value_blocks, place_blocks, group_blocks)
    )
    return carried


def empty_state(count_q, heads_here, head_width):
    return (
        jnp.full((count_q, heads_here), NEGATIVE, jnp.float32),
        jnp.zeros((count_q, heads_here), jnp.float32),
        jnp.zeros((count_q, heads_here, head_width), jnp.float32),
    )


def finish(carried):
    maxima, totals, running = carried
    return (running / totals[:, :, None]).reshape(running.shape[0], -1).astype(jnp.bfloat16)


def flash_kernel(
    steps_ref, sources_ref, bases_ref, q_ref, low_ref, high_ref, k_hbm, v_hbm, o_ref,
    kbuf, vbuf, sem, qm_sc, m_sc, l_sc, acc_sc, *, max_steps, heads, head_width
):
    half = pl.program_id(0)
    count = steps_ref[half]
    tile = kbuf.shape[1] // 2
    width = kbuf.shape[2]

    def copies(step, slot):
        result = []
        for j in range(2):
            source = pl.multiple_of(sources_ref[(half * max_steps + step) * 2 + j], tile)
            window = pl.ds(j * tile, tile)
            result.append(pltpu.make_async_copy(
                k_hbm.at[pl.ds(source, tile)], kbuf.at[slot, window], sem.at[0, slot, j]))
            result.append(pltpu.make_async_copy(
                v_hbm.at[pl.ds(source, tile)], vbuf.at[slot, window], sem.at[1, slot, j]))
        return result

    for copy in copies(0, 0):
        copy.start()
    column_head = lax.broadcasted_iota(jnp.int32, (1, width), 1) // head_width
    q = q_ref[0]
    for h in range(heads):
        qm_sc[h] = jnp.where(column_head == h, q, jnp.zeros_like(q))
    m_sc[...] = jnp.full(m_sc.shape, NEGATIVE, jnp.float32)
    l_sc[...] = jnp.zeros(l_sc.shape, jnp.float32)
    acc_sc[...] = jnp.zeros(acc_sc.shape, jnp.float32)
    low = low_ref[0]
    high = high_ref[0]

    def body(step, carry):
        slot = step % 2
        for copy in copies(step, slot):
            copy.wait()

        @pl.when(step + 1 < count)
        def _():
            for copy in copies(step + 1, 1 - slot):
                copy.start()

        base = bases_ref[half * max_steps + step]
        places = base + lax.broadcasted_iota(jnp.int32, (1, 2 * tile), 1)
        visible = (places >= low) & (places <= high)
        keys = kbuf[slot]
        values = vbuf[slot]
        for h in range(heads):
            scores = lax.dot_general(
                qm_sc[h], keys, (((1,), (1,)), ((), ())), preferred_element_type=jnp.float32
            ) * SCALING
            scores = jnp.where(visible, scores, NEGATIVE)
            previous = m_sc[h]
            updated = jnp.maximum(previous, jnp.max(scores, axis=1, keepdims=True))
            factor = jnp.exp(previous - updated)
            weights = jnp.exp(scores - updated)
            l_sc[h] = l_sc[h] * factor + jnp.sum(weights, axis=1, keepdims=True)
            acc_sc[h] = acc_sc[h] * factor + jnp.dot(
                weights.astype(jnp.bfloat16), values, preferred_element_type=jnp.float32
            )
            m_sc[h] = updated
        return carry

    lax.fori_loop(0, count, body, 0)
    out = jnp.zeros(acc_sc.shape[1:], jnp.float32)
    for h in range(heads):
        out = jnp.where(column_head == h, acc_sc[h] / l_sc[h], out)
    o_ref[0] = out.astype(o_ref.dtype)


def flash(queries, low, high, keys, values, steps, sources, bases, max_steps, heads):
    halves, tile, width = queries.shape
    head_width = width // heads
    kernel = functools.partial(
        flash_kernel, max_steps=max_steps, heads=heads, head_width=head_width
    )
    row_spec = pl.BlockSpec((1, tile, width), lambda h, *refs: (h, 0, 0))
    bound_spec = pl.BlockSpec((1, tile, 1), lambda h, *refs: (h, 0, 0))
    flops = 4 * halves * max_steps * tile * 2 * tile * width * heads
    return pl.pallas_call(
        kernel,
        out_shape=jax.ShapeDtypeStruct(queries.shape, jnp.bfloat16),
        grid_spec=pltpu.PrefetchScalarGridSpec(
            num_scalar_prefetch=3,
            grid=(halves,),
            in_specs=[
                row_spec,
                bound_spec,
                bound_spec,
                pl.BlockSpec(memory_space=pl.ANY),
                pl.BlockSpec(memory_space=pl.ANY),
            ],
            out_specs=row_spec,
            scratch_shapes=[
                pltpu.VMEM((2, 2 * tile, width), keys.dtype),
                pltpu.VMEM((2, 2 * tile, width), values.dtype),
                pltpu.SemaphoreType.DMA((2, 2, 2)),
                pltpu.VMEM((heads, tile, width), jnp.bfloat16),
                pltpu.VMEM((heads, tile, 1), jnp.float32),
                pltpu.VMEM((heads, tile, 1), jnp.float32),
                pltpu.VMEM((heads, tile, width), jnp.float32),
            ],
        ),
        compiler_params=pltpu.CompilerParams(dimension_semantics=("arbitrary",)),
        cost_estimate=pl.CostEstimate(
            flops=flops,
            transcendentals=halves * max_steps * tile * 2 * tile * heads,
            bytes_accessed=halves * max_steps * 2 * 2 * tile * width * 2,
        ),
    )(steps, sources, bases, queries, low, high, keys, values)


def on_device(
    tokens,
    block_order,
    request_lengths,
    enc_lengths,
    w_qkv,
    w_out,
    enc_kv,
    w_cq,
    w_co,
    w_up,
    w_down,
    w_next,
):
    rows_here = tokens.shape[0]
    model_width = tokens.shape[1]
    group_size = lax.axis_size("head")
    cycle_size = lax.axis_size("blk")
    block_rows = rows_here * group_size
    halfway = block_rows // 2
    group_width = w_qkv.shape[2]
    head_width = model_width // HEADS
    group_heads = group_width // head_width
    member = lax.axis_index("head")
    cycle_index = lax.axis_index("blk")
    encoder = lax.all_gather(enc_kv, "blk", axis=1, tiled=True)
    gathered = lax.all_gather(tokens, "head", axis=0, tiled=True)
    projected = jnp.einsum(
        "td,cde->cte", gathered, w_qkv, preferred_element_type=jnp.float32
    ).astype(jnp.bfloat16)
    block_start = cycle_index * block_rows
    query_places = position_of(
        block_order, block_start + jnp.arange(block_rows, dtype=jnp.int32), halfway
    )
    query_groups = group_of(query_places, request_lengths)
    queries = projected[0].reshape(block_rows, group_heads, head_width)
    slots = jnp.arange(2 * cycle_size, dtype=jnp.int32)
    holders = jnp.sum(jnp.where(block_order[:, None] == slots[None, :], slots[:, None], 0), axis=0)
    shards = lax.all_gather(projected[1:], "blk", axis=1, tiled=True)
    ends = jnp.cumsum(request_lengths).astype(jnp.int32)
    starts = ends - request_lengths
    pair = lax.dynamic_slice_in_dim(block_order, 2 * cycle_index, 2, 0)
    first_request = group_of(pair * halfway, request_lengths)
    low_block = starts[first_request] // halfway
    self_steps = (pair - low_block) // 2 + 1
    self_max = cycle_size
    firsts = jnp.minimum(
        low_block[:, None] + 2 * jnp.arange(self_max, dtype=jnp.int32)[None, :],
        2 * cycle_size - 1,
    )
    padded_holders = jnp.concatenate([holders, holders[:1]])
    self_sources = jnp.stack(
        [padded_holders[firsts], padded_holders[firsts + 1]], axis=-1
    ) * halfway
    attended = flash(
        projected[0].reshape(2, halfway, group_width),
        starts[query_groups].reshape(2, halfway, 1),
        query_places.reshape(2, halfway, 1),
        shards[0],
        shards[1],
        self_steps.astype(jnp.int32),
        self_sources.reshape(-1).astype(jnp.int32),
        (firsts * halfway).reshape(-1).astype(jnp.int32),
        self_max,
        group_heads,
    ).reshape(block_rows, group_width)
    first_holder = lax.dynamic_index_in_dim(holders, 2 * cycle_index, 0, keepdims=False)
    second_holder = lax.dynamic_index_in_dim(holders, 2 * cycle_index + 1, 0, keepdims=False)
    cache = jnp.concatenate(
        [
            lax.dynamic_slice_in_dim(shards, first_holder * halfway, halfway, 1),
            lax.dynamic_slice_in_dim(shards, second_holder * halfway, halfway, 1),
        ],
        axis=1,
    )
    mixed = lax.psum_scatter(
        jnp.dot(attended, w_out, preferred_element_type=jnp.float32),
        "head",
        scatter_dimension=0,
        tiled=True,
    )
    hidden = normalize(mixed + tokens.astype(jnp.float32))
    hidden_b = hidden.astype(jnp.bfloat16)
    block_hidden = lax.all_gather(hidden_b, "head", axis=0, tiled=True)
    w_cq_group = lax.dynamic_slice_in_dim(w_cq, member * group_width, group_width, 1)
    cross_query = jnp.dot(
        block_hidden, w_cq_group, preferred_element_type=jnp.float32
    ).astype(jnp.bfloat16)
    encoder_rows = encoder.shape[1]
    cross_max = (encoder_rows + halfway - 1 + 2 * halfway - 1) // (2 * halfway)
    padded_encoder = jnp.pad(
        encoder, ((0, 0), (0, cross_max * 2 * halfway + halfway - encoder_rows), (0, 0))
    )
    enc_ends = jnp.cumsum(enc_lengths).astype(jnp.int32)
    enc_starts = enc_ends - enc_lengths
    edge_groups = query_groups.reshape(2, halfway)
    cross_base = (enc_starts[edge_groups[:, 0]] // halfway) * halfway
    cross_steps = (enc_ends[edge_groups[:, -1]] - cross_base + 2 * halfway - 1) // (2 * halfway)
    cross_firsts = jnp.minimum(
        cross_base[:, None] + 2 * halfway * jnp.arange(cross_max, dtype=jnp.int32)[None, :],
        padded_encoder.shape[1] - 2 * halfway,
    )
    cross_sources = jnp.stack([cross_firsts, cross_firsts + halfway], axis=-1)
    crossed_group = flash(
        cross_query.reshape(2, halfway, group_width),
        enc_starts[query_groups].reshape(2, halfway, 1),
        (enc_ends[query_groups] - 1).reshape(2, halfway, 1),
        padded_encoder[0],
        padded_encoder[1],
        cross_steps.astype(jnp.int32),
        cross_sources.reshape(-1).astype(jnp.int32),
        cross_firsts.reshape(-1).astype(jnp.int32),
        cross_max,
        group_heads,
    ).reshape(block_rows, group_width)
    exchanged = lax.all_to_all(
        crossed_group.reshape(group_size, rows_here, group_width), "head", 0, 0, tiled=True
    )
    crossed = exchanged.transpose(1, 0, 2).reshape(rows_here, model_width)
    summed = jnp.dot(crossed, w_co, preferred_element_type=jnp.float32)
    second = normalize(summed + hidden)
    second_b = second.astype(jnp.bfloat16)
    inner = jax.nn.gelu(
        jnp.dot(second_b, w_up, preferred_element_type=jnp.float32), approximate=False
    ).astype(jnp.bfloat16)
    output = normalize(jnp.dot(inner, w_down, preferred_element_type=jnp.float32) + second)
    output_b = output.astype(jnp.bfloat16)
    block_output = lax.all_gather(output_b, "head", axis=0, tiled=True)
    next_qkv = jnp.einsum("td,cde->cte", block_output, w_next, preferred_element_type=jnp.float32)
    return (output, cache, next_qkv)


def solution(mesh):
    in_specs = (
        P(("blk", "head"), None),
        P(),
        P(),
        P(),
        P(None, None, "head"),
        P("head", None),
        P(None, "blk", "head"),
        P(),
        P(),
        P(),
        P(),
        P(None, None, "head"),
    )
    out_specs = (P(("blk", "head"), None), P(None, "blk", "head"), P(None, "blk", "head"))
    return jax.shard_map(
        on_device, mesh=mesh, in_specs=in_specs, out_specs=out_specs, check_vma=False
    )
```

```python
import functools
import math

import jax
import jax.numpy as jnp
from jax import lax
from jax.experimental import pallas as pl
from jax.experimental.pallas import tpu as pltpu
from jax.sharding import PartitionSpec as P

HEADS = 16


NEGATIVE = -1e30
SCALING = 0.125
EPSILON = 1e-05


def normalize(matrix):
    center = matrix - jnp.mean(matrix, axis=-1, keepdims=True)
    return center * lax.rsqrt(jnp.mean(center * center, axis=-1, keepdims=True) + EPSILON)


def position_of(order_table, indices, halfway):
    slots = jnp.arange(order_table.shape[0], dtype=jnp.int32)
    picked = jnp.sum(
        jnp.where((indices // halfway)[:, None] == slots[None, :], order_table[None, :], 0), axis=1
    )
    return picked * halfway + indices % halfway


def group_of(places, lengths):
    ends = jnp.cumsum(lengths)
    return jnp.sum((places[:, None] >= ends[None, :]).astype(jnp.int32), axis=1)


def online_update(carried, queries, key_rows, value_rows, visible):
    maxima, totals, running = carried
    heads_here = queries.shape[1]
    key_split = key_rows.reshape(key_rows.shape[0], heads_here, -1)
    value_split = value_rows.reshape(value_rows.shape[0], heads_here, -1)
    scores = (
        jnp.einsum("qhd,khd->qhk", queries, key_split, preferred_element_type=jnp.float32) * SCALING
    )
    scores = jnp.where(visible[:, None, :], scores, NEGATIVE)
    updated = jnp.maximum(maxima, jnp.max(scores, axis=2))
    factor = jnp.exp(maxima - updated)
    weights = jnp.exp(scores - updated[:, :, None])
    totals = totals * factor + jnp.sum(weights, axis=2)
    running = running * factor[:, :, None] + jnp.einsum(
        "qhk,khd->qhd",
        weights.astype(jnp.bfloat16),
        value_split,
        preferred_element_type=jnp.float32,
    )
    return (updated, totals, running)


def sweep(
    carried, queries, key_rows, value_rows, key_places, key_groups, query_places, query_groups
):
    length = key_rows.shape[0]
    block_size = math.gcd(length, 2048)
    blocks_count = length // block_size
    key_blocks = key_rows.reshape(blocks_count, block_size, key_rows.shape[1])
    value_blocks = value_rows.reshape(blocks_count, block_size, value_rows.shape[1])
    group_blocks = key_groups.reshape(blocks_count, block_size)
    if key_places is None:
        place_blocks = group_blocks
    else:
        place_blocks = key_places.reshape(blocks_count, block_size)

    def advance(status, element):
        key_block, value_block, place_block, group_block = element
        visible = group_block[None, :] == query_groups[:, None]
        if key_places is None:
            return (online_update(status, queries, key_block, value_block, visible), None)
        visible = visible & (place_block[None, :] <= query_places[:, None])
        updated = online_update(status, queries, key_block, value_block, visible)
        return (updated, None)

    carried, unused = lax.scan(
        advance, carried, (key_blocks, value_blocks, place_blocks, group_blocks)
    )
    return carried


def empty_state(count_q, heads_here, head_width):
    return (
        jnp.full((count_q, heads_here), NEGATIVE, jnp.float32),
        jnp.zeros((count_q, heads_here), jnp.float32),
        jnp.zeros((count_q, heads_here, head_width), jnp.float32),
    )


def finish(carried):
    maxima, totals, running = carried
    return (running / totals[:, :, None]).reshape(running.shape[0], -1).astype(jnp.bfloat16)


def flash_kernel(
    steps_ref, sources_ref, bases_ref, q_ref, low_ref, high_ref, k_hbm, v_hbm, o_ref,
    kbuf, vbuf, sem, qm_sc, m_sc, l_sc, acc_sc, *, max_steps, heads, head_width
):
    half = pl.program_id(0)
    count = steps_ref[half]
    tile = kbuf.shape[1] // 2
    width = kbuf.shape[2]

    def copies(step, slot):
        result = []
        for j in range(2):
            source = pl.multiple_of(sources_ref[(half * max_steps + step) * 2 + j], tile)
            window = pl.ds(j * tile, tile)
            result.append(pltpu.make_async_copy(
                k_hbm.at[pl.ds(source, tile)], kbuf.at[slot, window], sem.at[0, slot, j]))
            result.append(pltpu.make_async_copy(
                v_hbm.at[pl.ds(source, tile)], vbuf.at[slot, window], sem.at[1, slot, j]))
        return result

    for copy in copies(0, 0):
        copy.start()
    column_head = lax.broadcasted_iota(jnp.int32, (1, width), 1) // head_width
    q = q_ref[0]
    for h in range(heads):
        qm_sc[h] = jnp.where(column_head == h, q, jnp.zeros_like(q))
    m_sc[...] = jnp.full(m_sc.shape, NEGATIVE, jnp.float32)
    l_sc[...] = jnp.zeros(l_sc.shape, jnp.float32)
    acc_sc[...] = jnp.zeros(acc_sc.shape, jnp.float32)
    low = low_ref[0]
    high = high_ref[0]

    def body(step, carry):
        slot = step % 2
        for copy in copies(step, slot):
            copy.wait()

        @pl.when(step + 1 < count)
        def _():
            for copy in copies(step + 1, 1 - slot):
                copy.start()

        base = bases_ref[half * max_steps + step]
        places = base + lax.broadcasted_iota(jnp.int32, (1, 2 * tile), 1)
        visible = (places >= low) & (places <= high)
        keys = kbuf[slot]
        values = vbuf[slot]
        for h in range(heads):
            scores = lax.dot_general(
                qm_sc[h], keys, (((1,), (1,)), ((), ())), preferred_element_type=jnp.float32
            ) * SCALING
            scores = jnp.where(visible, scores, NEGATIVE)
            previous = m_sc[h]
            updated = jnp.maximum(previous, jnp.max(scores, axis=1, keepdims=True))
            factor = jnp.exp(previous - updated)
            weights = jnp.exp(scores - updated)
            l_sc[h] = l_sc[h] * factor + jnp.sum(weights, axis=1, keepdims=True)
            acc_sc[h] = acc_sc[h] * factor + jnp.dot(
                weights.astype(jnp.bfloat16), values, preferred_element_type=jnp.float32
            )
            m_sc[h] = updated
        return carry

    lax.fori_loop(0, count, body, 0)
    out = jnp.zeros(acc_sc.shape[1:], jnp.float32)
    for h in range(heads):
        out = jnp.where(column_head == h, acc_sc[h] / l_sc[h], out)
    o_ref[0] = out.astype(o_ref.dtype)


def flash(queries, low, high, keys, values, steps, sources, bases, max_steps, heads):
    halves, tile, width = queries.shape
    head_width = width // heads
    kernel = functools.partial(
        flash_kernel, max_steps=max_steps, heads=heads, head_width=head_width
    )
    row_spec = pl.BlockSpec((1, tile, width), lambda h, *refs: (h, 0, 0))
    bound_spec = pl.BlockSpec((1, tile, 1), lambda h, *refs: (h, 0, 0))
    flops = 4 * halves * max_steps * tile * 2 * tile * width * heads
    return pl.pallas_call(
        kernel,
        out_shape=jax.ShapeDtypeStruct(queries.shape, jnp.bfloat16),
        grid_spec=pltpu.PrefetchScalarGridSpec(
            num_scalar_prefetch=3,
            grid=(halves,),
            in_specs=[
                row_spec,
                bound_spec,
                bound_spec,
                pl.BlockSpec(memory_space=pl.ANY),
                pl.BlockSpec(memory_space=pl.ANY),
            ],
            out_specs=row_spec,
            scratch_shapes=[
                pltpu.VMEM((2, 2 * tile, width), keys.dtype),
                pltpu.VMEM((2, 2 * tile, width), values.dtype),
                pltpu.SemaphoreType.DMA((2, 2, 2)),
                pltpu.VMEM((heads, tile, width), jnp.bfloat16),
                pltpu.VMEM((heads, tile, 1), jnp.float32),
                pltpu.VMEM((heads, tile, 1), jnp.float32),
                pltpu.VMEM((heads, tile, width), jnp.float32),
            ],
        ),
        compiler_params=pltpu.CompilerParams(dimension_semantics=("arbitrary",)),
        cost_estimate=pl.CostEstimate(
            flops=flops,
            transcendentals=halves * max_steps * tile * 2 * tile * heads,
            bytes_accessed=halves * max_steps * 2 * 2 * tile * width * 2,
        ),
    )(steps, sources, bases, queries, low, high, keys, values)


def single_kernel(
    steps_ref, sources_ref, bases_ref, q_ref, low_ref, high_ref, kv_hbm, o_ref,
    buf, sem, m_sc, l_sc, acc_sc, *, max_steps, head_width
):
    half = pl.program_id(0)
    count = steps_ref[half]
    tile = buf.shape[1] // 2

    def copies(step, slot):
        result = []
        for j in range(2):
            source = pl.multiple_of(sources_ref[(half * max_steps + step) * 2 + j], tile)
            result.append(pltpu.make_async_copy(
                kv_hbm.at[pl.ds(source, tile)], buf.at[slot, pl.ds(j * tile, tile)], sem.at[slot, j]))
        return result

    for copy in copies(0, 0):
        copy.start()
    m_sc[...] = jnp.full(m_sc.shape, NEGATIVE, jnp.float32)
    l_sc[...] = jnp.zeros(l_sc.shape, jnp.float32)
    acc_sc[...] = jnp.zeros(acc_sc.shape, jnp.float32)
    q = q_ref[0]
    low = low_ref[0]
    high = high_ref[0]

    def body(step, carry):
        slot = step % 2
        for copy in copies(step, slot):
            copy.wait()

        @pl.when(step + 1 < count)
        def _():
            for copy in copies(step + 1, 1 - slot):
                copy.start()

        base = bases_ref[half * max_steps + step]
        places = base + lax.broadcasted_iota(jnp.int32, (1, 2 * tile), 1)
        visible = (places >= low) & (places <= high)
        block = buf[slot]
        keys = block[:, :head_width]
        values = block[:, head_width:]
        scores = lax.dot_general(
            q, keys, (((1,), (1,)), ((), ())), preferred_element_type=jnp.float32
        ) * SCALING
        scores = jnp.where(visible, scores, NEGATIVE)
        previous = m_sc[...]
        updated = jnp.maximum(previous, jnp.max(scores, axis=1, keepdims=True))
        factor = jnp.exp(previous - updated)
        weights = jnp.exp(scores - updated)
        l_sc[...] = l_sc[...] * factor + jnp.sum(weights, axis=1, keepdims=True)
        acc_sc[...] = acc_sc[...] * factor + jnp.dot(
            weights.astype(jnp.bfloat16), values, preferred_element_type=jnp.float32
        )
        m_sc[...] = updated
        return carry

    lax.fori_loop(0, count, body, 0)
    o_ref[0] = (acc_sc[...] / l_sc[...]).astype(o_ref.dtype)


def single(queries, low, high, packed, steps, sources, bases, max_steps):
    halves, tile, head_width = queries.shape
    kernel = functools.partial(single_kernel, max_steps=max_steps, head_width=head_width)
    row_spec = pl.BlockSpec((1, tile, head_width), lambda h, *refs: (h, 0, 0))
    bound_spec = pl.BlockSpec((1, tile, 1), lambda h, *refs: (h, 0, 0))
    return pl.pallas_call(
        kernel,
        out_shape=jax.ShapeDtypeStruct(queries.shape, jnp.bfloat16),
        grid_spec=pltpu.PrefetchScalarGridSpec(
            num_scalar_prefetch=3,
            grid=(halves,),
            in_specs=[row_spec, bound_spec, bound_spec, pl.BlockSpec(memory_space=pl.ANY)],
            out_specs=row_spec,
            scratch_shapes=[
                pltpu.VMEM((2, 2 * tile, packed.shape[1]), packed.dtype),
                pltpu.SemaphoreType.DMA((2, 2)),
                pltpu.VMEM((tile, 1), jnp.float32),
                pltpu.VMEM((tile, 1), jnp.float32),
                pltpu.VMEM((tile, head_width), jnp.float32),
            ],
        ),
        compiler_params=pltpu.CompilerParams(dimension_semantics=("arbitrary",)),
        cost_estimate=pl.CostEstimate(
            flops=2 * halves * (max_steps // 2) * tile * 2 * tile * head_width * 2,
            transcendentals=halves * (max_steps // 2) * tile * 2 * tile,
            bytes_accessed=halves * (max_steps // 2) * 2 * tile * packed.shape[1] * 2,
        ),
    )(steps, sources, bases, queries, low, high, packed)


def on_device(
    tokens,
    block_order,
    request_lengths,
    enc_lengths,
    w_qkv,
    w_out,
    enc_kv,
    w_cq,
    w_co,
    w_up,
    w_down,
    w_next,
):
    rows_here = tokens.shape[0]
    model_width = tokens.shape[1]
    group_size = lax.axis_size("head")
    cycle_size = lax.axis_size("zy") * lax.axis_size("x")
    block_rows = rows_here * group_size
    halfway = block_rows // 2
    group_width = w_qkv.shape[2]
    head_width = model_width // HEADS
    group_heads = group_width // head_width
    member = lax.axis_index("head")
    ring_size = lax.axis_size("x")
    ring_index = lax.axis_index("x")
    cycle_index = lax.axis_index("zy") * ring_size + ring_index
    encoder = lax.all_gather(enc_kv, ("zy", "x"), axis=1, tiled=True)
    gathered = lax.all_gather(tokens, "head", axis=0, tiled=True)
    projected = jnp.einsum(
        "td,cde->cte", gathered, w_qkv, preferred_element_type=jnp.float32
    ).astype(jnp.bfloat16)
    block_start = cycle_index * block_rows
    query_places = position_of(
        block_order, block_start + jnp.arange(block_rows, dtype=jnp.int32), halfway
    )
    query_groups = group_of(query_places, request_lengths)
    slots = jnp.arange(2 * cycle_size, dtype=jnp.int32)
    holders = jnp.sum(jnp.where(block_order[:, None] == slots[None, :], slots[:, None], 0), axis=0)
    per_head = projected.reshape(3, block_rows, group_heads, head_width).transpose(2, 1, 0, 3)
    per_head = per_head.reshape(group_heads, block_rows, 3 * head_width)
    mine = lax.all_to_all(per_head, "x", 0, 0, tiled=True)
    packed = lax.all_gather(mine[:, :, head_width:], "zy", axis=0, tiled=True)
    packed = packed.reshape(cycle_size * block_rows, 2 * head_width)
    ends = jnp.cumsum(request_lengths).astype(jnp.int32)
    starts = ends - request_lengths
    halves_here = 2 * ring_size
    first_half = lax.axis_index("zy") * halves_here
    pair = lax.dynamic_slice_in_dim(block_order, first_half, halves_here, 0)
    first_request = group_of(pair * halfway, request_lengths)
    low_block = starts[first_request] // halfway
    self_steps = (pair - low_block) // 2 + 1
    self_max = cycle_size
    firsts = jnp.minimum(
        low_block[:, None] + 2 * jnp.arange(self_max, dtype=jnp.int32)[None, :],
        2 * cycle_size - 1,
    )
    padded_holders = jnp.concatenate([holders, holders[:1]])
    self_sources = jnp.stack(
        [padded_holders[firsts], padded_holders[firsts + 1]], axis=-1
    ) * halfway
    places_here = (pair[:, None] * halfway + jnp.arange(halfway, dtype=jnp.int32)[None, :])
    groups_here = group_of(places_here.reshape(-1), request_lengths)
    single_out = single(
        mine[:, :, :head_width].reshape(halves_here, halfway, head_width),
        starts[groups_here].reshape(halves_here, halfway, 1),
        places_here.reshape(halves_here, halfway, 1),
        packed,
        self_steps.astype(jnp.int32),
        self_sources.reshape(-1).astype(jnp.int32),
        (firsts * halfway).reshape(-1).astype(jnp.int32),
        self_max,
    )
    returned = lax.all_to_all(
        single_out.reshape(ring_size, block_rows, head_width), "x", 0, 0, tiled=True
    )
    attended = returned.transpose(1, 0, 2).reshape(block_rows, group_width)
    group_blocks = lax.axis_index("zy") * ring_size + jnp.arange(ring_size, dtype=jnp.int32)
    cache_rows = jnp.stack(
        [holders[2 * group_blocks], holders[2 * group_blocks + 1]], axis=1
    )
    cache_parts = jnp.stack(
        [
            jnp.concatenate(
                [
                    lax.dynamic_slice_in_dim(packed, cache_rows[i, 0] * halfway, halfway, 0),
                    lax.dynamic_slice_in_dim(packed, cache_rows[i, 1] * halfway, halfway, 0),
                ],
                axis=0,
            )
            for i in range(ring_size)
        ]
    )
    cache_heads = lax.all_to_all(cache_parts, "x", 0, 0, tiled=True)
    cache = cache_heads.reshape(group_heads, block_rows, 2, head_width).transpose(2, 1, 0, 3)
    cache = cache.reshape(2, block_rows, group_width)
    mixed = lax.psum_scatter(
        jnp.dot(attended, w_out, preferred_element_type=jnp.float32),
        "head",
        scatter_dimension=0,
        tiled=True,
    )
    hidden = normalize(mixed + tokens.astype(jnp.float32))
    hidden_b = hidden.astype(jnp.bfloat16)
    block_hidden = lax.all_gather(hidden_b, "head", axis=0, tiled=True)
    w_cq_group = lax.dynamic_slice_in_dim(w_cq, member * group_width, group_width, 1)
    cross_query = jnp.dot(
        block_hidden, w_cq_group, preferred_element_type=jnp.float32
    ).astype(jnp.bfloat16)
    encoder_rows = encoder.shape[1]
    cross_max = (encoder_rows + halfway - 1 + 2 * halfway - 1) // (2 * halfway)
    padded_encoder = jnp.pad(
        encoder, ((0, 0), (0, cross_max * 2 * halfway + halfway - encoder_rows), (0, 0))
    )
    enc_ends = jnp.cumsum(enc_lengths).astype(jnp.int32)
    enc_starts = enc_ends - enc_lengths
    edge_groups = query_groups.reshape(2, halfway)
    cross_base = (enc_starts[edge_groups[:, 0]] // halfway) * halfway
    cross_steps = (enc_ends[edge_groups[:, -1]] - cross_base + 2 * halfway - 1) // (2 * halfway)
    cross_firsts = jnp.minimum(
        cross_base[:, None] + 2 * halfway * jnp.arange(cross_max, dtype=jnp.int32)[None, :],
        padded_encoder.shape[1] - 2 * halfway,
    )
    cross_sources = jnp.stack([cross_firsts, cross_firsts + halfway], axis=-1)
    crossed_group = flash(
        cross_query.reshape(2, halfway, group_width),
        enc_starts[query_groups].reshape(2, halfway, 1),
        (enc_ends[query_groups] - 1).reshape(2, halfway, 1),
        padded_encoder[0],
        padded_encoder[1],
        cross_steps.astype(jnp.int32),
        cross_sources.reshape(-1).astype(jnp.int32),
        cross_firsts.reshape(-1).astype(jnp.int32),
        cross_max,
        group_heads,
    ).reshape(block_rows, group_width)
    exchanged = lax.all_to_all(
        crossed_group.reshape(group_size, rows_here, group_width), "head", 0, 0, tiled=True
    )
    crossed = exchanged.transpose(1, 0, 2).reshape(rows_here, model_width)
    summed = jnp.dot(crossed, w_co, preferred_element_type=jnp.float32)
    second = normalize(summed + hidden)
    second_b = second.astype(jnp.bfloat16)
    inner = jax.nn.gelu(
        jnp.dot(second_b, w_up, preferred_element_type=jnp.float32), approximate=False
    ).astype(jnp.bfloat16)
    output = normalize(jnp.dot(inner, w_down, preferred_element_type=jnp.float32) + second)
    output_b = output.astype(jnp.bfloat16)
    block_output = lax.all_gather(output_b, "head", axis=0, tiled=True)
    next_qkv = jnp.einsum("td,cde->cte", block_output, w_next, preferred_element_type=jnp.float32)
    return (output, cache, next_qkv)


def solution(mesh):
    ring = 4
    devices = mesh.devices.reshape(mesh.shape["blk"] // ring, ring, mesh.shape["head"])
    fine = jax.sharding.Mesh(devices, ("zy", "x", "head"))
    rows = ("zy", "x", "head")
    blocks = ("zy", "x")
    in_specs = (
        P(rows, None),
        P(),
        P(),
        P(),
        P(None, None, "head"),
        P("head", None),
        P(None, blocks, "head"),
        P(),
        P(),
        P(),
        P(),
        P(None, None, "head"),
    )
    out_specs = (P(rows, None), P(None, blocks, "head"), P(None, blocks, "head"))
    return jax.shard_map(
        on_device, mesh=fine, in_specs=in_specs, out_specs=out_specs, check_vma=False
    )
```

```python
import functools
import math

import jax
import jax.numpy as jnp
from jax import lax
from jax.experimental import pallas as pl
from jax.experimental.pallas import tpu as pltpu
from jax.sharding import PartitionSpec as P

HEADS = 16


NEGATIVE = -1e30
SCALING = 0.125
EPSILON = 1e-05


def normalize(matrix):
    center = matrix - jnp.mean(matrix, axis=-1, keepdims=True)
    return center * lax.rsqrt(jnp.mean(center * center, axis=-1, keepdims=True) + EPSILON)


def position_of(order_table, indices, halfway):
    slots = jnp.arange(order_table.shape[0], dtype=jnp.int32)
    picked = jnp.sum(
        jnp.where((indices // halfway)[:, None] == slots[None, :], order_table[None, :], 0), axis=1
    )
    return picked * halfway + indices % halfway


def group_of(places, lengths):
    ends = jnp.cumsum(lengths)
    return jnp.sum((places[:, None] >= ends[None, :]).astype(jnp.int32), axis=1)


def online_update(carried, queries, key_rows, value_rows, visible):
    maxima, totals, running = carried
    heads_here = queries.shape[1]
    key_split = key_rows.reshape(key_rows.shape[0], heads_here, -1)
    value_split = value_rows.reshape(value_rows.shape[0], heads_here, -1)
    scores = (
        jnp.einsum("qhd,khd->qhk", queries, key_split, preferred_element_type=jnp.float32) * SCALING
    )
    scores = jnp.where(visible[:, None, :], scores, NEGATIVE)
    updated = jnp.maximum(maxima, jnp.max(scores, axis=2))
    factor = jnp.exp(maxima - updated)
    weights = jnp.exp(scores - updated[:, :, None])
    totals = totals * factor + jnp.sum(weights, axis=2)
    running = running * factor[:, :, None] + jnp.einsum(
        "qhk,khd->qhd",
        weights.astype(jnp.bfloat16),
        value_split,
        preferred_element_type=jnp.float32,
    )
    return (updated, totals, running)


def sweep(
    carried, queries, key_rows, value_rows, key_places, key_groups, query_places, query_groups
):
    length = key_rows.shape[0]
    block_size = math.gcd(length, 2048)
    blocks_count = length // block_size
    key_blocks = key_rows.reshape(blocks_count, block_size, key_rows.shape[1])
    value_blocks = value_rows.reshape(blocks_count, block_size, value_rows.shape[1])
    group_blocks = key_groups.reshape(blocks_count, block_size)
    if key_places is None:
        place_blocks = group_blocks
    else:
        place_blocks = key_places.reshape(blocks_count, block_size)

    def advance(status, element):
        key_block, value_block, place_block, group_block = element
        visible = group_block[None, :] == query_groups[:, None]
        if key_places is None:
            return (online_update(status, queries, key_block, value_block, visible), None)
        visible = visible & (place_block[None, :] <= query_places[:, None])
        updated = online_update(status, queries, key_block, value_block, visible)
        return (updated, None)

    carried, unused = lax.scan(
        advance, carried, (key_blocks, value_blocks, place_blocks, group_blocks)
    )
    return carried


def empty_state(count_q, heads_here, head_width):
    return (
        jnp.full((count_q, heads_here), NEGATIVE, jnp.float32),
        jnp.zeros((count_q, heads_here), jnp.float32),
        jnp.zeros((count_q, heads_here, head_width), jnp.float32),
    )


def finish(carried):
    maxima, totals, running = carried
    return (running / totals[:, :, None]).reshape(running.shape[0], -1).astype(jnp.bfloat16)


def flash_kernel(
    steps_ref, sources_ref, bases_ref, q_ref, low_ref, high_ref, k_hbm, v_hbm, o_ref,
    kbuf, vbuf, sem, qm_sc, m_sc, l_sc, acc_sc, *, max_steps, heads, head_width
):
    half = pl.program_id(0)
    count = steps_ref[half]
    tile = kbuf.shape[1] // 2
    width = kbuf.shape[2]

    def copies(step, slot):
        result = []
        for j in range(2):
            source = pl.multiple_of(sources_ref[(half * max_steps + step) * 2 + j], tile)
            window = pl.ds(j * tile, tile)
            result.append(pltpu.make_async_copy(
                k_hbm.at[pl.ds(source, tile)], kbuf.at[slot, window], sem.at[0, slot, j]))
            result.append(pltpu.make_async_copy(
                v_hbm.at[pl.ds(source, tile)], vbuf.at[slot, window], sem.at[1, slot, j]))
        return result

    for copy in copies(0, 0):
        copy.start()
    column_head = lax.broadcasted_iota(jnp.int32, (1, width), 1) // head_width
    q = q_ref[0]
    for h in range(heads):
        qm_sc[h] = jnp.where(column_head == h, q, jnp.zeros_like(q))
    m_sc[...] = jnp.full(m_sc.shape, NEGATIVE, jnp.float32)
    l_sc[...] = jnp.zeros(l_sc.shape, jnp.float32)
    acc_sc[...] = jnp.zeros(acc_sc.shape, jnp.float32)
    low = low_ref[0]
    high = high_ref[0]

    def body(step, carry):
        slot = step % 2
        for copy in copies(step, slot):
            copy.wait()

        @pl.when(step + 1 < count)
        def _():
            for copy in copies(step + 1, 1 - slot):
                copy.start()

        base = bases_ref[half * max_steps + step]
        places = base + lax.broadcasted_iota(jnp.int32, (1, 2 * tile), 1)
        visible = (places >= low) & (places <= high)
        keys = kbuf[slot]
        values = vbuf[slot]
        for h in range(heads):
            scores = lax.dot_general(
                qm_sc[h], keys, (((1,), (1,)), ((), ())), preferred_element_type=jnp.float32
            ) * SCALING
            scores = jnp.where(visible, scores, NEGATIVE)
            previous = m_sc[h]
            updated = jnp.maximum(previous, jnp.max(scores, axis=1, keepdims=True))
            factor = jnp.exp(previous - updated)
            weights = jnp.exp(scores - updated)
            l_sc[h] = l_sc[h] * factor + jnp.sum(weights, axis=1, keepdims=True)
            acc_sc[h] = acc_sc[h] * factor + jnp.dot(
                weights.astype(jnp.bfloat16), values, preferred_element_type=jnp.float32
            )
            m_sc[h] = updated
        return carry

    lax.fori_loop(0, count, body, 0)
    out = jnp.zeros(acc_sc.shape[1:], jnp.float32)
    for h in range(heads):
        out = jnp.where(column_head == h, acc_sc[h] / l_sc[h], out)
    o_ref[0] = out.astype(o_ref.dtype)


def flash(queries, low, high, keys, values, steps, sources, bases, max_steps, heads):
    halves, tile, width = queries.shape
    head_width = width // heads
    kernel = functools.partial(
        flash_kernel, max_steps=max_steps, heads=heads, head_width=head_width
    )
    row_spec = pl.BlockSpec((1, tile, width), lambda h, *refs: (h, 0, 0))
    bound_spec = pl.BlockSpec((1, tile, 1), lambda h, *refs: (h, 0, 0))
    flops = 4 * halves * max_steps * tile * 2 * tile * width * heads
    return pl.pallas_call(
        kernel,
        out_shape=jax.ShapeDtypeStruct(queries.shape, jnp.bfloat16),
        grid_spec=pltpu.PrefetchScalarGridSpec(
            num_scalar_prefetch=3,
            grid=(halves,),
            in_specs=[
                row_spec,
                bound_spec,
                bound_spec,
                pl.BlockSpec(memory_space=pl.ANY),
                pl.BlockSpec(memory_space=pl.ANY),
            ],
            out_specs=row_spec,
            scratch_shapes=[
                pltpu.VMEM((2, 2 * tile, width), keys.dtype),
                pltpu.VMEM((2, 2 * tile, width), values.dtype),
                pltpu.SemaphoreType.DMA((2, 2, 2)),
                pltpu.VMEM((heads, tile, width), jnp.bfloat16),
                pltpu.VMEM((heads, tile, 1), jnp.float32),
                pltpu.VMEM((heads, tile, 1), jnp.float32),
                pltpu.VMEM((heads, tile, width), jnp.float32),
            ],
        ),
        compiler_params=pltpu.CompilerParams(dimension_semantics=("arbitrary",)),
        cost_estimate=pl.CostEstimate(
            flops=flops,
            transcendentals=halves * max_steps * tile * 2 * tile * heads,
            bytes_accessed=halves * max_steps * 2 * 2 * tile * width * 2,
        ),
    )(steps, sources, bases, queries, low, high, keys, values)


def single_kernel(
    steps_ref, sources_ref, bases_ref, q_ref, low_ref, high_ref, kv_hbm, o_ref,
    buf, sem, m_sc, l_sc, acc_sc, *, max_steps, head_width, pieces
):
    half = pl.program_id(0)
    count = steps_ref[half]
    tile = buf.shape[1] // pieces

    def copies(step, slot):
        result = []
        for j in range(pieces):
            source = pl.multiple_of(sources_ref[(half * max_steps + step) * pieces + j], tile)
            result.append(pltpu.make_async_copy(
                kv_hbm.at[pl.ds(source, tile)], buf.at[slot, pl.ds(j * tile, tile)], sem.at[slot, j]))
        return result

    for copy in copies(0, 0):
        copy.start()
    m_sc[...] = jnp.full(m_sc.shape, NEGATIVE, jnp.float32)
    l_sc[...] = jnp.zeros(l_sc.shape, jnp.float32)
    acc_sc[...] = jnp.zeros(acc_sc.shape, jnp.float32)
    q = q_ref[0]
    low = low_ref[0]
    high = high_ref[0]

    def body(step, carry):
        slot = step % 2
        for copy in copies(step, slot):
            copy.wait()

        @pl.when(step + 1 < count)
        def _():
            for copy in copies(step + 1, 1 - slot):
                copy.start()

        base = bases_ref[half * max_steps + step]
        places = base + lax.broadcasted_iota(jnp.int32, (1, pieces * tile), 1)
        visible = (places >= low) & (places <= high)
        block = buf[slot]
        keys = block[:, :head_width]
        values = block[:, head_width:]
        scores = lax.dot_general(
            q, keys, (((1,), (1,)), ((), ())), preferred_element_type=jnp.float32
        ) * SCALING
        scores = jnp.where(visible, scores, NEGATIVE)
        previous = m_sc[...]
        updated = jnp.maximum(previous, jnp.max(scores, axis=1, keepdims=True))
        factor = jnp.exp(previous - updated)
        weights = jnp.exp(scores - updated)
        l_sc[...] = l_sc[...] * factor + jnp.sum(weights, axis=1, keepdims=True)
        acc_sc[...] = acc_sc[...] * factor + jnp.dot(
            weights.astype(jnp.bfloat16), values, preferred_element_type=jnp.float32
        )
        m_sc[...] = updated
        return carry

    lax.fori_loop(0, count, body, 0)
    o_ref[0] = (acc_sc[...] / l_sc[...]).astype(o_ref.dtype)


def single(queries, low, high, packed, steps, sources, bases, max_steps, pieces):
    halves, tile, head_width = queries.shape
    kernel = functools.partial(
        single_kernel, max_steps=max_steps, head_width=head_width, pieces=pieces
    )
    row_spec = pl.BlockSpec((1, tile, head_width), lambda h, *refs: (h, 0, 0))
    bound_spec = pl.BlockSpec((1, tile, 1), lambda h, *refs: (h, 0, 0))
    return pl.pallas_call(
        kernel,
        out_shape=jax.ShapeDtypeStruct(queries.shape, jnp.bfloat16),
        grid_spec=pltpu.PrefetchScalarGridSpec(
            num_scalar_prefetch=3,
            grid=(halves,),
            in_specs=[row_spec, bound_spec, bound_spec, pl.BlockSpec(memory_space=pl.ANY)],
            out_specs=row_spec,
            scratch_shapes=[
                pltpu.VMEM((2, pieces * tile, packed.shape[1]), packed.dtype),
                pltpu.SemaphoreType.DMA((2, pieces)),
                pltpu.VMEM((tile, 1), jnp.float32),
                pltpu.VMEM((tile, 1), jnp.float32),
                pltpu.VMEM((tile, head_width), jnp.float32),
            ],
        ),
        compiler_params=pltpu.CompilerParams(dimension_semantics=("arbitrary",)),
        cost_estimate=pl.CostEstimate(
            flops=2 * halves * (max_steps // 2) * tile * pieces * tile * head_width * 2,
            transcendentals=halves * (max_steps // 2) * tile * pieces * tile,
            bytes_accessed=halves * (max_steps // 2) * pieces * tile * packed.shape[1] * 2,
        ),
    )(steps, sources, bases, queries, low, high, packed)


def on_device(
    tokens,
    block_order,
    request_lengths,
    enc_lengths,
    w_qkv,
    w_out,
    enc_kv,
    w_cq,
    w_co,
    w_up,
    w_down,
    w_next,
):
    rows_here = tokens.shape[0]
    model_width = tokens.shape[1]
    group_size = lax.axis_size("head")
    cycle_size = lax.axis_size("zy") * lax.axis_size("x")
    block_rows = rows_here * group_size
    halfway = block_rows // 2
    group_width = w_qkv.shape[2]
    head_width = model_width // HEADS
    group_heads = group_width // head_width
    member = lax.axis_index("head")
    ring_size = lax.axis_size("x")
    ring_index = lax.axis_index("x")
    cycle_index = lax.axis_index("zy") * ring_size + ring_index
    encoder = lax.all_gather(enc_kv, ("zy", "x"), axis=1, tiled=True)
    gathered = lax.all_gather(tokens, "head", axis=0, tiled=True)
    projected = jnp.einsum(
        "td,cde->cte", gathered, w_qkv, preferred_element_type=jnp.float32
    ).astype(jnp.bfloat16)
    block_start = cycle_index * block_rows
    query_places = position_of(
        block_order, block_start + jnp.arange(block_rows, dtype=jnp.int32), halfway
    )
    query_groups = group_of(query_places, request_lengths)
    slots = jnp.arange(2 * cycle_size, dtype=jnp.int32)
    holders = jnp.sum(jnp.where(block_order[:, None] == slots[None, :], slots[:, None], 0), axis=0)
    per_head = projected.reshape(3, block_rows, group_heads, head_width).transpose(2, 1, 0, 3)
    per_head = per_head.reshape(group_heads, block_rows, 3 * head_width)
    mine = lax.all_to_all(per_head, "x", 0, 0, tiled=True)
    packed = lax.all_gather(mine[:, :, head_width:], "zy", axis=0, tiled=True)
    packed = packed.reshape(cycle_size * block_rows, 2 * head_width)
    ends = jnp.cumsum(request_lengths).astype(jnp.int32)
    starts = ends - request_lengths
    halves_here = 2 * ring_size
    first_half = lax.axis_index("zy") * halves_here
    pair = lax.dynamic_slice_in_dim(block_order, first_half, halves_here, 0)
    first_request = group_of(pair * halfway, request_lengths)
    low_block = starts[first_request] // halfway
    pieces = 4
    self_steps = (pair - low_block) // pieces + 1
    self_max = (2 * cycle_size + pieces - 1) // pieces
    firsts = low_block[:, None] + pieces * jnp.arange(self_max, dtype=jnp.int32)[None, :]
    self_sources = holders[
        jnp.minimum(firsts[:, :, None] + jnp.arange(pieces, dtype=jnp.int32), 2 * cycle_size - 1)
    ] * halfway
    places_here = (pair[:, None] * halfway + jnp.arange(halfway, dtype=jnp.int32)[None, :])
    groups_here = group_of(places_here.reshape(-1), request_lengths)
    single_out = single(
        mine[:, :, :head_width].reshape(halves_here, halfway, head_width),
        starts[groups_here].reshape(halves_here, halfway, 1),
        places_here.reshape(halves_here, halfway, 1),
        packed,
        self_steps.astype(jnp.int32),
        self_sources.reshape(-1).astype(jnp.int32),
        (firsts * halfway).reshape(-1).astype(jnp.int32),
        self_max,
        pieces,
    )
    returned = lax.all_to_all(
        single_out.reshape(ring_size, block_rows, head_width), "x", 0, 0, tiled=True
    )
    attended = returned.transpose(1, 0, 2).reshape(block_rows, group_width)
    group_blocks = lax.axis_index("zy") * ring_size + jnp.arange(ring_size, dtype=jnp.int32)
    cache_rows = jnp.stack(
        [holders[2 * group_blocks], holders[2 * group_blocks + 1]], axis=1
    )
    cache_parts = jnp.stack(
        [
            jnp.concatenate(
                [
                    lax.dynamic_slice_in_dim(packed, cache_rows[i, 0] * halfway, halfway, 0),
                    lax.dynamic_slice_in_dim(packed, cache_rows[i, 1] * halfway, halfway, 0),
                ],
                axis=0,
            )
            for i in range(ring_size)
        ]
    )
    cache_heads = lax.all_to_all(cache_parts, "x", 0, 0, tiled=True)
    cache = cache_heads.reshape(group_heads, block_rows, 2, head_width).transpose(2, 1, 0, 3)
    cache = cache.reshape(2, block_rows, group_width)
    mixed = lax.psum_scatter(
        jnp.dot(attended, w_out, preferred_element_type=jnp.float32),
        "head",
        scatter_dimension=0,
        tiled=True,
    )
    hidden = normalize(mixed + tokens.astype(jnp.float32))
    hidden_b = hidden.astype(jnp.bfloat16)
    block_hidden = lax.all_gather(hidden_b, "head", axis=0, tiled=True)
    w_cq_group = lax.dynamic_slice_in_dim(w_cq, member * group_width, group_width, 1)
    cross_query = jnp.dot(
        block_hidden, w_cq_group, preferred_element_type=jnp.float32
    ).astype(jnp.bfloat16)
    encoder_rows = encoder.shape[1]
    cross_max = (encoder_rows + halfway - 1 + 2 * halfway - 1) // (2 * halfway)
    padded_encoder = jnp.pad(
        encoder, ((0, 0), (0, cross_max * 2 * halfway + halfway - encoder_rows), (0, 0))
    )
    enc_ends = jnp.cumsum(enc_lengths).astype(jnp.int32)
    enc_starts = enc_ends - enc_lengths
    edge_groups = query_groups.reshape(2, halfway)
    cross_base = (enc_starts[edge_groups[:, 0]] // halfway) * halfway
    cross_steps = (enc_ends[edge_groups[:, -1]] - cross_base + 2 * halfway - 1) // (2 * halfway)
    cross_firsts = jnp.minimum(
        cross_base[:, None] + 2 * halfway * jnp.arange(cross_max, dtype=jnp.int32)[None, :],
        padded_encoder.shape[1] - 2 * halfway,
    )
    cross_sources = jnp.stack([cross_firsts, cross_firsts + halfway], axis=-1)
    crossed_group = flash(
        cross_query.reshape(2, halfway, group_width),
        enc_starts[query_groups].reshape(2, halfway, 1),
        (enc_ends[query_groups] - 1).reshape(2, halfway, 1),
        padded_encoder[0],
        padded_encoder[1],
        cross_steps.astype(jnp.int32),
        cross_sources.reshape(-1).astype(jnp.int32),
        cross_firsts.reshape(-1).astype(jnp.int32),
        cross_max,
        group_heads,
    ).reshape(block_rows, group_width)
    exchanged = lax.all_to_all(
        crossed_group.reshape(group_size, rows_here, group_width), "head", 0, 0, tiled=True
    )
    crossed = exchanged.transpose(1, 0, 2).reshape(rows_here, model_width)
    summed = jnp.dot(crossed, w_co, preferred_element_type=jnp.float32)
    second = normalize(summed + hidden)
    second_b = second.astype(jnp.bfloat16)
    inner = jax.nn.gelu(
        jnp.dot(second_b, w_up, preferred_element_type=jnp.float32), approximate=False
    ).astype(jnp.bfloat16)
    output = normalize(jnp.dot(inner, w_down, preferred_element_type=jnp.float32) + second)
    output_b = output.astype(jnp.bfloat16)
    block_output = lax.all_gather(output_b, "head", axis=0, tiled=True)
    next_qkv = jnp.einsum("td,cde->cte", block_output, w_next, preferred_element_type=jnp.float32)
    return (output, cache, next_qkv)


def solution(mesh):
    ring = 4
    devices = mesh.devices.reshape(mesh.shape["blk"] // ring, ring, mesh.shape["head"])
    fine = jax.sharding.Mesh(devices, ("zy", "x", "head"))
    rows = ("zy", "x", "head")
    blocks = ("zy", "x")
    in_specs = (
        P(rows, None),
        P(),
        P(),
        P(),
        P(None, None, "head"),
        P("head", None),
        P(None, blocks, "head"),
        P(),
        P(),
        P(),
        P(),
        P(None, None, "head"),
    )
    out_specs = (P(rows, None), P(None, blocks, "head"), P(None, blocks, "head"))
    return jax.shard_map(
        on_device, mesh=fine, in_specs=in_specs, out_specs=out_specs, check_vma=False
    )
```

```python
import functools
import math

import jax
import jax.numpy as jnp
from jax import lax
from jax.experimental import pallas as pl
from jax.experimental.pallas import tpu as pltpu
from jax.sharding import PartitionSpec as P

HEADS = 16


NEGATIVE = -1e30
SCALING = 0.125
EPSILON = 1e-05


def normalize(matrix):
    center = matrix - jnp.mean(matrix, axis=-1, keepdims=True)
    return center * lax.rsqrt(jnp.mean(center * center, axis=-1, keepdims=True) + EPSILON)


def position_of(order_table, indices, halfway):
    slots = jnp.arange(order_table.shape[0], dtype=jnp.int32)
    picked = jnp.sum(
        jnp.where((indices // halfway)[:, None] == slots[None, :], order_table[None, :], 0), axis=1
    )
    return picked * halfway + indices % halfway


def group_of(places, lengths):
    ends = jnp.cumsum(lengths)
    return jnp.sum((places[:, None] >= ends[None, :]).astype(jnp.int32), axis=1)


def online_update(carried, queries, key_rows, value_rows, visible):
    maxima, totals, running = carried
    heads_here = queries.shape[1]
    key_split = key_rows.reshape(key_rows.shape[0], heads_here, -1)
    value_split = value_rows.reshape(value_rows.shape[0], heads_here, -1)
    scores = (
        jnp.einsum("qhd,khd->qhk", queries, key_split, preferred_element_type=jnp.float32) * SCALING
    )
    scores = jnp.where(visible[:, None, :], scores, NEGATIVE)
    updated = jnp.maximum(maxima, jnp.max(scores, axis=2))
    factor = jnp.exp(maxima - updated)
    weights = jnp.exp(scores - updated[:, :, None])
    totals = totals * factor + jnp.sum(weights, axis=2)
    running = running * factor[:, :, None] + jnp.einsum(
        "qhk,khd->qhd",
        weights.astype(jnp.bfloat16),
        value_split,
        preferred_element_type=jnp.float32,
    )
    return (updated, totals, running)


def sweep(
    carried, queries, key_rows, value_rows, key_places, key_groups, query_places, query_groups
):
    length = key_rows.shape[0]
    block_size = math.gcd(length, 2048)
    blocks_count = length // block_size
    key_blocks = key_rows.reshape(blocks_count, block_size, key_rows.shape[1])
    value_blocks = value_rows.reshape(blocks_count, block_size, value_rows.shape[1])
    group_blocks = key_groups.reshape(blocks_count, block_size)
    if key_places is None:
        place_blocks = group_blocks
    else:
        place_blocks = key_places.reshape(blocks_count, block_size)

    def advance(status, element):
        key_block, value_block, place_block, group_block = element
        visible = group_block[None, :] == query_groups[:, None]
        if key_places is None:
            return (online_update(status, queries, key_block, value_block, visible), None)
        visible = visible & (place_block[None, :] <= query_places[:, None])
        updated = online_update(status, queries, key_block, value_block, visible)
        return (updated, None)

    carried, unused = lax.scan(
        advance, carried, (key_blocks, value_blocks, place_blocks, group_blocks)
    )
    return carried


def empty_state(count_q, heads_here, head_width):
    return (
        jnp.full((count_q, heads_here), NEGATIVE, jnp.float32),
        jnp.zeros((count_q, heads_here), jnp.float32),
        jnp.zeros((count_q, heads_here, head_width), jnp.float32),
    )


def finish(carried):
    maxima, totals, running = carried
    return (running / totals[:, :, None]).reshape(running.shape[0], -1).astype(jnp.bfloat16)


def flash_kernel(
    steps_ref, sources_ref, bases_ref, q_ref, low_ref, high_ref, k_hbm, v_hbm, o_ref,
    kbuf, vbuf, sem, qm_sc, m_sc, l_sc, acc_sc, *, max_steps, heads, head_width
):
    half = pl.program_id(0)
    count = steps_ref[half]
    tile = kbuf.shape[1] // 2
    width = kbuf.shape[2]

    def copies(step, slot):
        result = []
        for j in range(2):
            source = pl.multiple_of(sources_ref[(half * max_steps + step) * 2 + j], tile)
            window = pl.ds(j * tile, tile)
            result.append(pltpu.make_async_copy(
                k_hbm.at[pl.ds(source, tile)], kbuf.at[slot, window], sem.at[0, slot, j]))
            result.append(pltpu.make_async_copy(
                v_hbm.at[pl.ds(source, tile)], vbuf.at[slot, window], sem.at[1, slot, j]))
        return result

    for copy in copies(0, 0):
        copy.start()
    column_head = lax.broadcasted_iota(jnp.int32, (1, width), 1) // head_width
    q = q_ref[0]
    for h in range(heads):
        qm_sc[h] = jnp.where(column_head == h, q, jnp.zeros_like(q))
    m_sc[...] = jnp.full(m_sc.shape, NEGATIVE, jnp.float32)
    l_sc[...] = jnp.zeros(l_sc.shape, jnp.float32)
    acc_sc[...] = jnp.zeros(acc_sc.shape, jnp.float32)
    low = low_ref[0]
    high = high_ref[0]

    def body(step, carry):
        slot = step % 2
        for copy in copies(step, slot):
            copy.wait()

        @pl.when(step + 1 < count)
        def _():
            for copy in copies(step + 1, 1 - slot):
                copy.start()

        base = bases_ref[half * max_steps + step]
        places = base + lax.broadcasted_iota(jnp.int32, (1, 2 * tile), 1)
        visible = (places >= low) & (places <= high)
        keys = kbuf[slot]
        values = vbuf[slot]
        for h in range(heads):
            scores = lax.dot_general(
                qm_sc[h], keys, (((1,), (1,)), ((), ())), preferred_element_type=jnp.float32
            ) * SCALING
            scores = jnp.where(visible, scores, NEGATIVE)
            previous = m_sc[h]
            updated = jnp.maximum(previous, jnp.max(scores, axis=1, keepdims=True))
            factor = jnp.exp(previous - updated)
            weights = jnp.exp(scores - updated)
            l_sc[h] = l_sc[h] * factor + jnp.sum(weights, axis=1, keepdims=True)
            acc_sc[h] = acc_sc[h] * factor + jnp.dot(
                weights.astype(jnp.bfloat16), values, preferred_element_type=jnp.float32
            )
            m_sc[h] = updated
        return carry

    lax.fori_loop(0, count, body, 0)
    out = jnp.zeros(acc_sc.shape[1:], jnp.float32)
    for h in range(heads):
        out = jnp.where(column_head == h, acc_sc[h] / l_sc[h], out)
    o_ref[0] = out.astype(o_ref.dtype)


def flash(queries, low, high, keys, values, steps, sources, bases, max_steps, heads):
    halves, tile, width = queries.shape
    head_width = width // heads
    kernel = functools.partial(
        flash_kernel, max_steps=max_steps, heads=heads, head_width=head_width
    )
    row_spec = pl.BlockSpec((1, tile, width), lambda h, *refs: (h, 0, 0))
    bound_spec = pl.BlockSpec((1, tile, 1), lambda h, *refs: (h, 0, 0))
    flops = 4 * halves * max_steps * tile * 2 * tile * width * heads
    return pl.pallas_call(
        kernel,
        out_shape=jax.ShapeDtypeStruct(queries.shape, jnp.bfloat16),
        grid_spec=pltpu.PrefetchScalarGridSpec(
            num_scalar_prefetch=3,
            grid=(halves,),
            in_specs=[
                row_spec,
                bound_spec,
                bound_spec,
                pl.BlockSpec(memory_space=pl.ANY),
                pl.BlockSpec(memory_space=pl.ANY),
            ],
            out_specs=row_spec,
            scratch_shapes=[
                pltpu.VMEM((2, 2 * tile, width), keys.dtype),
                pltpu.VMEM((2, 2 * tile, width), values.dtype),
                pltpu.SemaphoreType.DMA((2, 2, 2)),
                pltpu.VMEM((heads, tile, width), jnp.bfloat16),
                pltpu.VMEM((heads, tile, 1), jnp.float32),
                pltpu.VMEM((heads, tile, 1), jnp.float32),
                pltpu.VMEM((heads, tile, width), jnp.float32),
            ],
        ),
        compiler_params=pltpu.CompilerParams(dimension_semantics=("arbitrary",)),
        cost_estimate=pl.CostEstimate(
            flops=flops,
            transcendentals=halves * max_steps * tile * 2 * tile * heads,
            bytes_accessed=halves * max_steps * 2 * 2 * tile * width * 2,
        ),
    )(steps, sources, bases, queries, low, high, keys, values)


def single_kernel(
    steps_ref, sources_ref, bases_ref, q_ref, low_ref, high_ref, kv_hbm, o_ref,
    buf, sem, m_sc, l_sc, acc_sc, *, max_steps, head_width, pieces
):
    half = pl.program_id(0)
    count = steps_ref[half]
    tile = buf.shape[1] // pieces

    def copies(step, slot):
        result = []
        for j in range(pieces):
            source = pl.multiple_of(sources_ref[(half * max_steps + step) * pieces + j], tile)
            result.append(pltpu.make_async_copy(
                kv_hbm.at[pl.ds(source, tile)], buf.at[slot, pl.ds(j * tile, tile)], sem.at[slot, j]))
        return result

    for copy in copies(0, 0):
        copy.start()
    m_sc[...] = jnp.full(m_sc.shape, NEGATIVE, jnp.float32)
    l_sc[...] = jnp.zeros(l_sc.shape, jnp.float32)
    acc_sc[...] = jnp.zeros(acc_sc.shape, jnp.float32)
    q = q_ref[0]
    low = low_ref[0]
    high = high_ref[0]

    def body(step, carry):
        slot = step % 2
        for copy in copies(step, slot):
            copy.wait()

        @pl.when(step + 1 < count)
        def _():
            for copy in copies(step + 1, 1 - slot):
                copy.start()

        base = bases_ref[half * max_steps + step]
        places = base + lax.broadcasted_iota(jnp.int32, (1, pieces * tile), 1)
        visible = (places >= low) & (places <= high)
        block = buf[slot]
        keys = block[:, :head_width]
        values = block[:, head_width:]
        scores = lax.dot_general(
            q, keys, (((1,), (1,)), ((), ())), preferred_element_type=jnp.float32
        ) * SCALING
        scores = jnp.where(visible, scores, NEGATIVE)
        previous = m_sc[...]
        updated = jnp.maximum(previous, jnp.max(scores, axis=1, keepdims=True))
        factor = jnp.exp(previous - updated)
        weights = jnp.exp(scores - updated)
        l_sc[...] = l_sc[...] * factor + jnp.sum(weights, axis=1, keepdims=True)
        acc_sc[...] = acc_sc[...] * factor + jnp.dot(
            weights.astype(jnp.bfloat16), values, preferred_element_type=jnp.float32
        )
        m_sc[...] = updated
        return carry

    lax.fori_loop(0, count, body, 0)
    o_ref[0] = (acc_sc[...] / l_sc[...]).astype(o_ref.dtype)


def single(queries, low, high, packed, steps, sources, bases, max_steps, pieces):
    halves, tile, head_width = queries.shape
    kernel = functools.partial(
        single_kernel, max_steps=max_steps, head_width=head_width, pieces=pieces
    )
    row_spec = pl.BlockSpec((1, tile, head_width), lambda h, *refs: (h, 0, 0))
    bound_spec = pl.BlockSpec((1, tile, 1), lambda h, *refs: (h, 0, 0))
    return pl.pallas_call(
        kernel,
        out_shape=jax.ShapeDtypeStruct(queries.shape, jnp.bfloat16),
        grid_spec=pltpu.PrefetchScalarGridSpec(
            num_scalar_prefetch=3,
            grid=(halves,),
            in_specs=[row_spec, bound_spec, bound_spec, pl.BlockSpec(memory_space=pl.ANY)],
            out_specs=row_spec,
            scratch_shapes=[
                pltpu.VMEM((2, pieces * tile, packed.shape[1]), packed.dtype),
                pltpu.SemaphoreType.DMA((2, pieces)),
                pltpu.VMEM((tile, 1), jnp.float32),
                pltpu.VMEM((tile, 1), jnp.float32),
                pltpu.VMEM((tile, head_width), jnp.float32),
            ],
        ),
        compiler_params=pltpu.CompilerParams(dimension_semantics=("arbitrary",)),
        cost_estimate=pl.CostEstimate(
            flops=2 * halves * (max_steps // 2) * tile * pieces * tile * head_width * 2,
            transcendentals=halves * (max_steps // 2) * tile * pieces * tile,
            bytes_accessed=halves * (max_steps // 2) * pieces * tile * packed.shape[1] * 2,
        ),
    )(steps, sources, bases, queries, low, high, packed)


def exchange_kernel(src_ref, out_ref, land, send_sem, recv_sem, *, axis, count, gather):
    me = lax.axis_index(axis)
    mesh_kind = pl.DeviceIdType.MESH
    barrier = pltpu.get_barrier_semaphore()
    for k in range(1, count):
        pl.semaphore_signal(
            barrier, inc=1, device_id={axis: lax.rem(me + k, count)}, device_id_type=mesh_kind
        )
    pl.semaphore_wait(barrier, count - 1)
    sends = []
    for k in range(1, count):
        peer = lax.rem(me + k, count)
        copy = pltpu.make_async_remote_copy(
            src_ref=src_ref if gather else src_ref.at[peer],
            dst_ref=land.at[me],
            send_sem=send_sem.at[k],
            recv_sem=recv_sem.at[me],
            device_id={axis: peer},
            device_id_type=mesh_kind,
        )
        copy.start()
        sends.append(copy)
    land[me] = src_ref[...] if gather else src_ref[me]
    for copy in sends:
        copy.wait_send()
    for k in range(1, count):
        sender = lax.rem(me + count - k, count)
        pltpu.make_async_remote_copy(
            src_ref=src_ref if gather else src_ref.at[sender],
            dst_ref=land.at[sender],
            send_sem=send_sem.at[k],
            recv_sem=recv_sem.at[sender],
            device_id={axis: sender},
            device_id_type=mesh_kind,
        ).wait_recv()
    out_ref[...] = land[...]


def exchange(value, axis, gather, collective):
    count = lax.axis_size(axis)
    piece = value.shape if gather else value.shape[1:]
    shape = (count,) + tuple(piece)
    kernel = functools.partial(exchange_kernel, axis=axis, count=count, gather=gather)
    return pl.pallas_call(
        kernel,
        out_shape=jax.ShapeDtypeStruct(shape, value.dtype),
        in_specs=[pl.BlockSpec(memory_space=pltpu.VMEM)],
        out_specs=pl.BlockSpec(memory_space=pltpu.VMEM),
        scratch_shapes=[
            pltpu.VMEM(shape, value.dtype),
            pltpu.SemaphoreType.DMA((count,)),
            pltpu.SemaphoreType.DMA((count,)),
        ],
        compiler_params=pltpu.CompilerParams(collective_id=collective, has_side_effects=True),
    )(value)


def on_device(
    tokens,
    block_order,
    request_lengths,
    enc_lengths,
    w_qkv,
    w_out,
    enc_kv,
    w_cq,
    w_co,
    w_up,
    w_down,
    w_next,
):
    rows_here = tokens.shape[0]
    model_width = tokens.shape[1]
    group_size = lax.axis_size("head")
    cycle_size = lax.axis_size("zy") * lax.axis_size("x")
    block_rows = rows_here * group_size
    halfway = block_rows // 2
    group_width = w_qkv.shape[2]
    head_width = model_width // HEADS
    group_heads = group_width // head_width
    member = lax.axis_index("head")
    ring_size = lax.axis_size("x")
    ring_index = lax.axis_index("x")
    cycle_index = lax.axis_index("zy") * ring_size + ring_index
    encoder = lax.all_gather(enc_kv, ("zy", "x"), axis=1, tiled=True)
    gathered = exchange(tokens, "head", True, 0).reshape(block_rows, model_width)
    projected = jnp.einsum(
        "td,cde->cte", gathered, w_qkv, preferred_element_type=jnp.float32
    ).astype(jnp.bfloat16)
    block_start = cycle_index * block_rows
    query_places = position_of(
        block_order, block_start + jnp.arange(block_rows, dtype=jnp.int32), halfway
    )
    query_groups = group_of(query_places, request_lengths)
    slots = jnp.arange(2 * cycle_size, dtype=jnp.int32)
    holders = jnp.sum(jnp.where(block_order[:, None] == slots[None, :], slots[:, None], 0), axis=0)
    per_head = projected.reshape(3, block_rows, group_heads, head_width).transpose(2, 1, 0, 3)
    per_head = per_head.reshape(group_heads, block_rows, 3 * head_width)
    mine = lax.all_to_all(per_head, "x", 0, 0, tiled=True)
    packed = lax.all_gather(mine[:, :, head_width:], "zy", axis=0, tiled=True)
    packed = packed.reshape(cycle_size * block_rows, 2 * head_width)
    ends = jnp.cumsum(request_lengths).astype(jnp.int32)
    starts = ends - request_lengths
    halves_here = 2 * ring_size
    first_half = lax.axis_index("zy") * halves_here
    pair = lax.dynamic_slice_in_dim(block_order, first_half, halves_here, 0)
    first_request = group_of(pair * halfway, request_lengths)
    low_block = starts[first_request] // halfway
    pieces = 4
    self_steps = (pair - low_block) // pieces + 1
    self_max = (2 * cycle_size + pieces - 1) // pieces
    firsts = low_block[:, None] + pieces * jnp.arange(self_max, dtype=jnp.int32)[None, :]
    self_sources = holders[
        jnp.minimum(firsts[:, :, None] + jnp.arange(pieces, dtype=jnp.int32), 2 * cycle_size - 1)
    ] * halfway
    places_here = (pair[:, None] * halfway + jnp.arange(halfway, dtype=jnp.int32)[None, :])
    groups_here = group_of(places_here.reshape(-1), request_lengths)
    single_out = single(
        mine[:, :, :head_width].reshape(halves_here, halfway, head_width),
        starts[groups_here].reshape(halves_here, halfway, 1),
        places_here.reshape(halves_here, halfway, 1),
        packed,
        self_steps.astype(jnp.int32),
        self_sources.reshape(-1).astype(jnp.int32),
        (firsts * halfway).reshape(-1).astype(jnp.int32),
        self_max,
        pieces,
    )
    returned = lax.all_to_all(
        single_out.reshape(ring_size, block_rows, head_width), "x", 0, 0, tiled=True
    )
    attended = returned.transpose(1, 0, 2).reshape(block_rows, group_width)
    group_blocks = lax.axis_index("zy") * ring_size + jnp.arange(ring_size, dtype=jnp.int32)
    cache_rows = jnp.stack(
        [holders[2 * group_blocks], holders[2 * group_blocks + 1]], axis=1
    )
    cache_parts = jnp.stack(
        [
            jnp.concatenate(
                [
                    lax.dynamic_slice_in_dim(packed, cache_rows[i, 0] * halfway, halfway, 0),
                    lax.dynamic_slice_in_dim(packed, cache_rows[i, 1] * halfway, halfway, 0),
                ],
                axis=0,
            )
            for i in range(ring_size)
        ]
    )
    cache_heads = lax.all_to_all(cache_parts, "x", 0, 0, tiled=True)
    cache = cache_heads.reshape(group_heads, block_rows, 2, head_width).transpose(2, 1, 0, 3)
    cache = cache.reshape(2, block_rows, group_width)
    mixed = lax.psum_scatter(
        jnp.dot(attended, w_out, preferred_element_type=jnp.float32),
        "head",
        scatter_dimension=0,
        tiled=True,
    )
    hidden = normalize(mixed + tokens.astype(jnp.float32))
    hidden_b = hidden.astype(jnp.bfloat16)
    block_hidden = exchange(hidden_b, "head", True, 0).reshape(block_rows, model_width)
    w_cq_group = lax.dynamic_slice_in_dim(w_cq, member * group_width, group_width, 1)
    cross_query = jnp.dot(
        block_hidden, w_cq_group, preferred_element_type=jnp.float32
    ).astype(jnp.bfloat16)
    encoder_rows = encoder.shape[1]
    cross_max = (encoder_rows + halfway - 1 + 2 * halfway - 1) // (2 * halfway)
    padded_encoder = jnp.pad(
        encoder, ((0, 0), (0, cross_max * 2 * halfway + halfway - encoder_rows), (0, 0))
    )
    enc_ends = jnp.cumsum(enc_lengths).astype(jnp.int32)
    enc_starts = enc_ends - enc_lengths
    edge_groups = query_groups.reshape(2, halfway)
    cross_base = (enc_starts[edge_groups[:, 0]] // halfway) * halfway
    cross_steps = (enc_ends[edge_groups[:, -1]] - cross_base + 2 * halfway - 1) // (2 * halfway)
    cross_firsts = jnp.minimum(
        cross_base[:, None] + 2 * halfway * jnp.arange(cross_max, dtype=jnp.int32)[None, :],
        padded_encoder.shape[1] - 2 * halfway,
    )
    cross_sources = jnp.stack([cross_firsts, cross_firsts + halfway], axis=-1)
    crossed_group = flash(
        cross_query.reshape(2, halfway, group_width),
        enc_starts[query_groups].reshape(2, halfway, 1),
        (enc_ends[query_groups] - 1).reshape(2, halfway, 1),
        padded_encoder[0],
        padded_encoder[1],
        cross_steps.astype(jnp.int32),
        cross_sources.reshape(-1).astype(jnp.int32),
        cross_firsts.reshape(-1).astype(jnp.int32),
        cross_max,
        group_heads,
    ).reshape(block_rows, group_width)
    exchanged = lax.all_to_all(
        crossed_group.reshape(group_size, rows_here, group_width), "head", 0, 0, tiled=True
    )
    crossed = exchanged.transpose(1, 0, 2).reshape(rows_here, model_width)
    summed = jnp.dot(crossed, w_co, preferred_element_type=jnp.float32)
    second = normalize(summed + hidden)
    second_b = second.astype(jnp.bfloat16)
    inner = jax.nn.gelu(
        jnp.dot(second_b, w_up, preferred_element_type=jnp.float32), approximate=False
    ).astype(jnp.bfloat16)
    output = normalize(jnp.dot(inner, w_down, preferred_element_type=jnp.float32) + second)
    output_b = output.astype(jnp.bfloat16)
    block_output = exchange(output_b, "head", True, 0).reshape(block_rows, model_width)
    next_qkv = jnp.einsum("td,cde->cte", block_output, w_next, preferred_element_type=jnp.float32)
    return (output, cache, next_qkv)


def solution(mesh):
    ring = 4
    devices = mesh.devices.reshape(mesh.shape["blk"] // ring, ring, mesh.shape["head"])
    fine = jax.sharding.Mesh(devices, ("zy", "x", "head"))
    rows = ("zy", "x", "head")
    blocks = ("zy", "x")
    in_specs = (
        P(rows, None),
        P(),
        P(),
        P(),
        P(None, None, "head"),
        P("head", None),
        P(None, blocks, "head"),
        P(),
        P(),
        P(),
        P(),
        P(None, None, "head"),
    )
    out_specs = (P(rows, None), P(None, blocks, "head"), P(None, blocks, "head"))
    return jax.shard_map(
        on_device, mesh=fine, in_specs=in_specs, out_specs=out_specs, check_vma=False
    )
```

```python
import functools
import math

import jax
import jax.numpy as jnp
from jax import lax
from jax.experimental import pallas as pl
from jax.experimental.pallas import tpu as pltpu
from jax.sharding import PartitionSpec as P

HEADS = 16


NEGATIVE = -1e30
SCALING = 0.125
EPSILON = 1e-05


def normalize(matrix):
    center = matrix - jnp.mean(matrix, axis=-1, keepdims=True)
    return center * lax.rsqrt(jnp.mean(center * center, axis=-1, keepdims=True) + EPSILON)


def position_of(order_table, indices, halfway):
    slots = jnp.arange(order_table.shape[0], dtype=jnp.int32)
    picked = jnp.sum(
        jnp.where((indices // halfway)[:, None] == slots[None, :], order_table[None, :], 0), axis=1
    )
    return picked * halfway + indices % halfway


def group_of(places, lengths):
    ends = jnp.cumsum(lengths)
    return jnp.sum((places[:, None] >= ends[None, :]).astype(jnp.int32), axis=1)


def prefix_below(places, bounds, amounts):
    return jnp.sum(
        jnp.where(places[..., None] >= bounds, amounts, 0), axis=-1
    ).astype(jnp.int32)


def lookup(table, indices):
    slots = jnp.arange(table.shape[0], dtype=jnp.int32)
    return jnp.sum(jnp.where(indices[..., None] == slots, table, 0), axis=-1).astype(jnp.int32)


def online_update(carried, queries, key_rows, value_rows, visible):
    maxima, totals, running = carried
    heads_here = queries.shape[1]
    key_split = key_rows.reshape(key_rows.shape[0], heads_here, -1)
    value_split = value_rows.reshape(value_rows.shape[0], heads_here, -1)
    scores = (
        jnp.einsum("qhd,khd->qhk", queries, key_split, preferred_element_type=jnp.float32) * SCALING
    )
    scores = jnp.where(visible[:, None, :], scores, NEGATIVE)
    updated = jnp.maximum(maxima, jnp.max(scores, axis=2))
    factor = jnp.exp(maxima - updated)
    weights = jnp.exp(scores - updated[:, :, None])
    totals = totals * factor + jnp.sum(weights, axis=2)
    running = running * factor[:, :, None] + jnp.einsum(
        "qhk,khd->qhd",
        weights.astype(jnp.bfloat16),
        value_split,
        preferred_element_type=jnp.float32,
    )
    return (updated, totals, running)


def sweep(
    carried, queries, key_rows, value_rows, key_places, key_groups, query_places, query_groups
):
    length = key_rows.shape[0]
    block_size = math.gcd(length, 2048)
    blocks_count = length // block_size
    key_blocks = key_rows.reshape(blocks_count, block_size, key_rows.shape[1])
    value_blocks = value_rows.reshape(blocks_count, block_size, value_rows.shape[1])
    group_blocks = key_groups.reshape(blocks_count, block_size)
    if key_places is None:
        place_blocks = group_blocks
    else:
        place_blocks = key_places.reshape(blocks_count, block_size)

    def advance(status, element):
        key_block, value_block, place_block, group_block = element
        visible = group_block[None, :] == query_groups[:, None]
        if key_places is None:
            return (online_update(status, queries, key_block, value_block, visible), None)
        visible = visible & (place_block[None, :] <= query_places[:, None])
        updated = online_update(status, queries, key_block, value_block, visible)
        return (updated, None)

    carried, unused = lax.scan(
        advance, carried, (key_blocks, value_blocks, place_blocks, group_blocks)
    )
    return carried


def empty_state(count_q, heads_here, head_width):
    return (
        jnp.full((count_q, heads_here), NEGATIVE, jnp.float32),
        jnp.zeros((count_q, heads_here), jnp.float32),
        jnp.zeros((count_q, heads_here, head_width), jnp.float32),
    )


def finish(carried):
    maxima, totals, running = carried
    return (running / totals[:, :, None]).reshape(running.shape[0], -1).astype(jnp.bfloat16)


def flash_kernel(
    steps_ref, sources_ref, bases_ref, q_ref, low_ref, high_ref, k_hbm, v_hbm, o_ref,
    kbuf, vbuf, sem, qm_sc, m_sc, l_sc, acc_sc, *, max_steps, heads, head_width
):
    half = pl.program_id(0)
    count = steps_ref[half]
    tile = kbuf.shape[1] // 2
    width = kbuf.shape[2]

    def copies(step, slot):
        result = []
        for j in range(2):
            source = pl.multiple_of(sources_ref[(half * max_steps + step) * 2 + j], tile)
            window = pl.ds(j * tile, tile)
            result.append(pltpu.make_async_copy(
                k_hbm.at[pl.ds(source, tile)], kbuf.at[slot, window], sem.at[0, slot, j]))
            result.append(pltpu.make_async_copy(
                v_hbm.at[pl.ds(source, tile)], vbuf.at[slot, window], sem.at[1, slot, j]))
        return result

    for copy in copies(0, 0):
        copy.start()
    column_head = lax.broadcasted_iota(jnp.int32, (1, width), 1) // head_width
    q = q_ref[0]
    for h in range(heads):
        qm_sc[h] = jnp.where(column_head == h, q, jnp.zeros_like(q))
    m_sc[...] = jnp.full(m_sc.shape, NEGATIVE, jnp.float32)
    l_sc[...] = jnp.zeros(l_sc.shape, jnp.float32)
    acc_sc[...] = jnp.zeros(acc_sc.shape, jnp.float32)
    low = low_ref[0]
    high = high_ref[0]

    def body(step, carry):
        slot = step % 2
        for copy in copies(step, slot):
            copy.wait()

        @pl.when(step + 1 < count)
        def _():
            for copy in copies(step + 1, 1 - slot):
                copy.start()

        base = bases_ref[half * max_steps + step]
        places = base + lax.broadcasted_iota(jnp.int32, (1, 2 * tile), 1)
        visible = (places >= low) & (places <= high)
        keys = kbuf[slot]
        values = vbuf[slot]
        for h in range(heads):
            scores = lax.dot_general(
                qm_sc[h], keys, (((1,), (1,)), ((), ())), preferred_element_type=jnp.float32
            ) * SCALING
            scores = jnp.where(visible, scores, NEGATIVE)
            previous = m_sc[h]
            updated = jnp.maximum(previous, jnp.max(scores, axis=1, keepdims=True))
            factor = jnp.exp(previous - updated)
            weights = jnp.exp(scores - updated)
            l_sc[h] = l_sc[h] * factor + jnp.sum(weights, axis=1, keepdims=True)
            acc_sc[h] = acc_sc[h] * factor + jnp.dot(
                weights.astype(jnp.bfloat16), values, preferred_element_type=jnp.float32
            )
            m_sc[h] = updated
        return carry

    lax.fori_loop(0, count, body, 0)
    out = jnp.zeros(acc_sc.shape[1:], jnp.float32)
    for h in range(heads):
        out = jnp.where(column_head == h, acc_sc[h] / l_sc[h], out)
    o_ref[0] = out.astype(o_ref.dtype)


def flash(queries, low, high, keys, values, steps, sources, bases, max_steps, heads):
    halves, tile, width = queries.shape
    head_width = width // heads
    kernel = functools.partial(
        flash_kernel, max_steps=max_steps, heads=heads, head_width=head_width
    )
    row_spec = pl.BlockSpec((1, tile, width), lambda h, *refs: (h, 0, 0))
    bound_spec = pl.BlockSpec((1, tile, 1), lambda h, *refs: (h, 0, 0))
    flops = 4 * halves * max_steps * tile * 2 * tile * width * heads
    return pl.pallas_call(
        kernel,
        out_shape=jax.ShapeDtypeStruct(queries.shape, jnp.bfloat16),
        grid_spec=pltpu.PrefetchScalarGridSpec(
            num_scalar_prefetch=3,
            grid=(halves,),
            in_specs=[
                row_spec,
                bound_spec,
                bound_spec,
                pl.BlockSpec(memory_space=pl.ANY),
                pl.BlockSpec(memory_space=pl.ANY),
            ],
            out_specs=row_spec,
            scratch_shapes=[
                pltpu.VMEM((2, 2 * tile, width), keys.dtype),
                pltpu.VMEM((2, 2 * tile, width), values.dtype),
                pltpu.SemaphoreType.DMA((2, 2, 2)),
                pltpu.VMEM((heads, tile, width), jnp.bfloat16),
                pltpu.VMEM((heads, tile, 1), jnp.float32),
                pltpu.VMEM((heads, tile, 1), jnp.float32),
                pltpu.VMEM((heads, tile, width), jnp.float32),
            ],
        ),
        compiler_params=pltpu.CompilerParams(dimension_semantics=("arbitrary",)),
        cost_estimate=pl.CostEstimate(
            flops=flops,
            transcendentals=halves * max_steps * tile * 2 * tile * heads,
            bytes_accessed=halves * max_steps * 2 * 2 * tile * width * 2,
        ),
    )(steps, sources, bases, queries, low, high, keys, values)


def single_kernel(
    steps_ref, sources_ref, bases_ref, q_ref, low_ref, high_ref, kv_hbm, o_ref,
    buf, sem, m_sc, l_sc, acc_sc, *, max_steps, head_width, pieces
):
    half = pl.program_id(0)
    count = steps_ref[half]
    tile = buf.shape[1] // pieces

    def copies(step, slot):
        result = []
        for j in range(pieces):
            source = pl.multiple_of(sources_ref[(half * max_steps + step) * pieces + j], tile)
            result.append(pltpu.make_async_copy(
                kv_hbm.at[pl.ds(source, tile)], buf.at[slot, pl.ds(j * tile, tile)], sem.at[slot, j]))
        return result

    for copy in copies(0, 0):
        copy.start()
    m_sc[...] = jnp.full(m_sc.shape, NEGATIVE, jnp.float32)
    l_sc[...] = jnp.zeros(l_sc.shape, jnp.float32)
    acc_sc[...] = jnp.zeros(acc_sc.shape, jnp.float32)
    q = q_ref[0]
    low = low_ref[0]
    high = high_ref[0]

    def body(step, carry):
        slot = step % 2
        for copy in copies(step, slot):
            copy.wait()

        @pl.when(step + 1 < count)
        def _():
            for copy in copies(step + 1, 1 - slot):
                copy.start()

        base = bases_ref[half * max_steps + step]
        places = base + lax.broadcasted_iota(jnp.int32, (1, pieces * tile), 1)
        visible = (places >= low) & (places <= high)
        block = buf[slot]
        keys = block[:, :head_width]
        values = block[:, head_width:]
        scores = lax.dot_general(
            q, keys, (((1,), (1,)), ((), ())), preferred_element_type=jnp.float32
        ) * SCALING
        scores = jnp.where(visible, scores, NEGATIVE)
        previous = m_sc[...]
        updated = jnp.maximum(previous, jnp.max(scores, axis=1, keepdims=True))
        factor = jnp.exp(previous - updated)
        weights = jnp.exp(scores - updated)
        l_sc[...] = l_sc[...] * factor + jnp.sum(weights, axis=1, keepdims=True)
        acc_sc[...] = acc_sc[...] * factor + jnp.dot(
            weights.astype(jnp.bfloat16), values, preferred_element_type=jnp.float32
        )
        m_sc[...] = updated
        return carry

    lax.fori_loop(0, count, body, 0)
    o_ref[0] = (acc_sc[...] / l_sc[...]).astype(o_ref.dtype)


def single(queries, low, high, packed, steps, sources, bases, max_steps, pieces):
    halves, tile, head_width = queries.shape
    kernel = functools.partial(
        single_kernel, max_steps=max_steps, head_width=head_width, pieces=pieces
    )
    row_spec = pl.BlockSpec((1, tile, head_width), lambda h, *refs: (h, 0, 0))
    bound_spec = pl.BlockSpec((1, tile, 1), lambda h, *refs: (h, 0, 0))
    return pl.pallas_call(
        kernel,
        out_shape=jax.ShapeDtypeStruct(queries.shape, jnp.bfloat16),
        grid_spec=pltpu.PrefetchScalarGridSpec(
            num_scalar_prefetch=3,
            grid=(halves,),
            in_specs=[row_spec, bound_spec, bound_spec, pl.BlockSpec(memory_space=pl.ANY)],
            out_specs=row_spec,
            scratch_shapes=[
                pltpu.VMEM((2, pieces * tile, packed.shape[1]), packed.dtype),
                pltpu.SemaphoreType.DMA((2, pieces)),
                pltpu.VMEM((tile, 1), jnp.float32),
                pltpu.VMEM((tile, 1), jnp.float32),
                pltpu.VMEM((tile, head_width), jnp.float32),
            ],
        ),
        compiler_params=pltpu.CompilerParams(dimension_semantics=("arbitrary",)),
        cost_estimate=pl.CostEstimate(
            flops=2 * halves * (max_steps // 2) * tile * pieces * tile * head_width * 2,
            transcendentals=halves * (max_steps // 2) * tile * pieces * tile,
            bytes_accessed=halves * (max_steps // 2) * pieces * tile * packed.shape[1] * 2,
        ),
    )(steps, sources, bases, queries, low, high, packed)


def on_device(
    tokens,
    block_order,
    request_lengths,
    enc_lengths,
    w_qkv,
    w_out,
    enc_kv,
    w_cq,
    w_co,
    w_up,
    w_down,
    w_next,
):
    rows_here = tokens.shape[0]
    model_width = tokens.shape[1]
    group_size = lax.axis_size("head")
    cycle_size = lax.axis_size("zy") * lax.axis_size("x")
    block_rows = rows_here * group_size
    halfway = block_rows // 2
    group_width = w_qkv.shape[2]
    head_width = model_width // HEADS
    group_heads = group_width // head_width
    member = lax.axis_index("head")
    ring_size = lax.axis_size("x")
    ring_index = lax.axis_index("x")
    cycle_index = lax.axis_index("zy") * ring_size + ring_index
    encoder = lax.all_gather(enc_kv, ("zy", "x"), axis=1, tiled=True)
    gathered = lax.all_gather(tokens, "head", axis=0, tiled=True)
    projected = jnp.einsum(
        "td,cde->cte", gathered, w_qkv, preferred_element_type=jnp.float32
    ).astype(jnp.bfloat16)
    block_start = cycle_index * block_rows
    query_places = position_of(
        block_order, block_start + jnp.arange(block_rows, dtype=jnp.int32), halfway
    )
    slots = jnp.arange(2 * cycle_size, dtype=jnp.int32)
    holders = jnp.sum(jnp.where(block_order[:, None] == slots[None, :], slots[:, None], 0), axis=0)
    per_head = projected.reshape(3, block_rows, group_heads, head_width).transpose(2, 1, 0, 3)
    per_head = per_head.reshape(group_heads, block_rows, 3 * head_width)
    mine = lax.all_to_all(per_head, "x", 0, 0, tiled=True)
    packed = lax.all_gather(mine[:, :, head_width:], "zy", axis=0, tiled=True)
    packed = packed.reshape(cycle_size * block_rows, 2 * head_width)
    ends = jnp.cumsum(request_lengths).astype(jnp.int32)
    starts = ends - request_lengths
    halves_here = 2 * ring_size
    first_half = lax.axis_index("zy") * halves_here
    pair = lax.dynamic_slice_in_dim(block_order, first_half, halves_here, 0)
    low_block = prefix_below(pair * halfway, ends, request_lengths) // halfway
    pieces = 4
    self_steps = (pair - low_block) // pieces + 1
    self_max = (2 * cycle_size + pieces - 1) // pieces
    firsts = low_block[:, None] + pieces * jnp.arange(self_max, dtype=jnp.int32)[None, :]
    self_sources = lookup(
        holders,
        jnp.minimum(firsts[:, :, None] + jnp.arange(pieces, dtype=jnp.int32), 2 * cycle_size - 1),
    ) * halfway
    places_here = (pair[:, None] * halfway + jnp.arange(halfway, dtype=jnp.int32)[None, :])
    single_out = single(
        mine[:, :, :head_width].reshape(halves_here, halfway, head_width),
        prefix_below(places_here, ends, request_lengths).reshape(halves_here, halfway, 1),
        places_here.reshape(halves_here, halfway, 1),
        packed,
        self_steps.astype(jnp.int32),
        self_sources.reshape(-1).astype(jnp.int32),
        (firsts * halfway).reshape(-1).astype(jnp.int32),
        self_max,
        pieces,
    )
    returned = lax.all_to_all(
        single_out.reshape(ring_size, block_rows, head_width), "x", 0, 0, tiled=True
    )
    attended = returned.transpose(1, 0, 2).reshape(block_rows, group_width)
    group_blocks = lax.axis_index("zy") * ring_size + jnp.arange(ring_size, dtype=jnp.int32)
    cache_rows = lookup(
        holders, jnp.stack([2 * group_blocks, 2 * group_blocks + 1], axis=1)
    )
    cache_parts = jnp.stack(
        [
            jnp.concatenate(
                [
                    lax.dynamic_slice_in_dim(packed, cache_rows[i, 0] * halfway, halfway, 0),
                    lax.dynamic_slice_in_dim(packed, cache_rows[i, 1] * halfway, halfway, 0),
                ],
                axis=0,
            )
            for i in range(ring_size)
        ]
    )
    cache_heads = lax.all_to_all(cache_parts, "x", 0, 0, tiled=True)
    cache = cache_heads.reshape(group_heads, block_rows, 2, head_width).transpose(2, 1, 0, 3)
    cache = cache.reshape(2, block_rows, group_width)
    mixed = lax.psum_scatter(
        jnp.dot(attended, w_out, preferred_element_type=jnp.float32),
        "head",
        scatter_dimension=0,
        tiled=True,
    )
    hidden = normalize(mixed + tokens.astype(jnp.float32))
    hidden_b = hidden.astype(jnp.bfloat16)
    block_hidden = lax.all_gather(hidden_b, "head", axis=0, tiled=True)
    w_cq_group = lax.dynamic_slice_in_dim(w_cq, member * group_width, group_width, 1)
    cross_query = jnp.dot(
        block_hidden, w_cq_group, preferred_element_type=jnp.float32
    ).astype(jnp.bfloat16)
    encoder_rows = encoder.shape[1]
    cross_max = (encoder_rows + halfway - 1 + 2 * halfway - 1) // (2 * halfway)
    padded_encoder = jnp.pad(
        encoder, ((0, 0), (0, cross_max * 2 * halfway + halfway - encoder_rows), (0, 0))
    )
    enc_low = prefix_below(query_places, ends, enc_lengths)
    enc_high = prefix_below(query_places, starts, enc_lengths) - 1
    cross_base = (enc_low.reshape(2, halfway)[:, 0] // halfway) * halfway
    cross_steps = (enc_high.reshape(2, halfway)[:, -1] + 1 - cross_base + 2 * halfway - 1) // (
        2 * halfway
    )
    cross_firsts = jnp.minimum(
        cross_base[:, None] + 2 * halfway * jnp.arange(cross_max, dtype=jnp.int32)[None, :],
        padded_encoder.shape[1] - 2 * halfway,
    )
    cross_sources = jnp.stack([cross_firsts, cross_firsts + halfway], axis=-1)
    crossed_group = flash(
        cross_query.reshape(2, halfway, group_width),
        enc_low.reshape(2, halfway, 1),
        enc_high.reshape(2, halfway, 1),
        padded_encoder[0],
        padded_encoder[1],
        cross_steps.astype(jnp.int32),
        cross_sources.reshape(-1).astype(jnp.int32),
        cross_firsts.reshape(-1).astype(jnp.int32),
        cross_max,
        group_heads,
    ).reshape(block_rows, group_width)
    exchanged = lax.all_to_all(
        crossed_group.reshape(group_size, rows_here, group_width), "head", 0, 0, tiled=True
    )
    crossed = exchanged.transpose(1, 0, 2).reshape(rows_here, model_width)
    summed = jnp.dot(crossed, w_co, preferred_element_type=jnp.float32)
    second = normalize(summed + hidden)
    second_b = second.astype(jnp.bfloat16)
    inner = jax.nn.gelu(
        jnp.dot(second_b, w_up, preferred_element_type=jnp.float32), approximate=False
    ).astype(jnp.bfloat16)
    output = normalize(jnp.dot(inner, w_down, preferred_element_type=jnp.float32) + second)
    output_b = output.astype(jnp.bfloat16)
    block_output = lax.all_gather(output_b, "head", axis=0, tiled=True)
    next_qkv = jnp.einsum("td,cde->cte", block_output, w_next, preferred_element_type=jnp.float32)
    return (output, cache, next_qkv)


def solution(mesh):
    ring = 4
    devices = mesh.devices.reshape(mesh.shape["blk"] // ring, ring, mesh.shape["head"])
    fine = jax.sharding.Mesh(devices, ("zy", "x", "head"))
    rows = ("zy", "x", "head")
    blocks = ("zy", "x")
    in_specs = (
        P(rows, None),
        P(),
        P(),
        P(),
        P(None, None, "head"),
        P("head", None),
        P(None, blocks, "head"),
        P(),
        P(),
        P(),
        P(),
        P(None, None, "head"),
    )
    out_specs = (P(rows, None), P(None, blocks, "head"), P(None, blocks, "head"))
    return jax.shard_map(
        on_device, mesh=fine, in_specs=in_specs, out_specs=out_specs, check_vma=False
    )
```

```python
import functools
import math

import jax
import jax.numpy as jnp
from jax import lax
from jax.experimental import pallas as pl
from jax.experimental.pallas import tpu as pltpu
from jax.sharding import PartitionSpec as P

HEADS = 16


NEGATIVE = -1e30
SCALING = 0.125
EPSILON = 1e-05


def normalize(matrix):
    center = matrix - jnp.mean(matrix, axis=-1, keepdims=True)
    return center * lax.rsqrt(jnp.mean(center * center, axis=-1, keepdims=True) + EPSILON)


def position_of(order_table, indices, halfway):
    slots = jnp.arange(order_table.shape[0], dtype=jnp.int32)
    picked = jnp.sum(
        jnp.where((indices // halfway)[:, None] == slots[None, :], order_table[None, :], 0), axis=1
    )
    return picked * halfway + indices % halfway


def group_of(places, lengths):
    ends = jnp.cumsum(lengths)
    return jnp.sum((places[:, None] >= ends[None, :]).astype(jnp.int32), axis=1)


def prefix_below(places, bounds, amounts):
    return jnp.sum(
        jnp.where(places[..., None] >= bounds, amounts, 0), axis=-1
    ).astype(jnp.int32)


def lookup(table, indices):
    slots = jnp.arange(table.shape[0], dtype=jnp.int32)
    return jnp.sum(jnp.where(indices[..., None] == slots, table, 0), axis=-1).astype(jnp.int32)


def online_update(carried, queries, key_rows, value_rows, visible):
    maxima, totals, running = carried
    heads_here = queries.shape[1]
    key_split = key_rows.reshape(key_rows.shape[0], heads_here, -1)
    value_split = value_rows.reshape(value_rows.shape[0], heads_here, -1)
    scores = (
        jnp.einsum("qhd,khd->qhk", queries, key_split, preferred_element_type=jnp.float32) * SCALING
    )
    scores = jnp.where(visible[:, None, :], scores, NEGATIVE)
    updated = jnp.maximum(maxima, jnp.max(scores, axis=2))
    factor = jnp.exp(maxima - updated)
    weights = jnp.exp(scores - updated[:, :, None])
    totals = totals * factor + jnp.sum(weights, axis=2)
    running = running * factor[:, :, None] + jnp.einsum(
        "qhk,khd->qhd",
        weights.astype(jnp.bfloat16),
        value_split,
        preferred_element_type=jnp.float32,
    )
    return (updated, totals, running)


def sweep(
    carried, queries, key_rows, value_rows, key_places, key_groups, query_places, query_groups
):
    length = key_rows.shape[0]
    block_size = math.gcd(length, 2048)
    blocks_count = length // block_size
    key_blocks = key_rows.reshape(blocks_count, block_size, key_rows.shape[1])
    value_blocks = value_rows.reshape(blocks_count, block_size, value_rows.shape[1])
    group_blocks = key_groups.reshape(blocks_count, block_size)
    if key_places is None:
        place_blocks = group_blocks
    else:
        place_blocks = key_places.reshape(blocks_count, block_size)

    def advance(status, element):
        key_block, value_block, place_block, group_block = element
        visible = group_block[None, :] == query_groups[:, None]
        if key_places is None:
            return (online_update(status, queries, key_block, value_block, visible), None)
        visible = visible & (place_block[None, :] <= query_places[:, None])
        updated = online_update(status, queries, key_block, value_block, visible)
        return (updated, None)

    carried, unused = lax.scan(
        advance, carried, (key_blocks, value_blocks, place_blocks, group_blocks)
    )
    return carried


def empty_state(count_q, heads_here, head_width):
    return (
        jnp.full((count_q, heads_here), NEGATIVE, jnp.float32),
        jnp.zeros((count_q, heads_here), jnp.float32),
        jnp.zeros((count_q, heads_here, head_width), jnp.float32),
    )


def finish(carried):
    maxima, totals, running = carried
    return (running / totals[:, :, None]).reshape(running.shape[0], -1).astype(jnp.bfloat16)


def flash_kernel(
    steps_ref, sources_ref, bases_ref, q_ref, low_ref, high_ref, k_hbm, v_hbm, o_ref,
    kbuf, vbuf, sem, qm_sc, m_sc, l_sc, acc_sc, *, max_steps, heads, head_width
):
    half = pl.program_id(0)
    count = steps_ref[half]
    tile = kbuf.shape[1] // 2
    width = kbuf.shape[2]

    def copies(step, slot):
        result = []
        for j in range(2):
            source = pl.multiple_of(sources_ref[(half * max_steps + step) * 2 + j], tile)
            window = pl.ds(j * tile, tile)
            result.append(pltpu.make_async_copy(
                k_hbm.at[pl.ds(source, tile)], kbuf.at[slot, window], sem.at[0, slot, j]))
            result.append(pltpu.make_async_copy(
                v_hbm.at[pl.ds(source, tile)], vbuf.at[slot, window], sem.at[1, slot, j]))
        return result

    for copy in copies(0, 0):
        copy.start()
    column_head = lax.broadcasted_iota(jnp.int32, (1, width), 1) // head_width
    q = q_ref[0]
    for h in range(heads):
        qm_sc[h] = jnp.where(column_head == h, q, jnp.zeros_like(q))
    m_sc[...] = jnp.full(m_sc.shape, NEGATIVE, jnp.float32)
    l_sc[...] = jnp.zeros(l_sc.shape, jnp.float32)
    acc_sc[...] = jnp.zeros(acc_sc.shape, jnp.float32)
    low = low_ref[0]
    high = high_ref[0]

    def body(step, carry):
        slot = step % 2
        for copy in copies(step, slot):
            copy.wait()

        @pl.when(step + 1 < count)
        def _():
            for copy in copies(step + 1, 1 - slot):
                copy.start()

        base = bases_ref[half * max_steps + step]
        places = base + lax.broadcasted_iota(jnp.int32, (1, 2 * tile), 1)
        visible = (places >= low) & (places <= high)
        keys = kbuf[slot]
        values = vbuf[slot]
        for h in range(heads):
            scores = lax.dot_general(
                qm_sc[h], keys, (((1,), (1,)), ((), ())), preferred_element_type=jnp.float32
            ) * SCALING
            scores = jnp.where(visible, scores, NEGATIVE)
            previous = m_sc[h]
            updated = jnp.maximum(previous, jnp.max(scores, axis=1, keepdims=True))
            factor = jnp.exp(previous - updated)
            weights = jnp.exp(scores - updated)
            l_sc[h] = l_sc[h] * factor + jnp.sum(weights, axis=1, keepdims=True)
            acc_sc[h] = acc_sc[h] * factor + jnp.dot(
                weights.astype(jnp.bfloat16), values, preferred_element_type=jnp.float32
            )
            m_sc[h] = updated
        return carry

    lax.fori_loop(0, count, body, 0)
    out = jnp.zeros(acc_sc.shape[1:], jnp.float32)
    for h in range(heads):
        out = jnp.where(column_head == h, acc_sc[h] / l_sc[h], out)
    o_ref[0] = out.astype(o_ref.dtype)


def flash(queries, low, high, keys, values, steps, sources, bases, max_steps, heads):
    halves, tile, width = queries.shape
    head_width = width // heads
    kernel = functools.partial(
        flash_kernel, max_steps=max_steps, heads=heads, head_width=head_width
    )
    row_spec = pl.BlockSpec((1, tile, width), lambda h, *refs: (h, 0, 0))
    bound_spec = pl.BlockSpec((1, tile, 1), lambda h, *refs: (h, 0, 0))
    flops = 4 * halves * max_steps * tile * 2 * tile * width * heads
    return pl.pallas_call(
        kernel,
        out_shape=jax.ShapeDtypeStruct(queries.shape, jnp.bfloat16),
        grid_spec=pltpu.PrefetchScalarGridSpec(
            num_scalar_prefetch=3,
            grid=(halves,),
            in_specs=[
                row_spec,
                bound_spec,
                bound_spec,
                pl.BlockSpec(memory_space=pl.ANY),
                pl.BlockSpec(memory_space=pl.ANY),
            ],
            out_specs=row_spec,
            scratch_shapes=[
                pltpu.VMEM((2, 2 * tile, width), keys.dtype),
                pltpu.VMEM((2, 2 * tile, width), values.dtype),
                pltpu.SemaphoreType.DMA((2, 2, 2)),
                pltpu.VMEM((heads, tile, width), jnp.bfloat16),
                pltpu.VMEM((heads, tile, 1), jnp.float32),
                pltpu.VMEM((heads, tile, 1), jnp.float32),
                pltpu.VMEM((heads, tile, width), jnp.float32),
            ],
        ),
        compiler_params=pltpu.CompilerParams(dimension_semantics=("arbitrary",)),
        cost_estimate=pl.CostEstimate(
            flops=flops,
            transcendentals=halves * max_steps * tile * 2 * tile * heads,
            bytes_accessed=halves * max_steps * 2 * 2 * tile * width * 2,
        ),
    )(steps, sources, bases, queries, low, high, keys, values)


def single_kernel(
    steps_ref, sources_ref, bases_ref, q_ref, low_ref, high_ref, m_ref, l_ref, acc_ref, kv_hbm,
    *rest, max_steps, pieces, first, last
):
    if last:
        o_ref, buf, sem, m_sc, l_sc, acc_sc = rest
    else:
        m_out, l_out, acc_out, buf, sem, m_sc, l_sc, acc_sc = rest
    half = pl.program_id(0)
    count = steps_ref[half]
    tile = buf.shape[1] // pieces
    head_width = q_ref.shape[2]

    def copies(step, slot):
        result = []
        for j in range(pieces):
            source = pl.multiple_of(sources_ref[(half * max_steps + step) * pieces + j], tile)
            result.append(pltpu.make_async_copy(
                kv_hbm.at[pl.ds(source, tile)], buf.at[slot, pl.ds(j * tile, tile)], sem.at[slot, j]))
        return result

    @pl.when(count > 0)
    def _():
        for copy in copies(0, 0):
            copy.start()

    if first:
        m_sc[...] = jnp.full(m_sc.shape, NEGATIVE, jnp.float32)
        l_sc[...] = jnp.zeros(l_sc.shape, jnp.float32)
        acc_sc[...] = jnp.zeros(acc_sc.shape, jnp.float32)
    else:
        m_sc[...] = m_ref[0]
        l_sc[...] = l_ref[0]
        acc_sc[...] = acc_ref[0]
    q = q_ref[0]
    low = low_ref[0]
    high = high_ref[0]
    lane = lax.broadcasted_iota(jnp.int32, (1, pieces * tile), 1)
    piece = lane // tile
    offset = lane - piece * tile

    def body(step, carry):
        slot = step % 2
        for copy in copies(step, slot):
            copy.wait()

        @pl.when(step + 1 < count)
        def _():
            for copy in copies(step + 1, 1 - slot):
                copy.start()

        row = (half * max_steps + step) * pieces
        base = jnp.zeros((1, pieces * tile), jnp.int32)
        for j in range(pieces):
            base = jnp.where(piece == j, bases_ref[row + j], base)
        places = base + offset
        visible = (places >= low) & (places <= high)
        block = buf[slot]
        keys = block[:, :head_width]
        values = block[:, head_width:]
        scores = lax.dot_general(
            q, keys, (((1,), (1,)), ((), ())), preferred_element_type=jnp.float32
        ) * SCALING
        scores = jnp.where(visible, scores, NEGATIVE)
        previous = m_sc[...]
        updated = jnp.maximum(previous, jnp.max(scores, axis=1, keepdims=True))
        factor = jnp.exp(previous - updated)
        weights = jnp.exp(scores - updated)
        l_sc[...] = l_sc[...] * factor + jnp.sum(weights, axis=1, keepdims=True)
        acc_sc[...] = acc_sc[...] * factor + jnp.dot(
            weights.astype(jnp.bfloat16), values, preferred_element_type=jnp.float32
        )
        m_sc[...] = updated
        return carry

    lax.fori_loop(0, count, body, 0)
    if last:
        o_ref[0] = (acc_sc[...] / l_sc[...]).astype(o_ref.dtype)
    else:
        m_out[0] = m_sc[...]
        l_out[0] = l_sc[...]
        acc_out[0] = acc_sc[...]


def single(queries, low, high, state, packed, steps, sources, bases, max_steps, pieces, first, last):
    halves, tile, head_width = queries.shape
    kernel = functools.partial(
        single_kernel, max_steps=max_steps, pieces=pieces, first=first, last=last
    )
    row_spec = pl.BlockSpec((1, tile, head_width), lambda h, *refs: (h, 0, 0))
    bound_spec = pl.BlockSpec((1, tile, 1), lambda h, *refs: (h, 0, 0))
    state_shapes = (
        jax.ShapeDtypeStruct((halves, tile, 1), jnp.float32),
        jax.ShapeDtypeStruct((halves, tile, 1), jnp.float32),
        jax.ShapeDtypeStruct((halves, tile, head_width), jnp.float32),
    )
    state_specs = [bound_spec, bound_spec, row_spec]
    if last:
        out_shape = jax.ShapeDtypeStruct(queries.shape, jnp.bfloat16)
        out_specs = row_spec
    else:
        out_shape = state_shapes
        out_specs = state_specs
    return pl.pallas_call(
        kernel,
        out_shape=out_shape,
        grid_spec=pltpu.PrefetchScalarGridSpec(
            num_scalar_prefetch=3,
            grid=(halves,),
            in_specs=[row_spec, bound_spec, bound_spec] + state_specs
            + [pl.BlockSpec(memory_space=pl.ANY)],
            out_specs=out_specs,
            scratch_shapes=[
                pltpu.VMEM((2, pieces * tile, packed.shape[1]), packed.dtype),
                pltpu.SemaphoreType.DMA((2, pieces)),
                pltpu.VMEM((tile, 1), jnp.float32),
                pltpu.VMEM((tile, 1), jnp.float32),
                pltpu.VMEM((tile, head_width), jnp.float32),
            ],
        ),
        compiler_params=pltpu.CompilerParams(dimension_semantics=("arbitrary",)),
        cost_estimate=pl.CostEstimate(
            flops=2 * halves * (max_steps // 4) * tile * pieces * tile * head_width * 2,
            transcendentals=halves * (max_steps // 4) * tile * pieces * tile,
            bytes_accessed=halves * (max_steps // 4) * pieces * tile * packed.shape[1] * 2,
        ),
    )(steps, sources, bases, queries, low, high, *state, packed)


def on_device(
    tokens,
    block_order,
    request_lengths,
    enc_lengths,
    w_qkv,
    w_out,
    enc_kv,
    w_cq,
    w_co,
    w_up,
    w_down,
    w_next,
):
    rows_here = tokens.shape[0]
    model_width = tokens.shape[1]
    group_size = lax.axis_size("head")
    cycle_size = lax.axis_size("zy") * lax.axis_size("x")
    block_rows = rows_here * group_size
    halfway = block_rows // 2
    group_width = w_qkv.shape[2]
    head_width = model_width // HEADS
    group_heads = group_width // head_width
    member = lax.axis_index("head")
    ring_size = lax.axis_size("x")
    ring_index = lax.axis_index("x")
    cycle_index = lax.axis_index("zy") * ring_size + ring_index
    encoder = lax.all_gather(enc_kv, ("zy", "x"), axis=1, tiled=True)
    gathered = lax.all_gather(tokens, "head", axis=0, tiled=True)
    projected = jnp.einsum(
        "td,cde->cte", gathered, w_qkv, preferred_element_type=jnp.float32
    ).astype(jnp.bfloat16)
    block_start = cycle_index * block_rows
    query_places = position_of(
        block_order, block_start + jnp.arange(block_rows, dtype=jnp.int32), halfway
    )
    slots = jnp.arange(2 * cycle_size, dtype=jnp.int32)
    holders = jnp.sum(jnp.where(block_order[:, None] == slots[None, :], slots[:, None], 0), axis=0)
    per_head = projected.reshape(3, block_rows, group_heads, head_width).transpose(2, 1, 0, 3)
    per_head = per_head.reshape(group_heads, block_rows, 3 * head_width)
    mine = lax.all_to_all(per_head, "x", 0, 0, tiled=True)
    parts = mine[:, :, head_width:].reshape(ring_size, 2, halfway, 2 * head_width)
    even = lax.all_gather(parts[:, 0], "zy", axis=0, tiled=True).reshape(-1, 2 * head_width)
    odd = lax.all_gather(parts[:, 1], "zy", axis=0, tiled=True).reshape(-1, 2 * head_width)
    ends = jnp.cumsum(request_lengths).astype(jnp.int32)
    starts = ends - request_lengths
    halves_here = 2 * ring_size
    first_half = lax.axis_index("zy") * halves_here
    pair = lax.dynamic_slice_in_dim(block_order, first_half, halves_here, 0)
    low_block = prefix_below(pair * halfway, ends, request_lengths) // halfway
    pieces = 4
    candidates = jnp.arange(2 * cycle_size, dtype=jnp.int32)
    in_range = (candidates[None, :] >= low_block[:, None]) & (candidates[None, :] <= pair[:, None])
    pass_max = (2 * cycle_size + pieces - 1) // pieces
    slots_all = jnp.arange(pass_max * pieces, dtype=jnp.int32)
    plans = []
    for parity in range(2):
        chosen = in_range & ((holders % 2) == parity)[None, :]
        rank = jnp.cumsum(chosen.astype(jnp.int32), axis=1) - 1
        count = jnp.sum(chosen.astype(jnp.int32), axis=1)
        picked = chosen[:, None, :] & (rank[:, None, :] == slots_all[None, :, None])
        listed = jnp.sum(jnp.where(picked, candidates, 0), axis=-1)
        listed = jnp.where(slots_all[None, :] >= count[:, None], 2 * cycle_size, listed)
        rows = jnp.sum(jnp.where(picked, (holders // 2) * halfway, 0), axis=-1)
        plans.append(
            (
                ((count + pieces - 1) // pieces).astype(jnp.int32),
                rows.reshape(-1).astype(jnp.int32),
                (listed * halfway).reshape(-1).astype(jnp.int32),
            )
        )
    places_here = (pair[:, None] * halfway + jnp.arange(halfway, dtype=jnp.int32)[None, :])
    self_queries = mine[:, :, :head_width].reshape(halves_here, halfway, head_width)
    self_low = prefix_below(places_here, ends, request_lengths).reshape(halves_here, halfway, 1)
    self_high = places_here.reshape(halves_here, halfway, 1)
    blank = (
        jnp.zeros((halves_here, halfway, 1), jnp.float32),
        jnp.zeros((halves_here, halfway, 1), jnp.float32),
        jnp.zeros((halves_here, halfway, head_width), jnp.float32),
    )
    state = single(
        self_queries, self_low, self_high, blank, even, *plans[0], pass_max, pieces, True, False
    )
    single_out = single(
        self_queries, self_low, self_high, state, odd, *plans[1], pass_max, pieces, False, True
    )
    returned = lax.all_to_all(
        single_out.reshape(ring_size, block_rows, head_width), "x", 0, 0, tiled=True
    )
    attended = returned.transpose(1, 0, 2).reshape(block_rows, group_width)
    group_blocks = lax.axis_index("zy") * ring_size + jnp.arange(ring_size, dtype=jnp.int32)
    cache_rows = lookup(
        holders, jnp.stack([2 * group_blocks, 2 * group_blocks + 1], axis=1)
    )
    def cache_piece(holder):
        start = (holder // 2) * halfway
        return jnp.where(
            holder % 2 == 0,
            lax.dynamic_slice_in_dim(even, start, halfway, 0),
            lax.dynamic_slice_in_dim(odd, start, halfway, 0),
        )

    cache_parts = jnp.stack(
        [
            jnp.concatenate([cache_piece(cache_rows[i, 0]), cache_piece(cache_rows[i, 1])], axis=0)
            for i in range(ring_size)
        ]
    )
    cache_heads = lax.all_to_all(cache_parts, "x", 0, 0, tiled=True)
    cache = cache_heads.reshape(group_heads, block_rows, 2, head_width).transpose(2, 1, 0, 3)
    cache = cache.reshape(2, block_rows, group_width)
    mixed = lax.psum_scatter(
        jnp.dot(attended, w_out, preferred_element_type=jnp.float32),
        "head",
        scatter_dimension=0,
        tiled=True,
    )
    hidden = normalize(mixed + tokens.astype(jnp.float32))
    hidden_b = hidden.astype(jnp.bfloat16)
    block_hidden = lax.all_gather(hidden_b, "head", axis=0, tiled=True)
    w_cq_group = lax.dynamic_slice_in_dim(w_cq, member * group_width, group_width, 1)
    cross_query = jnp.dot(
        block_hidden, w_cq_group, preferred_element_type=jnp.float32
    ).astype(jnp.bfloat16)
    encoder_rows = encoder.shape[1]
    cross_max = (encoder_rows + halfway - 1 + 2 * halfway - 1) // (2 * halfway)
    padded_encoder = jnp.pad(
        encoder, ((0, 0), (0, cross_max * 2 * halfway + halfway - encoder_rows), (0, 0))
    )
    enc_low = prefix_below(query_places, ends, enc_lengths)
    enc_high = prefix_below(query_places, starts, enc_lengths) - 1
    cross_base = (enc_low.reshape(2, halfway)[:, 0] // halfway) * halfway
    cross_steps = (enc_high.reshape(2, halfway)[:, -1] + 1 - cross_base + 2 * halfway - 1) // (
        2 * halfway
    )
    cross_firsts = jnp.minimum(
        cross_base[:, None] + 2 * halfway * jnp.arange(cross_max, dtype=jnp.int32)[None, :],
        padded_encoder.shape[1] - 2 * halfway,
    )
    cross_sources = jnp.stack([cross_firsts, cross_firsts + halfway], axis=-1)
    crossed_group = flash(
        cross_query.reshape(2, halfway, group_width),
        enc_low.reshape(2, halfway, 1),
        enc_high.reshape(2, halfway, 1),
        padded_encoder[0],
        padded_encoder[1],
        cross_steps.astype(jnp.int32),
        cross_sources.reshape(-1).astype(jnp.int32),
        cross_firsts.reshape(-1).astype(jnp.int32),
        cross_max,
        group_heads,
    ).reshape(block_rows, group_width)
    exchanged = lax.all_to_all(
        crossed_group.reshape(group_size, rows_here, group_width), "head", 0, 0, tiled=True
    )
    crossed = exchanged.transpose(1, 0, 2).reshape(rows_here, model_width)
    summed = jnp.dot(crossed, w_co, preferred_element_type=jnp.float32)
    second = normalize(summed + hidden)
    second_b = second.astype(jnp.bfloat16)
    inner = jax.nn.gelu(
        jnp.dot(second_b, w_up, preferred_element_type=jnp.float32), approximate=False
    ).astype(jnp.bfloat16)
    output = normalize(jnp.dot(inner, w_down, preferred_element_type=jnp.float32) + second)
    output_b = output.astype(jnp.bfloat16)
    block_output = lax.all_gather(output_b, "head", axis=0, tiled=True)
    next_qkv = jnp.einsum("td,cde->cte", block_output, w_next, preferred_element_type=jnp.float32)
    return (output, cache, next_qkv)


def solution(mesh):
    ring = 4
    devices = mesh.devices.reshape(mesh.shape["blk"] // ring, ring, mesh.shape["head"])
    fine = jax.sharding.Mesh(devices, ("zy", "x", "head"))
    rows = ("zy", "x", "head")
    blocks = ("zy", "x")
    in_specs = (
        P(rows, None),
        P(),
        P(),
        P(),
        P(None, None, "head"),
        P("head", None),
        P(None, blocks, "head"),
        P(),
        P(),
        P(),
        P(),
        P(None, None, "head"),
    )
    out_specs = (P(rows, None), P(None, blocks, "head"), P(None, blocks, "head"))
    return jax.shard_map(
        on_device, mesh=fine, in_specs=in_specs, out_specs=out_specs, check_vma=False
    )
```

```python
import functools
import math

import jax
import jax.numpy as jnp
from jax import lax
from jax.experimental import pallas as pl
from jax.experimental.pallas import tpu as pltpu
from jax.sharding import PartitionSpec as P

HEADS = 16


NEGATIVE = -1e30
SCALING = 0.125
EPSILON = 1e-05


def normalize(matrix):
    center = matrix - jnp.mean(matrix, axis=-1, keepdims=True)
    return center * lax.rsqrt(jnp.mean(center * center, axis=-1, keepdims=True) + EPSILON)


def position_of(order_table, indices, halfway):
    slots = jnp.arange(order_table.shape[0], dtype=jnp.int32)
    picked = jnp.sum(
        jnp.where((indices // halfway)[:, None] == slots[None, :], order_table[None, :], 0), axis=1
    )
    return picked * halfway + indices % halfway


def group_of(places, lengths):
    ends = jnp.cumsum(lengths)
    return jnp.sum((places[:, None] >= ends[None, :]).astype(jnp.int32), axis=1)


def prefix_below(places, bounds, amounts):
    return jnp.sum(
        jnp.where(places[..., None] >= bounds, amounts, 0), axis=-1
    ).astype(jnp.int32)


def lookup(table, indices):
    slots = jnp.arange(table.shape[0], dtype=jnp.int32)
    return jnp.sum(jnp.where(indices[..., None] == slots, table, 0), axis=-1).astype(jnp.int32)


def online_update(carried, queries, key_rows, value_rows, visible):
    maxima, totals, running = carried
    heads_here = queries.shape[1]
    key_split = key_rows.reshape(key_rows.shape[0], heads_here, -1)
    value_split = value_rows.reshape(value_rows.shape[0], heads_here, -1)
    scores = (
        jnp.einsum("qhd,khd->qhk", queries, key_split, preferred_element_type=jnp.float32) * SCALING
    )
    scores = jnp.where(visible[:, None, :], scores, NEGATIVE)
    updated = jnp.maximum(maxima, jnp.max(scores, axis=2))
    factor = jnp.exp(maxima - updated)
    weights = jnp.exp(scores - updated[:, :, None])
    totals = totals * factor + jnp.sum(weights, axis=2)
    running = running * factor[:, :, None] + jnp.einsum(
        "qhk,khd->qhd",
        weights.astype(jnp.bfloat16),
        value_split,
        preferred_element_type=jnp.float32,
    )
    return (updated, totals, running)


def sweep(
    carried, queries, key_rows, value_rows, key_places, key_groups, query_places, query_groups
):
    length = key_rows.shape[0]
    block_size = math.gcd(length, 2048)
    blocks_count = length // block_size
    key_blocks = key_rows.reshape(blocks_count, block_size, key_rows.shape[1])
    value_blocks = value_rows.reshape(blocks_count, block_size, value_rows.shape[1])
    group_blocks = key_groups.reshape(blocks_count, block_size)
    if key_places is None:
        place_blocks = group_blocks
    else:
        place_blocks = key_places.reshape(blocks_count, block_size)

    def advance(status, element):
        key_block, value_block, place_block, group_block = element
        visible = group_block[None, :] == query_groups[:, None]
        if key_places is None:
            return (online_update(status, queries, key_block, value_block, visible), None)
        visible = visible & (place_block[None, :] <= query_places[:, None])
        updated = online_update(status, queries, key_block, value_block, visible)
        return (updated, None)

    carried, unused = lax.scan(
        advance, carried, (key_blocks, value_blocks, place_blocks, group_blocks)
    )
    return carried


def empty_state(count_q, heads_here, head_width):
    return (
        jnp.full((count_q, heads_here), NEGATIVE, jnp.float32),
        jnp.zeros((count_q, heads_here), jnp.float32),
        jnp.zeros((count_q, heads_here, head_width), jnp.float32),
    )


def finish(carried):
    maxima, totals, running = carried
    return (running / totals[:, :, None]).reshape(running.shape[0], -1).astype(jnp.bfloat16)


def flash_kernel(
    steps_ref, sources_ref, bases_ref, q_ref, low_ref, high_ref, k_hbm, v_hbm, o_ref,
    kbuf, vbuf, sem, qm_sc, m_sc, l_sc, acc_sc, *, max_steps, heads, head_width
):
    half = pl.program_id(0)
    count = steps_ref[half]
    tile = kbuf.shape[1] // 2
    width = kbuf.shape[2]

    def copies(step, slot):
        result = []
        for j in range(2):
            source = pl.multiple_of(sources_ref[(half * max_steps + step) * 2 + j], tile)
            window = pl.ds(j * tile, tile)
            result.append(pltpu.make_async_copy(
                k_hbm.at[pl.ds(source, tile)], kbuf.at[slot, window], sem.at[0, slot, j]))
            result.append(pltpu.make_async_copy(
                v_hbm.at[pl.ds(source, tile)], vbuf.at[slot, window], sem.at[1, slot, j]))
        return result

    for copy in copies(0, 0):
        copy.start()
    column_head = lax.broadcasted_iota(jnp.int32, (1, width), 1) // head_width
    q = q_ref[0]
    for h in range(heads):
        qm_sc[h] = jnp.where(column_head == h, q, jnp.zeros_like(q))
    m_sc[...] = jnp.full(m_sc.shape, NEGATIVE, jnp.float32)
    l_sc[...] = jnp.zeros(l_sc.shape, jnp.float32)
    acc_sc[...] = jnp.zeros(acc_sc.shape, jnp.float32)
    low = low_ref[0]
    high = high_ref[0]

    def body(step, carry):
        slot = step % 2
        for copy in copies(step, slot):
            copy.wait()

        @pl.when(step + 1 < count)
        def _():
            for copy in copies(step + 1, 1 - slot):
                copy.start()

        base = bases_ref[half * max_steps + step]
        places = base + lax.broadcasted_iota(jnp.int32, (1, 2 * tile), 1)
        visible = (places >= low) & (places <= high)
        keys = kbuf[slot]
        values = vbuf[slot]
        for h in range(heads):
            scores = lax.dot_general(
                qm_sc[h], keys, (((1,), (1,)), ((), ())), preferred_element_type=jnp.float32
            ) * SCALING
            scores = jnp.where(visible, scores, NEGATIVE)
            previous = m_sc[h]
            updated = jnp.maximum(previous, jnp.max(scores, axis=1, keepdims=True))
            factor = jnp.exp(previous - updated)
            weights = jnp.exp(scores - updated)
            l_sc[h] = l_sc[h] * factor + jnp.sum(weights, axis=1, keepdims=True)
            acc_sc[h] = acc_sc[h] * factor + jnp.dot(
                weights.astype(jnp.bfloat16), values, preferred_element_type=jnp.float32
            )
            m_sc[h] = updated
        return carry

    lax.fori_loop(0, count, body, 0)
    out = jnp.zeros(acc_sc.shape[1:], jnp.float32)
    for h in range(heads):
        out = jnp.where(column_head == h, acc_sc[h] / l_sc[h], out)
    o_ref[0] = out.astype(o_ref.dtype)


def flash(queries, low, high, keys, values, steps, sources, bases, max_steps, heads):
    halves, tile, width = queries.shape
    head_width = width // heads
    kernel = functools.partial(
        flash_kernel, max_steps=max_steps, heads=heads, head_width=head_width
    )
    row_spec = pl.BlockSpec((1, tile, width), lambda h, *refs: (h, 0, 0))
    bound_spec = pl.BlockSpec((1, tile, 1), lambda h, *refs: (h, 0, 0))
    flops = 4 * halves * max_steps * tile * 2 * tile * width * heads
    return pl.pallas_call(
        kernel,
        out_shape=jax.ShapeDtypeStruct(queries.shape, jnp.bfloat16),
        grid_spec=pltpu.PrefetchScalarGridSpec(
            num_scalar_prefetch=3,
            grid=(halves,),
            in_specs=[
                row_spec,
                bound_spec,
                bound_spec,
                pl.BlockSpec(memory_space=pl.ANY),
                pl.BlockSpec(memory_space=pl.ANY),
            ],
            out_specs=row_spec,
            scratch_shapes=[
                pltpu.VMEM((2, 2 * tile, width), keys.dtype),
                pltpu.VMEM((2, 2 * tile, width), values.dtype),
                pltpu.SemaphoreType.DMA((2, 2, 2)),
                pltpu.VMEM((heads, tile, width), jnp.bfloat16),
                pltpu.VMEM((heads, tile, 1), jnp.float32),
                pltpu.VMEM((heads, tile, 1), jnp.float32),
                pltpu.VMEM((heads, tile, width), jnp.float32),
            ],
        ),
        compiler_params=pltpu.CompilerParams(dimension_semantics=("arbitrary",)),
        cost_estimate=pl.CostEstimate(
            flops=flops,
            transcendentals=halves * max_steps * tile * 2 * tile * heads,
            bytes_accessed=halves * max_steps * 2 * 2 * tile * width * 2,
        ),
    )(steps, sources, bases, queries, low, high, keys, values)


def single_kernel(
    steps_ref, sources_ref, bases_ref, limits_ref, q_ref, low_ref, high_ref, kv_hbm, o_ref,
    buf, sem, m_sc, l_sc, acc_sc, *, max_steps, head_width, pieces
):
    half = pl.program_id(0)
    count = steps_ref[half]
    tile = buf.shape[1] // pieces

    def copies(step, slot):
        result = []
        for j in range(pieces):
            source = pl.multiple_of(sources_ref[(half * max_steps + step) * pieces + j], tile)
            result.append(pltpu.make_async_copy(
                kv_hbm.at[pl.ds(source, tile)], buf.at[slot, pl.ds(j * tile, tile)], sem.at[slot, j]))
        return result

    for copy in copies(0, 0):
        copy.start()
    m_sc[...] = jnp.full(m_sc.shape, NEGATIVE, jnp.float32)
    l_sc[...] = jnp.zeros(l_sc.shape, jnp.float32)
    acc_sc[...] = jnp.zeros(acc_sc.shape, jnp.float32)
    q = q_ref[0]
    low = low_ref[0]
    high = high_ref[0]

    def body(step, carry):
        slot = step % 2
        for copy in copies(step, slot):
            copy.wait()

        @pl.when(step + 1 < count)
        def _():
            for copy in copies(step + 1, 1 - slot):
                copy.start()

        base = bases_ref[half * max_steps + step]
        keys = buf[slot, :, :head_width]
        values = buf[slot, :, head_width:]

        def update(masked):
            scores = lax.dot_general(
                q, keys, (((1,), (1,)), ((), ())), preferred_element_type=jnp.float32
            ) * SCALING
            if masked:
                places = base + lax.broadcasted_iota(jnp.int32, (1, pieces * tile), 1)
                visible = (places >= low) & (places <= high)
                scores = jnp.where(visible, scores, NEGATIVE)
            previous = m_sc[...]
            updated = jnp.maximum(previous, jnp.max(scores, axis=1, keepdims=True))
            factor = jnp.exp(previous - updated)
            weights = jnp.exp(scores - updated)
            l_sc[...] = l_sc[...] * factor + jnp.sum(weights, axis=1, keepdims=True)
            acc_sc[...] = acc_sc[...] * factor + jnp.dot(
                weights.astype(jnp.bfloat16), values, preferred_element_type=jnp.float32
            )
            m_sc[...] = updated

        full = (base >= limits_ref[2 * half]) & (base + pieces * tile - 1 <= limits_ref[2 * half + 1])

        @pl.when(full)
        def _():
            update(False)

        @pl.when(jnp.logical_not(full))
        def _():
            update(True)

        return carry

    lax.fori_loop(0, count, body, 0)
    o_ref[0] = (acc_sc[...] / l_sc[...]).astype(o_ref.dtype)


def single(queries, low, high, packed, steps, sources, bases, limits, max_steps, pieces):
    halves, tile, head_width = queries.shape
    kernel = functools.partial(
        single_kernel, max_steps=max_steps, head_width=head_width, pieces=pieces
    )
    row_spec = pl.BlockSpec((1, tile, head_width), lambda h, *refs: (h, 0, 0))
    bound_spec = pl.BlockSpec((1, tile, 1), lambda h, *refs: (h, 0, 0))
    return pl.pallas_call(
        kernel,
        out_shape=jax.ShapeDtypeStruct(queries.shape, jnp.bfloat16),
        grid_spec=pltpu.PrefetchScalarGridSpec(
            num_scalar_prefetch=4,
            grid=(halves,),
            in_specs=[row_spec, bound_spec, bound_spec, pl.BlockSpec(memory_space=pl.ANY)],
            out_specs=row_spec,
            scratch_shapes=[
                pltpu.VMEM((2, pieces * tile, packed.shape[1]), packed.dtype),
                pltpu.SemaphoreType.DMA((2, pieces)),
                pltpu.VMEM((tile, 1), jnp.float32),
                pltpu.VMEM((tile, 1), jnp.float32),
                pltpu.VMEM((tile, head_width), jnp.float32),
            ],
        ),
        compiler_params=pltpu.CompilerParams(dimension_semantics=("arbitrary",)),
        cost_estimate=pl.CostEstimate(
            flops=2 * halves * (max_steps // 2) * tile * pieces * tile * head_width * 2,
            transcendentals=halves * (max_steps // 2) * tile * pieces * tile,
            bytes_accessed=halves * (max_steps // 2) * pieces * tile * packed.shape[1] * 2,
        ),
    )(steps, sources, bases, limits, queries, low, high, packed)


def on_device(
    tokens,
    block_order,
    request_lengths,
    enc_lengths,
    w_qkv,
    w_out,
    enc_kv,
    w_cq,
    w_co,
    w_up,
    w_down,
    w_next,
):
    rows_here = tokens.shape[0]
    model_width = tokens.shape[1]
    group_size = lax.axis_size("head")
    cycle_size = lax.axis_size("zy") * lax.axis_size("x")
    block_rows = rows_here * group_size
    halfway = block_rows // 2
    group_width = w_qkv.shape[2]
    head_width = model_width // HEADS
    group_heads = group_width // head_width
    member = lax.axis_index("head")
    ring_size = lax.axis_size("x")
    ring_index = lax.axis_index("x")
    cycle_index = lax.axis_index("zy") * ring_size + ring_index
    encoder = lax.all_gather(enc_kv, ("zy", "x"), axis=1, tiled=True)
    gathered = lax.all_gather(tokens, "head", axis=0, tiled=True)
    projected = jnp.einsum(
        "td,cde->cte", gathered, w_qkv, preferred_element_type=jnp.float32
    ).astype(jnp.bfloat16)
    block_start = cycle_index * block_rows
    query_places = position_of(
        block_order, block_start + jnp.arange(block_rows, dtype=jnp.int32), halfway
    )
    slots = jnp.arange(2 * cycle_size, dtype=jnp.int32)
    holders = jnp.sum(jnp.where(block_order[:, None] == slots[None, :], slots[:, None], 0), axis=0)
    per_head = projected.reshape(3, block_rows, group_heads, head_width).transpose(2, 1, 0, 3)
    per_head = per_head.reshape(group_heads, block_rows, 3 * head_width)
    mine = lax.all_to_all(per_head, "x", 0, 0, tiled=True)
    packed = lax.all_gather(mine[:, :, head_width:], "zy", axis=0, tiled=True)
    packed = packed.reshape(cycle_size * block_rows, 2 * head_width)
    ends = jnp.cumsum(request_lengths).astype(jnp.int32)
    starts = ends - request_lengths
    halves_here = 2 * ring_size
    first_half = lax.axis_index("zy") * halves_here
    pair = lax.dynamic_slice_in_dim(block_order, first_half, halves_here, 0)
    low_block = prefix_below(pair * halfway, ends, request_lengths) // halfway
    pieces = 4
    self_steps = (pair - low_block) // pieces + 1
    self_max = (2 * cycle_size + pieces - 1) // pieces
    firsts = low_block[:, None] + pieces * jnp.arange(self_max, dtype=jnp.int32)[None, :]
    self_sources = lookup(
        holders,
        jnp.minimum(firsts[:, :, None] + jnp.arange(pieces, dtype=jnp.int32), 2 * cycle_size - 1),
    ) * halfway
    places_here = (pair[:, None] * halfway + jnp.arange(halfway, dtype=jnp.int32)[None, :])
    self_low = prefix_below(places_here, ends, request_lengths).reshape(halves_here, halfway)
    limits = jnp.stack([self_low[:, -1], places_here[:, 0]], axis=1).reshape(-1)
    single_out = single(
        mine[:, :, :head_width].reshape(halves_here, halfway, head_width),
        self_low.reshape(halves_here, halfway, 1),
        places_here.reshape(halves_here, halfway, 1),
        packed,
        self_steps.astype(jnp.int32),
        self_sources.reshape(-1).astype(jnp.int32),
        (firsts * halfway).reshape(-1).astype(jnp.int32),
        limits.astype(jnp.int32),
        self_max,
        pieces,
    )
    returned = lax.all_to_all(
        single_out.reshape(ring_size, block_rows, head_width), "x", 0, 0, tiled=True
    )
    attended = returned.transpose(1, 0, 2).reshape(block_rows, group_width)
    group_blocks = lax.axis_index("zy") * ring_size + jnp.arange(ring_size, dtype=jnp.int32)
    cache_rows = lookup(
        holders, jnp.stack([2 * group_blocks, 2 * group_blocks + 1], axis=1)
    )
    cache_parts = jnp.stack(
        [
            jnp.concatenate(
                [
                    lax.dynamic_slice_in_dim(packed, cache_rows[i, 0] * halfway, halfway, 0),
                    lax.dynamic_slice_in_dim(packed, cache_rows[i, 1] * halfway, halfway, 0),
                ],
                axis=0,
            )
            for i in range(ring_size)
        ]
    )
    cache_heads = lax.all_to_all(cache_parts, "x", 0, 0, tiled=True)
    cache = cache_heads.reshape(group_heads, block_rows, 2, head_width).transpose(2, 1, 0, 3)
    cache = cache.reshape(2, block_rows, group_width)
    mixed = lax.psum_scatter(
        jnp.dot(attended, w_out, preferred_element_type=jnp.float32),
        "head",
        scatter_dimension=0,
        tiled=True,
    )
    hidden = normalize(mixed + tokens.astype(jnp.float32))
    hidden_b = hidden.astype(jnp.bfloat16)
    block_hidden = lax.all_gather(hidden_b, "head", axis=0, tiled=True)
    w_cq_group = lax.dynamic_slice_in_dim(w_cq, member * group_width, group_width, 1)
    cross_query = jnp.dot(
        block_hidden, w_cq_group, preferred_element_type=jnp.float32
    ).astype(jnp.bfloat16)
    encoder_rows = encoder.shape[1]
    cross_max = (encoder_rows + halfway - 1 + 2 * halfway - 1) // (2 * halfway)
    padded_encoder = jnp.pad(
        encoder, ((0, 0), (0, cross_max * 2 * halfway + halfway - encoder_rows), (0, 0))
    )
    enc_low = prefix_below(query_places, ends, enc_lengths)
    enc_high = prefix_below(query_places, starts, enc_lengths) - 1
    cross_base = (enc_low.reshape(2, halfway)[:, 0] // halfway) * halfway
    cross_steps = (enc_high.reshape(2, halfway)[:, -1] + 1 - cross_base + 2 * halfway - 1) // (
        2 * halfway
    )
    cross_firsts = jnp.minimum(
        cross_base[:, None] + 2 * halfway * jnp.arange(cross_max, dtype=jnp.int32)[None, :],
        padded_encoder.shape[1] - 2 * halfway,
    )
    cross_sources = jnp.stack([cross_firsts, cross_firsts + halfway], axis=-1)
    crossed_group = flash(
        cross_query.reshape(2, halfway, group_width),
        enc_low.reshape(2, halfway, 1),
        enc_high.reshape(2, halfway, 1),
        padded_encoder[0],
        padded_encoder[1],
        cross_steps.astype(jnp.int32),
        cross_sources.reshape(-1).astype(jnp.int32),
        cross_firsts.reshape(-1).astype(jnp.int32),
        cross_max,
        group_heads,
    ).reshape(block_rows, group_width)
    exchanged = lax.all_to_all(
        crossed_group.reshape(group_size, rows_here, group_width), "head", 0, 0, tiled=True
    )
    crossed = exchanged.transpose(1, 0, 2).reshape(rows_here, model_width)
    summed = jnp.dot(crossed, w_co, preferred_element_type=jnp.float32)
    second = normalize(summed + hidden)
    second_b = second.astype(jnp.bfloat16)
    inner = jax.nn.gelu(
        jnp.dot(second_b, w_up, preferred_element_type=jnp.float32), approximate=False
    ).astype(jnp.bfloat16)
    output = normalize(jnp.dot(inner, w_down, preferred_element_type=jnp.float32) + second)
    output_b = output.astype(jnp.bfloat16)
    block_output = lax.all_gather(output_b, "head", axis=0, tiled=True)
    next_qkv = jnp.einsum("td,cde->cte", block_output, w_next, preferred_element_type=jnp.float32)
    return (output, cache, next_qkv)


def solution(mesh):
    ring = 4
    devices = mesh.devices.reshape(mesh.shape["blk"] // ring, ring, mesh.shape["head"])
    fine = jax.sharding.Mesh(devices, ("zy", "x", "head"))
    rows = ("zy", "x", "head")
    blocks = ("zy", "x")
    in_specs = (
        P(rows, None),
        P(),
        P(),
        P(),
        P(None, None, "head"),
        P("head", None),
        P(None, blocks, "head"),
        P(),
        P(),
        P(),
        P(),
        P(None, None, "head"),
    )
    out_specs = (P(rows, None), P(None, blocks, "head"), P(None, blocks, "head"))
    return jax.shard_map(
        on_device, mesh=fine, in_specs=in_specs, out_specs=out_specs, check_vma=False
    )
```

```python
import functools
import math

import jax
import jax.numpy as jnp
from jax import lax
from jax.experimental import pallas as pl
from jax.experimental.pallas import tpu as pltpu
from jax.sharding import PartitionSpec as P

HEADS = 16


NEGATIVE = -1e30
SCALING = 0.125
EPSILON = 1e-05


def normalize(matrix):
    center = matrix - jnp.mean(matrix, axis=-1, keepdims=True)
    return center * lax.rsqrt(jnp.mean(center * center, axis=-1, keepdims=True) + EPSILON)


def position_of(order_table, indices, halfway):
    slots = jnp.arange(order_table.shape[0], dtype=jnp.int32)
    picked = jnp.sum(
        jnp.where((indices // halfway)[:, None] == slots[None, :], order_table[None, :], 0), axis=1
    )
    return picked * halfway + indices % halfway


def group_of(places, lengths):
    ends = jnp.cumsum(lengths)
    return jnp.sum((places[:, None] >= ends[None, :]).astype(jnp.int32), axis=1)


def prefix_below(places, bounds, amounts):
    return jnp.sum(
        jnp.where(places[..., None] >= bounds, amounts, 0), axis=-1
    ).astype(jnp.int32)


def lookup(table, indices):
    slots = jnp.arange(table.shape[0], dtype=jnp.int32)
    return jnp.sum(jnp.where(indices[..., None] == slots, table, 0), axis=-1).astype(jnp.int32)


def online_update(carried, queries, key_rows, value_rows, visible):
    maxima, totals, running = carried
    heads_here = queries.shape[1]
    key_split = key_rows.reshape(key_rows.shape[0], heads_here, -1)
    value_split = value_rows.reshape(value_rows.shape[0], heads_here, -1)
    scores = (
        jnp.einsum("qhd,khd->qhk", queries, key_split, preferred_element_type=jnp.float32) * SCALING
    )
    scores = jnp.where(visible[:, None, :], scores, NEGATIVE)
    updated = jnp.maximum(maxima, jnp.max(scores, axis=2))
    factor = jnp.exp(maxima - updated)
    weights = jnp.exp(scores - updated[:, :, None])
    totals = totals * factor + jnp.sum(weights, axis=2)
    running = running * factor[:, :, None] + jnp.einsum(
        "qhk,khd->qhd",
        weights.astype(jnp.bfloat16),
        value_split,
        preferred_element_type=jnp.float32,
    )
    return (updated, totals, running)


def sweep(
    carried, queries, key_rows, value_rows, key_places, key_groups, query_places, query_groups
):
    length = key_rows.shape[0]
    block_size = math.gcd(length, 2048)
    blocks_count = length // block_size
    key_blocks = key_rows.reshape(blocks_count, block_size, key_rows.shape[1])
    value_blocks = value_rows.reshape(blocks_count, block_size, value_rows.shape[1])
    group_blocks = key_groups.reshape(blocks_count, block_size)
    if key_places is None:
        place_blocks = group_blocks
    else:
        place_blocks = key_places.reshape(blocks_count, block_size)

    def advance(status, element):
        key_block, value_block, place_block, group_block = element
        visible = group_block[None, :] == query_groups[:, None]
        if key_places is None:
            return (online_update(status, queries, key_block, value_block, visible), None)
        visible = visible & (place_block[None, :] <= query_places[:, None])
        updated = online_update(status, queries, key_block, value_block, visible)
        return (updated, None)

    carried, unused = lax.scan(
        advance, carried, (key_blocks, value_blocks, place_blocks, group_blocks)
    )
    return carried


def empty_state(count_q, heads_here, head_width):
    return (
        jnp.full((count_q, heads_here), NEGATIVE, jnp.float32),
        jnp.zeros((count_q, heads_here), jnp.float32),
        jnp.zeros((count_q, heads_here, head_width), jnp.float32),
    )


def finish(carried):
    maxima, totals, running = carried
    return (running / totals[:, :, None]).reshape(running.shape[0], -1).astype(jnp.bfloat16)


def flash_kernel(
    steps_ref, sources_ref, bases_ref, q_ref, low_ref, high_ref, k_hbm, v_hbm, o_ref,
    kbuf, vbuf, sem, qm_sc, m_sc, l_sc, acc_sc, *, max_steps, heads, head_width
):
    half = pl.program_id(0)
    count = steps_ref[half]
    tile = kbuf.shape[1] // 2
    width = kbuf.shape[2]

    def copies(step, slot):
        result = []
        for j in range(2):
            source = pl.multiple_of(sources_ref[(half * max_steps + step) * 2 + j], tile)
            window = pl.ds(j * tile, tile)
            result.append(pltpu.make_async_copy(
                k_hbm.at[pl.ds(source, tile)], kbuf.at[slot, window], sem.at[0, slot, j]))
            result.append(pltpu.make_async_copy(
                v_hbm.at[pl.ds(source, tile)], vbuf.at[slot, window], sem.at[1, slot, j]))
        return result

    for copy in copies(0, 0):
        copy.start()
    column_head = lax.broadcasted_iota(jnp.int32, (1, width), 1) // head_width
    q = q_ref[0]
    for h in range(heads):
        qm_sc[h] = jnp.where(column_head == h, q, jnp.zeros_like(q))
    m_sc[...] = jnp.full(m_sc.shape, NEGATIVE, jnp.float32)
    l_sc[...] = jnp.zeros(l_sc.shape, jnp.float32)
    acc_sc[...] = jnp.zeros(acc_sc.shape, jnp.float32)
    low = low_ref[0]
    high = high_ref[0]

    def body(step, carry):
        slot = step % 2
        for copy in copies(step, slot):
            copy.wait()

        @pl.when(step + 1 < count)
        def _():
            for copy in copies(step + 1, 1 - slot):
                copy.start()

        base = bases_ref[half * max_steps + step]
        places = base + lax.broadcasted_iota(jnp.int32, (1, 2 * tile), 1)
        visible = (places >= low) & (places <= high)
        keys = kbuf[slot]
        values = vbuf[slot]
        for h in range(heads):
            scores = lax.dot_general(
                qm_sc[h], keys, (((1,), (1,)), ((), ())), preferred_element_type=jnp.float32
            ) * SCALING
            scores = jnp.where(visible, scores, NEGATIVE)
            previous = m_sc[h]
            updated = jnp.maximum(previous, jnp.max(scores, axis=1, keepdims=True))
            factor = jnp.exp(previous - updated)
            weights = jnp.exp(scores - updated)
            l_sc[h] = l_sc[h] * factor + jnp.sum(weights, axis=1, keepdims=True)
            acc_sc[h] = acc_sc[h] * factor + jnp.dot(
                weights.astype(jnp.bfloat16), values, preferred_element_type=jnp.float32
            )
            m_sc[h] = updated
        return carry

    lax.fori_loop(0, count, body, 0)
    out = jnp.zeros(acc_sc.shape[1:], jnp.float32)
    for h in range(heads):
        out = jnp.where(column_head == h, acc_sc[h] / l_sc[h], out)
    o_ref[0] = out.astype(o_ref.dtype)


def flash(queries, low, high, keys, values, steps, sources, bases, max_steps, heads):
    halves, tile, width = queries.shape
    head_width = width // heads
    kernel = functools.partial(
        flash_kernel, max_steps=max_steps, heads=heads, head_width=head_width
    )
    row_spec = pl.BlockSpec((1, tile, width), lambda h, *refs: (h, 0, 0))
    bound_spec = pl.BlockSpec((1, tile, 1), lambda h, *refs: (h, 0, 0))
    flops = 4 * halves * max_steps * tile * 2 * tile * width * heads
    return pl.pallas_call(
        kernel,
        out_shape=jax.ShapeDtypeStruct(queries.shape, jnp.bfloat16),
        grid_spec=pltpu.PrefetchScalarGridSpec(
            num_scalar_prefetch=3,
            grid=(halves,),
            in_specs=[
                row_spec,
                bound_spec,
                bound_spec,
                pl.BlockSpec(memory_space=pl.ANY),
                pl.BlockSpec(memory_space=pl.ANY),
            ],
            out_specs=row_spec,
            scratch_shapes=[
                pltpu.VMEM((2, 2 * tile, width), keys.dtype),
                pltpu.VMEM((2, 2 * tile, width), values.dtype),
                pltpu.SemaphoreType.DMA((2, 2, 2)),
                pltpu.VMEM((heads, tile, width), jnp.bfloat16),
                pltpu.VMEM((heads, tile, 1), jnp.float32),
                pltpu.VMEM((heads, tile, 1), jnp.float32),
                pltpu.VMEM((heads, tile, width), jnp.float32),
            ],
        ),
        compiler_params=pltpu.CompilerParams(dimension_semantics=("arbitrary",)),
        cost_estimate=pl.CostEstimate(
            flops=flops,
            transcendentals=halves * max_steps * tile * 2 * tile * heads,
            bytes_accessed=halves * max_steps * 2 * 2 * tile * width * 2,
        ),
    )(steps, sources, bases, queries, low, high, keys, values)


def single_kernel(
    steps_ref, sources_ref, bases_ref, limits_ref, q_ref, low_ref, high_ref, kv_hbm, o_ref,
    buf, sem, m_sc, l_sc, acc_sc, *, max_steps, head_width, pieces
):
    half = pl.program_id(0)
    count = steps_ref[half]
    tile = buf.shape[1] // pieces

    def copies(step, slot):
        result = []
        for j in range(pieces):
            source = pl.multiple_of(sources_ref[(half * max_steps + step) * pieces + j], tile)
            result.append(pltpu.make_async_copy(
                kv_hbm.at[pl.ds(source, tile)], buf.at[slot, pl.ds(j * tile, tile)], sem.at[slot, j]))
        return result

    for copy in copies(0, 0):
        copy.start()
    m_sc[...] = jnp.full(m_sc.shape, NEGATIVE, jnp.float32)
    l_sc[...] = jnp.zeros(l_sc.shape, jnp.float32)
    acc_sc[...] = jnp.zeros(acc_sc.shape, jnp.float32)
    q = q_ref[0]
    low = low_ref[0]
    high = high_ref[0]

    def body(step, carry):
        slot = step % 2
        for copy in copies(step, slot):
            copy.wait()

        @pl.when(step + 1 < count)
        def _():
            for copy in copies(step + 1, 1 - slot):
                copy.start()

        base = bases_ref[half * max_steps + step]
        keys = buf[slot, :, :head_width]
        values = buf[slot, :, head_width:]

        def update(masked):
            scores = lax.dot_general(
                q, keys, (((1,), (1,)), ((), ())), preferred_element_type=jnp.float32
            ) * SCALING
            if masked:
                places = base + lax.broadcasted_iota(jnp.int32, (1, pieces * tile), 1)
                visible = (places >= low) & (places <= high)
                scores = jnp.where(visible, scores, NEGATIVE)
            previous = m_sc[...]
            updated = jnp.maximum(previous, jnp.max(scores, axis=1, keepdims=True))
            factor = jnp.exp(previous - updated)
            weights = jnp.exp(scores - updated)
            l_sc[...] = l_sc[...] * factor + jnp.sum(weights, axis=1, keepdims=True)
            acc_sc[...] = acc_sc[...] * factor + jnp.dot(
                weights.astype(jnp.bfloat16), values, preferred_element_type=jnp.float32
            )
            m_sc[...] = updated

        full = (base >= limits_ref[2 * half]) & (base + pieces * tile - 1 <= limits_ref[2 * half + 1])

        @pl.when(full)
        def _():
            update(False)

        @pl.when(jnp.logical_not(full))
        def _():
            update(True)

        return carry

    lax.fori_loop(0, count, body, 0)
    o_ref[0] = (acc_sc[...] / l_sc[...]).astype(o_ref.dtype)


def single(queries, low, high, packed, steps, sources, bases, limits, max_steps, pieces):
    halves, tile, head_width = queries.shape
    kernel = functools.partial(
        single_kernel, max_steps=max_steps, head_width=head_width, pieces=pieces
    )
    row_spec = pl.BlockSpec((1, tile, head_width), lambda h, *refs: (h, 0, 0))
    bound_spec = pl.BlockSpec((1, tile, 1), lambda h, *refs: (h, 0, 0))
    return pl.pallas_call(
        kernel,
        out_shape=jax.ShapeDtypeStruct(queries.shape, jnp.bfloat16),
        grid_spec=pltpu.PrefetchScalarGridSpec(
            num_scalar_prefetch=4,
            grid=(halves,),
            in_specs=[row_spec, bound_spec, bound_spec, pl.BlockSpec(memory_space=pl.ANY)],
            out_specs=row_spec,
            scratch_shapes=[
                pltpu.VMEM((2, pieces * tile, packed.shape[1]), packed.dtype),
                pltpu.SemaphoreType.DMA((2, pieces)),
                pltpu.VMEM((tile, 1), jnp.float32),
                pltpu.VMEM((tile, 1), jnp.float32),
                pltpu.VMEM((tile, head_width), jnp.float32),
            ],
        ),
        compiler_params=pltpu.CompilerParams(dimension_semantics=("arbitrary",)),
        cost_estimate=pl.CostEstimate(
            flops=2 * halves * (max_steps // 2) * tile * pieces * tile * head_width * 2,
            transcendentals=halves * (max_steps // 2) * tile * pieces * tile,
            bytes_accessed=halves * (max_steps // 2) * pieces * tile * packed.shape[1] * 2,
        ),
    )(steps, sources, bases, limits, queries, low, high, packed)


def on_device(
    tokens,
    block_order,
    request_lengths,
    enc_lengths,
    w_qkv,
    w_out,
    enc_kv,
    w_cq,
    w_co,
    w_up,
    w_down,
    w_next,
):
    rows_here = tokens.shape[0]
    model_width = tokens.shape[1]
    group_size = lax.axis_size("head")
    cycle_size = lax.axis_size("zy") * lax.axis_size("x")
    block_rows = rows_here * group_size
    halfway = block_rows // 2
    group_width = w_qkv.shape[2]
    head_width = model_width // HEADS
    group_heads = group_width // head_width
    member = lax.axis_index("head")
    ring_size = lax.axis_size("x")
    ring_index = lax.axis_index("x")
    cycle_index = lax.axis_index("zy") * ring_size + ring_index
    encoder = lax.all_gather(enc_kv, ("zy", "x"), axis=1, tiled=True)
    full_out = lax.all_to_all(
        jnp.broadcast_to(w_out[None], (group_size,) + w_out.shape), "head", 0, 0, tiled=True
    ).reshape(model_width, model_width)
    gathered = lax.all_gather(tokens, "head", axis=0, tiled=True)
    projected = jnp.einsum(
        "td,cde->cte", gathered, w_qkv, preferred_element_type=jnp.float32
    ).astype(jnp.bfloat16)
    block_start = cycle_index * block_rows
    query_places = position_of(
        block_order, block_start + jnp.arange(block_rows, dtype=jnp.int32), halfway
    )
    slots = jnp.arange(2 * cycle_size, dtype=jnp.int32)
    holders = jnp.sum(jnp.where(block_order[:, None] == slots[None, :], slots[:, None], 0), axis=0)
    per_head = projected.reshape(3, block_rows, group_heads, head_width).transpose(2, 1, 0, 3)
    per_head = per_head.reshape(group_heads, block_rows, 3 * head_width)
    mine = lax.all_to_all(per_head, "x", 0, 0, tiled=True)
    packed = lax.all_gather(mine[:, :, head_width:], "zy", axis=0, tiled=True)
    packed = packed.reshape(cycle_size * block_rows, 2 * head_width)
    ends = jnp.cumsum(request_lengths).astype(jnp.int32)
    starts = ends - request_lengths
    halves_here = 2 * ring_size
    first_half = lax.axis_index("zy") * halves_here
    pair = lax.dynamic_slice_in_dim(block_order, first_half, halves_here, 0)
    low_block = prefix_below(pair * halfway, ends, request_lengths) // halfway
    pieces = 4
    self_steps = (pair - low_block) // pieces + 1
    self_max = (2 * cycle_size + pieces - 1) // pieces
    firsts = low_block[:, None] + pieces * jnp.arange(self_max, dtype=jnp.int32)[None, :]
    self_sources = lookup(
        holders,
        jnp.minimum(firsts[:, :, None] + jnp.arange(pieces, dtype=jnp.int32), 2 * cycle_size - 1),
    ) * halfway
    places_here = (pair[:, None] * halfway + jnp.arange(halfway, dtype=jnp.int32)[None, :])
    self_low = prefix_below(places_here, ends, request_lengths).reshape(halves_here, halfway)
    limits = jnp.stack([self_low[:, -1], places_here[:, 0]], axis=1).reshape(-1)
    single_out = single(
        mine[:, :, :head_width].reshape(halves_here, halfway, head_width),
        self_low.reshape(halves_here, halfway, 1),
        places_here.reshape(halves_here, halfway, 1),
        packed,
        self_steps.astype(jnp.int32),
        self_sources.reshape(-1).astype(jnp.int32),
        (firsts * halfway).reshape(-1).astype(jnp.int32),
        limits.astype(jnp.int32),
        self_max,
        pieces,
    )
    owners = lax.all_to_all(
        single_out.reshape(ring_size * group_size, rows_here, head_width),
        ("x", "head"),
        0,
        0,
        tiled=True,
    )
    attended_rows = owners.reshape(ring_size, group_size, rows_here, head_width)
    attended_rows = attended_rows.transpose(2, 1, 0, 3).reshape(rows_here, model_width)
    group_blocks = lax.axis_index("zy") * ring_size + jnp.arange(ring_size, dtype=jnp.int32)
    cache_rows = lookup(
        holders, jnp.stack([2 * group_blocks, 2 * group_blocks + 1], axis=1)
    )
    cache_parts = jnp.stack(
        [
            jnp.concatenate(
                [
                    lax.dynamic_slice_in_dim(packed, cache_rows[i, 0] * halfway, halfway, 0),
                    lax.dynamic_slice_in_dim(packed, cache_rows[i, 1] * halfway, halfway, 0),
                ],
                axis=0,
            )
            for i in range(ring_size)
        ]
    )
    cache_heads = lax.all_to_all(cache_parts, "x", 0, 0, tiled=True)
    cache = cache_heads.reshape(group_heads, block_rows, 2, head_width).transpose(2, 1, 0, 3)
    cache = cache.reshape(2, block_rows, group_width)
    mixed = jnp.dot(attended_rows, full_out, preferred_element_type=jnp.float32)
    hidden = normalize(mixed + tokens.astype(jnp.float32))
    hidden_b = hidden.astype(jnp.bfloat16)
    block_hidden = lax.all_gather(hidden_b, "head", axis=0, tiled=True)
    w_cq_group = lax.dynamic_slice_in_dim(w_cq, member * group_width, group_width, 1)
    cross_query = jnp.dot(
        block_hidden, w_cq_group, preferred_element_type=jnp.float32
    ).astype(jnp.bfloat16)
    encoder_rows = encoder.shape[1]
    cross_max = (encoder_rows + halfway - 1 + 2 * halfway - 1) // (2 * halfway)
    padded_encoder = jnp.pad(
        encoder, ((0, 0), (0, cross_max * 2 * halfway + halfway - encoder_rows), (0, 0))
    )
    enc_low = prefix_below(query_places, ends, enc_lengths)
    enc_high = prefix_below(query_places, starts, enc_lengths) - 1
    cross_base = (enc_low.reshape(2, halfway)[:, 0] // halfway) * halfway
    cross_steps = (enc_high.reshape(2, halfway)[:, -1] + 1 - cross_base + 2 * halfway - 1) // (
        2 * halfway
    )
    cross_firsts = jnp.minimum(
        cross_base[:, None] + 2 * halfway * jnp.arange(cross_max, dtype=jnp.int32)[None, :],
        padded_encoder.shape[1] - 2 * halfway,
    )
    cross_sources = jnp.stack([cross_firsts, cross_firsts + halfway], axis=-1)
    crossed_group = flash(
        cross_query.reshape(2, halfway, group_width),
        enc_low.reshape(2, halfway, 1),
        enc_high.reshape(2, halfway, 1),
        padded_encoder[0],
        padded_encoder[1],
        cross_steps.astype(jnp.int32),
        cross_sources.reshape(-1).astype(jnp.int32),
        cross_firsts.reshape(-1).astype(jnp.int32),
        cross_max,
        group_heads,
    ).reshape(block_rows, group_width)
    exchanged = lax.all_to_all(
        crossed_group.reshape(group_size, rows_here, group_width), "head", 0, 0, tiled=True
    )
    crossed = exchanged.transpose(1, 0, 2).reshape(rows_here, model_width)
    summed = jnp.dot(crossed, w_co, preferred_element_type=jnp.float32)
    second = normalize(summed + hidden)
    second_b = second.astype(jnp.bfloat16)
    inner = jax.nn.gelu(
        jnp.dot(second_b, w_up, preferred_element_type=jnp.float32), approximate=False
    ).astype(jnp.bfloat16)
    output = normalize(jnp.dot(inner, w_down, preferred_element_type=jnp.float32) + second)
    output_b = output.astype(jnp.bfloat16)
    block_output = lax.all_gather(output_b, "head", axis=0, tiled=True)
    next_qkv = jnp.einsum("td,cde->cte", block_output, w_next, preferred_element_type=jnp.float32)
    return (output, cache, next_qkv)


def solution(mesh):
    ring = 4
    devices = mesh.devices.reshape(mesh.shape["blk"] // ring, ring, mesh.shape["head"])
    fine = jax.sharding.Mesh(devices, ("zy", "x", "head"))
    rows = ("zy", "x", "head")
    blocks = ("zy", "x")
    in_specs = (
        P(rows, None),
        P(),
        P(),
        P(),
        P(None, None, "head"),
        P("head", None),
        P(None, blocks, "head"),
        P(),
        P(),
        P(),
        P(),
        P(None, None, "head"),
    )
    out_specs = (P(rows, None), P(None, blocks, "head"), P(None, blocks, "head"))
    return jax.shard_map(
        on_device, mesh=fine, in_specs=in_specs, out_specs=out_specs, check_vma=False
    )
```

```python
import functools
import math

import jax
import jax.numpy as jnp
from jax import lax
from jax.experimental import pallas as pl
from jax.experimental.pallas import tpu as pltpu
from jax.sharding import PartitionSpec as P

HEADS = 16


NEGATIVE = -1e30
SCALING = 0.125
EPSILON = 1e-05


def normalize(matrix):
    center = matrix - jnp.mean(matrix, axis=-1, keepdims=True)
    return center * lax.rsqrt(jnp.mean(center * center, axis=-1, keepdims=True) + EPSILON)


def position_of(order_table, indices, halfway):
    slots = jnp.arange(order_table.shape[0], dtype=jnp.int32)
    picked = jnp.sum(
        jnp.where((indices // halfway)[:, None] == slots[None, :], order_table[None, :], 0), axis=1
    )
    return picked * halfway + indices % halfway


def group_of(places, lengths):
    ends = jnp.cumsum(lengths)
    return jnp.sum((places[:, None] >= ends[None, :]).astype(jnp.int32), axis=1)


def prefix_below(places, bounds, amounts):
    return jnp.sum(
        jnp.where(places[..., None] >= bounds, amounts, 0), axis=-1
    ).astype(jnp.int32)


def lookup(table, indices):
    slots = jnp.arange(table.shape[0], dtype=jnp.int32)
    return jnp.sum(jnp.where(indices[..., None] == slots, table, 0), axis=-1).astype(jnp.int32)


def online_update(carried, queries, key_rows, value_rows, visible):
    maxima, totals, running = carried
    heads_here = queries.shape[1]
    key_split = key_rows.reshape(key_rows.shape[0], heads_here, -1)
    value_split = value_rows.reshape(value_rows.shape[0], heads_here, -1)
    scores = (
        jnp.einsum("qhd,khd->qhk", queries, key_split, preferred_element_type=jnp.float32) * SCALING
    )
    scores = jnp.where(visible[:, None, :], scores, NEGATIVE)
    updated = jnp.maximum(maxima, jnp.max(scores, axis=2))
    factor = jnp.exp(maxima - updated)
    weights = jnp.exp(scores - updated[:, :, None])
    totals = totals * factor + jnp.sum(weights, axis=2)
    running = running * factor[:, :, None] + jnp.einsum(
        "qhk,khd->qhd",
        weights.astype(jnp.bfloat16),
        value_split,
        preferred_element_type=jnp.float32,
    )
    return (updated, totals, running)


def sweep(
    carried, queries, key_rows, value_rows, key_places, key_groups, query_places, query_groups
):
    length = key_rows.shape[0]
    block_size = math.gcd(length, 2048)
    blocks_count = length // block_size
    key_blocks = key_rows.reshape(blocks_count, block_size, key_rows.shape[1])
    value_blocks = value_rows.reshape(blocks_count, block_size, value_rows.shape[1])
    group_blocks = key_groups.reshape(blocks_count, block_size)
    if key_places is None:
        place_blocks = group_blocks
    else:
        place_blocks = key_places.reshape(blocks_count, block_size)

    def advance(status, element):
        key_block, value_block, place_block, group_block = element
        visible = group_block[None, :] == query_groups[:, None]
        if key_places is None:
            return (online_update(status, queries, key_block, value_block, visible), None)
        visible = visible & (place_block[None, :] <= query_places[:, None])
        updated = online_update(status, queries, key_block, value_block, visible)
        return (updated, None)

    carried, unused = lax.scan(
        advance, carried, (key_blocks, value_blocks, place_blocks, group_blocks)
    )
    return carried


def empty_state(count_q, heads_here, head_width):
    return (
        jnp.full((count_q, heads_here), NEGATIVE, jnp.float32),
        jnp.zeros((count_q, heads_here), jnp.float32),
        jnp.zeros((count_q, heads_here, head_width), jnp.float32),
    )


def finish(carried):
    maxima, totals, running = carried
    return (running / totals[:, :, None]).reshape(running.shape[0], -1).astype(jnp.bfloat16)


def flash_kernel(
    steps_ref, sources_ref, bases_ref, q_ref, low_ref, high_ref, k_hbm, v_hbm, o_ref,
    kbuf, vbuf, sem, qm_sc, m_sc, l_sc, acc_sc, *, max_steps, heads, head_width
):
    half = pl.program_id(0)
    count = steps_ref[half]
    tile = kbuf.shape[1] // 2
    width = kbuf.shape[2]

    def copies(step, slot):
        result = []
        for j in range(2):
            source = pl.multiple_of(sources_ref[(half * max_steps + step) * 2 + j], tile)
            window = pl.ds(j * tile, tile)
            result.append(pltpu.make_async_copy(
                k_hbm.at[pl.ds(source, tile)], kbuf.at[slot, window], sem.at[0, slot, j]))
            result.append(pltpu.make_async_copy(
                v_hbm.at[pl.ds(source, tile)], vbuf.at[slot, window], sem.at[1, slot, j]))
        return result

    for copy in copies(0, 0):
        copy.start()
    column_head = lax.broadcasted_iota(jnp.int32, (1, width), 1) // head_width
    q = q_ref[0]
    for h in range(heads):
        qm_sc[h] = jnp.where(column_head == h, q, jnp.zeros_like(q))
    m_sc[...] = jnp.full(m_sc.shape, NEGATIVE, jnp.float32)
    l_sc[...] = jnp.zeros(l_sc.shape, jnp.float32)
    acc_sc[...] = jnp.zeros(acc_sc.shape, jnp.float32)
    low = low_ref[0]
    high = high_ref[0]

    def body(step, carry):
        slot = step % 2
        for copy in copies(step, slot):
            copy.wait()

        @pl.when(step + 1 < count)
        def _():
            for copy in copies(step + 1, 1 - slot):
                copy.start()

        base = bases_ref[half * max_steps + step]
        places = base + lax.broadcasted_iota(jnp.int32, (1, 2 * tile), 1)
        visible = (places >= low) & (places <= high)
        keys = kbuf[slot]
        values = vbuf[slot]
        for h in range(heads):
            scores = lax.dot_general(
                qm_sc[h], keys, (((1,), (1,)), ((), ())), preferred_element_type=jnp.float32
            ) * SCALING
            scores = jnp.where(visible, scores, NEGATIVE)
            previous = m_sc[h]
            updated = jnp.maximum(previous, jnp.max(scores, axis=1, keepdims=True))
            factor = jnp.exp(previous - updated)
            weights = jnp.exp(scores - updated)
            l_sc[h] = l_sc[h] * factor + jnp.sum(weights, axis=1, keepdims=True)
            acc_sc[h] = acc_sc[h] * factor + jnp.dot(
                weights.astype(jnp.bfloat16), values, preferred_element_type=jnp.float32
            )
            m_sc[h] = updated
        return carry

    lax.fori_loop(0, count, body, 0)
    out = jnp.zeros(acc_sc.shape[1:], jnp.float32)
    for h in range(heads):
        out = jnp.where(column_head == h, acc_sc[h] / l_sc[h], out)
    o_ref[0] = out.astype(o_ref.dtype)


def flash(queries, low, high, keys, values, steps, sources, bases, max_steps, heads):
    halves, tile, width = queries.shape
    head_width = width // heads
    kernel = functools.partial(
        flash_kernel, max_steps=max_steps, heads=heads, head_width=head_width
    )
    row_spec = pl.BlockSpec((1, tile, width), lambda h, *refs: (h, 0, 0))
    bound_spec = pl.BlockSpec((1, tile, 1), lambda h, *refs: (h, 0, 0))
    flops = 4 * halves * max_steps * tile * 2 * tile * width * heads
    return pl.pallas_call(
        kernel,
        out_shape=jax.ShapeDtypeStruct(queries.shape, jnp.bfloat16),
        grid_spec=pltpu.PrefetchScalarGridSpec(
            num_scalar_prefetch=3,
            grid=(halves,),
            in_specs=[
                row_spec,
                bound_spec,
                bound_spec,
                pl.BlockSpec(memory_space=pl.ANY),
                pl.BlockSpec(memory_space=pl.ANY),
            ],
            out_specs=row_spec,
            scratch_shapes=[
                pltpu.VMEM((2, 2 * tile, width), keys.dtype),
                pltpu.VMEM((2, 2 * tile, width), values.dtype),
                pltpu.SemaphoreType.DMA((2, 2, 2)),
                pltpu.VMEM((heads, tile, width), jnp.bfloat16),
                pltpu.VMEM((heads, tile, 1), jnp.float32),
                pltpu.VMEM((heads, tile, 1), jnp.float32),
                pltpu.VMEM((heads, tile, width), jnp.float32),
            ],
        ),
        compiler_params=pltpu.CompilerParams(dimension_semantics=("arbitrary",)),
        cost_estimate=pl.CostEstimate(
            flops=flops,
            transcendentals=halves * max_steps * tile * 2 * tile * heads,
            bytes_accessed=halves * max_steps * 2 * 2 * tile * width * 2,
        ),
    )(steps, sources, bases, queries, low, high, keys, values)


def single_kernel(
    steps_ref, sources_ref, bases_ref, limits_ref, q_ref, low_ref, high_ref, kv_hbm, o_ref,
    buf, sem, m_sc, l_sc, acc_sc, *, max_steps, head_width, pieces
):
    half = pl.program_id(0)
    count = steps_ref[half]
    tile = buf.shape[1] // pieces

    def copies(step, slot):
        result = []
        for j in range(pieces):
            source = pl.multiple_of(sources_ref[(half * max_steps + step) * pieces + j], tile)
            result.append(pltpu.make_async_copy(
                kv_hbm.at[pl.ds(source, tile)], buf.at[slot, pl.ds(j * tile, tile)], sem.at[slot, j]))
        return result

    for copy in copies(0, 0):
        copy.start()
    m_sc[...] = jnp.full(m_sc.shape, NEGATIVE, jnp.float32)
    l_sc[...] = jnp.zeros(l_sc.shape, jnp.float32)
    acc_sc[...] = jnp.zeros(acc_sc.shape, jnp.float32)
    q = q_ref[0]
    low = low_ref[0]
    high = high_ref[0]

    def body(step, carry):
        slot = step % 2
        for copy in copies(step, slot):
            copy.wait()

        @pl.when(step + 1 < count)
        def _():
            for copy in copies(step + 1, 1 - slot):
                copy.start()

        base = bases_ref[half * max_steps + step]
        keys = buf[slot, :, :head_width]
        values = buf[slot, :, head_width:]

        def update(masked):
            scores = lax.dot_general(
                q, keys, (((1,), (1,)), ((), ())), preferred_element_type=jnp.float32
            ) * SCALING
            if masked:
                places = base + lax.broadcasted_iota(jnp.int32, (1, pieces * tile), 1)
                visible = (places >= low) & (places <= high)
                scores = jnp.where(visible, scores, NEGATIVE)
            previous = m_sc[...]
            updated = jnp.maximum(previous, jnp.max(scores, axis=1, keepdims=True))
            factor = jnp.exp(previous - updated)
            weights = jnp.exp(scores - updated)
            l_sc[...] = l_sc[...] * factor + jnp.sum(weights, axis=1, keepdims=True)
            acc_sc[...] = acc_sc[...] * factor + jnp.dot(
                weights.astype(jnp.bfloat16), values, preferred_element_type=jnp.float32
            )
            m_sc[...] = updated

        full = (base >= limits_ref[2 * half]) & (base + pieces * tile - 1 <= limits_ref[2 * half + 1])

        @pl.when(full)
        def _():
            update(False)

        @pl.when(jnp.logical_not(full))
        def _():
            update(True)

        return carry

    lax.fori_loop(0, count, body, 0)
    o_ref[0] = (acc_sc[...] / l_sc[...]).astype(o_ref.dtype)


def single(queries, low, high, packed, steps, sources, bases, limits, max_steps, pieces):
    halves, tile, head_width = queries.shape
    kernel = functools.partial(
        single_kernel, max_steps=max_steps, head_width=head_width, pieces=pieces
    )
    row_spec = pl.BlockSpec((1, tile, head_width), lambda h, *refs: (h, 0, 0))
    bound_spec = pl.BlockSpec((1, tile, 1), lambda h, *refs: (h, 0, 0))
    return pl.pallas_call(
        kernel,
        out_shape=jax.ShapeDtypeStruct(queries.shape, jnp.bfloat16),
        grid_spec=pltpu.PrefetchScalarGridSpec(
            num_scalar_prefetch=4,
            grid=(halves,),
            in_specs=[row_spec, bound_spec, bound_spec, pl.BlockSpec(memory_space=pl.ANY)],
            out_specs=row_spec,
            scratch_shapes=[
                pltpu.VMEM((2, pieces * tile, packed.shape[1]), packed.dtype),
                pltpu.SemaphoreType.DMA((2, pieces)),
                pltpu.VMEM((tile, 1), jnp.float32),
                pltpu.VMEM((tile, 1), jnp.float32),
                pltpu.VMEM((tile, head_width), jnp.float32),
            ],
        ),
        compiler_params=pltpu.CompilerParams(dimension_semantics=("arbitrary",)),
        cost_estimate=pl.CostEstimate(
            flops=2 * halves * (max_steps // 2) * tile * pieces * tile * head_width * 2,
            transcendentals=halves * (max_steps // 2) * tile * pieces * tile,
            bytes_accessed=halves * (max_steps // 2) * pieces * tile * packed.shape[1] * 2,
        ),
    )(steps, sources, bases, limits, queries, low, high, packed)


def on_device(
    tokens,
    block_order,
    request_lengths,
    enc_lengths,
    w_qkv,
    w_out,
    enc_kv,
    w_cq,
    w_co,
    w_up,
    w_down,
    w_next,
):
    rows_here = tokens.shape[0]
    model_width = tokens.shape[1]
    group_size = lax.axis_size("head")
    cycle_size = lax.axis_size("zy") * lax.axis_size("x")
    block_rows = rows_here * group_size
    halfway = block_rows // 2
    group_width = w_qkv.shape[2]
    head_width = model_width // HEADS
    group_heads = group_width // head_width
    member = lax.axis_index("head")
    ring_size = lax.axis_size("x")
    ring_index = lax.axis_index("x")
    cycle_index = lax.axis_index("zy") * ring_size + ring_index
    full_out = lax.all_to_all(
        jnp.broadcast_to(w_out[None], (group_size,) + w_out.shape), "head", 0, 0, tiled=True
    ).reshape(model_width, model_width)
    gathered = lax.all_gather(tokens, "head", axis=0, tiled=True)
    projected = jnp.einsum(
        "td,cde->cte", gathered, w_qkv, preferred_element_type=jnp.float32
    ).astype(jnp.bfloat16)
    block_start = cycle_index * block_rows
    query_places = position_of(
        block_order, block_start + jnp.arange(block_rows, dtype=jnp.int32), halfway
    )
    slots = jnp.arange(2 * cycle_size, dtype=jnp.int32)
    holders = jnp.sum(jnp.where(block_order[:, None] == slots[None, :], slots[:, None], 0), axis=0)
    per_head = projected.reshape(3, block_rows, group_heads, head_width).transpose(2, 1, 0, 3)
    per_head = per_head.reshape(group_heads, block_rows, 3 * head_width)
    mine = lax.all_to_all(per_head, "x", 0, 0, tiled=True)
    packed = lax.all_gather(mine[:, :, head_width:], "zy", axis=0, tiled=True)
    packed = packed.reshape(cycle_size * block_rows, 2 * head_width)
    full_out, packed, late_kv = lax.optimization_barrier((full_out, packed, enc_kv))
    encoder = lax.all_gather(late_kv, ("zy", "x"), axis=1, tiled=True)
    ends = jnp.cumsum(request_lengths).astype(jnp.int32)
    starts = ends - request_lengths
    halves_here = 2 * ring_size
    first_half = lax.axis_index("zy") * halves_here
    pair = lax.dynamic_slice_in_dim(block_order, first_half, halves_here, 0)
    low_block = prefix_below(pair * halfway, ends, request_lengths) // halfway
    pieces = 4
    self_steps = (pair - low_block) // pieces + 1
    self_max = (2 * cycle_size + pieces - 1) // pieces
    firsts = low_block[:, None] + pieces * jnp.arange(self_max, dtype=jnp.int32)[None, :]
    self_sources = lookup(
        holders,
        jnp.minimum(firsts[:, :, None] + jnp.arange(pieces, dtype=jnp.int32), 2 * cycle_size - 1),
    ) * halfway
    places_here = (pair[:, None] * halfway + jnp.arange(halfway, dtype=jnp.int32)[None, :])
    self_low = prefix_below(places_here, ends, request_lengths).reshape(halves_here, halfway)
    limits = jnp.stack([self_low[:, -1], places_here[:, 0]], axis=1).reshape(-1)
    single_out = single(
        mine[:, :, :head_width].reshape(halves_here, halfway, head_width),
        self_low.reshape(halves_here, halfway, 1),
        places_here.reshape(halves_here, halfway, 1),
        packed,
        self_steps.astype(jnp.int32),
        self_sources.reshape(-1).astype(jnp.int32),
        (firsts * halfway).reshape(-1).astype(jnp.int32),
        limits.astype(jnp.int32),
        self_max,
        pieces,
    )
    owners = lax.all_to_all(
        single_out.reshape(ring_size * group_size, rows_here, head_width),
        ("x", "head"),
        0,
        0,
        tiled=True,
    )
    attended_rows = owners.reshape(ring_size, group_size, rows_here, head_width)
    attended_rows = attended_rows.transpose(2, 1, 0, 3).reshape(rows_here, model_width)
    group_blocks = lax.axis_index("zy") * ring_size + jnp.arange(ring_size, dtype=jnp.int32)
    cache_rows = lookup(
        holders, jnp.stack([2 * group_blocks, 2 * group_blocks + 1], axis=1)
    )
    cache_parts = jnp.stack(
        [
            jnp.concatenate(
                [
                    lax.dynamic_slice_in_dim(packed, cache_rows[i, 0] * halfway, halfway, 0),
                    lax.dynamic_slice_in_dim(packed, cache_rows[i, 1] * halfway, halfway, 0),
                ],
                axis=0,
            )
            for i in range(ring_size)
        ]
    )
    cache_heads = lax.all_to_all(cache_parts, "x", 0, 0, tiled=True)
    cache = cache_heads.reshape(group_heads, block_rows, 2, head_width).transpose(2, 1, 0, 3)
    cache = cache.reshape(2, block_rows, group_width)
    mixed = jnp.dot(attended_rows, full_out, preferred_element_type=jnp.float32)
    hidden = normalize(mixed + tokens.astype(jnp.float32))
    hidden_b = hidden.astype(jnp.bfloat16)
    block_hidden = lax.all_gather(hidden_b, "head", axis=0, tiled=True)
    w_cq_group = lax.dynamic_slice_in_dim(w_cq, member * group_width, group_width, 1)
    cross_query = jnp.dot(
        block_hidden, w_cq_group, preferred_element_type=jnp.float32
    ).astype(jnp.bfloat16)
    encoder_rows = encoder.shape[1]
    cross_max = (encoder_rows + halfway - 1 + 2 * halfway - 1) // (2 * halfway)
    padded_encoder = jnp.pad(
        encoder, ((0, 0), (0, cross_max * 2 * halfway + halfway - encoder_rows), (0, 0))
    )
    enc_low = prefix_below(query_places, ends, enc_lengths)
    enc_high = prefix_below(query_places, starts, enc_lengths) - 1
    cross_base = (enc_low.reshape(2, halfway)[:, 0] // halfway) * halfway
    cross_steps = (enc_high.reshape(2, halfway)[:, -1] + 1 - cross_base + 2 * halfway - 1) // (
        2 * halfway
    )
    cross_firsts = jnp.minimum(
        cross_base[:, None] + 2 * halfway * jnp.arange(cross_max, dtype=jnp.int32)[None, :],
        padded_encoder.shape[1] - 2 * halfway,
    )
    cross_sources = jnp.stack([cross_firsts, cross_firsts + halfway], axis=-1)
    crossed_group = flash(
        cross_query.reshape(2, halfway, group_width),
        enc_low.reshape(2, halfway, 1),
        enc_high.reshape(2, halfway, 1),
        padded_encoder[0],
        padded_encoder[1],
        cross_steps.astype(jnp.int32),
        cross_sources.reshape(-1).astype(jnp.int32),
        cross_firsts.reshape(-1).astype(jnp.int32),
        cross_max,
        group_heads,
    ).reshape(block_rows, group_width)
    exchanged = lax.all_to_all(
        crossed_group.reshape(group_size, rows_here, group_width), "head", 0, 0, tiled=True
    )
    crossed = exchanged.transpose(1, 0, 2).reshape(rows_here, model_width)
    summed = jnp.dot(crossed, w_co, preferred_element_type=jnp.float32)
    second = normalize(summed + hidden)
    second_b = second.astype(jnp.bfloat16)
    inner = jax.nn.gelu(
        jnp.dot(second_b, w_up, preferred_element_type=jnp.float32), approximate=False
    ).astype(jnp.bfloat16)
    output = normalize(jnp.dot(inner, w_down, preferred_element_type=jnp.float32) + second)
    output_b = output.astype(jnp.bfloat16)
    block_output = lax.all_gather(output_b, "head", axis=0, tiled=True)
    next_qkv = jnp.einsum("td,cde->cte", block_output, w_next, preferred_element_type=jnp.float32)
    return (output, cache, next_qkv)


def solution(mesh):
    ring = 4
    devices = mesh.devices.reshape(mesh.shape["blk"] // ring, ring, mesh.shape["head"])
    fine = jax.sharding.Mesh(devices, ("zy", "x", "head"))
    rows = ("zy", "x", "head")
    blocks = ("zy", "x")
    in_specs = (
        P(rows, None),
        P(),
        P(),
        P(),
        P(None, None, "head"),
        P("head", None),
        P(None, blocks, "head"),
        P(),
        P(),
        P(),
        P(),
        P(None, None, "head"),
    )
    out_specs = (P(rows, None), P(None, blocks, "head"), P(None, blocks, "head"))
    return jax.shard_map(
        on_device, mesh=fine, in_specs=in_specs, out_specs=out_specs, check_vma=False
    )
```

```python
import functools
import math

import jax
import jax.numpy as jnp
from jax import lax
from jax.experimental import pallas as pl
from jax.experimental.pallas import tpu as pltpu
from jax.sharding import PartitionSpec as P

HEADS = 16


NEGATIVE = -1e30
SCALING = 0.125
EPSILON = 1e-05


def normalize(matrix):
    center = matrix - jnp.mean(matrix, axis=-1, keepdims=True)
    return center * lax.rsqrt(jnp.mean(center * center, axis=-1, keepdims=True) + EPSILON)


def position_of(order_table, indices, halfway):
    slots = jnp.arange(order_table.shape[0], dtype=jnp.int32)
    picked = jnp.sum(
        jnp.where((indices // halfway)[:, None] == slots[None, :], order_table[None, :], 0), axis=1
    )
    return picked * halfway + indices % halfway


def group_of(places, lengths):
    ends = jnp.cumsum(lengths)
    return jnp.sum((places[:, None] >= ends[None, :]).astype(jnp.int32), axis=1)


def prefix_below(places, bounds, amounts):
    return jnp.sum(
        jnp.where(places[..., None] >= bounds, amounts, 0), axis=-1
    ).astype(jnp.int32)


def lookup(table, indices):
    slots = jnp.arange(table.shape[0], dtype=jnp.int32)
    return jnp.sum(jnp.where(indices[..., None] == slots, table, 0), axis=-1).astype(jnp.int32)


def online_update(carried, queries, key_rows, value_rows, visible):
    maxima, totals, running = carried
    heads_here = queries.shape[1]
    key_split = key_rows.reshape(key_rows.shape[0], heads_here, -1)
    value_split = value_rows.reshape(value_rows.shape[0], heads_here, -1)
    scores = (
        jnp.einsum("qhd,khd->qhk", queries, key_split, preferred_element_type=jnp.float32) * SCALING
    )
    scores = jnp.where(visible[:, None, :], scores, NEGATIVE)
    updated = jnp.maximum(maxima, jnp.max(scores, axis=2))
    factor = jnp.exp(maxima - updated)
    weights = jnp.exp(scores - updated[:, :, None])
    totals = totals * factor + jnp.sum(weights, axis=2)
    running = running * factor[:, :, None] + jnp.einsum(
        "qhk,khd->qhd",
        weights.astype(jnp.bfloat16),
        value_split,
        preferred_element_type=jnp.float32,
    )
    return (updated, totals, running)


def sweep(
    carried, queries, key_rows, value_rows, key_places, key_groups, query_places, query_groups
):
    length = key_rows.shape[0]
    block_size = math.gcd(length, 2048)
    blocks_count = length // block_size
    key_blocks = key_rows.reshape(blocks_count, block_size, key_rows.shape[1])
    value_blocks = value_rows.reshape(blocks_count, block_size, value_rows.shape[1])
    group_blocks = key_groups.reshape(blocks_count, block_size)
    if key_places is None:
        place_blocks = group_blocks
    else:
        place_blocks = key_places.reshape(blocks_count, block_size)

    def advance(status, element):
        key_block, value_block, place_block, group_block = element
        visible = group_block[None, :] == query_groups[:, None]
        if key_places is None:
            return (online_update(status, queries, key_block, value_block, visible), None)
        visible = visible & (place_block[None, :] <= query_places[:, None])
        updated = online_update(status, queries, key_block, value_block, visible)
        return (updated, None)

    carried, unused = lax.scan(
        advance, carried, (key_blocks, value_blocks, place_blocks, group_blocks)
    )
    return carried


def empty_state(count_q, heads_here, head_width):
    return (
        jnp.full((count_q, heads_here), NEGATIVE, jnp.float32),
        jnp.zeros((count_q, heads_here), jnp.float32),
        jnp.zeros((count_q, heads_here, head_width), jnp.float32),
    )


def finish(carried):
    maxima, totals, running = carried
    return (running / totals[:, :, None]).reshape(running.shape[0], -1).astype(jnp.bfloat16)


def flash_kernel(
    steps_ref, sources_ref, bases_ref, q_ref, low_ref, high_ref, k_hbm, v_hbm, o_ref,
    kbuf, vbuf, sem, qm_sc, m_sc, l_sc, acc_sc, *, max_steps, heads, head_width
):
    half = pl.program_id(0)
    count = steps_ref[half]
    tile = kbuf.shape[1] // 2
    width = kbuf.shape[2]

    def copies(step, slot):
        result = []
        for j in range(2):
            source = pl.multiple_of(sources_ref[(half * max_steps + step) * 2 + j], tile)
            window = pl.ds(j * tile, tile)
            result.append(pltpu.make_async_copy(
                k_hbm.at[pl.ds(source, tile)], kbuf.at[slot, window], sem.at[0, slot, j]))
            result.append(pltpu.make_async_copy(
                v_hbm.at[pl.ds(source, tile)], vbuf.at[slot, window], sem.at[1, slot, j]))
        return result

    for copy in copies(0, 0):
        copy.start()
    column_head = lax.broadcasted_iota(jnp.int32, (1, width), 1) // head_width
    q = q_ref[0]
    for h in range(heads):
        qm_sc[h] = jnp.where(column_head == h, q, jnp.zeros_like(q))
    m_sc[...] = jnp.full(m_sc.shape, NEGATIVE, jnp.float32)
    l_sc[...] = jnp.zeros(l_sc.shape, jnp.float32)
    acc_sc[...] = jnp.zeros(acc_sc.shape, jnp.float32)
    low = low_ref[0]
    high = high_ref[0]

    def body(step, carry):
        slot = step % 2
        for copy in copies(step, slot):
            copy.wait()

        @pl.when(step + 1 < count)
        def _():
            for copy in copies(step + 1, 1 - slot):
                copy.start()

        base = bases_ref[half * max_steps + step]
        places = base + lax.broadcasted_iota(jnp.int32, (1, 2 * tile), 1)
        visible = (places >= low) & (places <= high)
        keys = kbuf[slot]
        values = vbuf[slot]
        for h in range(heads):
            scores = lax.dot_general(
                qm_sc[h], keys, (((1,), (1,)), ((), ())), preferred_element_type=jnp.float32
            ) * SCALING
            scores = jnp.where(visible, scores, NEGATIVE)
            previous = m_sc[h]
            updated = jnp.maximum(previous, jnp.max(scores, axis=1, keepdims=True))
            factor = jnp.exp(previous - updated)
            weights = jnp.exp(scores - updated)
            l_sc[h] = l_sc[h] * factor + jnp.sum(weights, axis=1, keepdims=True)
            acc_sc[h] = acc_sc[h] * factor + jnp.dot(
                weights.astype(jnp.bfloat16), values, preferred_element_type=jnp.float32
            )
            m_sc[h] = updated
        return carry

    lax.fori_loop(0, count, body, 0)
    out = jnp.zeros(acc_sc.shape[1:], jnp.float32)
    for h in range(heads):
        out = jnp.where(column_head == h, acc_sc[h] / l_sc[h], out)
    o_ref[0] = out.astype(o_ref.dtype)


def flash(queries, low, high, keys, values, steps, sources, bases, max_steps, heads):
    halves, tile, width = queries.shape
    head_width = width // heads
    kernel = functools.partial(
        flash_kernel, max_steps=max_steps, heads=heads, head_width=head_width
    )
    row_spec = pl.BlockSpec((1, tile, width), lambda h, *refs: (h, 0, 0))
    bound_spec = pl.BlockSpec((1, tile, 1), lambda h, *refs: (h, 0, 0))
    flops = 4 * halves * max_steps * tile * 2 * tile * width * heads
    return pl.pallas_call(
        kernel,
        out_shape=jax.ShapeDtypeStruct(queries.shape, jnp.bfloat16),
        grid_spec=pltpu.PrefetchScalarGridSpec(
            num_scalar_prefetch=3,
            grid=(halves,),
            in_specs=[
                row_spec,
                bound_spec,
                bound_spec,
                pl.BlockSpec(memory_space=pl.ANY),
                pl.BlockSpec(memory_space=pl.ANY),
            ],
            out_specs=row_spec,
            scratch_shapes=[
                pltpu.VMEM((2, 2 * tile, width), keys.dtype),
                pltpu.VMEM((2, 2 * tile, width), values.dtype),
                pltpu.SemaphoreType.DMA((2, 2, 2)),
                pltpu.VMEM((heads, tile, width), jnp.bfloat16),
                pltpu.VMEM((heads, tile, 1), jnp.float32),
                pltpu.VMEM((heads, tile, 1), jnp.float32),
                pltpu.VMEM((heads, tile, width), jnp.float32),
            ],
        ),
        compiler_params=pltpu.CompilerParams(dimension_semantics=("arbitrary",)),
        cost_estimate=pl.CostEstimate(
            flops=flops,
            transcendentals=halves * max_steps * tile * 2 * tile * heads,
            bytes_accessed=halves * max_steps * 2 * 2 * tile * width * 2,
        ),
    )(steps, sources, bases, queries, low, high, keys, values)


def single_kernel(
    steps_ref, sources_ref, bases_ref, limits_ref, q_ref, low_ref, high_ref, kv_hbm, o_ref,
    buf, sem, m_sc, l_sc, acc_sc, *, max_steps, head_width, pieces
):
    half = pl.program_id(0)
    count = steps_ref[half]
    tile = buf.shape[1] // pieces

    def copies(step, slot):
        result = []
        for j in range(pieces):
            source = pl.multiple_of(sources_ref[(half * max_steps + step) * pieces + j], tile)
            result.append(pltpu.make_async_copy(
                kv_hbm.at[pl.ds(source, tile)], buf.at[slot, pl.ds(j * tile, tile)], sem.at[slot, j]))
        return result

    for copy in copies(0, 0):
        copy.start()
    m_sc[...] = jnp.full(m_sc.shape, NEGATIVE, jnp.float32)
    l_sc[...] = jnp.zeros(l_sc.shape, jnp.float32)
    acc_sc[...] = jnp.zeros(acc_sc.shape, jnp.float32)
    q = q_ref[0]
    low = low_ref[0]
    high = high_ref[0]

    def body(step, carry):
        slot = step % 2
        for copy in copies(step, slot):
            copy.wait()

        @pl.when(step + 1 < count)
        def _():
            for copy in copies(step + 1, 1 - slot):
                copy.start()

        base = bases_ref[half * max_steps + step]
        keys = buf[slot, :, :head_width]
        values = buf[slot, :, head_width:]

        def update(masked):
            scores = lax.dot_general(
                q, keys, (((1,), (1,)), ((), ())), preferred_element_type=jnp.float32
            ) * SCALING
            if masked:
                places = base + lax.broadcasted_iota(jnp.int32, (1, pieces * tile), 1)
                visible = (places >= low) & (places <= high)
                scores = jnp.where(visible, scores, NEGATIVE)
            previous = m_sc[...]
            updated = jnp.maximum(previous, jnp.max(scores, axis=1, keepdims=True))
            factor = jnp.exp(previous - updated)
            weights = jnp.exp(scores - updated)
            l_sc[...] = l_sc[...] * factor + jnp.sum(weights, axis=1, keepdims=True)
            acc_sc[...] = acc_sc[...] * factor + jnp.dot(
                weights.astype(jnp.bfloat16), values, preferred_element_type=jnp.float32
            )
            m_sc[...] = updated

        full = (base >= limits_ref[2 * half]) & (base + pieces * tile - 1 <= limits_ref[2 * half + 1])

        @pl.when(full)
        def _():
            update(False)

        @pl.when(jnp.logical_not(full))
        def _():
            update(True)

        return carry

    lax.fori_loop(0, count, body, 0)
    o_ref[0] = (acc_sc[...] / l_sc[...]).astype(o_ref.dtype)


def single(queries, low, high, packed, steps, sources, bases, limits, max_steps, pieces):
    halves, tile, head_width = queries.shape
    kernel = functools.partial(
        single_kernel, max_steps=max_steps, head_width=head_width, pieces=pieces
    )
    row_spec = pl.BlockSpec((1, tile, head_width), lambda h, *refs: (h, 0, 0))
    bound_spec = pl.BlockSpec((1, tile, 1), lambda h, *refs: (h, 0, 0))
    return pl.pallas_call(
        kernel,
        out_shape=jax.ShapeDtypeStruct(queries.shape, jnp.bfloat16),
        grid_spec=pltpu.PrefetchScalarGridSpec(
            num_scalar_prefetch=4,
            grid=(halves,),
            in_specs=[row_spec, bound_spec, bound_spec, pl.BlockSpec(memory_space=pl.ANY)],
            out_specs=row_spec,
            scratch_shapes=[
                pltpu.VMEM((2, pieces * tile, packed.shape[1]), packed.dtype),
                pltpu.SemaphoreType.DMA((2, pieces)),
                pltpu.VMEM((tile, 1), jnp.float32),
                pltpu.VMEM((tile, 1), jnp.float32),
                pltpu.VMEM((tile, head_width), jnp.float32),
            ],
        ),
        compiler_params=pltpu.CompilerParams(dimension_semantics=("arbitrary",)),
        cost_estimate=pl.CostEstimate(
            flops=2 * halves * (max_steps // 2) * tile * pieces * tile * head_width * 2,
            transcendentals=halves * (max_steps // 2) * tile * pieces * tile,
            bytes_accessed=halves * (max_steps // 2) * pieces * tile * packed.shape[1] * 2,
        ),
    )(steps, sources, bases, limits, queries, low, high, packed)


def on_device(
    tokens,
    block_order,
    request_lengths,
    enc_lengths,
    w_qkv,
    w_out,
    enc_kv,
    w_cq,
    w_co,
    w_up,
    w_down,
    w_next,
):
    rows_here = tokens.shape[0]
    model_width = tokens.shape[1]
    group_size = lax.axis_size("head")
    cycle_size = lax.axis_size("zy") * lax.axis_size("x")
    block_rows = rows_here * group_size
    halfway = block_rows // 2
    group_width = w_qkv.shape[2]
    head_width = model_width // HEADS
    group_heads = group_width // head_width
    member = lax.axis_index("head")
    ring_size = lax.axis_size("x")
    ring_index = lax.axis_index("x")
    cycle_index = lax.axis_index("zy") * ring_size + ring_index
    full_out = lax.all_to_all(
        jnp.broadcast_to(w_out[None], (group_size,) + w_out.shape), "head", 0, 0, tiled=True
    ).reshape(model_width, model_width)
    gathered = lax.all_gather(tokens, "head", axis=0, tiled=True)
    projected = jnp.einsum(
        "td,cde->cte", gathered, w_qkv, preferred_element_type=jnp.float32
    ).astype(jnp.bfloat16)
    block_start = cycle_index * block_rows
    query_places = position_of(
        block_order, block_start + jnp.arange(block_rows, dtype=jnp.int32), halfway
    )
    slots = jnp.arange(2 * cycle_size, dtype=jnp.int32)
    holders = jnp.sum(jnp.where(block_order[:, None] == slots[None, :], slots[:, None], 0), axis=0)
    per_head = projected.reshape(3, block_rows, group_heads, head_width).transpose(2, 1, 0, 3)
    per_head = per_head.reshape(group_heads, block_rows, 3 * head_width)
    mine = lax.all_to_all(per_head, "x", 0, 0, tiled=True)
    packed = lax.all_gather(mine[:, :, head_width:], "zy", axis=0, tiled=True)
    packed = packed.reshape(cycle_size * block_rows, 2 * head_width)
    full_out, packed, late_kv = lax.optimization_barrier((full_out, packed, enc_kv))
    encoder = lax.all_gather(late_kv, ("zy", "x"), axis=1, tiled=True)
    ends = jnp.cumsum(request_lengths).astype(jnp.int32)
    starts = ends - request_lengths
    halves_here = 2 * ring_size
    first_half = lax.axis_index("zy") * halves_here
    pair = lax.dynamic_slice_in_dim(block_order, first_half, halves_here, 0)
    low_block = prefix_below(pair * halfway, ends, request_lengths) // halfway
    pieces = 4
    self_steps = (pair - low_block) // pieces + 1
    self_max = (2 * cycle_size + pieces - 1) // pieces
    firsts = low_block[:, None] + pieces * jnp.arange(self_max, dtype=jnp.int32)[None, :]
    self_sources = lookup(
        holders,
        jnp.minimum(firsts[:, :, None] + jnp.arange(pieces, dtype=jnp.int32), 2 * cycle_size - 1),
    ) * halfway
    places_here = (pair[:, None] * halfway + jnp.arange(halfway, dtype=jnp.int32)[None, :])
    self_low = prefix_below(places_here, ends, request_lengths).reshape(halves_here, halfway)
    limits = jnp.stack([self_low[:, -1], places_here[:, 0]], axis=1).reshape(-1)
    single_out = single(
        mine[:, :, :head_width].reshape(halves_here, halfway, head_width),
        self_low.reshape(halves_here, halfway, 1),
        places_here.reshape(halves_here, halfway, 1),
        packed,
        self_steps.astype(jnp.int32),
        self_sources.reshape(-1).astype(jnp.int32),
        (firsts * halfway).reshape(-1).astype(jnp.int32),
        limits.astype(jnp.int32),
        self_max,
        pieces,
    )
    owners = lax.all_to_all(
        single_out.reshape(ring_size * group_size, rows_here, head_width),
        ("x", "head"),
        0,
        0,
        tiled=True,
    )
    attended_rows = owners.reshape(ring_size, group_size, rows_here, head_width)
    attended_rows = attended_rows.transpose(2, 1, 0, 3).reshape(rows_here, model_width)
    group_blocks = lax.axis_index("zy") * ring_size + jnp.arange(ring_size, dtype=jnp.int32)
    cache_rows = lookup(
        holders, jnp.stack([2 * group_blocks, 2 * group_blocks + 1], axis=1)
    )
    cache_parts = jnp.stack(
        [
            jnp.concatenate(
                [
                    lax.dynamic_slice_in_dim(packed, cache_rows[i, 0] * halfway, halfway, 0),
                    lax.dynamic_slice_in_dim(packed, cache_rows[i, 1] * halfway, halfway, 0),
                ],
                axis=0,
            )
            for i in range(ring_size)
        ]
    )
    cache_heads = lax.all_to_all(cache_parts, "x", 0, 0, tiled=True)
    cache = cache_heads.reshape(group_heads, block_rows, 2, head_width).transpose(2, 1, 0, 3)
    cache = cache.reshape(2, block_rows, group_width)
    mixed = jnp.dot(attended_rows, full_out, preferred_element_type=jnp.float32)
    hidden = normalize(mixed + tokens.astype(jnp.float32))
    hidden_b = hidden.astype(jnp.bfloat16)
    own_query = jnp.dot(hidden_b, w_cq, preferred_element_type=jnp.float32).astype(jnp.bfloat16)
    cross_query = lax.all_to_all(
        own_query.reshape(rows_here, group_size, group_width).transpose(1, 0, 2),
        "head",
        0,
        0,
        tiled=True,
    ).reshape(block_rows, group_width)
    encoder_rows = encoder.shape[1]
    cross_max = (encoder_rows + halfway - 1 + 2 * halfway - 1) // (2 * halfway)
    padded_encoder = jnp.pad(
        encoder, ((0, 0), (0, cross_max * 2 * halfway + halfway - encoder_rows), (0, 0))
    )
    enc_low = prefix_below(query_places, ends, enc_lengths)
    enc_high = prefix_below(query_places, starts, enc_lengths) - 1
    cross_base = (enc_low.reshape(2, halfway)[:, 0] // halfway) * halfway
    cross_steps = (enc_high.reshape(2, halfway)[:, -1] + 1 - cross_base + 2 * halfway - 1) // (
        2 * halfway
    )
    cross_firsts = jnp.minimum(
        cross_base[:, None] + 2 * halfway * jnp.arange(cross_max, dtype=jnp.int32)[None, :],
        padded_encoder.shape[1] - 2 * halfway,
    )
    cross_sources = jnp.stack([cross_firsts, cross_firsts + halfway], axis=-1)
    crossed_group = flash(
        cross_query.reshape(2, halfway, group_width),
        enc_low.reshape(2, halfway, 1),
        enc_high.reshape(2, halfway, 1),
        padded_encoder[0],
        padded_encoder[1],
        cross_steps.astype(jnp.int32),
        cross_sources.reshape(-1).astype(jnp.int32),
        cross_firsts.reshape(-1).astype(jnp.int32),
        cross_max,
        group_heads,
    ).reshape(block_rows, group_width)
    exchanged = lax.all_to_all(
        crossed_group.reshape(group_size, rows_here, group_width), "head", 0, 0, tiled=True
    )
    crossed = exchanged.transpose(1, 0, 2).reshape(rows_here, model_width)
    summed = jnp.dot(crossed, w_co, preferred_element_type=jnp.float32)
    second = normalize(summed + hidden)
    second_b = second.astype(jnp.bfloat16)
    inner = jax.nn.gelu(
        jnp.dot(second_b, w_up, preferred_element_type=jnp.float32), approximate=False
    ).astype(jnp.bfloat16)
    output = normalize(jnp.dot(inner, w_down, preferred_element_type=jnp.float32) + second)
    output_b = output.astype(jnp.bfloat16)
    block_output = lax.all_gather(output_b, "head", axis=0, tiled=True)
    next_qkv = jnp.einsum("td,cde->cte", block_output, w_next, preferred_element_type=jnp.float32)
    return (output, cache, next_qkv)


def solution(mesh):
    ring = 4
    devices = mesh.devices.reshape(mesh.shape["blk"] // ring, ring, mesh.shape["head"])
    fine = jax.sharding.Mesh(devices, ("zy", "x", "head"))
    rows = ("zy", "x", "head")
    blocks = ("zy", "x")
    in_specs = (
        P(rows, None),
        P(),
        P(),
        P(),
        P(None, None, "head"),
        P("head", None),
        P(None, blocks, "head"),
        P(),
        P(),
        P(),
        P(),
        P(None, None, "head"),
    )
    out_specs = (P(rows, None), P(None, blocks, "head"), P(None, blocks, "head"))
    return jax.shard_map(
        on_device, mesh=fine, in_specs=in_specs, out_specs=out_specs, check_vma=False
    )
```

```python
import functools
import math

import jax
import jax.numpy as jnp
from jax import lax
from jax.experimental import pallas as pl
from jax.experimental.pallas import tpu as pltpu
from jax.sharding import PartitionSpec as P

HEADS = 16


NEGATIVE = -1e30
SCALING = 0.125
EPSILON = 1e-05


def normalize(matrix):
    center = matrix - jnp.mean(matrix, axis=-1, keepdims=True)
    return center * lax.rsqrt(jnp.mean(center * center, axis=-1, keepdims=True) + EPSILON)


def position_of(order_table, indices, halfway):
    slots = jnp.arange(order_table.shape[0], dtype=jnp.int32)
    picked = jnp.sum(
        jnp.where((indices // halfway)[:, None] == slots[None, :], order_table[None, :], 0), axis=1
    )
    return picked * halfway + indices % halfway


def group_of(places, lengths):
    ends = jnp.cumsum(lengths)
    return jnp.sum((places[:, None] >= ends[None, :]).astype(jnp.int32), axis=1)


def prefix_below(places, bounds, amounts):
    return jnp.sum(
        jnp.where(places[..., None] >= bounds, amounts, 0), axis=-1
    ).astype(jnp.int32)


def lookup(table, indices):
    slots = jnp.arange(table.shape[0], dtype=jnp.int32)
    return jnp.sum(jnp.where(indices[..., None] == slots, table, 0), axis=-1).astype(jnp.int32)


def online_update(carried, queries, key_rows, value_rows, visible):
    maxima, totals, running = carried
    heads_here = queries.shape[1]
    key_split = key_rows.reshape(key_rows.shape[0], heads_here, -1)
    value_split = value_rows.reshape(value_rows.shape[0], heads_here, -1)
    scores = (
        jnp.einsum("qhd,khd->qhk", queries, key_split, preferred_element_type=jnp.float32) * SCALING
    )
    scores = jnp.where(visible[:, None, :], scores, NEGATIVE)
    updated = jnp.maximum(maxima, jnp.max(scores, axis=2))
    factor = jnp.exp(maxima - updated)
    weights = jnp.exp(scores - updated[:, :, None])
    totals = totals * factor + jnp.sum(weights, axis=2)
    running = running * factor[:, :, None] + jnp.einsum(
        "qhk,khd->qhd",
        weights.astype(jnp.bfloat16),
        value_split,
        preferred_element_type=jnp.float32,
    )
    return (updated, totals, running)


def sweep(
    carried, queries, key_rows, value_rows, key_places, key_groups, query_places, query_groups
):
    length = key_rows.shape[0]
    block_size = math.gcd(length, 2048)
    blocks_count = length // block_size
    key_blocks = key_rows.reshape(blocks_count, block_size, key_rows.shape[1])
    value_blocks = value_rows.reshape(blocks_count, block_size, value_rows.shape[1])
    group_blocks = key_groups.reshape(blocks_count, block_size)
    if key_places is None:
        place_blocks = group_blocks
    else:
        place_blocks = key_places.reshape(blocks_count, block_size)

    def advance(status, element):
        key_block, value_block, place_block, group_block = element
        visible = group_block[None, :] == query_groups[:, None]
        if key_places is None:
            return (online_update(status, queries, key_block, value_block, visible), None)
        visible = visible & (place_block[None, :] <= query_places[:, None])
        updated = online_update(status, queries, key_block, value_block, visible)
        return (updated, None)

    carried, unused = lax.scan(
        advance, carried, (key_blocks, value_blocks, place_blocks, group_blocks)
    )
    return carried


def empty_state(count_q, heads_here, head_width):
    return (
        jnp.full((count_q, heads_here), NEGATIVE, jnp.float32),
        jnp.zeros((count_q, heads_here), jnp.float32),
        jnp.zeros((count_q, heads_here, head_width), jnp.float32),
    )


def finish(carried):
    maxima, totals, running = carried
    return (running / totals[:, :, None]).reshape(running.shape[0], -1).astype(jnp.bfloat16)


def flash_kernel(
    steps_ref, sources_ref, bases_ref, q_ref, low_ref, high_ref, k_hbm, v_hbm, o_ref,
    kbuf, vbuf, sem, qm_sc, m_sc, l_sc, acc_sc, *, max_steps, heads, head_width
):
    half = pl.program_id(0)
    count = steps_ref[half]
    tile = kbuf.shape[1] // 2
    width = kbuf.shape[2]

    def copies(step, slot):
        result = []
        for j in range(2):
            source = pl.multiple_of(sources_ref[(half * max_steps + step) * 2 + j], tile)
            window = pl.ds(j * tile, tile)
            result.append(pltpu.make_async_copy(
                k_hbm.at[pl.ds(source, tile)], kbuf.at[slot, window], sem.at[0, slot, j]))
            result.append(pltpu.make_async_copy(
                v_hbm.at[pl.ds(source, tile)], vbuf.at[slot, window], sem.at[1, slot, j]))
        return result

    for copy in copies(0, 0):
        copy.start()
    column_head = lax.broadcasted_iota(jnp.int32, (1, width), 1) // head_width
    q = q_ref[0]
    for h in range(heads):
        qm_sc[h] = jnp.where(column_head == h, q, jnp.zeros_like(q))
    m_sc[...] = jnp.full(m_sc.shape, NEGATIVE, jnp.float32)
    l_sc[...] = jnp.zeros(l_sc.shape, jnp.float32)
    acc_sc[...] = jnp.zeros(acc_sc.shape, jnp.float32)
    low = low_ref[0]
    high = high_ref[0]

    def body(step, carry):
        slot = step % 2
        for copy in copies(step, slot):
            copy.wait()

        @pl.when(step + 1 < count)
        def _():
            for copy in copies(step + 1, 1 - slot):
                copy.start()

        base = bases_ref[half * max_steps + step]
        places = base + lax.broadcasted_iota(jnp.int32, (1, 2 * tile), 1)
        visible = (places >= low) & (places <= high)
        keys = kbuf[slot]
        values = vbuf[slot]
        for h in range(heads):
            scores = lax.dot_general(
                qm_sc[h], keys, (((1,), (1,)), ((), ())), preferred_element_type=jnp.float32
            ) * SCALING
            scores = jnp.where(visible, scores, NEGATIVE)
            previous = m_sc[h]
            updated = jnp.maximum(previous, jnp.max(scores, axis=1, keepdims=True))
            factor = jnp.exp(previous - updated)
            weights = jnp.exp(scores - updated)
            l_sc[h] = l_sc[h] * factor + jnp.sum(weights, axis=1, keepdims=True)
            acc_sc[h] = acc_sc[h] * factor + jnp.dot(
                weights.astype(jnp.bfloat16), values, preferred_element_type=jnp.float32
            )
            m_sc[h] = updated
        return carry

    lax.fori_loop(0, count, body, 0)
    out = jnp.zeros(acc_sc.shape[1:], jnp.float32)
    for h in range(heads):
        out = jnp.where(column_head == h, acc_sc[h] / l_sc[h], out)
    o_ref[0] = out.astype(o_ref.dtype)


def flash(queries, low, high, keys, values, steps, sources, bases, max_steps, heads):
    halves, tile, width = queries.shape
    head_width = width // heads
    kernel = functools.partial(
        flash_kernel, max_steps=max_steps, heads=heads, head_width=head_width
    )
    row_spec = pl.BlockSpec((1, tile, width), lambda h, *refs: (h, 0, 0))
    bound_spec = pl.BlockSpec((1, tile, 1), lambda h, *refs: (h, 0, 0))
    flops = 4 * halves * max_steps * tile * 2 * tile * width * heads
    return pl.pallas_call(
        kernel,
        out_shape=jax.ShapeDtypeStruct(queries.shape, jnp.bfloat16),
        grid_spec=pltpu.PrefetchScalarGridSpec(
            num_scalar_prefetch=3,
            grid=(halves,),
            in_specs=[
                row_spec,
                bound_spec,
                bound_spec,
                pl.BlockSpec(memory_space=pl.ANY),
                pl.BlockSpec(memory_space=pl.ANY),
            ],
            out_specs=row_spec,
            scratch_shapes=[
                pltpu.VMEM((2, 2 * tile, width), keys.dtype),
                pltpu.VMEM((2, 2 * tile, width), values.dtype),
                pltpu.SemaphoreType.DMA((2, 2, 2)),
                pltpu.VMEM((heads, tile, width), jnp.bfloat16),
                pltpu.VMEM((heads, tile, 1), jnp.float32),
                pltpu.VMEM((heads, tile, 1), jnp.float32),
                pltpu.VMEM((heads, tile, width), jnp.float32),
            ],
        ),
        compiler_params=pltpu.CompilerParams(dimension_semantics=("arbitrary",)),
        cost_estimate=pl.CostEstimate(
            flops=flops,
            transcendentals=halves * max_steps * tile * 2 * tile * heads,
            bytes_accessed=halves * max_steps * 2 * 2 * tile * width * 2,
        ),
    )(steps, sources, bases, queries, low, high, keys, values)


def single_kernel(
    steps_ref, sources_ref, bases_ref, limits_ref, q_ref, low_ref, high_ref, kv_hbm, o_ref,
    buf, sem, m_sc, l_sc, acc_sc, *, max_steps, head_width, pieces
):
    half = pl.program_id(0)
    count = steps_ref[half]
    tile = buf.shape[1] // pieces

    def copies(step, slot):
        result = []
        for j in range(pieces):
            source = pl.multiple_of(sources_ref[(half * max_steps + step) * pieces + j], tile)
            result.append(pltpu.make_async_copy(
                kv_hbm.at[pl.ds(source, tile)], buf.at[slot, pl.ds(j * tile, tile)], sem.at[slot, j]))
        return result

    for copy in copies(0, 0):
        copy.start()
    m_sc[...] = jnp.full(m_sc.shape, NEGATIVE, jnp.float32)
    l_sc[...] = jnp.zeros(l_sc.shape, jnp.float32)
    acc_sc[...] = jnp.zeros(acc_sc.shape, jnp.float32)
    q = q_ref[0]
    low = low_ref[0]
    high = high_ref[0]

    def body(step, carry):
        slot = step % 2
        for copy in copies(step, slot):
            copy.wait()

        @pl.when(step + 1 < count)
        def _():
            for copy in copies(step + 1, 1 - slot):
                copy.start()

        base = bases_ref[half * max_steps + step]
        keys = buf[slot, :, :head_width]
        values = buf[slot, :, head_width:]

        def update(masked):
            scores = lax.dot_general(
                q, keys, (((1,), (1,)), ((), ())), preferred_element_type=jnp.float32
            ) * SCALING
            if masked:
                places = base + lax.broadcasted_iota(jnp.int32, (1, pieces * tile), 1)
                visible = (places >= low) & (places <= high)
                scores = jnp.where(visible, scores, NEGATIVE)
            previous = m_sc[...]
            updated = jnp.maximum(previous, jnp.max(scores, axis=1, keepdims=True))
            factor = jnp.exp(previous - updated)
            weights = jnp.exp(scores - updated)
            l_sc[...] = l_sc[...] * factor + jnp.sum(weights, axis=1, keepdims=True)
            acc_sc[...] = acc_sc[...] * factor + jnp.dot(
                weights.astype(jnp.bfloat16), values, preferred_element_type=jnp.float32
            )
            m_sc[...] = updated

        full = (base >= limits_ref[2 * half]) & (base + pieces * tile - 1 <= limits_ref[2 * half + 1])

        @pl.when(full)
        def _():
            update(False)

        @pl.when(jnp.logical_not(full))
        def _():
            update(True)

        return carry

    lax.fori_loop(0, count, body, 0)
    o_ref[0] = (acc_sc[...] / l_sc[...]).astype(o_ref.dtype)


def single(queries, low, high, packed, steps, sources, bases, limits, max_steps, pieces):
    halves, tile, head_width = queries.shape
    kernel = functools.partial(
        single_kernel, max_steps=max_steps, head_width=head_width, pieces=pieces
    )
    row_spec = pl.BlockSpec((1, tile, head_width), lambda h, *refs: (h, 0, 0))
    bound_spec = pl.BlockSpec((1, tile, 1), lambda h, *refs: (h, 0, 0))
    return pl.pallas_call(
        kernel,
        out_shape=jax.ShapeDtypeStruct(queries.shape, jnp.bfloat16),
        grid_spec=pltpu.PrefetchScalarGridSpec(
            num_scalar_prefetch=4,
            grid=(halves,),
            in_specs=[row_spec, bound_spec, bound_spec, pl.BlockSpec(memory_space=pl.ANY)],
            out_specs=row_spec,
            scratch_shapes=[
                pltpu.VMEM((2, pieces * tile, packed.shape[1]), packed.dtype),
                pltpu.SemaphoreType.DMA((2, pieces)),
                pltpu.VMEM((tile, 1), jnp.float32),
                pltpu.VMEM((tile, 1), jnp.float32),
                pltpu.VMEM((tile, head_width), jnp.float32),
            ],
        ),
        compiler_params=pltpu.CompilerParams(dimension_semantics=("arbitrary",)),
        cost_estimate=pl.CostEstimate(
            flops=2 * halves * (max_steps // 2) * tile * pieces * tile * head_width * 2,
            transcendentals=halves * (max_steps // 2) * tile * pieces * tile,
            bytes_accessed=halves * (max_steps // 2) * pieces * tile * packed.shape[1] * 2,
        ),
    )(steps, sources, bases, limits, queries, low, high, packed)


def on_device(
    tokens,
    block_order,
    request_lengths,
    enc_lengths,
    w_qkv,
    w_out,
    enc_kv,
    w_cq,
    w_co,
    w_up,
    w_down,
    w_next,
):
    rows_here = tokens.shape[0]
    model_width = tokens.shape[1]
    group_size = lax.axis_size("head")
    cycle_size = lax.axis_size("zy") * lax.axis_size("x")
    block_rows = rows_here * group_size
    halfway = block_rows // 2
    group_width = w_qkv.shape[2]
    head_width = model_width // HEADS
    group_heads = group_width // head_width
    member = lax.axis_index("head")
    ring_size = lax.axis_size("x")
    ring_index = lax.axis_index("x")
    cycle_index = lax.axis_index("zy") * ring_size + ring_index
    full_out = lax.all_to_all(
        jnp.broadcast_to(w_out[None], (group_size,) + w_out.shape), "head", 0, 0, tiled=True
    ).reshape(model_width, model_width)
    gathered = lax.all_gather(tokens, "head", axis=0, tiled=True)
    projected = jnp.einsum(
        "td,cde->cte", gathered, w_qkv, preferred_element_type=jnp.float32
    ).astype(jnp.bfloat16)
    block_start = cycle_index * block_rows
    query_places = position_of(
        block_order, block_start + jnp.arange(block_rows, dtype=jnp.int32), halfway
    )
    slots = jnp.arange(2 * cycle_size, dtype=jnp.int32)
    holders = jnp.sum(jnp.where(block_order[:, None] == slots[None, :], slots[:, None], 0), axis=0)
    per_head = projected.reshape(3, block_rows, group_heads, head_width).transpose(2, 1, 0, 3)
    per_head = per_head.reshape(group_heads, block_rows, 3 * head_width)
    mine = lax.all_to_all(per_head, "x", 0, 0, tiled=True)
    packed = lax.all_gather(mine[:, :, head_width:], "zy", axis=0, tiled=True)
    packed = packed.reshape(cycle_size * block_rows, 2 * head_width)
    full_out, packed, late_kv = lax.optimization_barrier((full_out, packed, enc_kv))
    encoder = lax.all_gather(late_kv, ("zy", "x"), axis=1, tiled=True)
    ends = jnp.cumsum(request_lengths).astype(jnp.int32)
    starts = ends - request_lengths
    halves_here = 2 * ring_size
    first_half = lax.axis_index("zy") * halves_here
    pair = lax.dynamic_slice_in_dim(block_order, first_half, halves_here, 0)
    low_block = prefix_below(pair * halfway, ends, request_lengths) // halfway
    pieces = 8
    self_steps = (pair - low_block) // pieces + 1
    self_max = (2 * cycle_size + pieces - 1) // pieces
    firsts = low_block[:, None] + pieces * jnp.arange(self_max, dtype=jnp.int32)[None, :]
    self_sources = lookup(
        holders,
        jnp.minimum(firsts[:, :, None] + jnp.arange(pieces, dtype=jnp.int32), 2 * cycle_size - 1),
    ) * halfway
    places_here = (pair[:, None] * halfway + jnp.arange(halfway, dtype=jnp.int32)[None, :])
    self_low = prefix_below(places_here, ends, request_lengths).reshape(halves_here, halfway)
    limits = jnp.stack([self_low[:, -1], places_here[:, 0]], axis=1).reshape(-1)
    single_out = single(
        mine[:, :, :head_width].reshape(halves_here, halfway, head_width),
        self_low.reshape(halves_here, halfway, 1),
        places_here.reshape(halves_here, halfway, 1),
        packed,
        self_steps.astype(jnp.int32),
        self_sources.reshape(-1).astype(jnp.int32),
        (firsts * halfway).reshape(-1).astype(jnp.int32),
        limits.astype(jnp.int32),
        self_max,
        pieces,
    )
    owners = lax.all_to_all(
        single_out.reshape(ring_size * group_size, rows_here, head_width),
        ("x", "head"),
        0,
        0,
        tiled=True,
    )
    attended_rows = owners.reshape(ring_size, group_size, rows_here, head_width)
    attended_rows = attended_rows.transpose(2, 1, 0, 3).reshape(rows_here, model_width)
    group_blocks = lax.axis_index("zy") * ring_size + jnp.arange(ring_size, dtype=jnp.int32)
    cache_rows = lookup(
        holders, jnp.stack([2 * group_blocks, 2 * group_blocks + 1], axis=1)
    )
    cache_parts = jnp.stack(
        [
            jnp.concatenate(
                [
                    lax.dynamic_slice_in_dim(packed, cache_rows[i, 0] * halfway, halfway, 0),
                    lax.dynamic_slice_in_dim(packed, cache_rows[i, 1] * halfway, halfway, 0),
                ],
                axis=0,
            )
            for i in range(ring_size)
        ]
    )
    cache_heads = lax.all_to_all(cache_parts, "x", 0, 0, tiled=True)
    cache = cache_heads.reshape(group_heads, block_rows, 2, head_width).transpose(2, 1, 0, 3)
    cache = cache.reshape(2, block_rows, group_width)
    mixed = jnp.dot(attended_rows, full_out, preferred_element_type=jnp.float32)
    hidden = normalize(mixed + tokens.astype(jnp.float32))
    hidden_b = hidden.astype(jnp.bfloat16)
    own_query = jnp.dot(hidden_b, w_cq, preferred_element_type=jnp.float32).astype(jnp.bfloat16)
    cross_query = lax.all_to_all(
        own_query.reshape(rows_here, group_size, group_width).transpose(1, 0, 2),
        "head",
        0,
        0,
        tiled=True,
    ).reshape(block_rows, group_width)
    encoder_rows = encoder.shape[1]
    cross_max = (encoder_rows + halfway - 1 + 2 * halfway - 1) // (2 * halfway)
    padded_encoder = jnp.pad(
        encoder, ((0, 0), (0, cross_max * 2 * halfway + halfway - encoder_rows), (0, 0))
    )
    enc_low = prefix_below(query_places, ends, enc_lengths)
    enc_high = prefix_below(query_places, starts, enc_lengths) - 1
    cross_base = (enc_low.reshape(2, halfway)[:, 0] // halfway) * halfway
    cross_steps = (enc_high.reshape(2, halfway)[:, -1] + 1 - cross_base + 2 * halfway - 1) // (
        2 * halfway
    )
    cross_firsts = jnp.minimum(
        cross_base[:, None] + 2 * halfway * jnp.arange(cross_max, dtype=jnp.int32)[None, :],
        padded_encoder.shape[1] - 2 * halfway,
    )
    cross_sources = jnp.stack([cross_firsts, cross_firsts + halfway], axis=-1)
    crossed_group = flash(
        cross_query.reshape(2, halfway, group_width),
        enc_low.reshape(2, halfway, 1),
        enc_high.reshape(2, halfway, 1),
        padded_encoder[0],
        padded_encoder[1],
        cross_steps.astype(jnp.int32),
        cross_sources.reshape(-1).astype(jnp.int32),
        cross_firsts.reshape(-1).astype(jnp.int32),
        cross_max,
        group_heads,
    ).reshape(block_rows, group_width)
    exchanged = lax.all_to_all(
        crossed_group.reshape(group_size, rows_here, group_width), "head", 0, 0, tiled=True
    )
    crossed = exchanged.transpose(1, 0, 2).reshape(rows_here, model_width)
    summed = jnp.dot(crossed, w_co, preferred_element_type=jnp.float32)
    second = normalize(summed + hidden)
    second_b = second.astype(jnp.bfloat16)
    inner = jax.nn.gelu(
        jnp.dot(second_b, w_up, preferred_element_type=jnp.float32), approximate=False
    ).astype(jnp.bfloat16)
    output = normalize(jnp.dot(inner, w_down, preferred_element_type=jnp.float32) + second)
    output_b = output.astype(jnp.bfloat16)
    block_output = lax.all_gather(output_b, "head", axis=0, tiled=True)
    next_qkv = jnp.einsum("td,cde->cte", block_output, w_next, preferred_element_type=jnp.float32)
    return (output, cache, next_qkv)


def solution(mesh):
    ring = 4
    devices = mesh.devices.reshape(mesh.shape["blk"] // ring, ring, mesh.shape["head"])
    fine = jax.sharding.Mesh(devices, ("zy", "x", "head"))
    rows = ("zy", "x", "head")
    blocks = ("zy", "x")
    in_specs = (
        P(rows, None),
        P(),
        P(),
        P(),
        P(None, None, "head"),
        P("head", None),
        P(None, blocks, "head"),
        P(),
        P(),
        P(),
        P(),
        P(None, None, "head"),
    )
    out_specs = (P(rows, None), P(None, blocks, "head"), P(None, blocks, "head"))
    return jax.shard_map(
        on_device, mesh=fine, in_specs=in_specs, out_specs=out_specs, check_vma=False
    )
```

```python
import functools
import math

import jax
import jax.numpy as jnp
from jax import lax
from jax.experimental import pallas as pl
from jax.experimental.pallas import tpu as pltpu
from jax.sharding import PartitionSpec as P

HEADS = 16


NEGATIVE = -1e30
SCALING = 0.125
EPSILON = 1e-05


def normalize(matrix):
    center = matrix - jnp.mean(matrix, axis=-1, keepdims=True)
    return center * lax.rsqrt(jnp.mean(center * center, axis=-1, keepdims=True) + EPSILON)


def position_of(order_table, indices, halfway):
    slots = jnp.arange(order_table.shape[0], dtype=jnp.int32)
    picked = jnp.sum(
        jnp.where((indices // halfway)[:, None] == slots[None, :], order_table[None, :], 0), axis=1
    )
    return picked * halfway + indices % halfway


def group_of(places, lengths):
    ends = jnp.cumsum(lengths)
    return jnp.sum((places[:, None] >= ends[None, :]).astype(jnp.int32), axis=1)


def prefix_below(places, bounds, amounts):
    return jnp.sum(
        jnp.where(places[..., None] >= bounds, amounts, 0), axis=-1
    ).astype(jnp.int32)


def lookup(table, indices):
    slots = jnp.arange(table.shape[0], dtype=jnp.int32)
    return jnp.sum(jnp.where(indices[..., None] == slots, table, 0), axis=-1).astype(jnp.int32)


def online_update(carried, queries, key_rows, value_rows, visible):
    maxima, totals, running = carried
    heads_here = queries.shape[1]
    key_split = key_rows.reshape(key_rows.shape[0], heads_here, -1)
    value_split = value_rows.reshape(value_rows.shape[0], heads_here, -1)
    scores = (
        jnp.einsum("qhd,khd->qhk", queries, key_split, preferred_element_type=jnp.float32) * SCALING
    )
    scores = jnp.where(visible[:, None, :], scores, NEGATIVE)
    updated = jnp.maximum(maxima, jnp.max(scores, axis=2))
    factor = jnp.exp(maxima - updated)
    weights = jnp.exp(scores - updated[:, :, None])
    totals = totals * factor + jnp.sum(weights, axis=2)
    running = running * factor[:, :, None] + jnp.einsum(
        "qhk,khd->qhd",
        weights.astype(jnp.bfloat16),
        value_split,
        preferred_element_type=jnp.float32,
    )
    return (updated, totals, running)


def sweep(
    carried, queries, key_rows, value_rows, key_places, key_groups, query_places, query_groups
):
    length = key_rows.shape[0]
    block_size = math.gcd(length, 2048)
    blocks_count = length // block_size
    key_blocks = key_rows.reshape(blocks_count, block_size, key_rows.shape[1])
    value_blocks = value_rows.reshape(blocks_count, block_size, value_rows.shape[1])
    group_blocks = key_groups.reshape(blocks_count, block_size)
    if key_places is None:
        place_blocks = group_blocks
    else:
        place_blocks = key_places.reshape(blocks_count, block_size)

    def advance(status, element):
        key_block, value_block, place_block, group_block = element
        visible = group_block[None, :] == query_groups[:, None]
        if key_places is None:
            return (online_update(status, queries, key_block, value_block, visible), None)
        visible = visible & (place_block[None, :] <= query_places[:, None])
        updated = online_update(status, queries, key_block, value_block, visible)
        return (updated, None)

    carried, unused = lax.scan(
        advance, carried, (key_blocks, value_blocks, place_blocks, group_blocks)
    )
    return carried


def empty_state(count_q, heads_here, head_width):
    return (
        jnp.full((count_q, heads_here), NEGATIVE, jnp.float32),
        jnp.zeros((count_q, heads_here), jnp.float32),
        jnp.zeros((count_q, heads_here, head_width), jnp.float32),
    )


def finish(carried):
    maxima, totals, running = carried
    return (running / totals[:, :, None]).reshape(running.shape[0], -1).astype(jnp.bfloat16)


def flash_kernel(
    steps_ref, sources_ref, bases_ref, q_ref, low_ref, high_ref, k_hbm, v_hbm, o_ref,
    kbuf, vbuf, sem, qm_sc, m_sc, l_sc, acc_sc, *, max_steps, heads, head_width
):
    half = pl.program_id(0)
    count = steps_ref[half]
    tile = kbuf.shape[1] // 2
    width = kbuf.shape[2]

    def copies(step, slot):
        result = []
        for j in range(2):
            source = pl.multiple_of(sources_ref[(half * max_steps + step) * 2 + j], tile)
            window = pl.ds(j * tile, tile)
            result.append(pltpu.make_async_copy(
                k_hbm.at[pl.ds(source, tile)], kbuf.at[slot, window], sem.at[0, slot, j]))
            result.append(pltpu.make_async_copy(
                v_hbm.at[pl.ds(source, tile)], vbuf.at[slot, window], sem.at[1, slot, j]))
        return result

    for copy in copies(0, 0):
        copy.start()
    column_head = lax.broadcasted_iota(jnp.int32, (1, width), 1) // head_width
    q = q_ref[0]
    for h in range(heads):
        qm_sc[h] = jnp.where(column_head == h, q, jnp.zeros_like(q))
    m_sc[...] = jnp.full(m_sc.shape, NEGATIVE, jnp.float32)
    l_sc[...] = jnp.zeros(l_sc.shape, jnp.float32)
    acc_sc[...] = jnp.zeros(acc_sc.shape, jnp.float32)
    low = low_ref[0]
    high = high_ref[0]

    def body(step, carry):
        slot = step % 2
        for copy in copies(step, slot):
            copy.wait()

        @pl.when(step + 1 < count)
        def _():
            for copy in copies(step + 1, 1 - slot):
                copy.start()

        base = bases_ref[half * max_steps + step]
        places = base + lax.broadcasted_iota(jnp.int32, (1, 2 * tile), 1)
        visible = (places >= low) & (places <= high)
        keys = kbuf[slot]
        values = vbuf[slot]
        for h in range(heads):
            scores = lax.dot_general(
                qm_sc[h], keys, (((1,), (1,)), ((), ())), preferred_element_type=jnp.float32
            ) * SCALING
            scores = jnp.where(visible, scores, NEGATIVE)
            previous = m_sc[h]
            updated = jnp.maximum(previous, jnp.max(scores, axis=1, keepdims=True))
            factor = jnp.exp(previous - updated)
            weights = jnp.exp(scores - updated)
            l_sc[h] = l_sc[h] * factor + jnp.sum(weights, axis=1, keepdims=True)
            acc_sc[h] = acc_sc[h] * factor + jnp.dot(
                weights.astype(jnp.bfloat16), values, preferred_element_type=jnp.float32
            )
            m_sc[h] = updated
        return carry

    lax.fori_loop(0, count, body, 0)
    out = jnp.zeros(acc_sc.shape[1:], jnp.float32)
    for h in range(heads):
        out = jnp.where(column_head == h, acc_sc[h] / l_sc[h], out)
    o_ref[0] = out.astype(o_ref.dtype)


def flash(queries, low, high, keys, values, steps, sources, bases, max_steps, heads):
    halves, tile, width = queries.shape
    head_width = width // heads
    kernel = functools.partial(
        flash_kernel, max_steps=max_steps, heads=heads, head_width=head_width
    )
    row_spec = pl.BlockSpec((1, tile, width), lambda h, *refs: (h, 0, 0))
    bound_spec = pl.BlockSpec((1, tile, 1), lambda h, *refs: (h, 0, 0))
    flops = 4 * halves * max_steps * tile * 2 * tile * width * heads
    return pl.pallas_call(
        kernel,
        out_shape=jax.ShapeDtypeStruct(queries.shape, jnp.bfloat16),
        grid_spec=pltpu.PrefetchScalarGridSpec(
            num_scalar_prefetch=3,
            grid=(halves,),
            in_specs=[
                row_spec,
                bound_spec,
                bound_spec,
                pl.BlockSpec(memory_space=pl.ANY),
                pl.BlockSpec(memory_space=pl.ANY),
            ],
            out_specs=row_spec,
            scratch_shapes=[
                pltpu.VMEM((2, 2 * tile, width), keys.dtype),
                pltpu.VMEM((2, 2 * tile, width), values.dtype),
                pltpu.SemaphoreType.DMA((2, 2, 2)),
                pltpu.VMEM((heads, tile, width), jnp.bfloat16),
                pltpu.VMEM((heads, tile, 1), jnp.float32),
                pltpu.VMEM((heads, tile, 1), jnp.float32),
                pltpu.VMEM((heads, tile, width), jnp.float32),
            ],
        ),
        compiler_params=pltpu.CompilerParams(dimension_semantics=("arbitrary",)),
        cost_estimate=pl.CostEstimate(
            flops=flops,
            transcendentals=halves * max_steps * tile * 2 * tile * heads,
            bytes_accessed=halves * max_steps * 2 * 2 * tile * width * 2,
        ),
    )(steps, sources, bases, queries, low, high, keys, values)


def single_kernel(
    steps_ref, sources_ref, bases_ref, limits_ref, q_ref, low_ref, high_ref, kv_hbm, o_ref,
    buf, sem, m_sc, l_sc, acc_sc, *, max_steps, head_width, pieces
):
    half = pl.program_id(0)
    count = steps_ref[half]
    tile = buf.shape[1] // pieces

    def copies(step, slot):
        result = []
        for j in range(pieces):
            source = pl.multiple_of(sources_ref[(half * max_steps + step) * pieces + j], tile)
            result.append(pltpu.make_async_copy(
                kv_hbm.at[pl.ds(source, tile)], buf.at[slot, pl.ds(j * tile, tile)], sem.at[slot, j]))
        return result

    for copy in copies(0, 0):
        copy.start()
    m_sc[...] = jnp.full(m_sc.shape, NEGATIVE, jnp.float32)
    l_sc[...] = jnp.zeros(l_sc.shape, jnp.float32)
    acc_sc[...] = jnp.zeros(acc_sc.shape, jnp.float32)
    q = q_ref[0]
    low = low_ref[0]
    high = high_ref[0]

    def body(step, carry):
        slot = step % 2
        for copy in copies(step, slot):
            copy.wait()

        @pl.when(step + 1 < count)
        def _():
            for copy in copies(step + 1, 1 - slot):
                copy.start()

        base = bases_ref[half * max_steps + step]
        keys = buf[slot, :, :head_width]
        values = buf[slot, :, head_width:]

        def update(masked):
            scores = lax.dot_general(
                q, keys, (((1,), (1,)), ((), ())), preferred_element_type=jnp.float32
            ) * SCALING
            if masked:
                places = base + lax.broadcasted_iota(jnp.int32, (1, pieces * tile), 1)
                visible = (places >= low) & (places <= high)
                scores = jnp.where(visible, scores, NEGATIVE)
            previous = m_sc[...]
            updated = jnp.maximum(previous, jnp.max(scores, axis=1, keepdims=True))
            factor = jnp.exp(previous - updated)
            weights = jnp.exp(scores - updated)
            l_sc[...] = l_sc[...] * factor + jnp.sum(weights, axis=1, keepdims=True)
            acc_sc[...] = acc_sc[...] * factor + jnp.dot(
                weights.astype(jnp.bfloat16), values, preferred_element_type=jnp.float32
            )
            m_sc[...] = updated

        full = (base >= limits_ref[2 * half]) & (base + pieces * tile - 1 <= limits_ref[2 * half + 1])

        @pl.when(full)
        def _():
            update(False)

        @pl.when(jnp.logical_not(full))
        def _():
            update(True)

        return carry

    lax.fori_loop(0, count, body, 0)
    o_ref[0] = (acc_sc[...] / l_sc[...]).astype(o_ref.dtype)


def single(queries, low, high, packed, steps, sources, bases, limits, max_steps, pieces):
    halves, tile, head_width = queries.shape
    kernel = functools.partial(
        single_kernel, max_steps=max_steps, head_width=head_width, pieces=pieces
    )
    row_spec = pl.BlockSpec((1, tile, head_width), lambda h, *refs: (h, 0, 0))
    bound_spec = pl.BlockSpec((1, tile, 1), lambda h, *refs: (h, 0, 0))
    return pl.pallas_call(
        kernel,
        out_shape=jax.ShapeDtypeStruct(queries.shape, jnp.bfloat16),
        grid_spec=pltpu.PrefetchScalarGridSpec(
            num_scalar_prefetch=4,
            grid=(halves,),
            in_specs=[row_spec, bound_spec, bound_spec, pl.BlockSpec(memory_space=pl.ANY)],
            out_specs=row_spec,
            scratch_shapes=[
                pltpu.VMEM((2, pieces * tile, packed.shape[1]), packed.dtype),
                pltpu.SemaphoreType.DMA((2, pieces)),
                pltpu.VMEM((tile, 1), jnp.float32),
                pltpu.VMEM((tile, 1), jnp.float32),
                pltpu.VMEM((tile, head_width), jnp.float32),
            ],
        ),
        compiler_params=pltpu.CompilerParams(dimension_semantics=("arbitrary",)),
        cost_estimate=pl.CostEstimate(
            flops=2 * halves * (max_steps // 2) * tile * pieces * tile * head_width * 2,
            transcendentals=halves * (max_steps // 2) * tile * pieces * tile,
            bytes_accessed=halves * (max_steps // 2) * pieces * tile * packed.shape[1] * 2,
        ),
    )(steps, sources, bases, limits, queries, low, high, packed)


def on_device(
    tokens,
    block_order,
    request_lengths,
    enc_lengths,
    w_qkv,
    w_out,
    enc_kv,
    w_cq,
    w_co,
    w_up,
    w_down,
    w_next,
):
    rows_here = tokens.shape[0]
    model_width = tokens.shape[1]
    group_size = lax.axis_size("head")
    cycle_size = lax.axis_size("zy") * lax.axis_size("x")
    block_rows = rows_here * group_size
    halfway = block_rows // 2
    group_width = w_qkv.shape[2]
    head_width = model_width // HEADS
    group_heads = group_width // head_width
    member = lax.axis_index("head")
    ring_size = lax.axis_size("x")
    ring_index = lax.axis_index("x")
    cycle_index = lax.axis_index("zy") * ring_size + ring_index
    full_out = lax.all_to_all(
        jnp.broadcast_to(w_out[None], (group_size,) + w_out.shape), "head", 0, 0, tiled=True
    ).reshape(model_width, model_width)
    enc_all = lax.all_to_all(
        jnp.broadcast_to(enc_kv[None], (cycle_size,) + enc_kv.shape), ("zy", "x"), 0, 0, tiled=True
    )
    gathered = lax.all_gather(tokens, "head", axis=0, tiled=True)
    projected = jnp.einsum(
        "td,cde->cte", gathered, w_qkv, preferred_element_type=jnp.float32
    ).astype(jnp.bfloat16)
    block_start = cycle_index * block_rows
    query_places = position_of(
        block_order, block_start + jnp.arange(block_rows, dtype=jnp.int32), halfway
    )
    slots = jnp.arange(2 * cycle_size, dtype=jnp.int32)
    holders = jnp.sum(jnp.where(block_order[:, None] == slots[None, :], slots[:, None], 0), axis=0)
    per_head = projected.reshape(3, block_rows, group_heads, head_width).transpose(2, 1, 0, 3)
    per_head = per_head.reshape(group_heads, block_rows, 3 * head_width)
    mine = lax.all_to_all(per_head, "x", 0, 0, tiled=True)
    packed = lax.all_gather(mine[:, :, head_width:], "zy", axis=0, tiled=True)
    packed = packed.reshape(cycle_size * block_rows, 2 * head_width)
    full_out, packed, enc_all = lax.optimization_barrier((full_out, packed, enc_all))
    encoder = enc_all.transpose(1, 0, 2, 3).reshape(
        2, cycle_size * enc_kv.shape[1], enc_kv.shape[2]
    )
    ends = jnp.cumsum(request_lengths).astype(jnp.int32)
    starts = ends - request_lengths
    halves_here = 2 * ring_size
    first_half = lax.axis_index("zy") * halves_here
    pair = lax.dynamic_slice_in_dim(block_order, first_half, halves_here, 0)
    low_block = prefix_below(pair * halfway, ends, request_lengths) // halfway
    pieces = 8
    self_steps = (pair - low_block) // pieces + 1
    self_max = (2 * cycle_size + pieces - 1) // pieces
    firsts = low_block[:, None] + pieces * jnp.arange(self_max, dtype=jnp.int32)[None, :]
    self_sources = lookup(
        holders,
        jnp.minimum(firsts[:, :, None] + jnp.arange(pieces, dtype=jnp.int32), 2 * cycle_size - 1),
    ) * halfway
    places_here = (pair[:, None] * halfway + jnp.arange(halfway, dtype=jnp.int32)[None, :])
    self_low = prefix_below(places_here, ends, request_lengths).reshape(halves_here, halfway)
    limits = jnp.stack([self_low[:, -1], places_here[:, 0]], axis=1).reshape(-1)
    single_out = single(
        mine[:, :, :head_width].reshape(halves_here, halfway, head_width),
        self_low.reshape(halves_here, halfway, 1),
        places_here.reshape(halves_here, halfway, 1),
        packed,
        self_steps.astype(jnp.int32),
        self_sources.reshape(-1).astype(jnp.int32),
        (firsts * halfway).reshape(-1).astype(jnp.int32),
        limits.astype(jnp.int32),
        self_max,
        pieces,
    )
    owners = lax.all_to_all(
        single_out.reshape(ring_size * group_size, rows_here, head_width),
        ("x", "head"),
        0,
        0,
        tiled=True,
    )
    attended_rows = owners.reshape(ring_size, group_size, rows_here, head_width)
    attended_rows = attended_rows.transpose(2, 1, 0, 3).reshape(rows_here, model_width)
    group_blocks = lax.axis_index("zy") * ring_size + jnp.arange(ring_size, dtype=jnp.int32)
    cache_rows = lookup(
        holders, jnp.stack([2 * group_blocks, 2 * group_blocks + 1], axis=1)
    )
    cache_parts = jnp.stack(
        [
            jnp.concatenate(
                [
                    lax.dynamic_slice_in_dim(packed, cache_rows[i, 0] * halfway, halfway, 0),
                    lax.dynamic_slice_in_dim(packed, cache_rows[i, 1] * halfway, halfway, 0),
                ],
                axis=0,
            )
            for i in range(ring_size)
        ]
    )
    cache_heads = lax.all_to_all(cache_parts, "x", 0, 0, tiled=True)
    cache = cache_heads.reshape(group_heads, block_rows, 2, head_width).transpose(2, 1, 0, 3)
    cache = cache.reshape(2, block_rows, group_width)
    mixed = jnp.dot(attended_rows, full_out, preferred_element_type=jnp.float32)
    hidden = normalize(mixed + tokens.astype(jnp.float32))
    hidden_b = hidden.astype(jnp.bfloat16)
    own_query = jnp.dot(hidden_b, w_cq, preferred_element_type=jnp.float32).astype(jnp.bfloat16)
    cross_query = lax.all_to_all(
        own_query.reshape(rows_here, group_size, group_width).transpose(1, 0, 2),
        "head",
        0,
        0,
        tiled=True,
    ).reshape(block_rows, group_width)
    encoder_rows = encoder.shape[1]
    cross_max = (encoder_rows + halfway - 1 + 2 * halfway - 1) // (2 * halfway)
    padded_encoder = jnp.pad(
        encoder, ((0, 0), (0, cross_max * 2 * halfway + halfway - encoder_rows), (0, 0))
    )
    enc_low = prefix_below(query_places, ends, enc_lengths)
    enc_high = prefix_below(query_places, starts, enc_lengths) - 1
    cross_base = (enc_low.reshape(2, halfway)[:, 0] // halfway) * halfway
    cross_steps = (enc_high.reshape(2, halfway)[:, -1] + 1 - cross_base + 2 * halfway - 1) // (
        2 * halfway
    )
    cross_firsts = jnp.minimum(
        cross_base[:, None] + 2 * halfway * jnp.arange(cross_max, dtype=jnp.int32)[None, :],
        padded_encoder.shape[1] - 2 * halfway,
    )
    cross_sources = jnp.stack([cross_firsts, cross_firsts + halfway], axis=-1)
    crossed_group = flash(
        cross_query.reshape(2, halfway, group_width),
        enc_low.reshape(2, halfway, 1),
        enc_high.reshape(2, halfway, 1),
        padded_encoder[0],
        padded_encoder[1],
        cross_steps.astype(jnp.int32),
        cross_sources.reshape(-1).astype(jnp.int32),
        cross_firsts.reshape(-1).astype(jnp.int32),
        cross_max,
        group_heads,
    ).reshape(block_rows, group_width)
    exchanged = lax.all_to_all(
        crossed_group.reshape(group_size, rows_here, group_width), "head", 0, 0, tiled=True
    )
    crossed = exchanged.transpose(1, 0, 2).reshape(rows_here, model_width)
    summed = jnp.dot(crossed, w_co, preferred_element_type=jnp.float32)
    second = normalize(summed + hidden)
    second_b = second.astype(jnp.bfloat16)
    inner = jax.nn.gelu(
        jnp.dot(second_b, w_up, preferred_element_type=jnp.float32), approximate=False
    ).astype(jnp.bfloat16)
    output = normalize(jnp.dot(inner, w_down, preferred_element_type=jnp.float32) + second)
    output_b = output.astype(jnp.bfloat16)
    block_output = lax.all_gather(output_b, "head", axis=0, tiled=True)
    next_qkv = jnp.einsum("td,cde->cte", block_output, w_next, preferred_element_type=jnp.float32)
    return (output, cache, next_qkv)


def solution(mesh):
    ring = 4
    devices = mesh.devices.reshape(mesh.shape["blk"] // ring, ring, mesh.shape["head"])
    fine = jax.sharding.Mesh(devices, ("zy", "x", "head"))
    rows = ("zy", "x", "head")
    blocks = ("zy", "x")
    in_specs = (
        P(rows, None),
        P(),
        P(),
        P(),
        P(None, None, "head"),
        P("head", None),
        P(None, blocks, "head"),
        P(),
        P(),
        P(),
        P(),
        P(None, None, "head"),
    )
    out_specs = (P(rows, None), P(None, blocks, "head"), P(None, blocks, "head"))
    return jax.shard_map(
        on_device, mesh=fine, in_specs=in_specs, out_specs=out_specs, check_vma=False
    )
```

```python
import functools
import math

import jax
import jax.numpy as jnp
from jax import lax
from jax.experimental import pallas as pl
from jax.experimental.pallas import tpu as pltpu
from jax.sharding import PartitionSpec as P

HEADS = 16


NEGATIVE = -1e30
SCALING = 0.125
EPSILON = 1e-05


def normalize(matrix):
    center = matrix - jnp.mean(matrix, axis=-1, keepdims=True)
    return center * lax.rsqrt(jnp.mean(center * center, axis=-1, keepdims=True) + EPSILON)


def position_of(order_table, indices, halfway):
    slots = jnp.arange(order_table.shape[0], dtype=jnp.int32)
    picked = jnp.sum(
        jnp.where((indices // halfway)[:, None] == slots[None, :], order_table[None, :], 0), axis=1
    )
    return picked * halfway + indices % halfway


def group_of(places, lengths):
    ends = jnp.cumsum(lengths)
    return jnp.sum((places[:, None] >= ends[None, :]).astype(jnp.int32), axis=1)


def prefix_below(places, bounds, amounts):
    return jnp.sum(
        jnp.where(places[..., None] >= bounds, amounts, 0), axis=-1
    ).astype(jnp.int32)


def lookup(table, indices):
    slots = jnp.arange(table.shape[0], dtype=jnp.int32)
    return jnp.sum(jnp.where(indices[..., None] == slots, table, 0), axis=-1).astype(jnp.int32)


def online_update(carried, queries, key_rows, value_rows, visible):
    maxima, totals, running = carried
    heads_here = queries.shape[1]
    key_split = key_rows.reshape(key_rows.shape[0], heads_here, -1)
    value_split = value_rows.reshape(value_rows.shape[0], heads_here, -1)
    scores = (
        jnp.einsum("qhd,khd->qhk", queries, key_split, preferred_element_type=jnp.float32) * SCALING
    )
    scores = jnp.where(visible[:, None, :], scores, NEGATIVE)
    updated = jnp.maximum(maxima, jnp.max(scores, axis=2))
    factor = jnp.exp(maxima - updated)
    weights = jnp.exp(scores - updated[:, :, None])
    totals = totals * factor + jnp.sum(weights, axis=2)
    running = running * factor[:, :, None] + jnp.einsum(
        "qhk,khd->qhd",
        weights.astype(jnp.bfloat16),
        value_split,
        preferred_element_type=jnp.float32,
    )
    return (updated, totals, running)


def sweep(
    carried, queries, key_rows, value_rows, key_places, key_groups, query_places, query_groups
):
    length = key_rows.shape[0]
    block_size = math.gcd(length, 2048)
    blocks_count = length // block_size
    key_blocks = key_rows.reshape(blocks_count, block_size, key_rows.shape[1])
    value_blocks = value_rows.reshape(blocks_count, block_size, value_rows.shape[1])
    group_blocks = key_groups.reshape(blocks_count, block_size)
    if key_places is None:
        place_blocks = group_blocks
    else:
        place_blocks = key_places.reshape(blocks_count, block_size)

    def advance(status, element):
        key_block, value_block, place_block, group_block = element
        visible = group_block[None, :] == query_groups[:, None]
        if key_places is None:
            return (online_update(status, queries, key_block, value_block, visible), None)
        visible = visible & (place_block[None, :] <= query_places[:, None])
        updated = online_update(status, queries, key_block, value_block, visible)
        return (updated, None)

    carried, unused = lax.scan(
        advance, carried, (key_blocks, value_blocks, place_blocks, group_blocks)
    )
    return carried


def empty_state(count_q, heads_here, head_width):
    return (
        jnp.full((count_q, heads_here), NEGATIVE, jnp.float32),
        jnp.zeros((count_q, heads_here), jnp.float32),
        jnp.zeros((count_q, heads_here, head_width), jnp.float32),
    )


def finish(carried):
    maxima, totals, running = carried
    return (running / totals[:, :, None]).reshape(running.shape[0], -1).astype(jnp.bfloat16)


def flash_kernel(
    steps_ref, sources_ref, bases_ref, q_ref, low_ref, high_ref, k_hbm, v_hbm, o_ref,
    kbuf, vbuf, sem, qm_sc, m_sc, l_sc, acc_sc, *, max_steps, heads, head_width
):
    half = pl.program_id(0)
    count = steps_ref[half]
    tile = kbuf.shape[1] // 2
    width = kbuf.shape[2]

    def copies(step, slot):
        result = []
        for j in range(2):
            source = pl.multiple_of(sources_ref[(half * max_steps + step) * 2 + j], tile)
            window = pl.ds(j * tile, tile)
            result.append(pltpu.make_async_copy(
                k_hbm.at[pl.ds(source, tile)], kbuf.at[slot, window], sem.at[0, slot, j]))
            result.append(pltpu.make_async_copy(
                v_hbm.at[pl.ds(source, tile)], vbuf.at[slot, window], sem.at[1, slot, j]))
        return result

    for copy in copies(0, 0):
        copy.start()
    column_head = lax.broadcasted_iota(jnp.int32, (1, width), 1) // head_width
    q = q_ref[0]
    for h in range(heads):
        qm_sc[h] = jnp.where(column_head == h, q, jnp.zeros_like(q))
    m_sc[...] = jnp.full(m_sc.shape, NEGATIVE, jnp.float32)
    l_sc[...] = jnp.zeros(l_sc.shape, jnp.float32)
    acc_sc[...] = jnp.zeros(acc_sc.shape, jnp.float32)
    low = low_ref[0]
    high = high_ref[0]

    def body(step, carry):
        slot = step % 2
        for copy in copies(step, slot):
            copy.wait()

        @pl.when(step + 1 < count)
        def _():
            for copy in copies(step + 1, 1 - slot):
                copy.start()

        base = bases_ref[half * max_steps + step]
        places = base + lax.broadcasted_iota(jnp.int32, (1, 2 * tile), 1)
        visible = (places >= low) & (places <= high)
        keys = kbuf[slot]
        values = vbuf[slot]
        for h in range(heads):
            scores = lax.dot_general(
                qm_sc[h], keys, (((1,), (1,)), ((), ())), preferred_element_type=jnp.float32
            ) * SCALING
            scores = jnp.where(visible, scores, NEGATIVE)
            previous = m_sc[h]
            updated = jnp.maximum(previous, jnp.max(scores, axis=1, keepdims=True))
            factor = jnp.exp(previous - updated)
            weights = jnp.exp(scores - updated)
            l_sc[h] = l_sc[h] * factor + jnp.sum(weights, axis=1, keepdims=True)
            acc_sc[h] = acc_sc[h] * factor + jnp.dot(
                weights.astype(jnp.bfloat16), values, preferred_element_type=jnp.float32
            )
            m_sc[h] = updated
        return carry

    lax.fori_loop(0, count, body, 0)
    out = jnp.zeros(acc_sc.shape[1:], jnp.float32)
    for h in range(heads):
        out = jnp.where(column_head == h, acc_sc[h] / l_sc[h], out)
    o_ref[0] = out.astype(o_ref.dtype)


def flash(queries, low, high, keys, values, steps, sources, bases, max_steps, heads):
    halves, tile, width = queries.shape
    head_width = width // heads
    kernel = functools.partial(
        flash_kernel, max_steps=max_steps, heads=heads, head_width=head_width
    )
    row_spec = pl.BlockSpec((1, tile, width), lambda h, *refs: (h, 0, 0))
    bound_spec = pl.BlockSpec((1, tile, 1), lambda h, *refs: (h, 0, 0))
    flops = 4 * halves * max_steps * tile * 2 * tile * width * heads
    return pl.pallas_call(
        kernel,
        out_shape=jax.ShapeDtypeStruct(queries.shape, jnp.bfloat16),
        grid_spec=pltpu.PrefetchScalarGridSpec(
            num_scalar_prefetch=3,
            grid=(halves,),
            in_specs=[
                row_spec,
                bound_spec,
                bound_spec,
                pl.BlockSpec(memory_space=pl.ANY),
                pl.BlockSpec(memory_space=pl.ANY),
            ],
            out_specs=row_spec,
            scratch_shapes=[
                pltpu.VMEM((2, 2 * tile, width), keys.dtype),
                pltpu.VMEM((2, 2 * tile, width), values.dtype),
                pltpu.SemaphoreType.DMA((2, 2, 2)),
                pltpu.VMEM((heads, tile, width), jnp.bfloat16),
                pltpu.VMEM((heads, tile, 1), jnp.float32),
                pltpu.VMEM((heads, tile, 1), jnp.float32),
                pltpu.VMEM((heads, tile, width), jnp.float32),
            ],
        ),
        compiler_params=pltpu.CompilerParams(dimension_semantics=("arbitrary",)),
        cost_estimate=pl.CostEstimate(
            flops=flops,
            transcendentals=halves * max_steps * tile * 2 * tile * heads,
            bytes_accessed=halves * max_steps * 2 * 2 * tile * width * 2,
        ),
    )(steps, sources, bases, queries, low, high, keys, values)


def single_kernel(
    steps_ref, sources_ref, bases_ref, limits_ref, q_ref, low_ref, high_ref, kv_hbm, o_ref,
    buf, sem, m_sc, l_sc, acc_sc, *, max_steps, head_width, pieces
):
    half = pl.program_id(0)
    count = steps_ref[half]
    tile = buf.shape[1] // pieces

    def copies(step, slot):
        result = []
        for j in range(pieces):
            source = pl.multiple_of(sources_ref[(half * max_steps + step) * pieces + j], tile)
            result.append(pltpu.make_async_copy(
                kv_hbm.at[pl.ds(source, tile)], buf.at[slot, pl.ds(j * tile, tile)], sem.at[slot, j]))
        return result

    for copy in copies(0, 0):
        copy.start()
    m_sc[...] = jnp.full(m_sc.shape, NEGATIVE, jnp.float32)
    l_sc[...] = jnp.zeros(l_sc.shape, jnp.float32)
    acc_sc[...] = jnp.zeros(acc_sc.shape, jnp.float32)
    q = q_ref[0]
    low = low_ref[0]
    high = high_ref[0]

    def body(step, carry):
        slot = step % 2
        for copy in copies(step, slot):
            copy.wait()

        @pl.when(step + 1 < count)
        def _():
            for copy in copies(step + 1, 1 - slot):
                copy.start()

        base = bases_ref[half * max_steps + step]
        keys = buf[slot, :, :head_width]
        values = buf[slot, :, head_width:]

        def update(masked):
            scores = lax.dot_general(
                q, keys, (((1,), (1,)), ((), ())), preferred_element_type=jnp.float32
            ) * SCALING
            if masked:
                places = base + lax.broadcasted_iota(jnp.int32, (1, pieces * tile), 1)
                visible = (places >= low) & (places <= high)
                scores = jnp.where(visible, scores, NEGATIVE)
            previous = m_sc[...]
            updated = jnp.maximum(previous, jnp.max(scores, axis=1, keepdims=True))
            factor = jnp.exp(previous - updated)
            weights = jnp.exp(scores - updated)
            l_sc[...] = l_sc[...] * factor + jnp.sum(weights, axis=1, keepdims=True)
            acc_sc[...] = acc_sc[...] * factor + jnp.dot(
                weights.astype(jnp.bfloat16), values, preferred_element_type=jnp.float32
            )
            m_sc[...] = updated

        full = (base >= limits_ref[2 * half]) & (base + pieces * tile - 1 <= limits_ref[2 * half + 1])

        @pl.when(full)
        def _():
            update(False)

        @pl.when(jnp.logical_not(full))
        def _():
            update(True)

        return carry

    lax.fori_loop(0, count, body, 0)
    o_ref[0] = (acc_sc[...] / l_sc[...]).astype(o_ref.dtype)


def single(queries, low, high, packed, steps, sources, bases, limits, max_steps, pieces):
    halves, tile, head_width = queries.shape
    kernel = functools.partial(
        single_kernel, max_steps=max_steps, head_width=head_width, pieces=pieces
    )
    row_spec = pl.BlockSpec((1, tile, head_width), lambda h, *refs: (h, 0, 0))
    bound_spec = pl.BlockSpec((1, tile, 1), lambda h, *refs: (h, 0, 0))
    return pl.pallas_call(
        kernel,
        out_shape=jax.ShapeDtypeStruct(queries.shape, jnp.bfloat16),
        grid_spec=pltpu.PrefetchScalarGridSpec(
            num_scalar_prefetch=4,
            grid=(halves,),
            in_specs=[row_spec, bound_spec, bound_spec, pl.BlockSpec(memory_space=pl.ANY)],
            out_specs=row_spec,
            scratch_shapes=[
                pltpu.VMEM((2, pieces * tile, packed.shape[1]), packed.dtype),
                pltpu.SemaphoreType.DMA((2, pieces)),
                pltpu.VMEM((tile, 1), jnp.float32),
                pltpu.VMEM((tile, 1), jnp.float32),
                pltpu.VMEM((tile, head_width), jnp.float32),
            ],
        ),
        compiler_params=pltpu.CompilerParams(dimension_semantics=("arbitrary",)),
        cost_estimate=pl.CostEstimate(
            flops=2 * halves * (max_steps // 2) * tile * pieces * tile * head_width * 2,
            transcendentals=halves * (max_steps // 2) * tile * pieces * tile,
            bytes_accessed=halves * (max_steps // 2) * pieces * tile * packed.shape[1] * 2,
        ),
    )(steps, sources, bases, limits, queries, low, high, packed)


def on_device(
    tokens,
    block_order,
    request_lengths,
    enc_lengths,
    w_qkv,
    w_out,
    enc_kv,
    w_cq,
    w_co,
    w_up,
    w_down,
    w_next,
):
    rows_here = tokens.shape[0]
    model_width = tokens.shape[1]
    group_size = lax.axis_size("head")
    cycle_size = lax.axis_size("zy") * lax.axis_size("x")
    block_rows = rows_here * group_size
    halfway = block_rows // 2
    group_width = w_qkv.shape[2]
    head_width = model_width // HEADS
    group_heads = group_width // head_width
    member = lax.axis_index("head")
    ring_size = lax.axis_size("x")
    ring_index = lax.axis_index("x")
    cycle_index = lax.axis_index("zy") * ring_size + ring_index
    full_out = lax.all_to_all(
        jnp.broadcast_to(w_out[None], (group_size,) + w_out.shape), "head", 0, 0, tiled=True
    ).reshape(model_width, model_width)
    gathered = lax.all_gather(tokens, "head", axis=0, tiled=True)
    projected = jnp.einsum(
        "td,cde->cte", gathered, w_qkv, preferred_element_type=jnp.float32
    ).astype(jnp.bfloat16)
    block_start = cycle_index * block_rows
    query_places = position_of(
        block_order, block_start + jnp.arange(block_rows, dtype=jnp.int32), halfway
    )
    slots = jnp.arange(2 * cycle_size, dtype=jnp.int32)
    holders = jnp.sum(jnp.where(block_order[:, None] == slots[None, :], slots[:, None], 0), axis=0)
    per_head = projected.reshape(3, block_rows, group_heads, head_width).transpose(2, 1, 0, 3)
    per_head = per_head.reshape(group_heads, block_rows, 3 * head_width)
    mine = lax.all_to_all(per_head, "x", 0, 0, tiled=True)
    packed = lax.all_gather(mine[:, :, head_width:], "zy", axis=0, tiled=True)
    packed = packed.reshape(cycle_size * block_rows, 2 * head_width)
    full_out, packed = lax.optimization_barrier((full_out, packed))
    ends = jnp.cumsum(request_lengths).astype(jnp.int32)
    starts = ends - request_lengths
    halves_here = 2 * ring_size
    first_half = lax.axis_index("zy") * halves_here
    pair = lax.dynamic_slice_in_dim(block_order, first_half, halves_here, 0)
    low_block = prefix_below(pair * halfway, ends, request_lengths) // halfway
    pieces = 8
    self_steps = (pair - low_block) // pieces + 1
    self_max = (2 * cycle_size + pieces - 1) // pieces
    firsts = low_block[:, None] + pieces * jnp.arange(self_max, dtype=jnp.int32)[None, :]
    self_sources = lookup(
        holders,
        jnp.minimum(firsts[:, :, None] + jnp.arange(pieces, dtype=jnp.int32), 2 * cycle_size - 1),
    ) * halfway
    places_here = (pair[:, None] * halfway + jnp.arange(halfway, dtype=jnp.int32)[None, :])
    self_low = prefix_below(places_here, ends, request_lengths).reshape(halves_here, halfway)
    limits = jnp.stack([self_low[:, -1], places_here[:, 0]], axis=1).reshape(-1)
    single_out = single(
        mine[:, :, :head_width].reshape(halves_here, halfway, head_width),
        self_low.reshape(halves_here, halfway, 1),
        places_here.reshape(halves_here, halfway, 1),
        packed,
        self_steps.astype(jnp.int32),
        self_sources.reshape(-1).astype(jnp.int32),
        (firsts * halfway).reshape(-1).astype(jnp.int32),
        limits.astype(jnp.int32),
        self_max,
        pieces,
    )
    single_out, late_kv = lax.optimization_barrier((single_out, enc_kv))
    enc_all = lax.all_to_all(
        jnp.broadcast_to(late_kv[None], (cycle_size,) + enc_kv.shape), ("zy", "x"), 0, 0, tiled=True
    )
    encoder = enc_all.transpose(1, 0, 2, 3).reshape(
        2, cycle_size * enc_kv.shape[1], enc_kv.shape[2]
    )
    owners = lax.all_to_all(
        single_out.reshape(ring_size * group_size, rows_here, head_width),
        ("x", "head"),
        0,
        0,
        tiled=True,
    )
    attended_rows = owners.reshape(ring_size, group_size, rows_here, head_width)
    attended_rows = attended_rows.transpose(2, 1, 0, 3).reshape(rows_here, model_width)
    group_blocks = lax.axis_index("zy") * ring_size + jnp.arange(ring_size, dtype=jnp.int32)
    cache_rows = lookup(
        holders, jnp.stack([2 * group_blocks, 2 * group_blocks + 1], axis=1)
    )
    cache_parts = jnp.stack(
        [
            jnp.concatenate(
                [
                    lax.dynamic_slice_in_dim(packed, cache_rows[i, 0] * halfway, halfway, 0),
                    lax.dynamic_slice_in_dim(packed, cache_rows[i, 1] * halfway, halfway, 0),
                ],
                axis=0,
            )
            for i in range(ring_size)
        ]
    )
    cache_heads = lax.all_to_all(cache_parts, "x", 0, 0, tiled=True)
    cache = cache_heads.reshape(group_heads, block_rows, 2, head_width).transpose(2, 1, 0, 3)
    cache = cache.reshape(2, block_rows, group_width)
    mixed = jnp.dot(attended_rows, full_out, preferred_element_type=jnp.float32)
    hidden = normalize(mixed + tokens.astype(jnp.float32))
    hidden_b = hidden.astype(jnp.bfloat16)
    own_query = jnp.dot(hidden_b, w_cq, preferred_element_type=jnp.float32).astype(jnp.bfloat16)
    cross_query = lax.all_to_all(
        own_query.reshape(rows_here, group_size, group_width).transpose(1, 0, 2),
        "head",
        0,
        0,
        tiled=True,
    ).reshape(block_rows, group_width)
    encoder_rows = encoder.shape[1]
    cross_max = (encoder_rows + halfway - 1 + 2 * halfway - 1) // (2 * halfway)
    padded_encoder = jnp.pad(
        encoder, ((0, 0), (0, cross_max * 2 * halfway + halfway - encoder_rows), (0, 0))
    )
    enc_low = prefix_below(query_places, ends, enc_lengths)
    enc_high = prefix_below(query_places, starts, enc_lengths) - 1
    cross_base = (enc_low.reshape(2, halfway)[:, 0] // halfway) * halfway
    cross_steps = (enc_high.reshape(2, halfway)[:, -1] + 1 - cross_base + 2 * halfway - 1) // (
        2 * halfway
    )
    cross_firsts = jnp.minimum(
        cross_base[:, None] + 2 * halfway * jnp.arange(cross_max, dtype=jnp.int32)[None, :],
        padded_encoder.shape[1] - 2 * halfway,
    )
    cross_sources = jnp.stack([cross_firsts, cross_firsts + halfway], axis=-1)
    crossed_group = flash(
        cross_query.reshape(2, halfway, group_width),
        enc_low.reshape(2, halfway, 1),
        enc_high.reshape(2, halfway, 1),
        padded_encoder[0],
        padded_encoder[1],
        cross_steps.astype(jnp.int32),
        cross_sources.reshape(-1).astype(jnp.int32),
        cross_firsts.reshape(-1).astype(jnp.int32),
        cross_max,
        group_heads,
    ).reshape(block_rows, group_width)
    exchanged = lax.all_to_all(
        crossed_group.reshape(group_size, rows_here, group_width), "head", 0, 0, tiled=True
    )
    crossed = exchanged.transpose(1, 0, 2).reshape(rows_here, model_width)
    summed = jnp.dot(crossed, w_co, preferred_element_type=jnp.float32)
    second = normalize(summed + hidden)
    second_b = second.astype(jnp.bfloat16)
    inner = jax.nn.gelu(
        jnp.dot(second_b, w_up, preferred_element_type=jnp.float32), approximate=False
    ).astype(jnp.bfloat16)
    output = normalize(jnp.dot(inner, w_down, preferred_element_type=jnp.float32) + second)
    output_b = output.astype(jnp.bfloat16)
    block_output = lax.all_gather(output_b, "head", axis=0, tiled=True)
    next_qkv = jnp.einsum("td,cde->cte", block_output, w_next, preferred_element_type=jnp.float32)
    return (output, cache, next_qkv)


def solution(mesh):
    ring = 4
    devices = mesh.devices.reshape(mesh.shape["blk"] // ring, ring, mesh.shape["head"])
    fine = jax.sharding.Mesh(devices, ("zy", "x", "head"))
    rows = ("zy", "x", "head")
    blocks = ("zy", "x")
    in_specs = (
        P(rows, None),
        P(),
        P(),
        P(),
        P(None, None, "head"),
        P("head", None),
        P(None, blocks, "head"),
        P(),
        P(),
        P(),
        P(),
        P(None, None, "head"),
    )
    out_specs = (P(rows, None), P(None, blocks, "head"), P(None, blocks, "head"))
    return jax.shard_map(
        on_device, mesh=fine, in_specs=in_specs, out_specs=out_specs, check_vma=False
    )
```

```python
import functools
import math

import jax
import jax.numpy as jnp
from jax import lax
from jax.experimental import pallas as pl
from jax.experimental.pallas import tpu as pltpu
from jax.sharding import PartitionSpec as P

HEADS = 16


NEGATIVE = -1e30
SCALING = 0.125
EPSILON = 1e-05


def normalize(matrix):
    center = matrix - jnp.mean(matrix, axis=-1, keepdims=True)
    return center * lax.rsqrt(jnp.mean(center * center, axis=-1, keepdims=True) + EPSILON)


def position_of(order_table, indices, halfway):
    slots = jnp.arange(order_table.shape[0], dtype=jnp.int32)
    picked = jnp.sum(
        jnp.where((indices // halfway)[:, None] == slots[None, :], order_table[None, :], 0), axis=1
    )
    return picked * halfway + indices % halfway


def group_of(places, lengths):
    ends = jnp.cumsum(lengths)
    return jnp.sum((places[:, None] >= ends[None, :]).astype(jnp.int32), axis=1)


def prefix_below(places, bounds, amounts):
    return jnp.sum(
        jnp.where(places[..., None] >= bounds, amounts, 0), axis=-1
    ).astype(jnp.int32)


def lookup(table, indices):
    slots = jnp.arange(table.shape[0], dtype=jnp.int32)
    return jnp.sum(jnp.where(indices[..., None] == slots, table, 0), axis=-1).astype(jnp.int32)


def online_update(carried, queries, key_rows, value_rows, visible):
    maxima, totals, running = carried
    heads_here = queries.shape[1]
    key_split = key_rows.reshape(key_rows.shape[0], heads_here, -1)
    value_split = value_rows.reshape(value_rows.shape[0], heads_here, -1)
    scores = (
        jnp.einsum("qhd,khd->qhk", queries, key_split, preferred_element_type=jnp.float32) * SCALING
    )
    scores = jnp.where(visible[:, None, :], scores, NEGATIVE)
    updated = jnp.maximum(maxima, jnp.max(scores, axis=2))
    factor = jnp.exp(maxima - updated)
    weights = jnp.exp(scores - updated[:, :, None])
    totals = totals * factor + jnp.sum(weights, axis=2)
    running = running * factor[:, :, None] + jnp.einsum(
        "qhk,khd->qhd",
        weights.astype(jnp.bfloat16),
        value_split,
        preferred_element_type=jnp.float32,
    )
    return (updated, totals, running)


def sweep(
    carried, queries, key_rows, value_rows, key_places, key_groups, query_places, query_groups
):
    length = key_rows.shape[0]
    block_size = math.gcd(length, 2048)
    blocks_count = length // block_size
    key_blocks = key_rows.reshape(blocks_count, block_size, key_rows.shape[1])
    value_blocks = value_rows.reshape(blocks_count, block_size, value_rows.shape[1])
    group_blocks = key_groups.reshape(blocks_count, block_size)
    if key_places is None:
        place_blocks = group_blocks
    else:
        place_blocks = key_places.reshape(blocks_count, block_size)

    def advance(status, element):
        key_block, value_block, place_block, group_block = element
        visible = group_block[None, :] == query_groups[:, None]
        if key_places is None:
            return (online_update(status, queries, key_block, value_block, visible), None)
        visible = visible & (place_block[None, :] <= query_places[:, None])
        updated = online_update(status, queries, key_block, value_block, visible)
        return (updated, None)

    carried, unused = lax.scan(
        advance, carried, (key_blocks, value_blocks, place_blocks, group_blocks)
    )
    return carried


def empty_state(count_q, heads_here, head_width):
    return (
        jnp.full((count_q, heads_here), NEGATIVE, jnp.float32),
        jnp.zeros((count_q, heads_here), jnp.float32),
        jnp.zeros((count_q, heads_here, head_width), jnp.float32),
    )


def finish(carried):
    maxima, totals, running = carried
    return (running / totals[:, :, None]).reshape(running.shape[0], -1).astype(jnp.bfloat16)


def flash_kernel(
    steps_ref, sources_ref, bases_ref, q_ref, low_ref, high_ref, k_hbm, v_hbm, o_ref,
    kbuf, vbuf, sem, qm_sc, m_sc, l_sc, acc_sc, *, max_steps, heads, head_width
):
    half = pl.program_id(0)
    count = steps_ref[half]
    tile = kbuf.shape[1] // 2
    width = kbuf.shape[2]

    def copies(step, slot):
        result = []
        for j in range(2):
            source = pl.multiple_of(sources_ref[(half * max_steps + step) * 2 + j], tile)
            window = pl.ds(j * tile, tile)
            result.append(pltpu.make_async_copy(
                k_hbm.at[pl.ds(source, tile)], kbuf.at[slot, window], sem.at[0, slot, j]))
            result.append(pltpu.make_async_copy(
                v_hbm.at[pl.ds(source, tile)], vbuf.at[slot, window], sem.at[1, slot, j]))
        return result

    for copy in copies(0, 0):
        copy.start()
    column_head = lax.broadcasted_iota(jnp.int32, (1, width), 1) // head_width
    q = q_ref[0]
    for h in range(heads):
        qm_sc[h] = jnp.where(column_head == h, q, jnp.zeros_like(q))
    m_sc[...] = jnp.full(m_sc.shape, NEGATIVE, jnp.float32)
    l_sc[...] = jnp.zeros(l_sc.shape, jnp.float32)
    acc_sc[...] = jnp.zeros(acc_sc.shape, jnp.float32)
    low = low_ref[0]
    high = high_ref[0]

    def body(step, carry):
        slot = step % 2
        for copy in copies(step, slot):
            copy.wait()

        @pl.when(step + 1 < count)
        def _():
            for copy in copies(step + 1, 1 - slot):
                copy.start()

        base = bases_ref[half * max_steps + step]
        places = base + lax.broadcasted_iota(jnp.int32, (1, 2 * tile), 1)
        visible = (places >= low) & (places <= high)
        keys = kbuf[slot]
        values = vbuf[slot]
        for h in range(heads):
            scores = lax.dot_general(
                qm_sc[h], keys, (((1,), (1,)), ((), ())), preferred_element_type=jnp.float32
            ) * SCALING
            scores = jnp.where(visible, scores, NEGATIVE)
            previous = m_sc[h]
            updated = jnp.maximum(previous, jnp.max(scores, axis=1, keepdims=True))
            factor = jnp.exp(previous - updated)
            weights = jnp.exp(scores - updated)
            l_sc[h] = l_sc[h] * factor + jnp.sum(weights, axis=1, keepdims=True)
            acc_sc[h] = acc_sc[h] * factor + jnp.dot(
                weights.astype(jnp.bfloat16), values, preferred_element_type=jnp.float32
            )
            m_sc[h] = updated
        return carry

    lax.fori_loop(0, count, body, 0)
    out = jnp.zeros(acc_sc.shape[1:], jnp.float32)
    for h in range(heads):
        out = jnp.where(column_head == h, acc_sc[h] / l_sc[h], out)
    o_ref[0] = out.astype(o_ref.dtype)


def flash(queries, low, high, keys, values, steps, sources, bases, max_steps, heads):
    halves, tile, width = queries.shape
    head_width = width // heads
    kernel = functools.partial(
        flash_kernel, max_steps=max_steps, heads=heads, head_width=head_width
    )
    row_spec = pl.BlockSpec((1, tile, width), lambda h, *refs: (h, 0, 0))
    bound_spec = pl.BlockSpec((1, tile, 1), lambda h, *refs: (h, 0, 0))
    flops = 4 * halves * max_steps * tile * 2 * tile * width * heads
    return pl.pallas_call(
        kernel,
        out_shape=jax.ShapeDtypeStruct(queries.shape, jnp.bfloat16),
        grid_spec=pltpu.PrefetchScalarGridSpec(
            num_scalar_prefetch=3,
            grid=(halves,),
            in_specs=[
                row_spec,
                bound_spec,
                bound_spec,
                pl.BlockSpec(memory_space=pl.ANY),
                pl.BlockSpec(memory_space=pl.ANY),
            ],
            out_specs=row_spec,
            scratch_shapes=[
                pltpu.VMEM((2, 2 * tile, width), keys.dtype),
                pltpu.VMEM((2, 2 * tile, width), values.dtype),
                pltpu.SemaphoreType.DMA((2, 2, 2)),
                pltpu.VMEM((heads, tile, width), jnp.bfloat16),
                pltpu.VMEM((heads, tile, 1), jnp.float32),
                pltpu.VMEM((heads, tile, 1), jnp.float32),
                pltpu.VMEM((heads, tile, width), jnp.float32),
            ],
        ),
        compiler_params=pltpu.CompilerParams(dimension_semantics=("arbitrary",)),
        cost_estimate=pl.CostEstimate(
            flops=flops,
            transcendentals=halves * max_steps * tile * 2 * tile * heads,
            bytes_accessed=halves * max_steps * 2 * 2 * tile * width * 2,
        ),
    )(steps, sources, bases, queries, low, high, keys, values)


def single_kernel(
    steps_ref, sources_ref, bases_ref, limits_ref, q_ref, low_ref, high_ref, kv_hbm, o_ref,
    buf, sem, m_sc, l_sc, acc_sc, *, max_steps, head_width, pieces
):
    half = pl.program_id(0)
    count = steps_ref[half]
    tile = buf.shape[1] // pieces

    def copies(step, slot):
        result = []
        for j in range(pieces):
            source = pl.multiple_of(sources_ref[(half * max_steps + step) * pieces + j], tile)
            result.append(pltpu.make_async_copy(
                kv_hbm.at[pl.ds(source, tile)], buf.at[slot, pl.ds(j * tile, tile)], sem.at[slot, j]))
        return result

    for copy in copies(0, 0):
        copy.start()
    m_sc[...] = jnp.full(m_sc.shape, NEGATIVE, jnp.float32)
    l_sc[...] = jnp.zeros(l_sc.shape, jnp.float32)
    acc_sc[...] = jnp.zeros(acc_sc.shape, jnp.float32)
    q = q_ref[0]
    low = low_ref[0]
    high = high_ref[0]

    def body(step, carry):
        slot = step % 2
        for copy in copies(step, slot):
            copy.wait()

        @pl.when(step + 1 < count)
        def _():
            for copy in copies(step + 1, 1 - slot):
                copy.start()

        base = bases_ref[half * max_steps + step]
        keys = buf[slot, :, :head_width]
        values = buf[slot, :, head_width:]

        def update(masked):
            scores = lax.dot_general(
                q, keys, (((1,), (1,)), ((), ())), preferred_element_type=jnp.float32
            ) * SCALING
            if masked:
                places = base + lax.broadcasted_iota(jnp.int32, (1, pieces * tile), 1)
                visible = (places >= low) & (places <= high)
                scores = jnp.where(visible, scores, NEGATIVE)
            previous = m_sc[...]
            updated = jnp.maximum(previous, jnp.max(scores, axis=1, keepdims=True))
            factor = jnp.exp(previous - updated)
            weights = jnp.exp(scores - updated)
            l_sc[...] = l_sc[...] * factor + jnp.sum(weights, axis=1, keepdims=True)
            acc_sc[...] = acc_sc[...] * factor + jnp.dot(
                weights.astype(jnp.bfloat16), values, preferred_element_type=jnp.float32
            )
            m_sc[...] = updated

        full = (base >= limits_ref[2 * half]) & (base + pieces * tile - 1 <= limits_ref[2 * half + 1])

        @pl.when(full)
        def _():
            update(False)

        @pl.when(jnp.logical_not(full))
        def _():
            update(True)

        return carry

    lax.fori_loop(0, count, body, 0)
    o_ref[0] = (acc_sc[...] / l_sc[...]).astype(o_ref.dtype)


def single(queries, low, high, packed, steps, sources, bases, limits, max_steps, pieces):
    halves, tile, head_width = queries.shape
    kernel = functools.partial(
        single_kernel, max_steps=max_steps, head_width=head_width, pieces=pieces
    )
    row_spec = pl.BlockSpec((1, tile, head_width), lambda h, *refs: (h, 0, 0))
    bound_spec = pl.BlockSpec((1, tile, 1), lambda h, *refs: (h, 0, 0))
    return pl.pallas_call(
        kernel,
        out_shape=jax.ShapeDtypeStruct(queries.shape, jnp.bfloat16),
        grid_spec=pltpu.PrefetchScalarGridSpec(
            num_scalar_prefetch=4,
            grid=(halves,),
            in_specs=[row_spec, bound_spec, bound_spec, pl.BlockSpec(memory_space=pl.ANY)],
            out_specs=row_spec,
            scratch_shapes=[
                pltpu.VMEM((2, pieces * tile, packed.shape[1]), packed.dtype),
                pltpu.SemaphoreType.DMA((2, pieces)),
                pltpu.VMEM((tile, 1), jnp.float32),
                pltpu.VMEM((tile, 1), jnp.float32),
                pltpu.VMEM((tile, head_width), jnp.float32),
            ],
        ),
        compiler_params=pltpu.CompilerParams(dimension_semantics=("arbitrary",)),
        cost_estimate=pl.CostEstimate(
            flops=2 * halves * (max_steps // 2) * tile * pieces * tile * head_width * 2,
            transcendentals=halves * (max_steps // 2) * tile * pieces * tile,
            bytes_accessed=halves * (max_steps // 2) * pieces * tile * packed.shape[1] * 2,
        ),
    )(steps, sources, bases, limits, queries, low, high, packed)


def on_device(
    tokens,
    block_order,
    request_lengths,
    enc_lengths,
    w_qkv,
    w_out,
    enc_kv,
    w_cq,
    w_co,
    w_up,
    w_down,
    w_next,
):
    rows_here = tokens.shape[0]
    model_width = tokens.shape[1]
    group_size = lax.axis_size("head")
    cycle_size = lax.axis_size("zy") * lax.axis_size("x")
    block_rows = rows_here * group_size
    halfway = block_rows // 2
    group_width = w_qkv.shape[2]
    head_width = model_width // HEADS
    group_heads = group_width // head_width
    member = lax.axis_index("head")
    ring_size = lax.axis_size("x")
    ring_index = lax.axis_index("x")
    cycle_index = lax.axis_index("zy") * ring_size + ring_index
    full_out = lax.all_to_all(
        jnp.broadcast_to(w_out[None], (group_size,) + w_out.shape), "head", 0, 0, tiled=True
    ).reshape(model_width, model_width)
    gathered = lax.all_gather(tokens, "head", axis=0, tiled=True)
    projected = jnp.einsum(
        "td,cde->cte", gathered, w_qkv, preferred_element_type=jnp.float32
    ).astype(jnp.bfloat16)
    block_start = cycle_index * block_rows
    query_places = position_of(
        block_order, block_start + jnp.arange(block_rows, dtype=jnp.int32), halfway
    )
    slots = jnp.arange(2 * cycle_size, dtype=jnp.int32)
    holders = jnp.sum(jnp.where(block_order[:, None] == slots[None, :], slots[:, None], 0), axis=0)
    per_head = projected.reshape(3, block_rows, group_heads, head_width).transpose(2, 1, 0, 3)
    per_head = per_head.reshape(group_heads, block_rows, 3 * head_width)
    lanes = 256
    mine = lax.all_to_all(
        per_head.reshape(group_heads, block_rows * 3 * head_width // lanes, lanes),
        "x",
        0,
        0,
        tiled=True,
    ).reshape(group_heads, block_rows, 3 * head_width)
    packed = lax.all_gather(mine[:, :, head_width:], "zy", axis=0, tiled=True)
    packed = packed.reshape(cycle_size * block_rows, 2 * head_width)
    full_out, packed, late_kv = lax.optimization_barrier((full_out, packed, enc_kv))
    encoder = lax.all_gather(late_kv, ("zy", "x"), axis=1, tiled=True)
    ends = jnp.cumsum(request_lengths).astype(jnp.int32)
    starts = ends - request_lengths
    halves_here = 2 * ring_size
    first_half = lax.axis_index("zy") * halves_here
    pair = lax.dynamic_slice_in_dim(block_order, first_half, halves_here, 0)
    low_block = prefix_below(pair * halfway, ends, request_lengths) // halfway
    pieces = 8
    self_steps = (pair - low_block) // pieces + 1
    self_max = (2 * cycle_size + pieces - 1) // pieces
    firsts = low_block[:, None] + pieces * jnp.arange(self_max, dtype=jnp.int32)[None, :]
    self_sources = lookup(
        holders,
        jnp.minimum(firsts[:, :, None] + jnp.arange(pieces, dtype=jnp.int32), 2 * cycle_size - 1),
    ) * halfway
    places_here = (pair[:, None] * halfway + jnp.arange(halfway, dtype=jnp.int32)[None, :])
    self_low = prefix_below(places_here, ends, request_lengths).reshape(halves_here, halfway)
    limits = jnp.stack([self_low[:, -1], places_here[:, 0]], axis=1).reshape(-1)
    single_out = single(
        mine[:, :, :head_width].reshape(halves_here, halfway, head_width),
        self_low.reshape(halves_here, halfway, 1),
        places_here.reshape(halves_here, halfway, 1),
        packed,
        self_steps.astype(jnp.int32),
        self_sources.reshape(-1).astype(jnp.int32),
        (firsts * halfway).reshape(-1).astype(jnp.int32),
        limits.astype(jnp.int32),
        self_max,
        pieces,
    )
    owners = lax.all_to_all(
        single_out.reshape(ring_size * group_size, rows_here, head_width),
        ("x", "head"),
        0,
        0,
        tiled=True,
    )
    attended_rows = owners.reshape(ring_size, group_size, rows_here, head_width)
    attended_rows = attended_rows.transpose(2, 1, 0, 3).reshape(rows_here, model_width)
    group_blocks = lax.axis_index("zy") * ring_size + jnp.arange(ring_size, dtype=jnp.int32)
    cache_rows = lookup(
        holders, jnp.stack([2 * group_blocks, 2 * group_blocks + 1], axis=1)
    )
    cache_parts = jnp.stack(
        [
            jnp.concatenate(
                [
                    lax.dynamic_slice_in_dim(packed, cache_rows[i, 0] * halfway, halfway, 0),
                    lax.dynamic_slice_in_dim(packed, cache_rows[i, 1] * halfway, halfway, 0),
                ],
                axis=0,
            )
            for i in range(ring_size)
        ]
    )
    cache_heads = lax.all_to_all(cache_parts, "x", 0, 0, tiled=True)
    cache = cache_heads.reshape(group_heads, block_rows, 2, head_width).transpose(2, 1, 0, 3)
    cache = cache.reshape(2, block_rows, group_width)
    mixed = jnp.dot(attended_rows, full_out, preferred_element_type=jnp.float32)
    hidden = normalize(mixed + tokens.astype(jnp.float32))
    hidden_b = hidden.astype(jnp.bfloat16)
    own_query = jnp.dot(hidden_b, w_cq, preferred_element_type=jnp.float32).astype(jnp.bfloat16)
    cross_query = lax.all_to_all(
        own_query.reshape(rows_here, group_size, group_width).transpose(1, 0, 2),
        "head",
        0,
        0,
        tiled=True,
    ).reshape(block_rows, group_width)
    encoder_rows = encoder.shape[1]
    cross_max = (encoder_rows + halfway - 1 + 2 * halfway - 1) // (2 * halfway)
    padded_encoder = jnp.pad(
        encoder, ((0, 0), (0, cross_max * 2 * halfway + halfway - encoder_rows), (0, 0))
    )
    enc_low = prefix_below(query_places, ends, enc_lengths)
    enc_high = prefix_below(query_places, starts, enc_lengths) - 1
    cross_base = (enc_low.reshape(2, halfway)[:, 0] // halfway) * halfway
    cross_steps = (enc_high.reshape(2, halfway)[:, -1] + 1 - cross_base + 2 * halfway - 1) // (
        2 * halfway
    )
    cross_firsts = jnp.minimum(
        cross_base[:, None] + 2 * halfway * jnp.arange(cross_max, dtype=jnp.int32)[None, :],
        padded_encoder.shape[1] - 2 * halfway,
    )
    cross_sources = jnp.stack([cross_firsts, cross_firsts + halfway], axis=-1)
    crossed_group = flash(
        cross_query.reshape(2, halfway, group_width),
        enc_low.reshape(2, halfway, 1),
        enc_high.reshape(2, halfway, 1),
        padded_encoder[0],
        padded_encoder[1],
        cross_steps.astype(jnp.int32),
        cross_sources.reshape(-1).astype(jnp.int32),
        cross_firsts.reshape(-1).astype(jnp.int32),
        cross_max,
        group_heads,
    ).reshape(block_rows, group_width)
    exchanged = lax.all_to_all(
        crossed_group.reshape(group_size, rows_here, group_width), "head", 0, 0, tiled=True
    )
    crossed = exchanged.transpose(1, 0, 2).reshape(rows_here, model_width)
    summed = jnp.dot(crossed, w_co, preferred_element_type=jnp.float32)
    second = normalize(summed + hidden)
    second_b = second.astype(jnp.bfloat16)
    inner = jax.nn.gelu(
        jnp.dot(second_b, w_up, preferred_element_type=jnp.float32), approximate=False
    ).astype(jnp.bfloat16)
    output = normalize(jnp.dot(inner, w_down, preferred_element_type=jnp.float32) + second)
    output_b = output.astype(jnp.bfloat16)
    block_output = lax.all_gather(output_b, "head", axis=0, tiled=True)
    next_qkv = jnp.einsum("td,cde->cte", block_output, w_next, preferred_element_type=jnp.float32)
    return (output, cache, next_qkv)


def solution(mesh):
    ring = 4
    devices = mesh.devices.reshape(mesh.shape["blk"] // ring, ring, mesh.shape["head"])
    fine = jax.sharding.Mesh(devices, ("zy", "x", "head"))
    rows = ("zy", "x", "head")
    blocks = ("zy", "x")
    in_specs = (
        P(rows, None),
        P(),
        P(),
        P(),
        P(None, None, "head"),
        P("head", None),
        P(None, blocks, "head"),
        P(),
        P(),
        P(),
        P(),
        P(None, None, "head"),
    )
    out_specs = (P(rows, None), P(None, blocks, "head"), P(None, blocks, "head"))
    return jax.shard_map(
        on_device, mesh=fine, in_specs=in_specs, out_specs=out_specs, check_vma=False
    )
```

```python
import functools
import math

import jax
import jax.numpy as jnp
from jax import lax
from jax.experimental import pallas as pl
from jax.experimental.pallas import tpu as pltpu
from jax.sharding import PartitionSpec as P

HEADS = 16


NEGATIVE = -1e30
SCALING = 0.125
EPSILON = 1e-05


def normalize(matrix):
    center = matrix - jnp.mean(matrix, axis=-1, keepdims=True)
    return center * lax.rsqrt(jnp.mean(center * center, axis=-1, keepdims=True) + EPSILON)


def position_of(order_table, indices, halfway):
    slots = jnp.arange(order_table.shape[0], dtype=jnp.int32)
    picked = jnp.sum(
        jnp.where((indices // halfway)[:, None] == slots[None, :], order_table[None, :], 0), axis=1
    )
    return picked * halfway + indices % halfway


def group_of(places, lengths):
    ends = jnp.cumsum(lengths)
    return jnp.sum((places[:, None] >= ends[None, :]).astype(jnp.int32), axis=1)


def prefix_below(places, bounds, amounts):
    return jnp.sum(
        jnp.where(places[..., None] >= bounds, amounts, 0), axis=-1
    ).astype(jnp.int32)


def lookup(table, indices):
    slots = jnp.arange(table.shape[0], dtype=jnp.int32)
    return jnp.sum(jnp.where(indices[..., None] == slots, table, 0), axis=-1).astype(jnp.int32)


def online_update(carried, queries, key_rows, value_rows, visible):
    maxima, totals, running = carried
    heads_here = queries.shape[1]
    key_split = key_rows.reshape(key_rows.shape[0], heads_here, -1)
    value_split = value_rows.reshape(value_rows.shape[0], heads_here, -1)
    scores = (
        jnp.einsum("qhd,khd->qhk", queries, key_split, preferred_element_type=jnp.float32) * SCALING
    )
    scores = jnp.where(visible[:, None, :], scores, NEGATIVE)
    updated = jnp.maximum(maxima, jnp.max(scores, axis=2))
    factor = jnp.exp(maxima - updated)
    weights = jnp.exp(scores - updated[:, :, None])
    totals = totals * factor + jnp.sum(weights, axis=2)
    running = running * factor[:, :, None] + jnp.einsum(
        "qhk,khd->qhd",
        weights.astype(jnp.bfloat16),
        value_split,
        preferred_element_type=jnp.float32,
    )
    return (updated, totals, running)


def sweep(
    carried, queries, key_rows, value_rows, key_places, key_groups, query_places, query_groups
):
    length = key_rows.shape[0]
    block_size = math.gcd(length, 2048)
    blocks_count = length // block_size
    key_blocks = key_rows.reshape(blocks_count, block_size, key_rows.shape[1])
    value_blocks = value_rows.reshape(blocks_count, block_size, value_rows.shape[1])
    group_blocks = key_groups.reshape(blocks_count, block_size)
    if key_places is None:
        place_blocks = group_blocks
    else:
        place_blocks = key_places.reshape(blocks_count, block_size)

    def advance(status, element):
        key_block, value_block, place_block, group_block = element
        visible = group_block[None, :] == query_groups[:, None]
        if key_places is None:
            return (online_update(status, queries, key_block, value_block, visible), None)
        visible = visible & (place_block[None, :] <= query_places[:, None])
        updated = online_update(status, queries, key_block, value_block, visible)
        return (updated, None)

    carried, unused = lax.scan(
        advance, carried, (key_blocks, value_blocks, place_blocks, group_blocks)
    )
    return carried


def empty_state(count_q, heads_here, head_width):
    return (
        jnp.full((count_q, heads_here), NEGATIVE, jnp.float32),
        jnp.zeros((count_q, heads_here), jnp.float32),
        jnp.zeros((count_q, heads_here, head_width), jnp.float32),
    )


def finish(carried):
    maxima, totals, running = carried
    return (running / totals[:, :, None]).reshape(running.shape[0], -1).astype(jnp.bfloat16)


def flash_kernel(
    steps_ref, sources_ref, bases_ref, q_ref, low_ref, high_ref, k_hbm, v_hbm, o_ref,
    kbuf, vbuf, sem, qm_sc, m_sc, l_sc, acc_sc, *, max_steps, heads, head_width
):
    half = pl.program_id(0)
    count = steps_ref[half]
    tile = kbuf.shape[1] // 2
    width = kbuf.shape[2]

    def copies(step, slot):
        result = []
        for j in range(2):
            source = pl.multiple_of(sources_ref[(half * max_steps + step) * 2 + j], tile)
            window = pl.ds(j * tile, tile)
            result.append(pltpu.make_async_copy(
                k_hbm.at[pl.ds(source, tile)], kbuf.at[slot, window], sem.at[0, slot, j]))
            result.append(pltpu.make_async_copy(
                v_hbm.at[pl.ds(source, tile)], vbuf.at[slot, window], sem.at[1, slot, j]))
        return result

    for copy in copies(0, 0):
        copy.start()
    column_head = lax.broadcasted_iota(jnp.int32, (1, width), 1) // head_width
    q = q_ref[0]
    for h in range(heads):
        qm_sc[h] = jnp.where(column_head == h, q, jnp.zeros_like(q))
    m_sc[...] = jnp.full(m_sc.shape, NEGATIVE, jnp.float32)
    l_sc[...] = jnp.zeros(l_sc.shape, jnp.float32)
    acc_sc[...] = jnp.zeros(acc_sc.shape, jnp.float32)
    low = low_ref[0]
    high = high_ref[0]

    def body(step, carry):
        slot = step % 2
        for copy in copies(step, slot):
            copy.wait()

        @pl.when(step + 1 < count)
        def _():
            for copy in copies(step + 1, 1 - slot):
                copy.start()

        base = bases_ref[half * max_steps + step]
        places = base + lax.broadcasted_iota(jnp.int32, (1, 2 * tile), 1)
        visible = (places >= low) & (places <= high)
        keys = kbuf[slot]
        values = vbuf[slot]
        for h in range(heads):
            scores = lax.dot_general(
                qm_sc[h], keys, (((1,), (1,)), ((), ())), preferred_element_type=jnp.float32
            ) * SCALING
            scores = jnp.where(visible, scores, NEGATIVE)
            previous = m_sc[h]
            updated = jnp.maximum(previous, jnp.max(scores, axis=1, keepdims=True))
            factor = jnp.exp(previous - updated)
            weights = jnp.exp(scores - updated)
            l_sc[h] = l_sc[h] * factor + jnp.sum(weights, axis=1, keepdims=True)
            acc_sc[h] = acc_sc[h] * factor + jnp.dot(
                weights.astype(jnp.bfloat16), values, preferred_element_type=jnp.float32
            )
            m_sc[h] = updated
        return carry

    lax.fori_loop(0, count, body, 0)
    out = jnp.zeros(acc_sc.shape[1:], jnp.float32)
    for h in range(heads):
        out = jnp.where(column_head == h, acc_sc[h] / l_sc[h], out)
    o_ref[0] = out.astype(o_ref.dtype)


def flash(queries, low, high, keys, values, steps, sources, bases, max_steps, heads):
    halves, tile, width = queries.shape
    head_width = width // heads
    kernel = functools.partial(
        flash_kernel, max_steps=max_steps, heads=heads, head_width=head_width
    )
    row_spec = pl.BlockSpec((1, tile, width), lambda h, *refs: (h, 0, 0))
    bound_spec = pl.BlockSpec((1, tile, 1), lambda h, *refs: (h, 0, 0))
    flops = 4 * halves * max_steps * tile * 2 * tile * width * heads
    return pl.pallas_call(
        kernel,
        out_shape=jax.ShapeDtypeStruct(queries.shape, jnp.bfloat16),
        grid_spec=pltpu.PrefetchScalarGridSpec(
            num_scalar_prefetch=3,
            grid=(halves,),
            in_specs=[
                row_spec,
                bound_spec,
                bound_spec,
                pl.BlockSpec(memory_space=pl.ANY),
                pl.BlockSpec(memory_space=pl.ANY),
            ],
            out_specs=row_spec,
            scratch_shapes=[
                pltpu.VMEM((2, 2 * tile, width), keys.dtype),
                pltpu.VMEM((2, 2 * tile, width), values.dtype),
                pltpu.SemaphoreType.DMA((2, 2, 2)),
                pltpu.VMEM((heads, tile, width), jnp.bfloat16),
                pltpu.VMEM((heads, tile, 1), jnp.float32),
                pltpu.VMEM((heads, tile, 1), jnp.float32),
                pltpu.VMEM((heads, tile, width), jnp.float32),
            ],
        ),
        compiler_params=pltpu.CompilerParams(dimension_semantics=("arbitrary",)),
        cost_estimate=pl.CostEstimate(
            flops=flops,
            transcendentals=halves * max_steps * tile * 2 * tile * heads,
            bytes_accessed=halves * max_steps * 2 * 2 * tile * width * 2,
        ),
    )(steps, sources, bases, queries, low, high, keys, values)


def single_kernel(
    steps_ref, sources_ref, bases_ref, limits_ref, q_ref, low_ref, high_ref, kv_hbm, o_ref,
    buf, sem, m_sc, l_sc, acc_sc, *, max_steps, head_width, pieces
):
    half = pl.program_id(0)
    count = steps_ref[half]
    tile = buf.shape[1] // pieces

    def copies(step, slot):
        result = []
        for j in range(pieces):
            source = pl.multiple_of(sources_ref[(half * max_steps + step) * pieces + j], tile)
            result.append(pltpu.make_async_copy(
                kv_hbm.at[pl.ds(source, tile)], buf.at[slot, pl.ds(j * tile, tile)], sem.at[slot, j]))
        return result

    for copy in copies(0, 0):
        copy.start()
    m_sc[...] = jnp.full(m_sc.shape, NEGATIVE, jnp.float32)
    l_sc[...] = jnp.zeros(l_sc.shape, jnp.float32)
    acc_sc[...] = jnp.zeros(acc_sc.shape, jnp.float32)
    q = q_ref[0]
    low = low_ref[0]
    high = high_ref[0]

    def body(step, carry):
        slot = step % 2
        for copy in copies(step, slot):
            copy.wait()

        @pl.when(step + 1 < count)
        def _():
            for copy in copies(step + 1, 1 - slot):
                copy.start()

        base = bases_ref[half * max_steps + step]
        keys = buf[slot, :, :head_width]
        values = buf[slot, :, head_width:]

        def update(masked):
            scores = lax.dot_general(
                q, keys, (((1,), (1,)), ((), ())), preferred_element_type=jnp.float32
            ) * SCALING
            if masked:
                places = base + lax.broadcasted_iota(jnp.int32, (1, pieces * tile), 1)
                visible = (places >= low) & (places <= high)
                scores = jnp.where(visible, scores, NEGATIVE)
            previous = m_sc[...]
            updated = jnp.maximum(previous, jnp.max(scores, axis=1, keepdims=True))
            factor = jnp.exp(previous - updated)
            weights = jnp.exp(scores - updated)
            l_sc[...] = l_sc[...] * factor + jnp.sum(weights, axis=1, keepdims=True)
            acc_sc[...] = acc_sc[...] * factor + jnp.dot(
                weights.astype(jnp.bfloat16), values, preferred_element_type=jnp.float32
            )
            m_sc[...] = updated

        full = (base >= limits_ref[2 * half]) & (base + pieces * tile - 1 <= limits_ref[2 * half + 1])

        @pl.when(full)
        def _():
            update(False)

        @pl.when(jnp.logical_not(full))
        def _():
            update(True)

        return carry

    lax.fori_loop(0, count, body, 0)
    o_ref[0] = (acc_sc[...] / l_sc[...]).astype(o_ref.dtype)


def single(queries, low, high, packed, steps, sources, bases, limits, max_steps, pieces):
    halves, tile, head_width = queries.shape
    kernel = functools.partial(
        single_kernel, max_steps=max_steps, head_width=head_width, pieces=pieces
    )
    row_spec = pl.BlockSpec((1, tile, head_width), lambda h, *refs: (h, 0, 0))
    bound_spec = pl.BlockSpec((1, tile, 1), lambda h, *refs: (h, 0, 0))
    return pl.pallas_call(
        kernel,
        out_shape=jax.ShapeDtypeStruct(queries.shape, jnp.bfloat16),
        grid_spec=pltpu.PrefetchScalarGridSpec(
            num_scalar_prefetch=4,
            grid=(halves,),
            in_specs=[row_spec, bound_spec, bound_spec, pl.BlockSpec(memory_space=pl.ANY)],
            out_specs=row_spec,
            scratch_shapes=[
                pltpu.VMEM((2, pieces * tile, packed.shape[1]), packed.dtype),
                pltpu.SemaphoreType.DMA((2, pieces)),
                pltpu.VMEM((tile, 1), jnp.float32),
                pltpu.VMEM((tile, 1), jnp.float32),
                pltpu.VMEM((tile, head_width), jnp.float32),
            ],
        ),
        compiler_params=pltpu.CompilerParams(dimension_semantics=("arbitrary",)),
        cost_estimate=pl.CostEstimate(
            flops=2 * halves * (max_steps // 2) * tile * pieces * tile * head_width * 2,
            transcendentals=halves * (max_steps // 2) * tile * pieces * tile,
            bytes_accessed=halves * (max_steps // 2) * pieces * tile * packed.shape[1] * 2,
        ),
    )(steps, sources, bases, limits, queries, low, high, packed)


def on_device(
    tokens,
    block_order,
    request_lengths,
    enc_lengths,
    w_qkv,
    w_out,
    enc_kv,
    w_cq,
    w_co,
    w_up,
    w_down,
    w_next,
):
    rows_here = tokens.shape[0]
    model_width = tokens.shape[1]
    group_size = lax.axis_size("head")
    cycle_size = lax.axis_size("zy") * lax.axis_size("x")
    block_rows = rows_here * group_size
    halfway = block_rows // 2
    group_width = w_qkv.shape[2]
    head_width = model_width // HEADS
    group_heads = group_width // head_width
    member = lax.axis_index("head")
    ring_size = lax.axis_size("x")
    ring_index = lax.axis_index("x")
    cycle_index = lax.axis_index("zy") * ring_size + ring_index
    full_out = lax.all_to_all(
        jnp.broadcast_to(w_out[None], (group_size,) + w_out.shape), "head", 0, 0, tiled=True
    ).reshape(model_width, model_width)
    gathered = lax.all_gather(tokens, "head", axis=0, tiled=True)
    projected = jnp.einsum(
        "td,cde->cte", gathered, w_qkv, preferred_element_type=jnp.float32
    ).astype(jnp.bfloat16)
    block_start = cycle_index * block_rows
    query_places = position_of(
        block_order, block_start + jnp.arange(block_rows, dtype=jnp.int32), halfway
    )
    slots = jnp.arange(2 * cycle_size, dtype=jnp.int32)
    holders = jnp.sum(jnp.where(block_order[:, None] == slots[None, :], slots[:, None], 0), axis=0)
    per_head = projected.reshape(3, block_rows, group_heads, head_width).transpose(2, 1, 0, 3)
    per_head = per_head.reshape(group_heads, block_rows, 3 * head_width)
    mine = lax.all_to_all(per_head, "x", 0, 0, tiled=True)
    packed = lax.all_gather(mine[:, :, head_width:], "zy", axis=0, tiled=True)
    packed = packed.reshape(cycle_size * block_rows, 2 * head_width)
    full_out, packed, late_kv = lax.optimization_barrier((full_out, packed, enc_kv))
    encoder = lax.all_gather(late_kv, ("zy", "x"), axis=1, tiled=True)
    ends = jnp.cumsum(request_lengths).astype(jnp.int32)
    starts = ends - request_lengths
    halves_here = 2 * ring_size
    first_half = lax.axis_index("zy") * halves_here
    pair = lax.dynamic_slice_in_dim(block_order, first_half, halves_here, 0)
    low_block = prefix_below(pair * halfway, ends, request_lengths) // halfway
    pieces = 16
    self_steps = (pair - low_block) // pieces + 1
    self_max = (2 * cycle_size + pieces - 1) // pieces
    firsts = low_block[:, None] + pieces * jnp.arange(self_max, dtype=jnp.int32)[None, :]
    self_sources = lookup(
        holders,
        jnp.minimum(firsts[:, :, None] + jnp.arange(pieces, dtype=jnp.int32), 2 * cycle_size - 1),
    ) * halfway
    places_here = (pair[:, None] * halfway + jnp.arange(halfway, dtype=jnp.int32)[None, :])
    self_low = prefix_below(places_here, ends, request_lengths).reshape(halves_here, halfway)
    limits = jnp.stack([self_low[:, -1], places_here[:, 0]], axis=1).reshape(-1)
    single_out = single(
        mine[:, :, :head_width].reshape(halves_here, halfway, head_width),
        self_low.reshape(halves_here, halfway, 1),
        places_here.reshape(halves_here, halfway, 1),
        packed,
        self_steps.astype(jnp.int32),
        self_sources.reshape(-1).astype(jnp.int32),
        (firsts * halfway).reshape(-1).astype(jnp.int32),
        limits.astype(jnp.int32),
        self_max,
        pieces,
    )
    owners = lax.all_to_all(
        single_out.reshape(ring_size * group_size, rows_here, head_width),
        ("x", "head"),
        0,
        0,
        tiled=True,
    )
    attended_rows = owners.reshape(ring_size, group_size, rows_here, head_width)
    attended_rows = attended_rows.transpose(2, 1, 0, 3).reshape(rows_here, model_width)
    group_blocks = lax.axis_index("zy") * ring_size + jnp.arange(ring_size, dtype=jnp.int32)
    cache_rows = lookup(
        holders, jnp.stack([2 * group_blocks, 2 * group_blocks + 1], axis=1)
    )
    cache_parts = jnp.stack(
        [
            jnp.concatenate(
                [
                    lax.dynamic_slice_in_dim(packed, cache_rows[i, 0] * halfway, halfway, 0),
                    lax.dynamic_slice_in_dim(packed, cache_rows[i, 1] * halfway, halfway, 0),
                ],
                axis=0,
            )
            for i in range(ring_size)
        ]
    )
    cache_heads = lax.all_to_all(cache_parts, "x", 0, 0, tiled=True)
    cache = cache_heads.reshape(group_heads, block_rows, 2, head_width).transpose(2, 1, 0, 3)
    cache = cache.reshape(2, block_rows, group_width)
    mixed = jnp.dot(attended_rows, full_out, preferred_element_type=jnp.float32)
    hidden = normalize(mixed + tokens.astype(jnp.float32))
    hidden_b = hidden.astype(jnp.bfloat16)
    own_query = jnp.dot(hidden_b, w_cq, preferred_element_type=jnp.float32).astype(jnp.bfloat16)
    cross_query = lax.all_to_all(
        own_query.reshape(rows_here, group_size, group_width).transpose(1, 0, 2),
        "head",
        0,
        0,
        tiled=True,
    ).reshape(block_rows, group_width)
    encoder_rows = encoder.shape[1]
    cross_max = (encoder_rows + halfway - 1 + 2 * halfway - 1) // (2 * halfway)
    padded_encoder = jnp.pad(
        encoder, ((0, 0), (0, cross_max * 2 * halfway + halfway - encoder_rows), (0, 0))
    )
    enc_low = prefix_below(query_places, ends, enc_lengths)
    enc_high = prefix_below(query_places, starts, enc_lengths) - 1
    cross_base = (enc_low.reshape(2, halfway)[:, 0] // halfway) * halfway
    cross_steps = (enc_high.reshape(2, halfway)[:, -1] + 1 - cross_base + 2 * halfway - 1) // (
        2 * halfway
    )
    cross_firsts = jnp.minimum(
        cross_base[:, None] + 2 * halfway * jnp.arange(cross_max, dtype=jnp.int32)[None, :],
        padded_encoder.shape[1] - 2 * halfway,
    )
    cross_sources = jnp.stack([cross_firsts, cross_firsts + halfway], axis=-1)
    crossed_group = flash(
        cross_query.reshape(2, halfway, group_width),
        enc_low.reshape(2, halfway, 1),
        enc_high.reshape(2, halfway, 1),
        padded_encoder[0],
        padded_encoder[1],
        cross_steps.astype(jnp.int32),
        cross_sources.reshape(-1).astype(jnp.int32),
        cross_firsts.reshape(-1).astype(jnp.int32),
        cross_max,
        group_heads,
    ).reshape(block_rows, group_width)
    exchanged = lax.all_to_all(
        crossed_group.reshape(group_size, rows_here, group_width), "head", 0, 0, tiled=True
    )
    crossed = exchanged.transpose(1, 0, 2).reshape(rows_here, model_width)
    summed = jnp.dot(crossed, w_co, preferred_element_type=jnp.float32)
    second = normalize(summed + hidden)
    second_b = second.astype(jnp.bfloat16)
    inner = jax.nn.gelu(
        jnp.dot(second_b, w_up, preferred_element_type=jnp.float32), approximate=False
    ).astype(jnp.bfloat16)
    output = normalize(jnp.dot(inner, w_down, preferred_element_type=jnp.float32) + second)
    output_b = output.astype(jnp.bfloat16)
    block_output = lax.all_gather(output_b, "head", axis=0, tiled=True)
    next_qkv = jnp.einsum("td,cde->cte", block_output, w_next, preferred_element_type=jnp.float32)
    return (output, cache, next_qkv)


def solution(mesh):
    ring = 4
    devices = mesh.devices.reshape(mesh.shape["blk"] // ring, ring, mesh.shape["head"])
    fine = jax.sharding.Mesh(devices, ("zy", "x", "head"))
    rows = ("zy", "x", "head")
    blocks = ("zy", "x")
    in_specs = (
        P(rows, None),
        P(),
        P(),
        P(),
        P(None, None, "head"),
        P("head", None),
        P(None, blocks, "head"),
        P(),
        P(),
        P(),
        P(),
        P(None, None, "head"),
    )
    out_specs = (P(rows, None), P(None, blocks, "head"), P(None, blocks, "head"))
    return jax.shard_map(
        on_device, mesh=fine, in_specs=in_specs, out_specs=out_specs, check_vma=False
    )
```

```python
import functools
import math

import jax
import jax.numpy as jnp
from jax import lax
from jax.experimental import pallas as pl
from jax.experimental.pallas import tpu as pltpu
from jax.sharding import PartitionSpec as P

HEADS = 16


NEGATIVE = -1e30
SCALING = 0.125
EPSILON = 1e-05


def normalize(matrix):
    center = matrix - jnp.mean(matrix, axis=-1, keepdims=True)
    return center * lax.rsqrt(jnp.mean(center * center, axis=-1, keepdims=True) + EPSILON)


def position_of(order_table, indices, halfway):
    slots = jnp.arange(order_table.shape[0], dtype=jnp.int32)
    picked = jnp.sum(
        jnp.where((indices // halfway)[:, None] == slots[None, :], order_table[None, :], 0), axis=1
    )
    return picked * halfway + indices % halfway


def group_of(places, lengths):
    ends = jnp.cumsum(lengths)
    return jnp.sum((places[:, None] >= ends[None, :]).astype(jnp.int32), axis=1)


def prefix_below(places, bounds, amounts):
    return jnp.sum(
        jnp.where(places[..., None] >= bounds, amounts, 0), axis=-1
    ).astype(jnp.int32)


def lookup(table, indices):
    slots = jnp.arange(table.shape[0], dtype=jnp.int32)
    return jnp.sum(jnp.where(indices[..., None] == slots, table, 0), axis=-1).astype(jnp.int32)


def online_update(carried, queries, key_rows, value_rows, visible):
    maxima, totals, running = carried
    heads_here = queries.shape[1]
    key_split = key_rows.reshape(key_rows.shape[0], heads_here, -1)
    value_split = value_rows.reshape(value_rows.shape[0], heads_here, -1)
    scores = (
        jnp.einsum("qhd,khd->qhk", queries, key_split, preferred_element_type=jnp.float32) * SCALING
    )
    scores = jnp.where(visible[:, None, :], scores, NEGATIVE)
    updated = jnp.maximum(maxima, jnp.max(scores, axis=2))
    factor = jnp.exp(maxima - updated)
    weights = jnp.exp(scores - updated[:, :, None])
    totals = totals * factor + jnp.sum(weights, axis=2)
    running = running * factor[:, :, None] + jnp.einsum(
        "qhk,khd->qhd",
        weights.astype(jnp.bfloat16),
        value_split,
        preferred_element_type=jnp.float32,
    )
    return (updated, totals, running)


def sweep(
    carried, queries, key_rows, value_rows, key_places, key_groups, query_places, query_groups
):
    length = key_rows.shape[0]
    block_size = math.gcd(length, 2048)
    blocks_count = length // block_size
    key_blocks = key_rows.reshape(blocks_count, block_size, key_rows.shape[1])
    value_blocks = value_rows.reshape(blocks_count, block_size, value_rows.shape[1])
    group_blocks = key_groups.reshape(blocks_count, block_size)
    if key_places is None:
        place_blocks = group_blocks
    else:
        place_blocks = key_places.reshape(blocks_count, block_size)

    def advance(status, element):
        key_block, value_block, place_block, group_block = element
        visible = group_block[None, :] == query_groups[:, None]
        if key_places is None:
            return (online_update(status, queries, key_block, value_block, visible), None)
        visible = visible & (place_block[None, :] <= query_places[:, None])
        updated = online_update(status, queries, key_block, value_block, visible)
        return (updated, None)

    carried, unused = lax.scan(
        advance, carried, (key_blocks, value_blocks, place_blocks, group_blocks)
    )
    return carried


def empty_state(count_q, heads_here, head_width):
    return (
        jnp.full((count_q, heads_here), NEGATIVE, jnp.float32),
        jnp.zeros((count_q, heads_here), jnp.float32),
        jnp.zeros((count_q, heads_here, head_width), jnp.float32),
    )


def finish(carried):
    maxima, totals, running = carried
    return (running / totals[:, :, None]).reshape(running.shape[0], -1).astype(jnp.bfloat16)


def flash_kernel(
    steps_ref, sources_ref, bases_ref, q_ref, low_ref, high_ref, k_hbm, v_hbm, o_ref,
    kbuf, vbuf, sem, qm_sc, m_sc, l_sc, acc_sc, *, max_steps, heads, head_width
):
    half = pl.program_id(0)
    count = steps_ref[half]
    tile = kbuf.shape[1] // 2
    width = kbuf.shape[2]

    def copies(step, slot):
        result = []
        for j in range(2):
            source = pl.multiple_of(sources_ref[(half * max_steps + step) * 2 + j], tile)
            window = pl.ds(j * tile, tile)
            result.append(pltpu.make_async_copy(
                k_hbm.at[pl.ds(source, tile)], kbuf.at[slot, window], sem.at[0, slot, j]))
            result.append(pltpu.make_async_copy(
                v_hbm.at[pl.ds(source, tile)], vbuf.at[slot, window], sem.at[1, slot, j]))
        return result

    for copy in copies(0, 0):
        copy.start()
    column_head = lax.broadcasted_iota(jnp.int32, (1, width), 1) // head_width
    q = q_ref[0]
    for h in range(heads):
        qm_sc[h] = jnp.where(column_head == h, q, jnp.zeros_like(q))
    m_sc[...] = jnp.full(m_sc.shape, NEGATIVE, jnp.float32)
    l_sc[...] = jnp.zeros(l_sc.shape, jnp.float32)
    acc_sc[...] = jnp.zeros(acc_sc.shape, jnp.float32)
    low = low_ref[0]
    high = high_ref[0]

    def body(step, carry):
        slot = step % 2
        for copy in copies(step, slot):
            copy.wait()

        @pl.when(step + 1 < count)
        def _():
            for copy in copies(step + 1, 1 - slot):
                copy.start()

        base = bases_ref[half * max_steps + step]
        places = base + lax.broadcasted_iota(jnp.int32, (1, 2 * tile), 1)
        visible = (places >= low) & (places <= high)
        keys = kbuf[slot]
        values = vbuf[slot]
        for h in range(heads):
            scores = lax.dot_general(
                qm_sc[h], keys, (((1,), (1,)), ((), ())), preferred_element_type=jnp.float32
            ) * SCALING
            scores = jnp.where(visible, scores, NEGATIVE)
            previous = m_sc[h]
            updated = jnp.maximum(previous, jnp.max(scores, axis=1, keepdims=True))
            factor = jnp.exp(previous - updated)
            weights = jnp.exp(scores - updated)
            l_sc[h] = l_sc[h] * factor + jnp.sum(weights, axis=1, keepdims=True)
            acc_sc[h] = acc_sc[h] * factor + jnp.dot(
                weights.astype(jnp.bfloat16), values, preferred_element_type=jnp.float32
            )
            m_sc[h] = updated
        return carry

    lax.fori_loop(0, count, body, 0)
    out = jnp.zeros(acc_sc.shape[1:], jnp.float32)
    for h in range(heads):
        out = jnp.where(column_head == h, acc_sc[h] / l_sc[h], out)
    o_ref[0] = out.astype(o_ref.dtype)


def flash(queries, low, high, keys, values, steps, sources, bases, max_steps, heads):
    halves, tile, width = queries.shape
    head_width = width // heads
    kernel = functools.partial(
        flash_kernel, max_steps=max_steps, heads=heads, head_width=head_width
    )
    row_spec = pl.BlockSpec((1, tile, width), lambda h, *refs: (h, 0, 0))
    bound_spec = pl.BlockSpec((1, tile, 1), lambda h, *refs: (h, 0, 0))
    flops = 4 * halves * max_steps * tile * 2 * tile * width * heads
    return pl.pallas_call(
        kernel,
        out_shape=jax.ShapeDtypeStruct(queries.shape, jnp.bfloat16),
        grid_spec=pltpu.PrefetchScalarGridSpec(
            num_scalar_prefetch=3,
            grid=(halves,),
            in_specs=[
                row_spec,
                bound_spec,
                bound_spec,
                pl.BlockSpec(memory_space=pl.ANY),
                pl.BlockSpec(memory_space=pl.ANY),
            ],
            out_specs=row_spec,
            scratch_shapes=[
                pltpu.VMEM((2, 2 * tile, width), keys.dtype),
                pltpu.VMEM((2, 2 * tile, width), values.dtype),
                pltpu.SemaphoreType.DMA((2, 2, 2)),
                pltpu.VMEM((heads, tile, width), jnp.bfloat16),
                pltpu.VMEM((heads, tile, 1), jnp.float32),
                pltpu.VMEM((heads, tile, 1), jnp.float32),
                pltpu.VMEM((heads, tile, width), jnp.float32),
            ],
        ),
        compiler_params=pltpu.CompilerParams(dimension_semantics=("arbitrary",)),
        cost_estimate=pl.CostEstimate(
            flops=flops,
            transcendentals=halves * max_steps * tile * 2 * tile * heads,
            bytes_accessed=halves * max_steps * 2 * 2 * tile * width * 2,
        ),
    )(steps, sources, bases, queries, low, high, keys, values)


def single_kernel(
    steps_ref, sources_ref, bases_ref, limits_ref, q_ref, low_ref, high_ref, kv_hbm, o_ref,
    buf, sem, m_sc, l_sc, acc_sc, *, max_steps, head_width, pieces
):
    half = pl.program_id(0)
    count = steps_ref[half]
    tile = buf.shape[1] // pieces

    def copies(step, slot):
        result = []
        for j in range(pieces):
            source = pl.multiple_of(sources_ref[(half * max_steps + step) * pieces + j], tile)
            result.append(pltpu.make_async_copy(
                kv_hbm.at[pl.ds(source, tile)], buf.at[slot, pl.ds(j * tile, tile)], sem.at[slot, j]))
        return result

    for copy in copies(0, 0):
        copy.start()
    m_sc[...] = jnp.full(m_sc.shape, NEGATIVE, jnp.float32)
    l_sc[...] = jnp.zeros(l_sc.shape, jnp.float32)
    acc_sc[...] = jnp.zeros(acc_sc.shape, jnp.float32)
    q = q_ref[0]
    low = low_ref[0]
    high = high_ref[0]

    def body(step, carry):
        slot = step % 2
        for copy in copies(step, slot):
            copy.wait()

        @pl.when(step + 1 < count)
        def _():
            for copy in copies(step + 1, 1 - slot):
                copy.start()

        base = bases_ref[half * max_steps + step]
        keys = buf[slot, :, :head_width]
        values = buf[slot, :, head_width:]

        def update(masked):
            scores = lax.dot_general(
                q, keys, (((1,), (1,)), ((), ())), preferred_element_type=jnp.float32
            ) * SCALING
            if masked:
                places = base + lax.broadcasted_iota(jnp.int32, (1, pieces * tile), 1)
                visible = (places >= low) & (places <= high)
                scores = jnp.where(visible, scores, NEGATIVE)
            previous = m_sc[...]
            updated = jnp.maximum(previous, jnp.max(scores, axis=1, keepdims=True))
            factor = jnp.exp(previous - updated)
            weights = jnp.exp(scores - updated)
            l_sc[...] = l_sc[...] * factor + jnp.sum(weights, axis=1, keepdims=True)
            acc_sc[...] = acc_sc[...] * factor + jnp.dot(
                weights.astype(jnp.bfloat16), values, preferred_element_type=jnp.float32
            )
            m_sc[...] = updated

        full = (base >= limits_ref[2 * half]) & (base + pieces * tile - 1 <= limits_ref[2 * half + 1])

        @pl.when(full)
        def _():
            update(False)

        @pl.when(jnp.logical_not(full))
        def _():
            update(True)

        return carry

    lax.fori_loop(0, count, body, 0)
    o_ref[0] = (acc_sc[...] / l_sc[...]).astype(o_ref.dtype)


def single(queries, low, high, packed, steps, sources, bases, limits, max_steps, pieces):
    halves, tile, head_width = queries.shape
    kernel = functools.partial(
        single_kernel, max_steps=max_steps, head_width=head_width, pieces=pieces
    )
    row_spec = pl.BlockSpec((1, tile, head_width), lambda h, *refs: (h, 0, 0))
    bound_spec = pl.BlockSpec((1, tile, 1), lambda h, *refs: (h, 0, 0))
    return pl.pallas_call(
        kernel,
        out_shape=jax.ShapeDtypeStruct(queries.shape, jnp.bfloat16),
        grid_spec=pltpu.PrefetchScalarGridSpec(
            num_scalar_prefetch=4,
            grid=(halves,),
            in_specs=[row_spec, bound_spec, bound_spec, pl.BlockSpec(memory_space=pl.ANY)],
            out_specs=row_spec,
            scratch_shapes=[
                pltpu.VMEM((2, pieces * tile, packed.shape[1]), packed.dtype),
                pltpu.SemaphoreType.DMA((2, pieces)),
                pltpu.VMEM((tile, 1), jnp.float32),
                pltpu.VMEM((tile, 1), jnp.float32),
                pltpu.VMEM((tile, head_width), jnp.float32),
            ],
        ),
        compiler_params=pltpu.CompilerParams(dimension_semantics=("arbitrary",)),
        cost_estimate=pl.CostEstimate(
            flops=2 * halves * (max_steps // 2) * tile * pieces * tile * head_width * 2,
            transcendentals=halves * (max_steps // 2) * tile * pieces * tile,
            bytes_accessed=halves * (max_steps // 2) * pieces * tile * packed.shape[1] * 2,
        ),
    )(steps, sources, bases, limits, queries, low, high, packed)


def on_device(
    tokens,
    block_order,
    request_lengths,
    enc_lengths,
    w_qkv,
    w_out,
    enc_kv,
    w_cq,
    w_co,
    w_up,
    w_down,
    w_next,
):
    rows_here = tokens.shape[0]
    model_width = tokens.shape[1]
    group_size = lax.axis_size("head")
    cycle_size = lax.axis_size("zy") * lax.axis_size("x")
    block_rows = rows_here * group_size
    halfway = block_rows // 2
    group_width = w_qkv.shape[2]
    head_width = model_width // HEADS
    group_heads = group_width // head_width
    member = lax.axis_index("head")
    ring_size = lax.axis_size("x")
    ring_index = lax.axis_index("x")
    cycle_index = lax.axis_index("zy") * ring_size + ring_index
    full_out = lax.all_to_all(
        jnp.broadcast_to(w_out[None], (group_size,) + w_out.shape), "head", 0, 0, tiled=True
    ).reshape(model_width, model_width)
    gathered = lax.all_gather(tokens, "head", axis=0, tiled=True)
    projected = jnp.einsum(
        "td,cde->cte", gathered, w_qkv, preferred_element_type=jnp.float32
    ).astype(jnp.bfloat16)
    block_start = cycle_index * block_rows
    query_places = position_of(
        block_order, block_start + jnp.arange(block_rows, dtype=jnp.int32), halfway
    )
    slots = jnp.arange(2 * cycle_size, dtype=jnp.int32)
    holders = jnp.sum(jnp.where(block_order[:, None] == slots[None, :], slots[:, None], 0), axis=0)
    per_head = projected.reshape(3, block_rows, group_heads, head_width).transpose(2, 1, 0, 3)
    per_head = per_head.reshape(group_heads, block_rows, 3 * head_width)
    mine_kv = lax.all_to_all(per_head[:, :, head_width:], "x", 0, 0, tiled=True)
    packed = lax.all_gather(mine_kv, "zy", axis=0, tiled=True)
    own_queries, mine_kv = lax.optimization_barrier((per_head[:, :, :head_width], mine_kv))
    mine_q = lax.all_to_all(own_queries, "x", 0, 0, tiled=True)
    packed = packed.reshape(cycle_size * block_rows, 2 * head_width)
    full_out, packed, late_kv, mine_q = lax.optimization_barrier(
        (full_out, packed, enc_kv, mine_q)
    )
    encoder = lax.all_gather(late_kv, ("zy", "x"), axis=1, tiled=True)
    ends = jnp.cumsum(request_lengths).astype(jnp.int32)
    starts = ends - request_lengths
    halves_here = 2 * ring_size
    first_half = lax.axis_index("zy") * halves_here
    pair = lax.dynamic_slice_in_dim(block_order, first_half, halves_here, 0)
    low_block = prefix_below(pair * halfway, ends, request_lengths) // halfway
    pieces = 8
    self_steps = (pair - low_block) // pieces + 1
    self_max = (2 * cycle_size + pieces - 1) // pieces
    firsts = low_block[:, None] + pieces * jnp.arange(self_max, dtype=jnp.int32)[None, :]
    self_sources = lookup(
        holders,
        jnp.minimum(firsts[:, :, None] + jnp.arange(pieces, dtype=jnp.int32), 2 * cycle_size - 1),
    ) * halfway
    places_here = (pair[:, None] * halfway + jnp.arange(halfway, dtype=jnp.int32)[None, :])
    self_low = prefix_below(places_here, ends, request_lengths).reshape(halves_here, halfway)
    limits = jnp.stack([self_low[:, -1], places_here[:, 0]], axis=1).reshape(-1)
    single_out = single(
        mine_q.reshape(halves_here, halfway, head_width),
        self_low.reshape(halves_here, halfway, 1),
        places_here.reshape(halves_here, halfway, 1),
        packed,
        self_steps.astype(jnp.int32),
        self_sources.reshape(-1).astype(jnp.int32),
        (firsts * halfway).reshape(-1).astype(jnp.int32),
        limits.astype(jnp.int32),
        self_max,
        pieces,
    )
    owners = lax.all_to_all(
        single_out.reshape(ring_size * group_size, rows_here, head_width),
        ("x", "head"),
        0,
        0,
        tiled=True,
    )
    attended_rows = owners.reshape(ring_size, group_size, rows_here, head_width)
    attended_rows = attended_rows.transpose(2, 1, 0, 3).reshape(rows_here, model_width)
    group_blocks = lax.axis_index("zy") * ring_size + jnp.arange(ring_size, dtype=jnp.int32)
    cache_rows = lookup(
        holders, jnp.stack([2 * group_blocks, 2 * group_blocks + 1], axis=1)
    )
    cache_parts = jnp.stack(
        [
            jnp.concatenate(
                [
                    lax.dynamic_slice_in_dim(packed, cache_rows[i, 0] * halfway, halfway, 0),
                    lax.dynamic_slice_in_dim(packed, cache_rows[i, 1] * halfway, halfway, 0),
                ],
                axis=0,
            )
            for i in range(ring_size)
        ]
    )
    cache_heads = lax.all_to_all(cache_parts, "x", 0, 0, tiled=True)
    cache = cache_heads.reshape(group_heads, block_rows, 2, head_width).transpose(2, 1, 0, 3)
    cache = cache.reshape(2, block_rows, group_width)
    mixed = jnp.dot(attended_rows, full_out, preferred_element_type=jnp.float32)
    hidden = normalize(mixed + tokens.astype(jnp.float32))
    hidden_b = hidden.astype(jnp.bfloat16)
    own_query = jnp.dot(hidden_b, w_cq, preferred_element_type=jnp.float32).astype(jnp.bfloat16)
    cross_query = lax.all_to_all(
        own_query.reshape(rows_here, group_size, group_width).transpose(1, 0, 2),
        "head",
        0,
        0,
        tiled=True,
    ).reshape(block_rows, group_width)
    encoder_rows = encoder.shape[1]
    cross_max = (encoder_rows + halfway - 1 + 2 * halfway - 1) // (2 * halfway)
    padded_encoder = jnp.pad(
        encoder, ((0, 0), (0, cross_max * 2 * halfway + halfway - encoder_rows), (0, 0))
    )
    enc_low = prefix_below(query_places, ends, enc_lengths)
    enc_high = prefix_below(query_places, starts, enc_lengths) - 1
    cross_base = (enc_low.reshape(2, halfway)[:, 0] // halfway) * halfway
    cross_steps = (enc_high.reshape(2, halfway)[:, -1] + 1 - cross_base + 2 * halfway - 1) // (
        2 * halfway
    )
    cross_firsts = jnp.minimum(
        cross_base[:, None] + 2 * halfway * jnp.arange(cross_max, dtype=jnp.int32)[None, :],
        padded_encoder.shape[1] - 2 * halfway,
    )
    cross_sources = jnp.stack([cross_firsts, cross_firsts + halfway], axis=-1)
    crossed_group = flash(
        cross_query.reshape(2, halfway, group_width),
        enc_low.reshape(2, halfway, 1),
        enc_high.reshape(2, halfway, 1),
        padded_encoder[0],
        padded_encoder[1],
        cross_steps.astype(jnp.int32),
        cross_sources.reshape(-1).astype(jnp.int32),
        cross_firsts.reshape(-1).astype(jnp.int32),
        cross_max,
        group_heads,
    ).reshape(block_rows, group_width)
    exchanged = lax.all_to_all(
        crossed_group.reshape(group_size, rows_here, group_width), "head", 0, 0, tiled=True
    )
    crossed = exchanged.transpose(1, 0, 2).reshape(rows_here, model_width)
    summed = jnp.dot(crossed, w_co, preferred_element_type=jnp.float32)
    second = normalize(summed + hidden)
    second_b = second.astype(jnp.bfloat16)
    inner = jax.nn.gelu(
        jnp.dot(second_b, w_up, preferred_element_type=jnp.float32), approximate=False
    ).astype(jnp.bfloat16)
    output = normalize(jnp.dot(inner, w_down, preferred_element_type=jnp.float32) + second)
    output_b = output.astype(jnp.bfloat16)
    block_output = lax.all_gather(output_b, "head", axis=0, tiled=True)
    next_qkv = jnp.einsum("td,cde->cte", block_output, w_next, preferred_element_type=jnp.float32)
    return (output, cache, next_qkv)


def solution(mesh):
    ring = 4
    devices = mesh.devices.reshape(mesh.shape["blk"] // ring, ring, mesh.shape["head"])
    fine = jax.sharding.Mesh(devices, ("zy", "x", "head"))
    rows = ("zy", "x", "head")
    blocks = ("zy", "x")
    in_specs = (
        P(rows, None),
        P(),
        P(),
        P(),
        P(None, None, "head"),
        P("head", None),
        P(None, blocks, "head"),
        P(),
        P(),
        P(),
        P(),
        P(None, None, "head"),
    )
    out_specs = (P(rows, None), P(None, blocks, "head"), P(None, blocks, "head"))
    return jax.shard_map(
        on_device, mesh=fine, in_specs=in_specs, out_specs=out_specs, check_vma=False
    )
```

```python
import functools
import math

import jax
import jax.numpy as jnp
from jax import lax
from jax.experimental import pallas as pl
from jax.experimental.pallas import tpu as pltpu
from jax.sharding import PartitionSpec as P

HEADS = 16


NEGATIVE = -1e30
SCALING = 0.125
EPSILON = 1e-05


def normalize(matrix):
    center = matrix - jnp.mean(matrix, axis=-1, keepdims=True)
    return center * lax.rsqrt(jnp.mean(center * center, axis=-1, keepdims=True) + EPSILON)


def position_of(order_table, indices, halfway):
    slots = jnp.arange(order_table.shape[0], dtype=jnp.int32)
    picked = jnp.sum(
        jnp.where((indices // halfway)[:, None] == slots[None, :], order_table[None, :], 0), axis=1
    )
    return picked * halfway + indices % halfway


def group_of(places, lengths):
    ends = jnp.cumsum(lengths)
    return jnp.sum((places[:, None] >= ends[None, :]).astype(jnp.int32), axis=1)


def prefix_below(places, bounds, amounts):
    return jnp.sum(
        jnp.where(places[..., None] >= bounds, amounts, 0), axis=-1
    ).astype(jnp.int32)


def lookup(table, indices):
    slots = jnp.arange(table.shape[0], dtype=jnp.int32)
    return jnp.sum(jnp.where(indices[..., None] == slots, table, 0), axis=-1).astype(jnp.int32)


def online_update(carried, queries, key_rows, value_rows, visible):
    maxima, totals, running = carried
    heads_here = queries.shape[1]
    key_split = key_rows.reshape(key_rows.shape[0], heads_here, -1)
    value_split = value_rows.reshape(value_rows.shape[0], heads_here, -1)
    scores = (
        jnp.einsum("qhd,khd->qhk", queries, key_split, preferred_element_type=jnp.float32) * SCALING
    )
    scores = jnp.where(visible[:, None, :], scores, NEGATIVE)
    updated = jnp.maximum(maxima, jnp.max(scores, axis=2))
    factor = jnp.exp(maxima - updated)
    weights = jnp.exp(scores - updated[:, :, None])
    totals = totals * factor + jnp.sum(weights, axis=2)
    running = running * factor[:, :, None] + jnp.einsum(
        "qhk,khd->qhd",
        weights.astype(jnp.bfloat16),
        value_split,
        preferred_element_type=jnp.float32,
    )
    return (updated, totals, running)


def sweep(
    carried, queries, key_rows, value_rows, key_places, key_groups, query_places, query_groups
):
    length = key_rows.shape[0]
    block_size = math.gcd(length, 2048)
    blocks_count = length // block_size
    key_blocks = key_rows.reshape(blocks_count, block_size, key_rows.shape[1])
    value_blocks = value_rows.reshape(blocks_count, block_size, value_rows.shape[1])
    group_blocks = key_groups.reshape(blocks_count, block_size)
    if key_places is None:
        place_blocks = group_blocks
    else:
        place_blocks = key_places.reshape(blocks_count, block_size)

    def advance(status, element):
        key_block, value_block, place_block, group_block = element
        visible = group_block[None, :] == query_groups[:, None]
        if key_places is None:
            return (online_update(status, queries, key_block, value_block, visible), None)
        visible = visible & (place_block[None, :] <= query_places[:, None])
        updated = online_update(status, queries, key_block, value_block, visible)
        return (updated, None)

    carried, unused = lax.scan(
        advance, carried, (key_blocks, value_blocks, place_blocks, group_blocks)
    )
    return carried


def empty_state(count_q, heads_here, head_width):
    return (
        jnp.full((count_q, heads_here), NEGATIVE, jnp.float32),
        jnp.zeros((count_q, heads_here), jnp.float32),
        jnp.zeros((count_q, heads_here, head_width), jnp.float32),
    )


def finish(carried):
    maxima, totals, running = carried
    return (running / totals[:, :, None]).reshape(running.shape[0], -1).astype(jnp.bfloat16)


def flash_kernel(
    steps_ref, sources_ref, bases_ref, q_ref, low_ref, high_ref, k_hbm, v_hbm, o_ref,
    kbuf, vbuf, sem, qm_sc, m_sc, l_sc, acc_sc, *, max_steps, heads, head_width
):
    half = pl.program_id(0)
    count = steps_ref[half]
    tile = kbuf.shape[1] // 2
    width = kbuf.shape[2]

    def copies(step, slot):
        result = []
        for j in range(2):
            source = pl.multiple_of(sources_ref[(half * max_steps + step) * 2 + j], tile)
            window = pl.ds(j * tile, tile)
            result.append(pltpu.make_async_copy(
                k_hbm.at[pl.ds(source, tile)], kbuf.at[slot, window], sem.at[0, slot, j]))
            result.append(pltpu.make_async_copy(
                v_hbm.at[pl.ds(source, tile)], vbuf.at[slot, window], sem.at[1, slot, j]))
        return result

    for copy in copies(0, 0):
        copy.start()
    column_head = lax.broadcasted_iota(jnp.int32, (1, width), 1) // head_width
    q = q_ref[0]
    for h in range(heads):
        qm_sc[h] = jnp.where(column_head == h, q, jnp.zeros_like(q))
    m_sc[...] = jnp.full(m_sc.shape, NEGATIVE, jnp.float32)
    l_sc[...] = jnp.zeros(l_sc.shape, jnp.float32)
    acc_sc[...] = jnp.zeros(acc_sc.shape, jnp.float32)
    low = low_ref[0]
    high = high_ref[0]

    def body(step, carry):
        slot = step % 2
        for copy in copies(step, slot):
            copy.wait()

        @pl.when(step + 1 < count)
        def _():
            for copy in copies(step + 1, 1 - slot):
                copy.start()

        base = bases_ref[half * max_steps + step]
        places = base + lax.broadcasted_iota(jnp.int32, (1, 2 * tile), 1)
        visible = (places >= low) & (places <= high)
        keys = kbuf[slot]
        values = vbuf[slot]
        for h in range(heads):
            scores = lax.dot_general(
                qm_sc[h], keys, (((1,), (1,)), ((), ())), preferred_element_type=jnp.float32
            ) * SCALING
            scores = jnp.where(visible, scores, NEGATIVE)
            previous = m_sc[h]
            updated = jnp.maximum(previous, jnp.max(scores, axis=1, keepdims=True))
            factor = jnp.exp(previous - updated)
            weights = jnp.exp(scores - updated)
            l_sc[h] = l_sc[h] * factor + jnp.sum(weights, axis=1, keepdims=True)
            acc_sc[h] = acc_sc[h] * factor + jnp.dot(
                weights.astype(jnp.bfloat16), values, preferred_element_type=jnp.float32
            )
            m_sc[h] = updated
        return carry

    lax.fori_loop(0, count, body, 0)
    out = jnp.zeros(acc_sc.shape[1:], jnp.float32)
    for h in range(heads):
        out = jnp.where(column_head == h, acc_sc[h] / l_sc[h], out)
    o_ref[0] = out.astype(o_ref.dtype)


def flash(queries, low, high, keys, values, steps, sources, bases, max_steps, heads):
    halves, tile, width = queries.shape
    head_width = width // heads
    kernel = functools.partial(
        flash_kernel, max_steps=max_steps, heads=heads, head_width=head_width
    )
    row_spec = pl.BlockSpec((1, tile, width), lambda h, *refs: (h, 0, 0))
    bound_spec = pl.BlockSpec((1, tile, 1), lambda h, *refs: (h, 0, 0))
    flops = 4 * halves * max_steps * tile * 2 * tile * width * heads
    return pl.pallas_call(
        kernel,
        out_shape=jax.ShapeDtypeStruct(queries.shape, jnp.bfloat16),
        grid_spec=pltpu.PrefetchScalarGridSpec(
            num_scalar_prefetch=3,
            grid=(halves,),
            in_specs=[
                row_spec,
                bound_spec,
                bound_spec,
                pl.BlockSpec(memory_space=pl.ANY),
                pl.BlockSpec(memory_space=pl.ANY),
            ],
            out_specs=row_spec,
            scratch_shapes=[
                pltpu.VMEM((2, 2 * tile, width), keys.dtype),
                pltpu.VMEM((2, 2 * tile, width), values.dtype),
                pltpu.SemaphoreType.DMA((2, 2, 2)),
                pltpu.VMEM((heads, tile, width), jnp.bfloat16),
                pltpu.VMEM((heads, tile, 1), jnp.float32),
                pltpu.VMEM((heads, tile, 1), jnp.float32),
                pltpu.VMEM((heads, tile, width), jnp.float32),
            ],
        ),
        compiler_params=pltpu.CompilerParams(dimension_semantics=("arbitrary",)),
        cost_estimate=pl.CostEstimate(
            flops=flops,
            transcendentals=halves * max_steps * tile * 2 * tile * heads,
            bytes_accessed=halves * max_steps * 2 * 2 * tile * width * 2,
        ),
    )(steps, sources, bases, queries, low, high, keys, values)


def single_kernel(
    steps_ref, sources_ref, bases_ref, limits_ref, q_ref, low_ref, high_ref, kv_hbm, o_ref,
    buf, sem, m_sc, l_sc, acc_sc, *, max_steps, head_width, pieces
):
    half = pl.program_id(0)
    count = steps_ref[half]
    tile = buf.shape[1] // pieces

    def copies(step, slot):
        result = []
        for j in range(pieces):
            source = pl.multiple_of(sources_ref[(half * max_steps + step) * pieces + j], tile)
            result.append(pltpu.make_async_copy(
                kv_hbm.at[pl.ds(source, tile)], buf.at[slot, pl.ds(j * tile, tile)], sem.at[slot, j]))
        return result

    for copy in copies(0, 0):
        copy.start()
    m_sc[...] = jnp.full(m_sc.shape, NEGATIVE, jnp.float32)
    l_sc[...] = jnp.zeros(l_sc.shape, jnp.float32)
    acc_sc[...] = jnp.zeros(acc_sc.shape, jnp.float32)
    q = q_ref[0]
    low = low_ref[0]
    high = high_ref[0]

    def body(step, carry):
        slot = step % 2
        for copy in copies(step, slot):
            copy.wait()

        @pl.when(step + 1 < count)
        def _():
            for copy in copies(step + 1, 1 - slot):
                copy.start()

        base = bases_ref[half * max_steps + step]
        keys = buf[slot, :, :head_width]
        values = buf[slot, :, head_width:]

        def update(masked):
            scores = lax.dot_general(
                q, keys, (((1,), (1,)), ((), ())), preferred_element_type=jnp.float32
            ) * SCALING
            if masked:
                places = base + lax.broadcasted_iota(jnp.int32, (1, pieces * tile), 1)
                visible = (places >= low) & (places <= high)
                scores = jnp.where(visible, scores, NEGATIVE)
            previous = m_sc[...]
            updated = jnp.maximum(previous, jnp.max(scores, axis=1, keepdims=True))
            factor = jnp.exp(previous - updated)
            weights = jnp.exp(scores - updated)
            l_sc[...] = l_sc[...] * factor + jnp.sum(weights, axis=1, keepdims=True)
            acc_sc[...] = acc_sc[...] * factor + jnp.dot(
                weights.astype(jnp.bfloat16), values, preferred_element_type=jnp.float32
            )
            m_sc[...] = updated

        full = (base >= limits_ref[2 * half]) & (base + pieces * tile - 1 <= limits_ref[2 * half + 1])

        @pl.when(full)
        def _():
            update(False)

        @pl.when(jnp.logical_not(full))
        def _():
            update(True)

        return carry

    lax.fori_loop(0, count, body, 0)
    o_ref[0] = (acc_sc[...] / l_sc[...]).astype(o_ref.dtype)


def single(queries, low, high, packed, steps, sources, bases, limits, max_steps, pieces):
    halves, tile, head_width = queries.shape
    kernel = functools.partial(
        single_kernel, max_steps=max_steps, head_width=head_width, pieces=pieces
    )
    row_spec = pl.BlockSpec((1, tile, head_width), lambda h, *refs: (h, 0, 0))
    bound_spec = pl.BlockSpec((1, tile, 1), lambda h, *refs: (h, 0, 0))
    return pl.pallas_call(
        kernel,
        out_shape=jax.ShapeDtypeStruct(queries.shape, jnp.bfloat16),
        grid_spec=pltpu.PrefetchScalarGridSpec(
            num_scalar_prefetch=4,
            grid=(halves,),
            in_specs=[row_spec, bound_spec, bound_spec, pl.BlockSpec(memory_space=pl.ANY)],
            out_specs=row_spec,
            scratch_shapes=[
                pltpu.VMEM((2, pieces * tile, packed.shape[1]), packed.dtype),
                pltpu.SemaphoreType.DMA((2, pieces)),
                pltpu.VMEM((tile, 1), jnp.float32),
                pltpu.VMEM((tile, 1), jnp.float32),
                pltpu.VMEM((tile, head_width), jnp.float32),
            ],
        ),
        compiler_params=pltpu.CompilerParams(dimension_semantics=("arbitrary",)),
        cost_estimate=pl.CostEstimate(
            flops=2 * halves * (max_steps // 2) * tile * pieces * tile * head_width * 2,
            transcendentals=halves * (max_steps // 2) * tile * pieces * tile,
            bytes_accessed=halves * (max_steps // 2) * pieces * tile * packed.shape[1] * 2,
        ),
    )(steps, sources, bases, limits, queries, low, high, packed)


def on_device(
    tokens,
    block_order,
    request_lengths,
    enc_lengths,
    w_qkv,
    w_out,
    enc_kv,
    w_cq,
    w_co,
    w_up,
    w_down,
    w_next,
):
    rows_here = tokens.shape[0]
    model_width = tokens.shape[1]
    group_size = lax.axis_size("head")
    cycle_size = lax.axis_size("zy") * lax.axis_size("x")
    block_rows = rows_here * group_size
    halfway = block_rows // 2
    group_width = w_qkv.shape[2]
    head_width = model_width // HEADS
    group_heads = group_width // head_width
    member = lax.axis_index("head")
    ring_size = lax.axis_size("x")
    ring_index = lax.axis_index("x")
    cycle_index = lax.axis_index("zy") * ring_size + ring_index
    full_out = lax.all_to_all(
        jnp.broadcast_to(w_out[None], (group_size,) + w_out.shape), "head", 0, 0, tiled=True
    ).reshape(model_width, model_width)
    gathered = lax.all_gather(tokens, "head", axis=0, tiled=True)
    projected = jnp.einsum(
        "td,cde->cte", gathered, w_qkv, preferred_element_type=jnp.float32
    ).astype(jnp.bfloat16)
    block_start = cycle_index * block_rows
    query_places = position_of(
        block_order, block_start + jnp.arange(block_rows, dtype=jnp.int32), halfway
    )
    slots = jnp.arange(2 * cycle_size, dtype=jnp.int32)
    holders = jnp.sum(jnp.where(block_order[:, None] == slots[None, :], slots[:, None], 0), axis=0)
    per_head = projected.reshape(3, block_rows, group_heads, head_width).transpose(2, 1, 0, 3)
    per_head = per_head.reshape(group_heads, block_rows, 3 * head_width)
    mine = lax.all_to_all(per_head, "x", 0, 0, tiled=True)
    packed = lax.all_gather(mine[:, :, head_width:], "zy", axis=0, tiled=True)
    packed = packed.reshape(cycle_size * block_rows, 2 * head_width)
    enc_ring = lax.all_to_all(
        jnp.broadcast_to(enc_kv[None], (ring_size,) + enc_kv.shape), "x", 0, 0, tiled=True
    )
    enc_ring = enc_ring.transpose(1, 0, 2, 3).reshape(
        2, ring_size * enc_kv.shape[1], enc_kv.shape[2]
    )
    full_out, packed, late_kv = lax.optimization_barrier((full_out, packed, enc_ring))
    encoder = lax.all_gather(late_kv, "zy", axis=1, tiled=True)
    ends = jnp.cumsum(request_lengths).astype(jnp.int32)
    starts = ends - request_lengths
    halves_here = 2 * ring_size
    first_half = lax.axis_index("zy") * halves_here
    pair = lax.dynamic_slice_in_dim(block_order, first_half, halves_here, 0)
    low_block = prefix_below(pair * halfway, ends, request_lengths) // halfway
    pieces = 8
    self_steps = (pair - low_block) // pieces + 1
    self_max = (2 * cycle_size + pieces - 1) // pieces
    firsts = low_block[:, None] + pieces * jnp.arange(self_max, dtype=jnp.int32)[None, :]
    self_sources = lookup(
        holders,
        jnp.minimum(firsts[:, :, None] + jnp.arange(pieces, dtype=jnp.int32), 2 * cycle_size - 1),
    ) * halfway
    places_here = (pair[:, None] * halfway + jnp.arange(halfway, dtype=jnp.int32)[None, :])
    self_low = prefix_below(places_here, ends, request_lengths).reshape(halves_here, halfway)
    limits = jnp.stack([self_low[:, -1], places_here[:, 0]], axis=1).reshape(-1)
    single_out = single(
        mine[:, :, :head_width].reshape(halves_here, halfway, head_width),
        self_low.reshape(halves_here, halfway, 1),
        places_here.reshape(halves_here, halfway, 1),
        packed,
        self_steps.astype(jnp.int32),
        self_sources.reshape(-1).astype(jnp.int32),
        (firsts * halfway).reshape(-1).astype(jnp.int32),
        limits.astype(jnp.int32),
        self_max,
        pieces,
    )
    owners = lax.all_to_all(
        single_out.reshape(ring_size * group_size, rows_here, head_width),
        ("x", "head"),
        0,
        0,
        tiled=True,
    )
    attended_rows = owners.reshape(ring_size, group_size, rows_here, head_width)
    attended_rows = attended_rows.transpose(2, 1, 0, 3).reshape(rows_here, model_width)
    group_blocks = lax.axis_index("zy") * ring_size + jnp.arange(ring_size, dtype=jnp.int32)
    cache_rows = lookup(
        holders, jnp.stack([2 * group_blocks, 2 * group_blocks + 1], axis=1)
    )
    cache_parts = jnp.stack(
        [
            jnp.concatenate(
                [
                    lax.dynamic_slice_in_dim(packed, cache_rows[i, 0] * halfway, halfway, 0),
                    lax.dynamic_slice_in_dim(packed, cache_rows[i, 1] * halfway, halfway, 0),
                ],
                axis=0,
            )
            for i in range(ring_size)
        ]
    )
    cache_heads = lax.all_to_all(cache_parts, "x", 0, 0, tiled=True)
    cache = cache_heads.reshape(group_heads, block_rows, 2, head_width).transpose(2, 1, 0, 3)
    cache = cache.reshape(2, block_rows, group_width)
    mixed = jnp.dot(attended_rows, full_out, preferred_element_type=jnp.float32)
    hidden = normalize(mixed + tokens.astype(jnp.float32))
    hidden_b = hidden.astype(jnp.bfloat16)
    own_query = jnp.dot(hidden_b, w_cq, preferred_element_type=jnp.float32).astype(jnp.bfloat16)
    cross_query = lax.all_to_all(
        own_query.reshape(rows_here, group_size, group_width).transpose(1, 0, 2),
        "head",
        0,
        0,
        tiled=True,
    ).reshape(block_rows, group_width)
    encoder_rows = encoder.shape[1]
    cross_max = (encoder_rows + halfway - 1 + 2 * halfway - 1) // (2 * halfway)
    padded_encoder = jnp.pad(
        encoder, ((0, 0), (0, cross_max * 2 * halfway + halfway - encoder_rows), (0, 0))
    )
    enc_low = prefix_below(query_places, ends, enc_lengths)
    enc_high = prefix_below(query_places, starts, enc_lengths) - 1
    cross_base = (enc_low.reshape(2, halfway)[:, 0] // halfway) * halfway
    cross_steps = (enc_high.reshape(2, halfway)[:, -1] + 1 - cross_base + 2 * halfway - 1) // (
        2 * halfway
    )
    cross_firsts = jnp.minimum(
        cross_base[:, None] + 2 * halfway * jnp.arange(cross_max, dtype=jnp.int32)[None, :],
        padded_encoder.shape[1] - 2 * halfway,
    )
    cross_sources = jnp.stack([cross_firsts, cross_firsts + halfway], axis=-1)
    crossed_group = flash(
        cross_query.reshape(2, halfway, group_width),
        enc_low.reshape(2, halfway, 1),
        enc_high.reshape(2, halfway, 1),
        padded_encoder[0],
        padded_encoder[1],
        cross_steps.astype(jnp.int32),
        cross_sources.reshape(-1).astype(jnp.int32),
        cross_firsts.reshape(-1).astype(jnp.int32),
        cross_max,
        group_heads,
    ).reshape(block_rows, group_width)
    exchanged = lax.all_to_all(
        crossed_group.reshape(group_size, rows_here, group_width), "head", 0, 0, tiled=True
    )
    crossed = exchanged.transpose(1, 0, 2).reshape(rows_here, model_width)
    summed = jnp.dot(crossed, w_co, preferred_element_type=jnp.float32)
    second = normalize(summed + hidden)
    second_b = second.astype(jnp.bfloat16)
    inner = jax.nn.gelu(
        jnp.dot(second_b, w_up, preferred_element_type=jnp.float32), approximate=False
    ).astype(jnp.bfloat16)
    output = normalize(jnp.dot(inner, w_down, preferred_element_type=jnp.float32) + second)
    output_b = output.astype(jnp.bfloat16)
    block_output = lax.all_gather(output_b, "head", axis=0, tiled=True)
    next_qkv = jnp.einsum("td,cde->cte", block_output, w_next, preferred_element_type=jnp.float32)
    return (output, cache, next_qkv)


def solution(mesh):
    ring = 4
    devices = mesh.devices.reshape(mesh.shape["blk"] // ring, ring, mesh.shape["head"])
    fine = jax.sharding.Mesh(devices, ("zy", "x", "head"))
    rows = ("zy", "x", "head")
    blocks = ("zy", "x")
    in_specs = (
        P(rows, None),
        P(),
        P(),
        P(),
        P(None, None, "head"),
        P("head", None),
        P(None, blocks, "head"),
        P(),
        P(),
        P(),
        P(),
        P(None, None, "head"),
    )
    out_specs = (P(rows, None), P(None, blocks, "head"), P(None, blocks, "head"))
    return jax.shard_map(
        on_device, mesh=fine, in_specs=in_specs, out_specs=out_specs, check_vma=False
    )
```

```python
import functools
import math

import jax
import jax.numpy as jnp
from jax import lax
from jax.experimental import pallas as pl
from jax.experimental.pallas import tpu as pltpu
from jax.sharding import PartitionSpec as P

HEADS = 16


NEGATIVE = -1e30
SCALING = 0.125
EPSILON = 1e-05


def normalize(matrix):
    center = matrix - jnp.mean(matrix, axis=-1, keepdims=True)
    return center * lax.rsqrt(jnp.mean(center * center, axis=-1, keepdims=True) + EPSILON)


def position_of(order_table, indices, halfway):
    slots = jnp.arange(order_table.shape[0], dtype=jnp.int32)
    picked = jnp.sum(
        jnp.where((indices // halfway)[:, None] == slots[None, :], order_table[None, :], 0), axis=1
    )
    return picked * halfway + indices % halfway


def group_of(places, lengths):
    ends = jnp.cumsum(lengths)
    return jnp.sum((places[:, None] >= ends[None, :]).astype(jnp.int32), axis=1)


def prefix_below(places, bounds, amounts):
    return jnp.sum(
        jnp.where(places[..., None] >= bounds, amounts, 0), axis=-1
    ).astype(jnp.int32)


def lookup(table, indices):
    slots = jnp.arange(table.shape[0], dtype=jnp.int32)
    return jnp.sum(jnp.where(indices[..., None] == slots, table, 0), axis=-1).astype(jnp.int32)


def online_update(carried, queries, key_rows, value_rows, visible):
    maxima, totals, running = carried
    heads_here = queries.shape[1]
    key_split = key_rows.reshape(key_rows.shape[0], heads_here, -1)
    value_split = value_rows.reshape(value_rows.shape[0], heads_here, -1)
    scores = (
        jnp.einsum("qhd,khd->qhk", queries, key_split, preferred_element_type=jnp.float32) * SCALING
    )
    scores = jnp.where(visible[:, None, :], scores, NEGATIVE)
    updated = jnp.maximum(maxima, jnp.max(scores, axis=2))
    factor = jnp.exp(maxima - updated)
    weights = jnp.exp(scores - updated[:, :, None])
    totals = totals * factor + jnp.sum(weights, axis=2)
    running = running * factor[:, :, None] + jnp.einsum(
        "qhk,khd->qhd",
        weights.astype(jnp.bfloat16),
        value_split,
        preferred_element_type=jnp.float32,
    )
    return (updated, totals, running)


def sweep(
    carried, queries, key_rows, value_rows, key_places, key_groups, query_places, query_groups
):
    length = key_rows.shape[0]
    block_size = math.gcd(length, 2048)
    blocks_count = length // block_size
    key_blocks = key_rows.reshape(blocks_count, block_size, key_rows.shape[1])
    value_blocks = value_rows.reshape(blocks_count, block_size, value_rows.shape[1])
    group_blocks = key_groups.reshape(blocks_count, block_size)
    if key_places is None:
        place_blocks = group_blocks
    else:
        place_blocks = key_places.reshape(blocks_count, block_size)

    def advance(status, element):
        key_block, value_block, place_block, group_block = element
        visible = group_block[None, :] == query_groups[:, None]
        if key_places is None:
            return (online_update(status, queries, key_block, value_block, visible), None)
        visible = visible & (place_block[None, :] <= query_places[:, None])
        updated = online_update(status, queries, key_block, value_block, visible)
        return (updated, None)

    carried, unused = lax.scan(
        advance, carried, (key_blocks, value_blocks, place_blocks, group_blocks)
    )
    return carried


def empty_state(count_q, heads_here, head_width):
    return (
        jnp.full((count_q, heads_here), NEGATIVE, jnp.float32),
        jnp.zeros((count_q, heads_here), jnp.float32),
        jnp.zeros((count_q, heads_here, head_width), jnp.float32),
    )


def finish(carried):
    maxima, totals, running = carried
    return (running / totals[:, :, None]).reshape(running.shape[0], -1).astype(jnp.bfloat16)


def flash_kernel(
    steps_ref, sources_ref, bases_ref, q_ref, low_ref, high_ref, k_hbm, v_hbm, o_ref,
    kbuf, vbuf, sem, qm_sc, m_sc, l_sc, acc_sc, *, max_steps, heads, head_width
):
    half = pl.program_id(0)
    count = steps_ref[half]
    tile = kbuf.shape[1] // 2
    width = kbuf.shape[2]

    def copies(step, slot):
        result = []
        for j in range(2):
            source = pl.multiple_of(sources_ref[(half * max_steps + step) * 2 + j], tile)
            window = pl.ds(j * tile, tile)
            result.append(pltpu.make_async_copy(
                k_hbm.at[pl.ds(source, tile)], kbuf.at[slot, window], sem.at[0, slot, j]))
            result.append(pltpu.make_async_copy(
                v_hbm.at[pl.ds(source, tile)], vbuf.at[slot, window], sem.at[1, slot, j]))
        return result

    for copy in copies(0, 0):
        copy.start()
    column_head = lax.broadcasted_iota(jnp.int32, (1, width), 1) // head_width
    q = q_ref[0]
    for h in range(heads):
        qm_sc[h] = jnp.where(column_head == h, q, jnp.zeros_like(q))
    m_sc[...] = jnp.full(m_sc.shape, NEGATIVE, jnp.float32)
    l_sc[...] = jnp.zeros(l_sc.shape, jnp.float32)
    acc_sc[...] = jnp.zeros(acc_sc.shape, jnp.float32)
    low = low_ref[0]
    high = high_ref[0]

    def body(step, carry):
        slot = step % 2
        for copy in copies(step, slot):
            copy.wait()

        @pl.when(step + 1 < count)
        def _():
            for copy in copies(step + 1, 1 - slot):
                copy.start()

        base = bases_ref[half * max_steps + step]
        places = base + lax.broadcasted_iota(jnp.int32, (1, 2 * tile), 1)
        visible = (places >= low) & (places <= high)
        keys = kbuf[slot]
        values = vbuf[slot]
        for h in range(heads):
            scores = lax.dot_general(
                qm_sc[h], keys, (((1,), (1,)), ((), ())), preferred_element_type=jnp.float32
            ) * SCALING
            scores = jnp.where(visible, scores, NEGATIVE)
            previous = m_sc[h]
            updated = jnp.maximum(previous, jnp.max(scores, axis=1, keepdims=True))
            factor = jnp.exp(previous - updated)
            weights = jnp.exp(scores - updated)
            l_sc[h] = l_sc[h] * factor + jnp.sum(weights, axis=1, keepdims=True)
            acc_sc[h] = acc_sc[h] * factor + jnp.dot(
                weights.astype(jnp.bfloat16), values, preferred_element_type=jnp.float32
            )
            m_sc[h] = updated
        return carry

    lax.fori_loop(0, count, body, 0)
    out = jnp.zeros(acc_sc.shape[1:], jnp.float32)
    for h in range(heads):
        out = jnp.where(column_head == h, acc_sc[h] / l_sc[h], out)
    o_ref[0] = out.astype(o_ref.dtype)


def flash(queries, low, high, keys, values, steps, sources, bases, max_steps, heads):
    halves, tile, width = queries.shape
    head_width = width // heads
    kernel = functools.partial(
        flash_kernel, max_steps=max_steps, heads=heads, head_width=head_width
    )
    row_spec = pl.BlockSpec((1, tile, width), lambda h, *refs: (h, 0, 0))
    bound_spec = pl.BlockSpec((1, tile, 1), lambda h, *refs: (h, 0, 0))
    flops = 4 * halves * max_steps * tile * 2 * tile * width * heads
    return pl.pallas_call(
        kernel,
        out_shape=jax.ShapeDtypeStruct(queries.shape, jnp.bfloat16),
        grid_spec=pltpu.PrefetchScalarGridSpec(
            num_scalar_prefetch=3,
            grid=(halves,),
            in_specs=[
                row_spec,
                bound_spec,
                bound_spec,
                pl.BlockSpec(memory_space=pl.ANY),
                pl.BlockSpec(memory_space=pl.ANY),
            ],
            out_specs=row_spec,
            scratch_shapes=[
                pltpu.VMEM((2, 2 * tile, width), keys.dtype),
                pltpu.VMEM((2, 2 * tile, width), values.dtype),
                pltpu.SemaphoreType.DMA((2, 2, 2)),
                pltpu.VMEM((heads, tile, width), jnp.bfloat16),
                pltpu.VMEM((heads, tile, 1), jnp.float32),
                pltpu.VMEM((heads, tile, 1), jnp.float32),
                pltpu.VMEM((heads, tile, width), jnp.float32),
            ],
        ),
        compiler_params=pltpu.CompilerParams(dimension_semantics=("arbitrary",)),
        cost_estimate=pl.CostEstimate(
            flops=flops,
            transcendentals=halves * max_steps * tile * 2 * tile * heads,
            bytes_accessed=halves * max_steps * 2 * 2 * tile * width * 2,
        ),
    )(steps, sources, bases, queries, low, high, keys, values)


def single_kernel(
    steps_ref, sources_ref, bases_ref, limits_ref, q_ref, low_ref, high_ref, kv_hbm, o_ref,
    buf, sem, m_sc, l_sc, acc_sc, *, max_steps, head_width, pieces
):
    half = pl.program_id(0)
    count = steps_ref[half]
    tile = buf.shape[1] // pieces

    def copies(step, slot):
        result = []
        for j in range(pieces):
            source = pl.multiple_of(sources_ref[(half * max_steps + step) * pieces + j], tile)
            result.append(pltpu.make_async_copy(
                kv_hbm.at[pl.ds(source, tile)], buf.at[slot, pl.ds(j * tile, tile)], sem.at[slot, j]))
        return result

    for copy in copies(0, 0):
        copy.start()
    m_sc[...] = jnp.full(m_sc.shape, NEGATIVE, jnp.float32)
    l_sc[...] = jnp.zeros(l_sc.shape, jnp.float32)
    acc_sc[...] = jnp.zeros(acc_sc.shape, jnp.float32)
    q = q_ref[0]
    low = low_ref[0]
    high = high_ref[0]

    def body(step, carry):
        slot = step % 2
        for copy in copies(step, slot):
            copy.wait()

        @pl.when(step + 1 < count)
        def _():
            for copy in copies(step + 1, 1 - slot):
                copy.start()

        base = bases_ref[half * max_steps + step]
        keys = buf[slot, :, :head_width]
        values = buf[slot, :, head_width:]

        def update(masked):
            scores = lax.dot_general(
                q, keys, (((1,), (1,)), ((), ())), preferred_element_type=jnp.float32
            ) * SCALING
            if masked:
                places = base + lax.broadcasted_iota(jnp.int32, (1, pieces * tile), 1)
                visible = (places >= low) & (places <= high)
                scores = jnp.where(visible, scores, NEGATIVE)
            previous = m_sc[...]
            updated = jnp.maximum(previous, jnp.max(scores, axis=1, keepdims=True))
            factor = jnp.exp(previous - updated)
            weights = jnp.exp(scores - updated)
            l_sc[...] = l_sc[...] * factor + jnp.sum(weights, axis=1, keepdims=True)
            acc_sc[...] = acc_sc[...] * factor + jnp.dot(
                weights.astype(jnp.bfloat16), values, preferred_element_type=jnp.float32
            )
            m_sc[...] = updated

        full = (base >= limits_ref[2 * half]) & (base + pieces * tile - 1 <= limits_ref[2 * half + 1])

        @pl.when(full)
        def _():
            update(False)

        @pl.when(jnp.logical_not(full))
        def _():
            update(True)

        return carry

    lax.fori_loop(0, count, body, 0)
    o_ref[0] = (acc_sc[...] / l_sc[...]).astype(o_ref.dtype)


def single(queries, low, high, packed, steps, sources, bases, limits, max_steps, pieces):
    halves, tile, head_width = queries.shape
    kernel = functools.partial(
        single_kernel, max_steps=max_steps, head_width=head_width, pieces=pieces
    )
    row_spec = pl.BlockSpec((1, tile, head_width), lambda h, *refs: (h, 0, 0))
    bound_spec = pl.BlockSpec((1, tile, 1), lambda h, *refs: (h, 0, 0))
    return pl.pallas_call(
        kernel,
        out_shape=jax.ShapeDtypeStruct(queries.shape, jnp.bfloat16),
        grid_spec=pltpu.PrefetchScalarGridSpec(
            num_scalar_prefetch=4,
            grid=(halves,),
            in_specs=[row_spec, bound_spec, bound_spec, pl.BlockSpec(memory_space=pl.ANY)],
            out_specs=row_spec,
            scratch_shapes=[
                pltpu.VMEM((2, pieces * tile, packed.shape[1]), packed.dtype),
                pltpu.SemaphoreType.DMA((2, pieces)),
                pltpu.VMEM((tile, 1), jnp.float32),
                pltpu.VMEM((tile, 1), jnp.float32),
                pltpu.VMEM((tile, head_width), jnp.float32),
            ],
        ),
        compiler_params=pltpu.CompilerParams(dimension_semantics=("arbitrary",)),
        cost_estimate=pl.CostEstimate(
            flops=2 * halves * (max_steps // 2) * tile * pieces * tile * head_width * 2,
            transcendentals=halves * (max_steps // 2) * tile * pieces * tile,
            bytes_accessed=halves * (max_steps // 2) * pieces * tile * packed.shape[1] * 2,
        ),
    )(steps, sources, bases, limits, queries, low, high, packed)


def on_device(
    tokens,
    block_order,
    request_lengths,
    enc_lengths,
    w_qkv,
    w_out,
    enc_kv,
    w_cq,
    w_co,
    w_up,
    w_down,
    w_next,
):
    rows_here = tokens.shape[0]
    model_width = tokens.shape[1]
    group_size = lax.axis_size("head")
    cycle_size = lax.axis_size("zy") * lax.axis_size("x")
    block_rows = rows_here * group_size
    halfway = block_rows // 2
    group_width = w_qkv.shape[2]
    head_width = model_width // HEADS
    group_heads = group_width // head_width
    member = lax.axis_index("head")
    ring_size = lax.axis_size("x")
    ring_index = lax.axis_index("x")
    cycle_index = lax.axis_index("zy") * ring_size + ring_index
    full_out = lax.all_to_all(
        jnp.broadcast_to(w_out[None], (group_size,) + w_out.shape), "head", 0, 0, tiled=True
    ).reshape(model_width, model_width)
    gathered = lax.all_gather(tokens, "head", axis=0, tiled=True)
    projected = jnp.einsum(
        "td,cde->cte", gathered, w_qkv, preferred_element_type=jnp.float32
    ).astype(jnp.bfloat16)
    block_start = cycle_index * block_rows
    query_places = position_of(
        block_order, block_start + jnp.arange(block_rows, dtype=jnp.int32), halfway
    )
    slots = jnp.arange(2 * cycle_size, dtype=jnp.int32)
    holders = jnp.sum(jnp.where(block_order[:, None] == slots[None, :], slots[:, None], 0), axis=0)
    per_head = projected.reshape(3, block_rows, group_heads, head_width).transpose(2, 1, 0, 3)
    per_head = per_head.reshape(group_heads, block_rows, 3 * head_width)
    mine = lax.all_to_all(per_head, "x", 0, 0, tiled=True)
    packed = lax.all_gather(mine[:, :, head_width:], "zy", axis=0, tiled=True)
    packed = packed.reshape(cycle_size * block_rows, 2 * head_width)
    full_out, enc_after = lax.optimization_barrier((full_out, enc_kv))
    enc_ring = lax.all_to_all(
        jnp.broadcast_to(enc_after[None], (ring_size,) + enc_kv.shape), "x", 0, 0, tiled=True
    )
    enc_ring = enc_ring.transpose(1, 0, 2, 3).reshape(
        2, ring_size * enc_kv.shape[1], enc_kv.shape[2]
    )
    full_out, packed, late_kv = lax.optimization_barrier((full_out, packed, enc_ring))
    encoder = lax.all_gather(late_kv, "zy", axis=1, tiled=True)
    ends = jnp.cumsum(request_lengths).astype(jnp.int32)
    starts = ends - request_lengths
    halves_here = 2 * ring_size
    first_half = lax.axis_index("zy") * halves_here
    pair = lax.dynamic_slice_in_dim(block_order, first_half, halves_here, 0)
    low_block = prefix_below(pair * halfway, ends, request_lengths) // halfway
    pieces = 8
    self_steps = (pair - low_block) // pieces + 1
    self_max = (2 * cycle_size + pieces - 1) // pieces
    firsts = low_block[:, None] + pieces * jnp.arange(self_max, dtype=jnp.int32)[None, :]
    self_sources = lookup(
        holders,
        jnp.minimum(firsts[:, :, None] + jnp.arange(pieces, dtype=jnp.int32), 2 * cycle_size - 1),
    ) * halfway
    places_here = (pair[:, None] * halfway + jnp.arange(halfway, dtype=jnp.int32)[None, :])
    self_low = prefix_below(places_here, ends, request_lengths).reshape(halves_here, halfway)
    limits = jnp.stack([self_low[:, -1], places_here[:, 0]], axis=1).reshape(-1)
    single_out = single(
        mine[:, :, :head_width].reshape(halves_here, halfway, head_width),
        self_low.reshape(halves_here, halfway, 1),
        places_here.reshape(halves_here, halfway, 1),
        packed,
        self_steps.astype(jnp.int32),
        self_sources.reshape(-1).astype(jnp.int32),
        (firsts * halfway).reshape(-1).astype(jnp.int32),
        limits.astype(jnp.int32),
        self_max,
        pieces,
    )
    owners = lax.all_to_all(
        single_out.reshape(ring_size * group_size, rows_here, head_width),
        ("x", "head"),
        0,
        0,
        tiled=True,
    )
    attended_rows = owners.reshape(ring_size, group_size, rows_here, head_width)
    attended_rows = attended_rows.transpose(2, 1, 0, 3).reshape(rows_here, model_width)
    group_blocks = lax.axis_index("zy") * ring_size + jnp.arange(ring_size, dtype=jnp.int32)
    cache_rows = lookup(
        holders, jnp.stack([2 * group_blocks, 2 * group_blocks + 1], axis=1)
    )
    cache_parts = jnp.stack(
        [
            jnp.concatenate(
                [
                    lax.dynamic_slice_in_dim(packed, cache_rows[i, 0] * halfway, halfway, 0),
                    lax.dynamic_slice_in_dim(packed, cache_rows[i, 1] * halfway, halfway, 0),
                ],
                axis=0,
            )
            for i in range(ring_size)
        ]
    )
    cache_heads = lax.all_to_all(cache_parts, "x", 0, 0, tiled=True)
    cache = cache_heads.reshape(group_heads, block_rows, 2, head_width).transpose(2, 1, 0, 3)
    cache = cache.reshape(2, block_rows, group_width)
    mixed = jnp.dot(attended_rows, full_out, preferred_element_type=jnp.float32)
    hidden = normalize(mixed + tokens.astype(jnp.float32))
    hidden_b = hidden.astype(jnp.bfloat16)
    own_query = jnp.dot(hidden_b, w_cq, preferred_element_type=jnp.float32).astype(jnp.bfloat16)
    cross_query = lax.all_to_all(
        own_query.reshape(rows_here, group_size, group_width).transpose(1, 0, 2),
        "head",
        0,
        0,
        tiled=True,
    ).reshape(block_rows, group_width)
    encoder_rows = encoder.shape[1]
    cross_max = (encoder_rows + halfway - 1 + 2 * halfway - 1) // (2 * halfway)
    padded_encoder = jnp.pad(
        encoder, ((0, 0), (0, cross_max * 2 * halfway + halfway - encoder_rows), (0, 0))
    )
    enc_low = prefix_below(query_places, ends, enc_lengths)
    enc_high = prefix_below(query_places, starts, enc_lengths) - 1
    cross_base = (enc_low.reshape(2, halfway)[:, 0] // halfway) * halfway
    cross_steps = (enc_high.reshape(2, halfway)[:, -1] + 1 - cross_base + 2 * halfway - 1) // (
        2 * halfway
    )
    cross_firsts = jnp.minimum(
        cross_base[:, None] + 2 * halfway * jnp.arange(cross_max, dtype=jnp.int32)[None, :],
        padded_encoder.shape[1] - 2 * halfway,
    )
    cross_sources = jnp.stack([cross_firsts, cross_firsts + halfway], axis=-1)
    crossed_group = flash(
        cross_query.reshape(2, halfway, group_width),
        enc_low.reshape(2, halfway, 1),
        enc_high.reshape(2, halfway, 1),
        padded_encoder[0],
        padded_encoder[1],
        cross_steps.astype(jnp.int32),
        cross_sources.reshape(-1).astype(jnp.int32),
        cross_firsts.reshape(-1).astype(jnp.int32),
        cross_max,
        group_heads,
    ).reshape(block_rows, group_width)
    exchanged = lax.all_to_all(
        crossed_group.reshape(group_size, rows_here, group_width), "head", 0, 0, tiled=True
    )
    crossed = exchanged.transpose(1, 0, 2).reshape(rows_here, model_width)
    summed = jnp.dot(crossed, w_co, preferred_element_type=jnp.float32)
    second = normalize(summed + hidden)
    second_b = second.astype(jnp.bfloat16)
    inner = jax.nn.gelu(
        jnp.dot(second_b, w_up, preferred_element_type=jnp.float32), approximate=False
    ).astype(jnp.bfloat16)
    output = normalize(jnp.dot(inner, w_down, preferred_element_type=jnp.float32) + second)
    output_b = output.astype(jnp.bfloat16)
    block_output = lax.all_gather(output_b, "head", axis=0, tiled=True)
    next_qkv = jnp.einsum("td,cde->cte", block_output, w_next, preferred_element_type=jnp.float32)
    return (output, cache, next_qkv)


def solution(mesh):
    ring = 4
    devices = mesh.devices.reshape(mesh.shape["blk"] // ring, ring, mesh.shape["head"])
    fine = jax.sharding.Mesh(devices, ("zy", "x", "head"))
    rows = ("zy", "x", "head")
    blocks = ("zy", "x")
    in_specs = (
        P(rows, None),
        P(),
        P(),
        P(),
        P(None, None, "head"),
        P("head", None),
        P(None, blocks, "head"),
        P(),
        P(),
        P(),
        P(),
        P(None, None, "head"),
    )
    out_specs = (P(rows, None), P(None, blocks, "head"), P(None, blocks, "head"))
    return jax.shard_map(
        on_device, mesh=fine, in_specs=in_specs, out_specs=out_specs, check_vma=False
    )
```

```python
import functools
import math

import jax
import jax.numpy as jnp
from jax import lax
from jax.experimental import pallas as pl
from jax.experimental.pallas import tpu as pltpu
from jax.sharding import PartitionSpec as P

HEADS = 16


NEGATIVE = -1e30
SCALING = 0.125
EPSILON = 1e-05


def normalize(matrix):
    center = matrix - jnp.mean(matrix, axis=-1, keepdims=True)
    return center * lax.rsqrt(jnp.mean(center * center, axis=-1, keepdims=True) + EPSILON)


def position_of(order_table, indices, halfway):
    slots = jnp.arange(order_table.shape[0], dtype=jnp.int32)
    picked = jnp.sum(
        jnp.where((indices // halfway)[:, None] == slots[None, :], order_table[None, :], 0), axis=1
    )
    return picked * halfway + indices % halfway


def group_of(places, lengths):
    ends = jnp.cumsum(lengths)
    return jnp.sum((places[:, None] >= ends[None, :]).astype(jnp.int32), axis=1)


def prefix_below(places, bounds, amounts):
    return jnp.sum(
        jnp.where(places[..., None] >= bounds, amounts, 0), axis=-1
    ).astype(jnp.int32)


def lookup(table, indices):
    slots = jnp.arange(table.shape[0], dtype=jnp.int32)
    return jnp.sum(jnp.where(indices[..., None] == slots, table, 0), axis=-1).astype(jnp.int32)


def online_update(carried, queries, key_rows, value_rows, visible):
    maxima, totals, running = carried
    heads_here = queries.shape[1]
    key_split = key_rows.reshape(key_rows.shape[0], heads_here, -1)
    value_split = value_rows.reshape(value_rows.shape[0], heads_here, -1)
    scores = (
        jnp.einsum("qhd,khd->qhk", queries, key_split, preferred_element_type=jnp.float32) * SCALING
    )
    scores = jnp.where(visible[:, None, :], scores, NEGATIVE)
    updated = jnp.maximum(maxima, jnp.max(scores, axis=2))
    factor = jnp.exp(maxima - updated)
    weights = jnp.exp(scores - updated[:, :, None])
    totals = totals * factor + jnp.sum(weights, axis=2)
    running = running * factor[:, :, None] + jnp.einsum(
        "qhk,khd->qhd",
        weights.astype(jnp.bfloat16),
        value_split,
        preferred_element_type=jnp.float32,
    )
    return (updated, totals, running)


def sweep(
    carried, queries, key_rows, value_rows, key_places, key_groups, query_places, query_groups
):
    length = key_rows.shape[0]
    block_size = math.gcd(length, 2048)
    blocks_count = length // block_size
    key_blocks = key_rows.reshape(blocks_count, block_size, key_rows.shape[1])
    value_blocks = value_rows.reshape(blocks_count, block_size, value_rows.shape[1])
    group_blocks = key_groups.reshape(blocks_count, block_size)
    if key_places is None:
        place_blocks = group_blocks
    else:
        place_blocks = key_places.reshape(blocks_count, block_size)

    def advance(status, element):
        key_block, value_block, place_block, group_block = element
        visible = group_block[None, :] == query_groups[:, None]
        if key_places is None:
            return (online_update(status, queries, key_block, value_block, visible), None)
        visible = visible & (place_block[None, :] <= query_places[:, None])
        updated = online_update(status, queries, key_block, value_block, visible)
        return (updated, None)

    carried, unused = lax.scan(
        advance, carried, (key_blocks, value_blocks, place_blocks, group_blocks)
    )
    return carried


def empty_state(count_q, heads_here, head_width):
    return (
        jnp.full((count_q, heads_here), NEGATIVE, jnp.float32),
        jnp.zeros((count_q, heads_here), jnp.float32),
        jnp.zeros((count_q, heads_here, head_width), jnp.float32),
    )


def finish(carried):
    maxima, totals, running = carried
    return (running / totals[:, :, None]).reshape(running.shape[0], -1).astype(jnp.bfloat16)


def flash_kernel(
    steps_ref, sources_ref, bases_ref, q_ref, low_ref, high_ref, k_hbm, v_hbm, o_ref,
    kbuf, vbuf, sem, qm_sc, m_sc, l_sc, acc_sc, *, max_steps, heads, head_width
):
    half = pl.program_id(0)
    count = steps_ref[half]
    tile = kbuf.shape[1] // 2
    width = kbuf.shape[2]

    def copies(step, slot):
        result = []
        for j in range(2):
            source = pl.multiple_of(sources_ref[(half * max_steps + step) * 2 + j], tile)
            window = pl.ds(j * tile, tile)
            result.append(pltpu.make_async_copy(
                k_hbm.at[pl.ds(source, tile)], kbuf.at[slot, window], sem.at[0, slot, j]))
            result.append(pltpu.make_async_copy(
                v_hbm.at[pl.ds(source, tile)], vbuf.at[slot, window], sem.at[1, slot, j]))
        return result

    for copy in copies(0, 0):
        copy.start()
    column_head = lax.broadcasted_iota(jnp.int32, (1, width), 1) // head_width
    q = q_ref[0]
    for h in range(heads):
        qm_sc[h] = jnp.where(column_head == h, q, jnp.zeros_like(q))
    m_sc[...] = jnp.full(m_sc.shape, NEGATIVE, jnp.float32)
    l_sc[...] = jnp.zeros(l_sc.shape, jnp.float32)
    acc_sc[...] = jnp.zeros(acc_sc.shape, jnp.float32)
    low = low_ref[0]
    high = high_ref[0]

    def body(step, carry):
        slot = step % 2
        for copy in copies(step, slot):
            copy.wait()

        @pl.when(step + 1 < count)
        def _():
            for copy in copies(step + 1, 1 - slot):
                copy.start()

        base = bases_ref[half * max_steps + step]
        places = base + lax.broadcasted_iota(jnp.int32, (1, 2 * tile), 1)
        visible = (places >= low) & (places <= high)
        keys = kbuf[slot]
        values = vbuf[slot]
        for h in range(heads):
            scores = lax.dot_general(
                qm_sc[h], keys, (((1,), (1,)), ((), ())), preferred_element_type=jnp.float32
            ) * SCALING
            scores = jnp.where(visible, scores, NEGATIVE)
            previous = m_sc[h]
            updated = jnp.maximum(previous, jnp.max(scores, axis=1, keepdims=True))
            factor = jnp.exp(previous - updated)
            weights = jnp.exp(scores - updated)
            l_sc[h] = l_sc[h] * factor + jnp.sum(weights, axis=1, keepdims=True)
            acc_sc[h] = acc_sc[h] * factor + jnp.dot(
                weights.astype(jnp.bfloat16), values, preferred_element_type=jnp.float32
            )
            m_sc[h] = updated
        return carry

    lax.fori_loop(0, count, body, 0)
    out = jnp.zeros(acc_sc.shape[1:], jnp.float32)
    for h in range(heads):
        out = jnp.where(column_head == h, acc_sc[h] / l_sc[h], out)
    o_ref[0] = out.astype(o_ref.dtype)


def flash(queries, low, high, keys, values, steps, sources, bases, max_steps, heads):
    halves, tile, width = queries.shape
    head_width = width // heads
    kernel = functools.partial(
        flash_kernel, max_steps=max_steps, heads=heads, head_width=head_width
    )
    row_spec = pl.BlockSpec((1, tile, width), lambda h, *refs: (h, 0, 0))
    bound_spec = pl.BlockSpec((1, tile, 1), lambda h, *refs: (h, 0, 0))
    flops = 4 * halves * max_steps * tile * 2 * tile * width * heads
    return pl.pallas_call(
        kernel,
        out_shape=jax.ShapeDtypeStruct(queries.shape, jnp.bfloat16),
        grid_spec=pltpu.PrefetchScalarGridSpec(
            num_scalar_prefetch=3,
            grid=(halves,),
            in_specs=[
                row_spec,
                bound_spec,
                bound_spec,
                pl.BlockSpec(memory_space=pl.ANY),
                pl.BlockSpec(memory_space=pl.ANY),
            ],
            out_specs=row_spec,
            scratch_shapes=[
                pltpu.VMEM((2, 2 * tile, width), keys.dtype),
                pltpu.VMEM((2, 2 * tile, width), values.dtype),
                pltpu.SemaphoreType.DMA((2, 2, 2)),
                pltpu.VMEM((heads, tile, width), jnp.bfloat16),
                pltpu.VMEM((heads, tile, 1), jnp.float32),
                pltpu.VMEM((heads, tile, 1), jnp.float32),
                pltpu.VMEM((heads, tile, width), jnp.float32),
            ],
        ),
        compiler_params=pltpu.CompilerParams(dimension_semantics=("arbitrary",)),
        cost_estimate=pl.CostEstimate(
            flops=flops,
            transcendentals=halves * max_steps * tile * 2 * tile * heads,
            bytes_accessed=halves * max_steps * 2 * 2 * tile * width * 2,
        ),
    )(steps, sources, bases, queries, low, high, keys, values)


def single_kernel(
    steps_ref, sources_ref, bases_ref, limits_ref, q_ref, low_ref, high_ref, kv_hbm, o_ref,
    buf, sem, m_sc, l_sc, acc_sc, *, max_steps, head_width, pieces
):
    half = pl.program_id(0)
    count = steps_ref[half]
    tile = buf.shape[1] // pieces

    def copies(step, slot):
        result = []
        for j in range(pieces):
            source = pl.multiple_of(sources_ref[(half * max_steps + step) * pieces + j], tile)
            result.append(pltpu.make_async_copy(
                kv_hbm.at[pl.ds(source, tile)], buf.at[slot, pl.ds(j * tile, tile)], sem.at[slot, j]))
        return result

    for copy in copies(0, 0):
        copy.start()
    m_sc[...] = jnp.full(m_sc.shape, NEGATIVE, jnp.float32)
    l_sc[...] = jnp.zeros(l_sc.shape, jnp.float32)
    acc_sc[...] = jnp.zeros(acc_sc.shape, jnp.float32)
    q = q_ref[0]
    low = low_ref[0]
    high = high_ref[0]

    def body(step, carry):
        slot = step % 2
        for copy in copies(step, slot):
            copy.wait()

        @pl.when(step + 1 < count)
        def _():
            for copy in copies(step + 1, 1 - slot):
                copy.start()

        base = bases_ref[half * max_steps + step]
        keys = buf[slot, :, :head_width]
        values = buf[slot, :, head_width:]

        def update(masked):
            scores = lax.dot_general(
                q, keys, (((1,), (1,)), ((), ())), preferred_element_type=jnp.float32
            ) * SCALING
            if masked:
                places = base + lax.broadcasted_iota(jnp.int32, (1, pieces * tile), 1)
                visible = (places >= low) & (places <= high)
                scores = jnp.where(visible, scores, NEGATIVE)
            previous = m_sc[...]
            updated = jnp.maximum(previous, jnp.max(scores, axis=1, keepdims=True))
            factor = jnp.exp(previous - updated)
            weights = jnp.exp(scores - updated)
            l_sc[...] = l_sc[...] * factor + jnp.sum(weights, axis=1, keepdims=True)
            acc_sc[...] = acc_sc[...] * factor + jnp.dot(
                weights.astype(jnp.bfloat16), values, preferred_element_type=jnp.float32
            )
            m_sc[...] = updated

        full = (base >= limits_ref[2 * half]) & (base + pieces * tile - 1 <= limits_ref[2 * half + 1])

        @pl.when(full)
        def _():
            update(False)

        @pl.when(jnp.logical_not(full))
        def _():
            update(True)

        return carry

    lax.fori_loop(0, count, body, 0)
    o_ref[0] = (acc_sc[...] / l_sc[...]).astype(o_ref.dtype)


def single(queries, low, high, packed, steps, sources, bases, limits, max_steps, pieces):
    halves, tile, head_width = queries.shape
    kernel = functools.partial(
        single_kernel, max_steps=max_steps, head_width=head_width, pieces=pieces
    )
    row_spec = pl.BlockSpec((1, tile, head_width), lambda h, *refs: (h, 0, 0))
    bound_spec = pl.BlockSpec((1, tile, 1), lambda h, *refs: (h, 0, 0))
    return pl.pallas_call(
        kernel,
        out_shape=jax.ShapeDtypeStruct(queries.shape, jnp.bfloat16),
        grid_spec=pltpu.PrefetchScalarGridSpec(
            num_scalar_prefetch=4,
            grid=(halves,),
            in_specs=[row_spec, bound_spec, bound_spec, pl.BlockSpec(memory_space=pl.ANY)],
            out_specs=row_spec,
            scratch_shapes=[
                pltpu.VMEM((2, pieces * tile, packed.shape[1]), packed.dtype),
                pltpu.SemaphoreType.DMA((2, pieces)),
                pltpu.VMEM((tile, 1), jnp.float32),
                pltpu.VMEM((tile, 1), jnp.float32),
                pltpu.VMEM((tile, head_width), jnp.float32),
            ],
        ),
        compiler_params=pltpu.CompilerParams(dimension_semantics=("arbitrary",)),
        cost_estimate=pl.CostEstimate(
            flops=2 * halves * (max_steps // 2) * tile * pieces * tile * head_width * 2,
            transcendentals=halves * (max_steps // 2) * tile * pieces * tile,
            bytes_accessed=halves * (max_steps // 2) * pieces * tile * packed.shape[1] * 2,
        ),
    )(steps, sources, bases, limits, queries, low, high, packed)


def on_device(
    tokens,
    block_order,
    request_lengths,
    enc_lengths,
    w_qkv,
    w_out,
    enc_kv,
    w_cq,
    w_co,
    w_up,
    w_down,
    w_next,
):
    rows_here = tokens.shape[0]
    model_width = tokens.shape[1]
    group_size = lax.axis_size("head")
    cycle_size = lax.axis_size("zy") * lax.axis_size("x")
    block_rows = rows_here * group_size
    halfway = block_rows // 2
    group_width = w_qkv.shape[2]
    head_width = model_width // HEADS
    group_heads = group_width // head_width
    member = lax.axis_index("head")
    ring_size = lax.axis_size("x")
    ring_index = lax.axis_index("x")
    cycle_index = lax.axis_index("zy") * ring_size + ring_index
    full_out = lax.all_to_all(
        jnp.broadcast_to(w_out[None], (group_size,) + w_out.shape), "head", 0, 0, tiled=True
    ).reshape(model_width, model_width)
    gathered = lax.all_gather(tokens, "head", axis=0, tiled=True)
    projected = jnp.einsum(
        "td,cde->cte", gathered, w_qkv, preferred_element_type=jnp.float32
    ).astype(jnp.bfloat16)
    block_start = cycle_index * block_rows
    query_places = position_of(
        block_order, block_start + jnp.arange(block_rows, dtype=jnp.int32), halfway
    )
    slots = jnp.arange(2 * cycle_size, dtype=jnp.int32)
    holders = jnp.sum(jnp.where(block_order[:, None] == slots[None, :], slots[:, None], 0), axis=0)
    per_head = projected.reshape(3, block_rows, group_heads, head_width).transpose(2, 1, 0, 3)
    per_head = per_head.reshape(group_heads, block_rows, 3 * head_width)
    mine = lax.all_to_all(per_head, "x", 0, 0, tiled=True)
    packed = lax.all_gather(mine[:, :, head_width:], "zy", axis=0, tiled=True)
    packed = packed.reshape(cycle_size * block_rows, 2 * head_width)
    full_out, enc_after = lax.optimization_barrier((full_out, enc_kv))
    enc_ring = lax.all_to_all(
        jnp.broadcast_to(enc_after[None], (ring_size,) + enc_kv.shape), "x", 0, 0, tiled=True
    )
    enc_ring = enc_ring.transpose(1, 0, 2, 3).reshape(
        2, ring_size * enc_kv.shape[1], enc_kv.shape[2]
    )
    full_out, packed, late_kv = lax.optimization_barrier((full_out, packed, enc_ring))
    encoder = lax.all_gather(late_kv, "zy", axis=1, tiled=True)
    ends = jnp.cumsum(request_lengths).astype(jnp.int32)
    starts = ends - request_lengths
    halves_here = 2 * ring_size
    first_half = lax.axis_index("zy") * halves_here
    pair = lax.dynamic_slice_in_dim(block_order, first_half, halves_here, 0)
    low_block = prefix_below(pair * halfway, ends, request_lengths) // halfway
    pieces = 16
    self_steps = (pair - low_block) // pieces + 1
    self_max = (2 * cycle_size + pieces - 1) // pieces
    firsts = low_block[:, None] + pieces * jnp.arange(self_max, dtype=jnp.int32)[None, :]
    self_sources = lookup(
        holders,
        jnp.minimum(firsts[:, :, None] + jnp.arange(pieces, dtype=jnp.int32), 2 * cycle_size - 1),
    ) * halfway
    places_here = (pair[:, None] * halfway + jnp.arange(halfway, dtype=jnp.int32)[None, :])
    self_low = prefix_below(places_here, ends, request_lengths).reshape(halves_here, halfway)
    limits = jnp.stack([self_low[:, -1], places_here[:, 0]], axis=1).reshape(-1)
    single_out = single(
        mine[:, :, :head_width].reshape(halves_here, halfway, head_width),
        self_low.reshape(halves_here, halfway, 1),
        places_here.reshape(halves_here, halfway, 1),
        packed,
        self_steps.astype(jnp.int32),
        self_sources.reshape(-1).astype(jnp.int32),
        (firsts * halfway).reshape(-1).astype(jnp.int32),
        limits.astype(jnp.int32),
        self_max,
        pieces,
    )
    owners = lax.all_to_all(
        single_out.reshape(ring_size * group_size, rows_here, head_width),
        ("x", "head"),
        0,
        0,
        tiled=True,
    )
    attended_rows = owners.reshape(ring_size, group_size, rows_here, head_width)
    attended_rows = attended_rows.transpose(2, 1, 0, 3).reshape(rows_here, model_width)
    group_blocks = lax.axis_index("zy") * ring_size + jnp.arange(ring_size, dtype=jnp.int32)
    cache_rows = lookup(
        holders, jnp.stack([2 * group_blocks, 2 * group_blocks + 1], axis=1)
    )
    cache_parts = jnp.stack(
        [
            jnp.concatenate(
                [
                    lax.dynamic_slice_in_dim(packed, cache_rows[i, 0] * halfway, halfway, 0),
                    lax.dynamic_slice_in_dim(packed, cache_rows[i, 1] * halfway, halfway, 0),
                ],
                axis=0,
            )
            for i in range(ring_size)
        ]
    )
    cache_heads = lax.all_to_all(cache_parts, "x", 0, 0, tiled=True)
    cache = cache_heads.reshape(group_heads, block_rows, 2, head_width).transpose(2, 1, 0, 3)
    cache = cache.reshape(2, block_rows, group_width)
    mixed = jnp.dot(attended_rows, full_out, preferred_element_type=jnp.float32)
    hidden = normalize(mixed + tokens.astype(jnp.float32))
    hidden_b = hidden.astype(jnp.bfloat16)
    own_query = jnp.dot(hidden_b, w_cq, preferred_element_type=jnp.float32).astype(jnp.bfloat16)
    cross_query = lax.all_to_all(
        own_query.reshape(rows_here, group_size, group_width).transpose(1, 0, 2),
        "head",
        0,
        0,
        tiled=True,
    ).reshape(block_rows, group_width)
    encoder_rows = encoder.shape[1]
    cross_max = (encoder_rows + halfway - 1 + 2 * halfway - 1) // (2 * halfway)
    padded_encoder = jnp.pad(
        encoder, ((0, 0), (0, cross_max * 2 * halfway + halfway - encoder_rows), (0, 0))
    )
    enc_low = prefix_below(query_places, ends, enc_lengths)
    enc_high = prefix_below(query_places, starts, enc_lengths) - 1
    cross_base = (enc_low.reshape(2, halfway)[:, 0] // halfway) * halfway
    cross_steps = (enc_high.reshape(2, halfway)[:, -1] + 1 - cross_base + 2 * halfway - 1) // (
        2 * halfway
    )
    cross_firsts = jnp.minimum(
        cross_base[:, None] + 2 * halfway * jnp.arange(cross_max, dtype=jnp.int32)[None, :],
        padded_encoder.shape[1] - 2 * halfway,
    )
    cross_sources = jnp.stack([cross_firsts, cross_firsts + halfway], axis=-1)
    crossed_group = flash(
        cross_query.reshape(2, halfway, group_width),
        enc_low.reshape(2, halfway, 1),
        enc_high.reshape(2, halfway, 1),
        padded_encoder[0],
        padded_encoder[1],
        cross_steps.astype(jnp.int32),
        cross_sources.reshape(-1).astype(jnp.int32),
        cross_firsts.reshape(-1).astype(jnp.int32),
        cross_max,
        group_heads,
    ).reshape(block_rows, group_width)
    exchanged = lax.all_to_all(
        crossed_group.reshape(group_size, rows_here, group_width), "head", 0, 0, tiled=True
    )
    crossed = exchanged.transpose(1, 0, 2).reshape(rows_here, model_width)
    summed = jnp.dot(crossed, w_co, preferred_element_type=jnp.float32)
    second = normalize(summed + hidden)
    second_b = second.astype(jnp.bfloat16)
    inner = jax.nn.gelu(
        jnp.dot(second_b, w_up, preferred_element_type=jnp.float32), approximate=False
    ).astype(jnp.bfloat16)
    output = normalize(jnp.dot(inner, w_down, preferred_element_type=jnp.float32) + second)
    output_b = output.astype(jnp.bfloat16)
    block_output = lax.all_gather(output_b, "head", axis=0, tiled=True)
    next_qkv = jnp.einsum("td,cde->cte", block_output, w_next, preferred_element_type=jnp.float32)
    return (output, cache, next_qkv)


def solution(mesh):
    ring = 4
    devices = mesh.devices.reshape(mesh.shape["blk"] // ring, ring, mesh.shape["head"])
    fine = jax.sharding.Mesh(devices, ("zy", "x", "head"))
    rows = ("zy", "x", "head")
    blocks = ("zy", "x")
    in_specs = (
        P(rows, None),
        P(),
        P(),
        P(),
        P(None, None, "head"),
        P("head", None),
        P(None, blocks, "head"),
        P(),
        P(),
        P(),
        P(),
        P(None, None, "head"),
    )
    out_specs = (P(rows, None), P(None, blocks, "head"), P(None, blocks, "head"))
    return jax.shard_map(
        on_device, mesh=fine, in_specs=in_specs, out_specs=out_specs, check_vma=False
    )
```
